32 devices in a mesh: pix: 8 (over z, y), ch: 4 (over x, core).
Axes of the slice: x: 2, y: 2, z: 4, core: 2. Of those that a mesh axis runs over, the one named last changes fastest.
Arguments:
- features: bfloat16 [64, 128, 2048], P('pix', None, 'ch'), may hold values from -6 to 6
- pixel_mask: int32 [64, 128], P('pix'), may hold values from 0 to 1, as said below
- reduce_weight: bfloat16 [2048, 512], P(None, 'ch'), may hold values from -0.125 to 0.125
- reduce_gain: float32 [512], P('ch'), may hold values from 0.5 to 1.5
- reduce_bias: float32 [512], P('ch'), may hold values from -1.5 to 1.5
- dilated_weight: bfloat16 [3, 3, 512, 512], P(None, None, 'ch'), may hold values from -0.09375 to 0.09375
- dilated_gain: float32 [512], P('ch'), may hold values from 0.5 to 1.5
- dilated_bias: float32 [512], P('ch'), may hold values from -1.5 to 1.5
- expand_weight: bfloat16 [512, 2048], P('ch'), may hold values from -0.25 to 0.25
- expand_gain: float32 [2048], P('ch'), may hold values from 0.5 to 1.5
- expand_bias: float32 [2048], P('ch'), may hold values from -1.5 to 1.5
- aspp_weight: bfloat16 [3, 3, 3, 2048, 256], P(None, None, None, 'ch'), may hold values from -0.046875 to 0.046875
- aspp_gain: float32 [3, 256], P(None, 'ch'), may hold values from 0.5 to 1.5
- aspp_bias: float32 [3, 256], P(None, 'ch'), may hold values from -1.5 to 1.5
- task_weight: bfloat16 [3, 256, 23], P(None, 'ch'), may hold values from -0.21875 to 0.21875
- cotangent: float32 [64, 128, 23], P('pix'), may hold values from -24 to 24
Outputs:
- predictions: float32 [64, 128, 23], P('pix')
- features_grad: bfloat16 [64, 128, 2048], P('pix', None, 'ch')
- reduce_weight_grad: float32 [2048, 512], P('pix', 'ch')
- reduce_gain_grad: float32 [512], P('ch')
- reduce_bias_grad: float32 [512], P('ch')
- dilated_weight_grad: float32 [3, 3, 512, 512], P(None, None, 'ch', 'pix')
- dilated_gain_grad: float32 [512], P('ch')
- dilated_bias_grad: float32 [512], P('ch')
- expand_weight_grad: float32 [512, 2048], P('ch', 'pix')
- expand_gain_grad: float32 [2048], P('ch')
- expand_bias_grad: float32 [2048], P('ch')
- aspp_weight_grad: float32 [3, 3, 3, 2048, 256], P(None, None, None, 'ch', 'pix')
- aspp_gain_grad: float32 [3, 256], P(None, 'ch')
- aspp_bias_grad: float32 [3, 256], P(None, 'ch')
- task_weight_grad: float32 [3, 256, 23], P(None, 'ch')
The draws below stay inside these ranges and needn't reach their ends.
Inputs may be any that keep to these rules, and one draw needn't show every extreme that they name: `pixel_mask`: each row holds padding; the share of image pixels rises from about 0.3 in the first rows to about 0.9 in the last.
All inputs are finite; a program needn't handle non-finite values.
Results may differ from the reference program's by a relative error of at most 0.025.
Values may be sent and summed in bfloat16 or wider, within the bound.
A program may use at most 256 MiB of HBM per device.

```python
import jax
import jax.numpy as jnp
from jax import lax

C_IN = 2048
MID = 512
ASPP = 256
CLS = 19
WIDTH = 128
HEIGHT = 64
OUTS = 23


def draw_pixel_mask(key, part):
    row_index = jnp.arange(HEIGHT)
    threshold = 300 + 600 * row_index // HEIGHT
    ticket = jax.random.randint(key, (HEIGHT, WIDTH), 0, 1000)
    return (ticket < threshold[:, None]).astype(jnp.int32)


def draw_cotangent(key, part):
    place = jnp.arange(HEIGHT).astype(jnp.float32) / HEIGHT
    columns = jnp.arange(OUTS)
    base = jnp.clip(jax.random.normal(key, (HEIGHT, WIDTH, OUTS), jnp.float32), -4.0, 4.0)
    top = 6.0
    rising = jnp.exp(jnp.log(top) * place)
    falling = jnp.exp(jnp.log(top) * (1.0 - place))
    segment_cols = (columns < CLS)[None, :]
    depth_cols = (columns == CLS)[None, :]
    factor = jnp.where(segment_cols, rising[:, None], jnp.where(depth_cols, falling[:, None], 1.0))
    return (base * factor[:, None, :]).astype(jnp.float32)


def block_levels(stream_key, dims, cuts, low, top_value):
    level = 1.0
    for dim, parts in cuts:
        draws = jax.random.uniform(jax.random.fold_in(jax.random.fold_in(stream_key, 6), dim), (parts,), jnp.float32, low / len(cuts), top_value / len(cuts))
        level = level * jnp.repeat(jnp.exp(draws), dims[dim] // parts).reshape((-1,) + (1,) * (len(dims) - 1 - dim))
    return level


def gaussian(own_key, extent, deviation, bound, split=(), kind=jnp.bfloat16):
    values = jax.random.normal(own_key, extent, jnp.float32) * deviation
    if len(split) > 0:
        values = block_levels(own_key, extent, split, -0.22, 0.18) * values
    return jnp.clip(values, min=-bound, max=bound).astype(kind)


def setup_inputs(seed: int = 0) -> dict:
    keys = jax.random.split(jax.random.key(seed), 17)
    features = gaussian(keys[0], (HEIGHT, WIDTH, C_IN), 1.0, 6.0, ((0, 8), (2, 4)))
    pixel_mask = draw_pixel_mask(jax.random.fold_in(keys[16], 71), 0)
    reduce_weight = gaussian(keys[2], (C_IN, MID), C_IN ** -0.5, 0.125, ((1, 4),))
    reduce_gain = jnp.clip(1.0 + 0.1 * jax.random.normal(keys[3], (MID,), jnp.float32), 0.5, 1.5)
    reduce_bias = gaussian(keys[4], (MID,), 0.3, 1.5, ((0, 4),), jnp.float32)
    dilated_weight = gaussian(keys[5], (3, 3, MID, MID), (9 * MID) ** -0.5, 0.09375, ((2, 4),))
    dilated_gain = jnp.clip(1.0 + 0.1 * jax.random.normal(keys[6], (MID,), jnp.float32), 0.5, 1.5)
    dilated_bias = gaussian(keys[7], (MID,), 0.3, 1.5, ((0, 4),), jnp.float32)
    expand_weight = gaussian(keys[8], (MID, C_IN), MID ** -0.5, 0.25, ((0, 4),))
    expand_gain = jnp.clip(1.0 + 0.1 * jax.random.normal(keys[9], (C_IN,), jnp.float32), 0.5, 1.5)
    expand_bias = gaussian(keys[10], (C_IN,), 0.3, 1.5, ((0, 4),), jnp.float32)
    aspp_weight = gaussian(keys[11], (3, 3, 3, C_IN, ASPP), (9 * C_IN) ** -0.5, 0.046875, ((3, 4),))
    aspp_gain = jnp.clip(1.0 + 0.1 * jax.random.normal(keys[12], (3, ASPP), jnp.float32), 0.5, 1.5)
    aspp_bias = gaussian(keys[13], (3, ASPP), 0.3, 1.5, ((1, 4),), jnp.float32)
    task_weight = gaussian(keys[14], (3, ASPP, OUTS), (3 * ASPP) ** -0.5, 0.21875, ((1, 4),))
    cotangent = draw_cotangent(jax.random.fold_in(keys[16], 71), 0)
    return {"features": features, "pixel_mask": pixel_mask, "reduce_weight": reduce_weight, "reduce_gain": reduce_gain, "reduce_bias": reduce_bias, "dilated_weight": dilated_weight, "dilated_gain": dilated_gain, "dilated_bias": dilated_bias, "expand_weight": expand_weight, "expand_gain": expand_gain, "expand_bias": expand_bias, "aspp_weight": aspp_weight, "aspp_gain": aspp_gain, "aspp_bias": aspp_bias, "task_weight": task_weight, "cotangent": cotangent}


@jax.custom_vjp
def low(v):
    return lax.optimization_barrier(v.astype(jnp.bfloat16)).astype(jnp.float32)

@jax.custom_vjp
def low_back(v):
    return v

def low_keep(v):
    return (low(v), None)

def low_pass(kept, grad):
    return (grad,)

def back_keep(v):
    return (v, None)

def back_low(kept, grad):
    return (low(grad),)
low.defvjp(low_keep, low_pass)
low_back.defvjp(back_keep, back_low)
epsilon = 1e-05
highest = lax.Precision.HIGHEST
aspp_rates = (12, 24, 36)

def conv_same(value, kernel, rate):
    result = lax.conv_general_dilated(value[None], kernel, (1, 1), [(rate, rate), (rate, rate)], rhs_dilation=(rate, rate), dimension_numbers=('NHWC', 'HWIO', 'NHWC'), precision=highest)
    return result[0]

def normalize(hidden, weight):
    count = jnp.sum(weight)
    center = lax.optimization_barrier(jnp.sum(hidden * weight, axis=(0, 1))) / count
    variance = lax.optimization_barrier(jnp.sum(weight * (hidden - center) ** 2, axis=(0, 1))) / count
    return (hidden - center) * lax.rsqrt(variance + epsilon)

def task_scales(gram):
    norms = jnp.sqrt(jnp.diagonal(gram) + 1e-06)
    proj = gram / norms[None, :]
    vector = proj[0, 0] - proj[0, 1:]
    matrix = proj[0, 0] - proj[0, 1:][None, :] - proj[1:, 0][:, None] + proj[1:, 1:]
    determinant = matrix[0, 0] * matrix[1, 1] - matrix[0, 1] * matrix[1, 0]
    second = (vector[0] * matrix[1, 1] - vector[1] * matrix[1, 0]) / determinant
    third = (vector[1] * matrix[0, 0] - vector[0] * matrix[0, 1]) / determinant
    return jnp.stack([1.0 - second - third, second, third])

def reference(features, pixel_mask, reduce_weight, reduce_gain, reduce_bias, dilated_weight, dilated_gain, dilated_bias, expand_weight, expand_gain, expand_bias, aspp_weight, aspp_gain, aspp_bias, task_weight, cotangent):
    valid = pixel_mask.astype(jnp.float32)
    plane = valid[:, :, None]
    branch_mask = valid[:, :, None, None]

    def trunk(inputs, weight_one, gain_one, bias_one, weight_two, gain_two, bias_two, weight_three, gain_three, bias_three, weight_aspp, gain_aspp, bias_aspp):
        masked = inputs * plane
        hidden_one = low_back(jnp.einsum('hwc,cd->hwd', masked, weight_one, precision=highest))
        act_one = low(jax.nn.silu(normalize(hidden_one, plane) * gain_one + bias_one) * plane)
        hidden_two = low_back(conv_same(act_one, weight_two, 2))
        act_two = low(jax.nn.silu(normalize(hidden_two, plane) * gain_two + bias_two) * plane)
        hidden_three = low_back(jnp.einsum('hwd,dc->hwc', act_two, weight_three, precision=highest))
        trunk_out = low(jax.nn.silu(normalize(hidden_three, plane) * gain_three + bias_three + masked) * plane)
        branch_sum = low_back(jnp.stack([conv_same(trunk_out, weight_aspp[j], aspp_rates[j]) for j in range(3)], axis=2))
        return jax.nn.silu(normalize(branch_sum, branch_mask) * gain_aspp + bias_aspp) * branch_mask

    def heads(branch_out, weight_task):
        return jnp.einsum('hwjc,jco->hwo', low(branch_out), weight_task, precision=highest)
    params = (features.astype(jnp.float32), reduce_weight.astype(jnp.float32), reduce_gain, reduce_bias, dilated_weight.astype(jnp.float32), dilated_gain, dilated_bias, expand_weight.astype(jnp.float32), expand_gain, expand_bias, aspp_weight.astype(jnp.float32), aspp_gain, aspp_bias)
    branch_out, trunk_back = jax.vjp(trunk, *params)
    predictions, heads_back = jax.vjp(heads, branch_out, task_weight.astype(jnp.float32))
    target = cotangent * plane
    columns = jnp.arange(OUTS)
    task_of = (columns >= CLS).astype(jnp.int32) + (columns >= CLS + 1).astype(jnp.int32)
    select = (task_of[:, None] == jnp.arange(3)[None, :]).astype(jnp.float32)
    task_grads = jnp.stack([heads_back(target * select[:, t])[0] for t in range(3)])
    task_weight_grad = heads_back(target)[1]
    gram = jnp.einsum('thwjc,shwjc->ts', task_grads, task_grads, precision=highest)
    scales = task_scales(gram)
    branch_grad = jnp.einsum('t,thwjc->hwjc', scales, task_grads, precision=highest)
    grads = trunk_back(branch_grad)
    return (predictions, grads[0].astype(jnp.bfloat16), grads[1], grads[2], grads[3], grads[4], grads[5], grads[6], grads[7], grads[8], grads[9], grads[10], grads[11], grads[12], task_weight_grad)
```

```python
import jax
import jax.numpy as jnp
from jax import lax
from jax.experimental import pallas as pl
from jax.experimental.pallas import tpu as pltpu
from jax.sharding import PartitionSpec as P

CLS = 19


epsilon = 1e-05
highest = lax.Precision.HIGHEST
aspp_rates = (12, 24, 36)
inner_rate = 2


def from_behind(value, axis, steps):
    count = lax.axis_size(axis)
    first, last = (max(0, -steps), min(count, count - steps))
    return lax.ppermute(value, axis, [(source, source + steps) for source in range(first, last)])


def with_halo(shard, sides, width):
    for axis, dim in sides:
        devices, length = (lax.axis_size(axis), shard.shape[dim])
        up = [(i, (i + 1) % devices) for i in range(devices - 1)]
        down = [(j, i) for i, j in up]
        last = lax.slice_in_dim(shard, length - width, length, axis=dim)
        first = lax.slice_in_dim(shard, 0, width, axis=dim)
        before = lax.ppermute(last, axis, up)
        after = lax.ppermute(first, axis, down)
        shard = jnp.concatenate([before, shard, after], axis=dim)
    return shard


def silu_slope(value):
    sigma = jax.nn.sigmoid(value)
    return sigma * (1.0 + value * (1.0 - sigma))


def shift_cols(value, offset):
    if offset == 0:
        return value
    margin = abs(offset)
    widths = [(0, 0)] * value.ndim
    widths[1] = (margin, margin)
    padded = jnp.pad(value, widths)
    return lax.slice_in_dim(padded, margin + offset, margin + offset + value.shape[1], axis=1)


def moved(piece, distance):
    return from_behind(piece, "pix", -distance)


def shift_rows(value, offset):
    if offset == 0:
        return value
    steps_over, inner = divmod(offset, value.shape[0])
    first = moved(value, steps_over)[inner:]
    if inner == 0:
        return first
    second = moved(value, steps_over + 1)[:inner]
    return jnp.concatenate([first, second], axis=0)


def halo_rows(value):
    return with_halo(value, (("pix", 0),), inner_rate)


def gather_channels(value):
    return lax.all_gather(value, "ch", axis=1, tiled=True)


def sum_channels(value):
    return lax.psum_scatter(
        value.astype(jnp.bfloat16), "ch", scatter_dimension=1, tiled=True
    ).astype(jnp.float32)


def normalized(hidden, valid, axes):
    total, count = lax.psum(
        (jnp.sum(hidden * valid, axis=axes, keepdims=True), jnp.sum(valid)), "pix"
    )
    center = total / count
    spread_sum = lax.psum(jnp.sum(valid * (hidden - center) ** 2, axis=axes, keepdims=True), "pix")
    variance = spread_sum / count
    scale = lax.rsqrt(variance + epsilon)
    return ((hidden - center) * scale, scale, count)


def norm_grad(grad_out, centered, scale, gain, count, valid, axes):
    sum_out, sum_cross = lax.psum(
        (
            jnp.sum(grad_out, axis=axes, keepdims=True),
            jnp.sum(grad_out * centered, axis=axes, keepdims=True),
        ),
        "pix",
    )
    grad_in = gain * scale * (grad_out - valid * (sum_out + centered * sum_cross) / count)
    return (grad_in, sum_cross, sum_out)


def task_scales(gram):
    norms = jnp.sqrt(jnp.diagonal(gram) + 1e-06)
    proj = gram / norms[None, :]
    vector = proj[0, 0] - proj[0, 1:]
    matrix = proj[0, 0] - proj[0, 1:][None, :] - proj[1:, 0][:, None] + proj[1:, 1:]
    determinant = matrix[0, 0] * matrix[1, 1] - matrix[0, 1] * matrix[1, 0]
    second = (vector[0] * matrix[1, 1] - vector[1] * matrix[1, 0]) / determinant
    third = (vector[1] * matrix[0, 0] - vector[0] * matrix[0, 1]) / determinant
    return jnp.stack([1.0 - second - third, second, third])


def on_device(
    features,
    pixel_mask,
    reduce_weight,
    reduce_gain,
    reduce_bias,
    dilated_weight,
    dilated_gain,
    dilated_bias,
    expand_weight,
    expand_gain,
    expand_bias,
    aspp_weight,
    aspp_gain,
    aspp_bias,
    task_weight,
    cotangent,
):
    rows_here, width, local_in = features.shape
    pixels = rows_here * width
    local_mid = reduce_weight.shape[1]
    full_mid = dilated_weight.shape[3]
    branch_width = aspp_weight.shape[4]
    outs_count = task_weight.shape[2]
    valid = pixel_mask.astype(jnp.float32).reshape(pixels, 1)
    valid_branch = valid[None]
    masked = features.reshape(pixels, local_in) * valid.astype(jnp.bfloat16)
    inputs_full = gather_channels(masked)
    hidden_one = jnp.dot(inputs_full, reduce_weight, preferred_element_type=jnp.float32)
    norm_one, scale_one, count = normalized(hidden_one, valid, (0,))
    pre_one = norm_one * reduce_gain + reduce_bias
    act_one = (jax.nn.silu(pre_one) * valid).astype(jnp.bfloat16)
    padded_one = halo_rows(act_one.reshape(rows_here, width, local_mid))
    partial_value = jnp.zeros((pixels, full_mid), jnp.float32)
    for a in range(3):
        for b in range(3):
            shifted = shift_cols(padded_one[2 * a : 2 * a + rows_here], (b - 1) * inner_rate)
            partial_value = partial_value + jnp.dot(
                shifted.reshape(pixels, local_mid),
                dilated_weight[a, b],
                preferred_element_type=jnp.float32,
            )
    hidden_two = sum_channels(partial_value)
    norm_two, scale_two, _ = normalized(hidden_two, valid, (0,))
    pre_two = norm_two * dilated_gain + dilated_bias
    act_two = (jax.nn.silu(pre_two) * valid).astype(jnp.bfloat16)
    hidden_three = sum_channels(jnp.dot(act_two, expand_weight, preferred_element_type=jnp.float32))
    norm_three, scale_three, _ = normalized(hidden_three, valid, (0,))
    pre_three = norm_three * expand_gain + expand_bias + masked.astype(jnp.float32)
    trunk_out = (
        (jax.nn.silu(pre_three) * valid).astype(jnp.bfloat16).reshape(rows_here, width, local_in)
    )
    kept_rows = []
    partials = []
    for j in range(3):
        rate = aspp_rates[j]
        running = jnp.zeros((pixels, branch_width), jnp.float32)
        shifted_rows = []
        for a in range(3):
            row_shift = shift_rows(trunk_out, (a - 1) * rate)
            shifted_rows.append(row_shift)
            for b in range(3):
                shifted = shift_cols(row_shift, (b - 1) * rate)
                running = running + jnp.dot(
                    shifted.reshape(pixels, local_in),
                    aspp_weight[j, a, b],
                    preferred_element_type=jnp.float32,
                )
        kept_rows.append(shifted_rows)
        partials.append(running)
    branch_sum = sum_channels(jnp.stack(partials).reshape(3 * pixels, branch_width)).reshape(
        3, pixels, -1
    )
    branch_gain = aspp_gain[:, None, :]
    norm_branch, scale_branch, _ = normalized(branch_sum, valid_branch, (1,))
    pre_branch = norm_branch * branch_gain + aspp_bias[:, None, :]
    branch_out = (jax.nn.silu(pre_branch) * valid_branch).astype(jnp.bfloat16)
    predictions = lax.psum(
        jnp.einsum(
            "jpc,jco->po", branch_out, task_weight, preferred_element_type=jnp.float32
        ).astype(jnp.bfloat16),
        "ch",
    ).astype(jnp.float32)
    columns = jnp.arange(outs_count)
    task_of = (columns >= CLS).astype(jnp.int32) + (columns >= CLS + 1).astype(jnp.int32)
    select = (task_of[:, None] == jnp.arange(3)[None, :]).astype(jnp.float32)
    target = cotangent.reshape(pixels, outs_count) * valid
    task_float = task_weight.astype(jnp.float32)
    task_grads = jnp.einsum("po,ot,jco->tjpc", target, select, task_float, precision=highest)
    gram = lax.psum(
        jnp.einsum("tjpc,sjpc->ts", task_grads, task_grads, precision=highest), ("pix", "ch")
    )
    scales = task_scales(gram)
    branch_grad = jnp.einsum("t,tjpc->jpc", scales, task_grads, precision=highest)
    task_weight_grad = lax.psum(
        jnp.einsum("jpc,po->jco", branch_out.astype(jnp.float32), target, precision=highest), "pix"
    )
    grad_pre_branch = branch_grad * valid_branch * silu_slope(pre_branch)
    grad_branch, aspp_gain_grad, aspp_bias_grad = norm_grad(
        grad_pre_branch, norm_branch, scale_branch, branch_gain, count, valid_branch, (1,)
    )
    grad_full = gather_channels(grad_branch.astype(jnp.bfloat16).reshape(3 * pixels, -1)).reshape(
        3, rows_here, width, -1
    )
    grad_trunk = jnp.zeros((pixels, local_in), jnp.float32)
    aspp_list = []
    for j in range(3):
        rate = aspp_rates[j]
        grad_flat = grad_full[j].reshape(pixels, -1)
        per_row = []
        for a in range(3):
            back_rows = shift_rows(grad_full[j], -(a - 1) * rate)
            per_col = []
            for b in range(3):
                shifted = shift_cols(back_rows, -(b - 1) * rate)
                grad_trunk = grad_trunk + jnp.einsum(
                    "pa,ca->pc",
                    shifted.reshape(pixels, -1),
                    aspp_weight[j, a, b],
                    preferred_element_type=jnp.float32,
                )
                forward_tap = shift_cols(kept_rows[j][a], (b - 1) * rate).reshape(pixels, local_in)
                per_col.append(
                    jnp.einsum(
                        "pc,pa->ca", forward_tap, grad_flat, preferred_element_type=jnp.float32
                    )
                )
            per_row.append(jnp.stack(per_col))
        aspp_list.append(jnp.stack(per_row))
    aspp_weight_local = jnp.stack(aspp_list)
    grad_pre_three = grad_trunk * valid * silu_slope(pre_three)
    grad_three, expand_gain_grad, expand_bias_grad = norm_grad(
        grad_pre_three, norm_three, scale_three, expand_gain, count, valid, (0,)
    )
    grad_three_full = gather_channels(grad_three.astype(jnp.bfloat16))
    grad_act_two = jnp.einsum(
        "pc,dc->pd", grad_three_full, expand_weight, preferred_element_type=jnp.float32
    )
    expand_weight_local = jnp.einsum(
        "pd,pc->dc", act_two, grad_three_full, preferred_element_type=jnp.float32
    )
    grad_pre_two = grad_act_two * valid * silu_slope(pre_two)
    grad_two, dilated_gain_grad, dilated_bias_grad = norm_grad(
        grad_pre_two, norm_two, scale_two, dilated_gain, count, valid, (0,)
    )
    grad_two_full = gather_channels(grad_two.astype(jnp.bfloat16))
    padded_grad = halo_rows(grad_two_full.reshape(rows_here, width, full_mid))
    grad_act_one = jnp.zeros((pixels, local_mid), jnp.float32)
    dilated_rows = []
    for a in range(3):
        dilated_cols = []
        for b in range(3):
            shifted = shift_cols(
                padded_grad[4 - 2 * a : 4 - 2 * a + rows_here], -(b - 1) * inner_rate
            )
            grad_act_one = grad_act_one + jnp.einsum(
                "pe,de->pd",
                shifted.reshape(pixels, full_mid),
                dilated_weight[a, b],
                preferred_element_type=jnp.float32,
            )
            forward_tap = shift_cols(
                padded_one[2 * a : 2 * a + rows_here], (b - 1) * inner_rate
            ).reshape(pixels, local_mid)
            dilated_cols.append(
                jnp.einsum(
                    "pd,pe->de", forward_tap, grad_two_full, preferred_element_type=jnp.float32
                )
            )
        dilated_rows.append(jnp.stack(dilated_cols))
    dilated_weight_local = jnp.stack(dilated_rows)
    grad_pre_one = grad_act_one * valid * silu_slope(pre_one)
    grad_one, reduce_gain_grad, reduce_bias_grad = norm_grad(
        grad_pre_one, norm_one, scale_one, reduce_gain, count, valid, (0,)
    )
    grad_one_low = grad_one.astype(jnp.bfloat16)
    input_sum = sum_channels(
        jnp.einsum("pd,cd->pc", grad_one_low, reduce_weight, preferred_element_type=jnp.float32)
    )
    features_grad = (
        ((input_sum + grad_pre_three) * valid)
        .astype(jnp.bfloat16)
        .reshape(rows_here, width, local_in)
    )
    reduce_weight_local = jnp.einsum(
        "pc,pd->cd", inputs_full, grad_one_low, preferred_element_type=jnp.float32
    )
    reduce_weight_grad, dilated_weight_grad, expand_weight_grad, aspp_weight_grad = (
        lax.psum_scatter(reduce_weight_local, "pix", scatter_dimension=0, tiled=True),
        lax.psum_scatter(dilated_weight_local, "pix", scatter_dimension=3, tiled=True),
        lax.psum_scatter(expand_weight_local, "pix", scatter_dimension=1, tiled=True),
        lax.psum_scatter(aspp_weight_local, "pix", scatter_dimension=4, tiled=True),
    )
    return (
        predictions.reshape(rows_here, width, outs_count),
        features_grad,
        reduce_weight_grad,
        reduce_gain_grad.reshape(-1),
        reduce_bias_grad.reshape(-1),
        dilated_weight_grad,
        dilated_gain_grad.reshape(-1),
        dilated_bias_grad.reshape(-1),
        expand_weight_grad,
        expand_gain_grad.reshape(-1),
        expand_bias_grad.reshape(-1),
        aspp_weight_grad,
        aspp_gain_grad.reshape(3, -1),
        aspp_bias_grad.reshape(3, -1),
        task_weight_grad,
    )


MESH = pl.DeviceIdType.MESH
ROW_CLASSES, COL_CLASSES = 2, 4
PHASES = ROW_CLASSES * COL_CLASSES
SPLIT = 4
FAR_FIRST = (6, 7, 4, 5, 2, 3, 1)
f32, bf16 = jnp.float32, jnp.bfloat16
VMEM_BYTES = 60 << 20


def shape(dims, dtype):
    return jax.ShapeDtypeStruct(dims, dtype)


def call(name, cid, kernel, arrays, outs, scratch):
    vmem = pl.BlockSpec(memory_space=pltpu.VMEM)
    return pl.pallas_call(
        kernel,
        out_shape=outs,
        in_specs=[vmem] * len(arrays),
        out_specs=[vmem] * len(outs),
        scratch_shapes=scratch,
        compiler_params=pltpu.CompilerParams(
            collective_id=cid, has_side_effects=True, vmem_limit_bytes=VMEM_BYTES
        ),
        name=name,
    )(*arrays)


def dma(*dims):
    return pltpu.SemaphoreType.DMA(dims)


def greet(ch, pix):
    p, c = lax.axis_index("pix"), lax.axis_index("ch")
    barrier = pltpu.get_barrier_semaphore()
    for k in ch:
        pl.semaphore_signal(barrier, inc=1, device_id=(p, c ^ k), device_id_type=MESH)
    for k in pix:
        pl.semaphore_signal(barrier, inc=1, device_id=(p ^ k, c), device_id_type=MESH)
    return barrier, len(ch) + len(pix)


def push(src, dst, send, recv, device):
    copy = pltpu.make_async_remote_copy(
        src_ref=src,
        dst_ref=dst,
        send_sem=send,
        recv_sem=recv,
        device_id=device,
        device_id_type=MESH,
    )
    copy.start()
    return copy


def keep(src, dst, sem):
    copy = pltpu.make_async_copy(src, dst, sem)
    copy.start()
    return copy


def rows(start, size):
    return pl.ds(pl.multiple_of(start, size), size)


def fold(x):
    return jnp.sum(x.reshape(x.shape[0] // 8, 8, x.shape[1]), axis=0)


def total(x):
    return jnp.sum(x, axis=0, keepdims=True)


def loop(steps, body, init):
    return lax.fori_loop(0, steps, body, init)


def sum_over_ch(part, tile, tiles, own, out, near, cross, near_sems, far_sems):
    p, c = lax.axis_index("pix"), lax.axis_index("ch")
    k, x = lax.rem(c, 2), c // 2
    n = own.shape[2]
    copies = []
    for t in range(tiles):
        at = pl.ds(t * tile, tile)
        value = part(t)
        for d in range(SPLIT):
            block = value[:, d * n : (d + 1) * n]
            own[d, at] = block
            out[d, at] = block.astype(bf16)
        copies.append(
            [
                push(
                    out.at[2 * h + 1 - k, at],
                    near.at[h, at],
                    near_sems.at[0, t, h],
                    near_sems.at[1, t, h],
                    (p, c ^ 1),
                )
                for h in range(2)
            ]
        )
    crossing = []
    for t in range(tiles):
        at = pl.ds(t * tile, tile)
        for copy in copies[t]:
            copy.wait()
        cross[0, at] = (own[2 * (1 - x) + k, at] + near[1 - x, at].astype(f32)).astype(bf16)
        crossing.append(
            push(cross.at[0, at], cross.at[1, at], far_sems.at[0, t], far_sems.at[1, t], (p, c ^ 2))
        )

    def result(t):
        at = pl.ds(t * tile, tile)
        crossing[t].wait()
        return own[2 * x + k, at] + near[x, at].astype(f32) + cross[1, at].astype(f32)

    return result


def sum_scratch(pixels, n, tiles):
    return [
        pltpu.VMEM((SPLIT, pixels, n), f32),
        pltpu.VMEM((SPLIT, pixels, n), bf16),
        pltpu.VMEM((2, pixels, n), bf16),
        pltpu.VMEM((2, pixels, n), bf16),
        dma(2, tiles, 2),
        dma(2, tiles),
    ]


def pix_exchange(send, recv, sems):
    p, c = lax.axis_index("pix"), lax.axis_index("ch")
    copies = [
        push(send, recv.at[p], sems.at[0, k], sems.at[1, k], (p ^ k, c)) for k in FAR_FIRST
    ]
    recv[p] = send[...]
    for copy in copies:
        copy.wait()


def norm_stats(hidden, valid, pixels, send, recv, sems):
    n = hidden.shape[1]
    tile = 128
    repeat = n // 128

    def mask(at):
        v = valid[at]
        return v if repeat == 1 else jnp.concatenate([v] * repeat, axis=1)

    def first(i, carry):
        at = rows(i * tile, tile)
        v = mask(at)
        return carry[0] + fold(hidden[at] * v), carry[1] + fold(v)

    zero = jnp.zeros((8, n), f32)
    sums, count = loop(pixels // tile, first, (zero, zero))
    sums, count = total(sums), total(count)
    center = sums / jnp.maximum(count, 1.0)

    def second(i, carry):
        at = rows(i * tile, tile)
        apart = hidden[at] - center
        return carry + fold(mask(at) * apart * apart)

    spread = total(loop(pixels // tile, second, zero))
    send[0:1] = sums
    send[1:2] = spread
    send[2:3] = count
    pix_exchange(send, recv, sems)
    return join(recv, PHASES)


def join(recv, parts):
    sums, count = recv[0, 0:1], recv[0, 2:3]
    for i in range(1, parts):
        sums, count = sums + recv[i, 0:1], count + recv[i, 2:3]
    center = sums / count
    spread = jnp.zeros_like(sums)
    for i in range(parts):
        n = recv[i, 2:3]
        apart = recv[i, 0:1] / jnp.maximum(n, 1.0) - center
        spread = spread + recv[i, 1:2] + n * apart * apart
    return center, lax.rsqrt(spread / count + epsilon), count


def stat_scratch(n):
    return [pltpu.VMEM((8, n), f32), pltpu.VMEM((PHASES, 8, n), f32), dma(2, PHASES)]


def silu(x):
    return x / (1.0 + jnp.exp(-x))


def gather_over_ch(full, n, tile, tiles, near_sems, far_sems, hop_sems, ready):
    p, c = lax.axis_index("pix"), lax.axis_index("ch")

    def part(owner, t):
        return full.at[pl.ds(t * tile, tile), rows(owner * n, n)]

    near, far, hops = [], [], []
    for t in range(tiles):
        ready(t)
        src = part(c, t)
        far.append(push(src, src, far_sems.at[0, t], far_sems.at[1, t], (p, c ^ 2)))
        near.append(push(src, src, near_sems.at[0, t], near_sems.at[1, t], (p, c ^ 1)))
    for t in range(tiles):
        far[t].wait_recv()
        src = part(c ^ 2, t)
        hops.append(push(src, src, hop_sems.at[0, t], hop_sems.at[1, t], (p, c ^ 1)))
    for t in range(tiles):
        far[t].wait_send()
        near[t].wait()
        hops[t].wait()


def gather_scratch(tiles):
    return [dma(2, tiles), dma(2, tiles), dma(2, tiles)]


def to_classes(x):
    rows, cols, n = x.shape
    x = x.reshape(rows // ROW_CLASSES, ROW_CLASSES, cols // COL_CLASSES, COL_CLASSES, n)
    return x.transpose(1, 3, 0, 2, 4).reshape(PHASES, -1, n)


def from_classes(x, rows, cols):
    n = x.shape[-1]
    x = x.reshape(ROW_CLASSES, COL_CLASSES, rows // ROW_CLASSES, cols // COL_CLASSES, n)
    return x.transpose(2, 0, 3, 1, 4).reshape(rows, cols, n)


TILES = 4


def stage_one(feat, valid, weight, expand, affine, heads, targets, square, *refs):
    (masked, reduce_rows, expand_cols, heads_all, targets_all, square_all, norm, padded, stat) = refs[:9]
    (wide, hidden, own, out, near, cross, near_sems, far_sems, send, recv, stat_sems) = refs[9:20]
    (weight_sems, pix_sems, local_sems, halo_sems) = refs[20:]
    p, c = lax.axis_index("pix"), lax.axis_index("ch")
    pixels, local_in = feat.shape
    local_mid = weight.shape[1]
    tile = pixels // TILES
    barrier, expected = greet((1, 2, 3), FAR_FIRST)
    for r in range(8):
        for g in range(local_in // 128):
            lanes = slice(g * 128, (g + 1) * 128)
            wide[g] = feat[r * 128 : (r + 1) * 128, lanes].astype(f32)
            for b in range(COL_CLASSES):
                block = ((r % ROW_CLASSES) * COL_CLASSES + b) * 128 + (r // ROW_CLASSES) * 32
                value = wide[g, pl.ds(b, 32, stride=COL_CLASSES), :] * valid[block : block + 32]
                masked[block : block + 32, lanes] = value.astype(bf16)
    pl.semaphore_wait(barrier, expected)

    def pieces(to):
        return (
            (weight.at[rows(to * local_in, local_in), :], reduce_rows.at[:, rows(c * local_mid, local_mid)]),
            (expand.at[:, rows(to * local_in, local_in)], expand_cols.at[rows(c * local_mid, local_mid), :]),
            (heads, heads_all.at[c]),
        )

    copies = [
        [push(*pieces(c ^ k)[i], weight_sems.at[0, k, i], weight_sems.at[1, k, i], (p, c ^ k)) for k in (2, 3, 1)]
        for i in range(3)
    ]
    local = [keep(*pieces(c)[i], local_sems.at[i]) for i in range(3)]
    local.append(keep(targets.at[p], targets_all.at[p], local_sems.at[3]))
    local.append(keep(square, square_all.at[p], local_sems.at[4]))
    routed = [
        push(targets.at[p ^ k], targets_all.at[p], pix_sems.at[0, k, 0], pix_sems.at[1, k, 0], (p ^ k, c))
        for k in FAR_FIRST
    ] + [push(square, square_all.at[p], pix_sems.at[0, k, 1], pix_sems.at[1, k, 1], (p ^ k, c)) for k in FAR_FIRST]
    for copy in copies[0]:
        copy.wait()
    local[0].wait()

    def part(t):
        return jnp.dot(masked[t * tile : (t + 1) * tile], reduce_rows[...], preferred_element_type=f32)

    result = sum_over_ch(part, tile, TILES, own, out, near, cross, near_sems, far_sems)
    for t in range(TILES):
        hidden[t * tile : (t + 1) * tile] = result(t)
    for copy in routed + copies[1] + copies[2] + local[1:]:
        copy.wait()
    center, scale, count = norm_stats(hidden, valid, pixels, send, recv, stat_sems)
    stat[0:1] = center
    stat[1:2] = scale
    stat[2:3] = count
    for i in range(PHASES):
        at = pl.ds(i * 128, 128)
        value = (hidden[at] - center) * scale
        norm[at] = value
        act = silu(value * affine[0:1] + affine[1:2]) * valid[at]
        padded[i, 1:5] = act.astype(bf16).reshape(4, 32, local_mid)
    up = lambda: pltpu.make_async_remote_copy(
        src_ref=padded.at[:, 4],
        dst_ref=padded.at[:, 0],
        send_sem=halo_sems.at[0, 0],
        recv_sem=halo_sems.at[1, 0],
        device_id=(p + 1, c),
        device_id_type=MESH,
    )
    down = lambda: pltpu.make_async_remote_copy(
        src_ref=padded.at[:, 1],
        dst_ref=padded.at[:, 5],
        send_sem=halo_sems.at[0, 1],
        recv_sem=halo_sems.at[1, 1],
        device_id=(p - 1, c),
        device_id_type=MESH,
    )
    first, last = p == 0, p == PHASES - 1

    @pl.when(jnp.logical_not(last))
    def _():
        up().start()

    @pl.when(jnp.logical_not(first))
    def _():
        down().start()

    @pl.when(last)
    def _():
        padded[:, 5] = jnp.zeros((PHASES, 32, local_mid), bf16)

    @pl.when(first)
    def _():
        padded[:, 0] = jnp.zeros((PHASES, 32, local_mid), bf16)

    @pl.when(jnp.logical_not(last))
    def _():
        up().wait_send()
        down().wait_recv()

    @pl.when(jnp.logical_not(first))
    def _():
        down().wait_send()
        up().wait_recv()


def run_stage_one(cid, feat, valid, weight, expand, affine, heads, targets, square):
    pixels, local_in = feat.shape
    local_mid = weight.shape[1]
    mid = SPLIT * local_mid
    outs = [
        shape((pixels, local_in), bf16),
        shape((local_in, mid), bf16),
        shape((mid, local_in), bf16),
        shape((SPLIT,) + heads.shape, f32),
        shape(targets.shape, f32),
        shape((PHASES,) + square.shape, f32),
        shape((pixels, local_mid), f32),
        shape((PHASES, 6, 32, local_mid), bf16),
        shape((8, local_mid), f32),
    ]
    scratch = (
        [pltpu.VMEM((local_in // 128, 128, 128), f32), pltpu.VMEM((pixels, local_mid), f32)]
        + sum_scratch(pixels, local_mid, TILES)
        + stat_scratch(local_mid)
        + [dma(2, SPLIT, 3), dma(2, PHASES, 2), dma(5), dma(2, 2)]
    )
    return call("stage_one", cid, stage_one, [feat, valid, weight, expand, affine, heads, targets, square], outs, scratch)


def stage_two(padded, valid, weight, affine, *refs):
    (norm, full, taps, stat) = refs[:4]
    (hidden, own, out, near, cross, near_sems, far_sems, send, recv, stat_sems) = refs[4:14]
    (g_near, g_far, g_hop) = refs[14:]
    p, c = lax.axis_index("pix"), lax.axis_index("ch")
    pixels = valid.shape[0]
    local_mid = padded.shape[3]
    tile = pixels // TILES
    barrier, expected = greet((1, 2), FAR_FIRST)
    place = lax.broadcasted_iota(jnp.int32, (192, local_mid), 0) % 32
    for i in range(PHASES):
        beta = i % COL_CLASSES
        plain = padded[i].reshape(192, local_mid)
        wide = plain.astype(f32)
        if beta >= 2:
            moved_by = jnp.where(place == 0, 0.0, pltpu.roll(wide, 1, 0)).astype(bf16)
        else:
            moved_by = jnp.where(place == 31, 0.0, pltpu.roll(wide, 191, 0)).astype(bf16)
        for a in range(3):
            at = slice(a * 32, a * 32 + 128)
            for b, other, value in (
                (1, beta, plain),
                (0, (beta + 2) % 4, moved_by if beta >= 2 else plain),
                (2, (beta + 2) % 4, plain if beta >= 2 else moved_by),
            ):
                to = (i - beta + other) * 128
                col = (a * 3 + b) * local_mid
                taps[to : to + 128, col : col + local_mid] = value[at]
    pl.semaphore_wait(barrier, expected)

    def part(t):
        return jnp.dot(taps[t * tile : (t + 1) * tile], weight[...], preferred_element_type=f32)

    result = sum_over_ch(part, tile, TILES, own, out, near, cross, near_sems, far_sems)
    for t in range(TILES):
        hidden[t * tile : (t + 1) * tile] = result(t)
    center, scale, count = norm_stats(hidden, valid, pixels, send, recv, stat_sems)
    stat[0:1] = center
    stat[1:2] = scale
    stat[2:3] = count

    def ready(t):
        for i in range(tile // 128):
            at = pl.ds(t * tile + i * 128, 128)
            value = (hidden[at] - center) * scale
            norm[at] = value
            act = silu(value * affine[0:1] + affine[1:2]) * valid[at]
            full[at, rows(c * local_mid, local_mid)] = act.astype(bf16)

    gather_over_ch(full, local_mid, tile, TILES, g_near, g_far, g_hop, ready)


def run_stage_two(cid, padded, valid, weight, affine):
    pixels, local_mid = valid.shape[0], padded.shape[3]
    outs = [
        shape((pixels, local_mid), f32),
        shape((pixels, SPLIT * local_mid), bf16),
        shape((pixels, 9 * local_mid), bf16),
        shape((8, local_mid), f32),
    ]
    scratch = (
        [pltpu.VMEM((pixels, local_mid), f32)]
        + sum_scratch(pixels, local_mid, TILES)
        + stat_scratch(local_mid)
        + gather_scratch(TILES)
    )
    return call("stage_two", cid, stage_two, [padded, valid, weight, affine], outs, scratch)


def stage_three(full, weight, masked, valid, affine, *refs):
    (norm, classes, stat) = refs[:3]
    (hidden, trunk, send, recv, stat_sems, class_sems, own_sem) = refs[3:]
    p, c = lax.axis_index("pix"), lax.axis_index("ch")
    pixels, n = masked.shape
    barrier, expected = greet((), FAR_FIRST)
    tile = pixels // TILES
    for t in range(TILES):
        at = pl.ds(t * tile, tile)
        hidden[at] = jnp.dot(full[at], weight[...], preferred_element_type=f32)
    pl.semaphore_wait(barrier, expected)
    center, scale, count = norm_stats(hidden, valid, pixels, send, recv, stat_sems)
    stat[0:1] = center
    stat[1:2] = scale
    stat[2:3] = count

    def finish(to):
        def half(i, carry):
            at = rows(to * 128 + i * 32, 32)
            value = (hidden[at] - center) * scale
            norm[at] = value
            pre = value * affine[0:1] + affine[1:2] + masked[at].astype(f32)
            v = valid[at]
            trunk[at] = (silu(pre) * jnp.concatenate([v] * (n // 128), axis=1)).astype(bf16)
            return carry

        loop(4, half, 0)

    copies = []
    for k in FAR_FIRST:
        to = p ^ k
        finish(to)
        copies.append(
            push(
                trunk.at[rows(to * 128, 128)],
                classes.at[rows(p * 128, 128)],
                class_sems.at[0, k],
                class_sems.at[1, k],
                (to, c),
            )
        )
    finish(p)
    copies.append(keep(trunk.at[rows(p * 128, 128)], classes.at[rows(p * 128, 128)], own_sem.at[0]))
    for copy in copies:
        copy.wait()


def run_stage_three(cid, full, weight, masked, valid, affine):
    pixels, n = masked.shape
    outs = [shape((pixels, n), f32), shape((pixels, n), bf16), shape((8, n), f32)]
    scratch = (
        [pltpu.VMEM((pixels, n), f32), pltpu.VMEM((pixels, n), bf16)]
        + stat_scratch(n)
        + [dma(2, PHASES), dma(1)]
    )
    return call("stage_three", cid, stage_three, [full, weight, masked, valid, affine], outs, scratch)


RATE_ROWS = tuple(rate // ROW_CLASSES for rate in aspp_rates)
RATE_COLS = tuple(rate // COL_CLASSES for rate in aspp_rates)


def load_pyramid(weight, wide, sems):
    m = weight.shape[4]
    return [
        [keep(weight.at[j, a, b], wide.at[3 * j + a, :, b * m : (b + 1) * m], sems.at[3 * j + a, b]) for b in range(3)]
        for j in range(3)
        for a in range(3)
    ]


def move_cols(x, by):
    place = lax.broadcasted_iota(jnp.int32, x.shape, 0) % 32
    rolled = pltpu.roll(x, by % x.shape[0], 0)
    return jnp.where(place < by, 0.0, rolled) if by > 0 else jnp.where(place >= 32 + by, 0.0, rolled)


def ch_exchange(send, recv, sems):
    p, c = lax.axis_index("pix"), lax.axis_index("ch")
    copies = [push(send, recv.at[c], sems.at[0, k], sems.at[1, k], (p, c ^ k)) for k in (2, 3, 1)]
    recv[c] = send[...]
    for copy in copies:
        copy.wait()


def add_up(recv, parts):
    value = recv[0]
    for i in range(1, parts):
        value = value + recv[i]
    return value


def task_vector(square, weights):
    product = square * weights
    row = lax.broadcasted_iota(jnp.int32, (32, 32), 0)
    col = lax.broadcasted_iota(jnp.int32, (32, 32), 1)

    def task(i):
        return (i >= CLS).astype(jnp.int32) + (i >= CLS + 1).astype(jnp.int32)

    def entry(t, s):
        return jnp.sum(
            jnp.sum(jnp.where((task(row) == t) & (task(col) == s), product, 0.0), axis=1, keepdims=True),
            axis=0,
            keepdims=True,
        )

    gram = [[entry(t, s) for s in range(3)] for t in range(3)]
    norms = [jnp.sqrt(gram[k][k] + 1e-06) for k in range(3)]
    proj = [[gram[i][k] / norms[k] for k in range(3)] for i in range(3)]
    vector = [proj[0][0] - proj[0][b] for b in (1, 2)]
    matrix = [[proj[0][0] - proj[0][b] - proj[a][0] + proj[a][b] for b in (1, 2)] for a in (1, 2)]
    determinant = matrix[0][0] * matrix[1][1] - matrix[0][1] * matrix[1][0]
    second = (vector[0] * matrix[1][1] - vector[1] * matrix[1][0]) / determinant
    third = (vector[1] * matrix[0][0] - vector[0] * matrix[0][1]) / determinant
    which = task(lax.broadcasted_iota(jnp.int32, (32, 1), 0))
    return jnp.where(which == 0, 1.0 - second - third, jnp.where(which == 1, second, third))


def slope(x):
    s = 1.0 / (1.0 + jnp.exp(-x))
    return s * (1.0 + x * (1.0 - s))


def pyramid(trunk, weight, affine, heads, targets, square, *refs):
    (full, predictions, head_grad, sums, other) = refs[:5]
    refs = refs[1:]
    (wide, sides, own, out, near, cross, hidden, pre, grad, branch) = refs[4:14]
    (s_send, s_ch, s_mid, s_pix, b_send, b_ch, b_mid, b_pix) = refs[14:22]
    (h_send, h_ch, h_mid, h_pix, h_sum, p_send, p_ch) = refs[22:29]
    (w_sems, near_sems, far_sems, ch_sems, pix_sems, g_near, g_far, g_hop, y_sems) = refs[29:]
    p, c = lax.axis_index("pix"), lax.axis_index("ch")
    k, x = lax.rem(c, 2), c // 2
    m = weight.shape[4]
    quarter = targets.shape[0] // SPLIT
    barrier, expected = greet((1, 2, 3), FAR_FIRST)
    loads = load_pyramid(weight, wide, w_sems)
    contract0 = (((0,), (0,)), ((), ()))
    contract1 = (((1,), (1,)), ((), ()))
    head = heads[...]
    scaled = head * task_vector(
        add_up(square, PHASES)[:, :32], lax.dot_general(head, head, contract1, precision=highest)
    )
    mine = rows(c * quarter, quarter)
    target, mask = targets[mine, :32], targets[mine, 32:33]
    grad[...] = jnp.dot(target, scaled, precision=highest) * mask
    pl.semaphore_wait(barrier, expected)
    to_other = push(trunk, other, y_sems.at[0], y_sems.at[1], (p ^ 1, c))

    copies = []
    for j in range(3):
        s, q = RATE_ROWS[j] * 32, RATE_COLS[j]
        for a in (1, 0, 2):
            for load in loads[3 * j + a]:
                load.wait()
            if a == 1:
                sides[...] = jnp.dot(trunk[...], wide[3 * j + 1], preferred_element_type=f32)
            elif a == 0:
                sides[s:] += jnp.dot(trunk[: 1024 - s], wide[3 * j], preferred_element_type=f32)
            else:
                sides[: 1024 - s] += jnp.dot(trunk[s:], wide[3 * j + 2], preferred_element_type=f32)
        for d in range(SPLIT):
            at = slice(d * quarter, (d + 1) * quarter)
            value = (
                sides[at, m : 2 * m]
                + move_cols(sides[at, :m], q)
                + move_cols(sides[at, 2 * m :], -q)
            )
            own[d, j] = value
            out[d, j] = value.astype(bf16)
        copies.append(
            [
                push(out.at[2 * h + 1 - k, j], near.at[h, j], near_sems.at[0, j, h], near_sems.at[1, j, h], (p, c ^ 1))
                for h in range(2)
            ]
        )
        if j > 0:
            copies[j - 1] = cross_chips(copies[j - 1], j - 1, own, near, cross, far_sems)
    copies[2] = cross_chips(copies[2], 2, own, near, cross, far_sems)
    count = total(jnp.broadcast_to(mask, (quarter, 128)))[:, :1]
    for j in range(3):
        copies[j].wait()
        value = own[2 * x + k, j] + near[x, j].astype(f32) + cross[1, j].astype(f32)
        at = slice(j * m, (j + 1) * m)
        hidden[:, at] = value
        first = total(value * mask)
        apart = value - first / jnp.maximum(count, 1.0)
        s_send[j : j + 1] = first
        s_send[3 + j : 4 + j] = total(apart * apart * mask)
    s_send[6:7] = jnp.broadcast_to(count, (1, m))
    s_send[7:8] = jnp.zeros((1, m), f32)

    def merge(recv, parts):
        number = recv[0, 6:7]
        for i in range(1, parts):
            number = number + recv[i, 6:7]
        whole, spread = recv[0, 0:3], recv[0, 3:6]
        for i in range(1, parts):
            whole, spread = whole + recv[i, 0:3], spread + recv[i, 3:6]
        center = whole / jnp.maximum(number, 1.0)
        for i in range(parts):
            n = recv[i, 6:7]
            apart = recv[i, 0:3] / jnp.maximum(n, 1.0) - center
            spread = spread + n * apart * apart
        return whole, spread, number

    ch_exchange(s_send, s_ch, ch_sems.at[0])
    whole, spread, number = merge(s_ch, SPLIT)
    s_mid[0:3] = whole
    s_mid[3:6] = spread
    s_mid[6:7] = number
    s_mid[7:8] = jnp.zeros((1, m), f32)
    pix_exchange(s_mid, s_pix, pix_sems.at[0])
    whole, spread, number = merge(s_pix, PHASES)
    center, scale = whole / number, lax.rsqrt(spread / number + epsilon)
    for j in range(3):
        at = slice(j * m, (j + 1) * m)
        norm = (hidden[:, at] - center[j : j + 1]) * scale[j : j + 1]
        hidden[:, at] = norm
        value = norm * affine[0:1, at] + affine[1:2, at]
        branch[:, at] = (silu(value) * mask).astype(bf16)
        back = grad[:, at] * slope(value)
        grad[:, at] = back
        b_send[j : j + 1] = total(back)
        b_send[3 + j : 4 + j] = total(back * norm)
    b_send[6:8] = jnp.zeros((2, m), f32)
    p_send[...] = lax.dot_general(
        head.astype(bf16), branch[...], contract1, preferred_element_type=f32
    )
    h_send[...] = lax.dot_general(
        target, branch[...].astype(f32), contract0, precision=highest, preferred_element_type=f32
    )
    background = [
        [push(p_send, p_ch.at[c], ch_sems.at[1, 0, i], ch_sems.at[1, 1, i], (p, c ^ i)) for i in (2, 3, 1)],
        [
            push(h_send.at[rows((c ^ i) * 8, 8)], h_ch.at[c], ch_sems.at[2, 0, i], ch_sems.at[2, 1, i], (p, c ^ i))
            for i in (2, 3, 1)
        ],
    ]
    p_ch[c] = p_send[...]
    h_ch[c] = h_send[rows(c * 8, 8)]
    ch_exchange(b_send, b_ch, ch_sems.at[3])
    b_mid[...] = add_up(b_ch, SPLIT)
    for copy in background[0] + background[1]:
        copy.wait()
    h_mid[...] = add_up(h_ch, SPLIT)
    sending = [
        push(b_mid, b_pix.at[p], pix_sems.at[1, 0, i], pix_sems.at[1, 1, i], (p ^ i, c)) for i in FAR_FIRST
    ]
    b_pix[p] = b_mid[...]

    def half(to):
        return p_ch.at[to // 2, :, rows(lax.rem(to, 2) * 128, 128)]

    background = [
        push(half(p ^ i), predictions.at[p], pix_sems.at[2, 0, i], pix_sems.at[2, 1, i], (p ^ i, c)) for i in FAR_FIRST
    ] + [push(h_mid, h_pix.at[p], pix_sems.at[3, 0, i], pix_sems.at[3, 1, i], (p ^ i, c)) for i in FAR_FIRST]
    predictions[p] = half(p)[...]
    h_pix[p] = h_mid[...]
    for copy in sending:
        copy.wait()
    summed = add_up(b_pix, PHASES)
    sums[...] = summed
    for j in range(3):
        at = slice(j * m, (j + 1) * m)
        value = grad[:, at] - mask * (summed[j : j + 1] + hidden[:, at] * summed[3 + j : 4 + j]) / number
        full[mine, at] = (affine[0:1, at] * scale[j : j + 1] * value).astype(bf16)
    far = push(full.at[mine], full.at[mine], g_far.at[0], g_far.at[1], (p, c ^ 2))
    by = push(full.at[mine], full.at[mine], g_near.at[0], g_near.at[1], (p, c ^ 1))
    for copy in background:
        copy.wait()
    own_rows = add_up(h_pix, PHASES)
    h_sum[...] = own_rows
    head_grad[rows(c * 8, 8)] = own_rows
    last = [
        push(h_sum, head_grad.at[rows(c * 8, 8)], ch_sems.at[4, 0, i], ch_sems.at[4, 1, i], (p, c ^ i))
        for i in (2, 3, 1)
    ]
    far.wait_recv()
    theirs = rows((c ^ 2) * quarter, quarter)
    hop = push(full.at[theirs], full.at[theirs], g_hop.at[0], g_hop.at[1], (p, c ^ 1))
    far.wait_send()
    by.wait()
    hop.wait()
    for copy in last:
        copy.wait()
    to_other.wait()


def cross_chips(near_copies, j, own, near, cross, sems):
    p, c = lax.axis_index("pix"), lax.axis_index("ch")
    k, x = lax.rem(c, 2), c // 2
    for copy in near_copies:
        copy.wait()
    cross[0, j] = (own[2 * (1 - x) + k, j] + near[1 - x, j].astype(f32)).astype(bf16)
    return push(cross.at[0, j], cross.at[1, j], sems.at[0, j], sems.at[1, j], (p, c ^ 2))


def run_pyramid(cid, trunk, weight, affine, heads, targets, square):
    pixels, n = trunk.shape
    m = weight.shape[4]
    quarter = pixels // SPLIT
    outs = [
        shape((pixels, 3 * m), bf16),
        shape((PHASES, 32, 128), f32),
        shape((32, 3 * m), f32),
        shape((8, m), f32),
        shape((pixels, n), bf16),
    ]
    small = [pltpu.VMEM((8, m), f32), pltpu.VMEM((SPLIT, 8, m), f32), pltpu.VMEM((8, m), f32), pltpu.VMEM((PHASES, 8, m), f32)]
    scratch = (
        [
            pltpu.VMEM((9, n, 3 * m), bf16),
            pltpu.VMEM((pixels, 3 * m), f32),
            pltpu.VMEM((SPLIT, 3, quarter, m), f32),
            pltpu.VMEM((SPLIT, 3, quarter, m), bf16),
            pltpu.VMEM((2, 3, quarter, m), bf16),
            pltpu.VMEM((2, 3, quarter, m), bf16),
            pltpu.VMEM((quarter, 3 * m), f32),
            pltpu.VMEM((8, 128), f32),
            pltpu.VMEM((quarter, 3 * m), f32),
            pltpu.VMEM((quarter, 3 * m), bf16),
        ]
        + small
        + small
        + [
            pltpu.VMEM((32, 3 * m), f32),
            pltpu.VMEM((SPLIT, 8, 3 * m), f32),
            pltpu.VMEM((8, 3 * m), f32),
            pltpu.VMEM((PHASES, 8, 3 * m), f32),
            pltpu.VMEM((8, 3 * m), f32),
            pltpu.VMEM((32, quarter), f32),
            pltpu.VMEM((SPLIT, 32, quarter), f32),
        ]
        + [dma(9, 3), dma(2, 3, 2), dma(2, 3), dma(5, 2, SPLIT), dma(4, 2, PHASES), dma(2), dma(2), dma(2), dma(2)]
    )
    vmem = pl.BlockSpec(memory_space=pltpu.VMEM)
    specs = [vmem] * 6
    specs[1] = pl.BlockSpec(memory_space=pl.ANY)
    return pl.pallas_call(
        pyramid,
        out_shape=outs,
        in_specs=specs,
        out_specs=[vmem] * len(outs),
        scratch_shapes=scratch,
        compiler_params=pltpu.CompilerParams(
            collective_id=cid, has_side_effects=True, vmem_limit_bytes=VMEM_BYTES
        ),
        name="pyramid",
    )(trunk, weight, affine, heads, targets, square)


def packed_sums(values, send):
    i = 0
    for value in values:
        for g in range(value.shape[1] // 128):
            send[i : i + 1] = value[:, g * 128 : (g + 1) * 128]
            i += 1


def unpacked_sums(recv, rows_each, count):
    out, i = [], 0
    for _ in range(count):
        parts = []
        for _ in range(rows_each):
            value = recv[0, i : i + 1]
            for d in range(1, PHASES):
                value = value + recv[d, i : i + 1]
            parts.append(value)
            i += 1
        out.append(parts[0] if rows_each == 1 else jnp.concatenate(parts, axis=1))
    return out


def spread_lanes(v, n):
    return v if n == 128 else jnp.concatenate([v] * (n // 128), axis=1)


def backward(
    grads, trunk, other, weight, norm3, masked, valid, expand, affine3, norm2, affine2, full2, taps, dilated,
    norm1, affine1, reduce_rows, stats1, stats2, stats3, *refs
):
    outs, scratch = refs[:8], refs[8:]
    (features_grad, aspp_parts, dilated_grad, expand_grad, reduce_grad, sums3_out, sums2_out, sums1_out) = outs
    (wide, moved, acc, dsend, drecv, tpad, picked, picked_in, turned, zsend, zown) = scratch[:11]
    (gp3, g3, own, out, near, cross, hidden, gp2, g2, prod, edges, g1) = scratch[11:23]
    gp1, lanes = gp2, own
    (st3, st3r, st2, st2r, st1, st1r, e_part, e_mid, e_sum, d_part, d_sum, r_part, r_mid, r_sum) = scratch[23:37]
    (w_sems, d_sems, y_sems, z_sems, near_sems, far_sems, st_sems, gn, gf, gh, gn1, gf1, gh1, edge_sems, ch_sems, pix_sems, own_sems) = scratch[37:]
    p, c = lax.axis_index("pix"), lax.axis_index("ch")
    y, z = lax.rem(p, 2), p // 2
    pixels, n = norm3.shape
    m = weight.shape[4]
    mid = norm2.shape[1]
    tile = pixels // TILES
    contract0 = (((0,), (0,)), ((), ()))
    contract1 = (((1,), (1,)), ((), ()))
    count = stats1[2:3, :1]
    barrier, expected = greet((1, 2, 3), FAR_FIRST)
    loads = load_pyramid(weight, wide, w_sems)

    row = lax.broadcasted_iota(jnp.int32, (m, m), 0)
    col = lax.broadcasted_iota(jnp.int32, (m, m), 1)
    source = (2 * ((col % 128) // 32) + col // 128) * 32 + col % 32
    pick = jnp.where(row == source, 1.0, 0.0).astype(bf16)
    for j in range(3):
        value = jnp.dot(grads[:, j * m : (j + 1) * m], pick, preferred_element_type=f32).astype(bf16)
        picked[0, j] = value[:, :128]
        picked[1, j] = value[:, 128:]
    pl.semaphore_wait(barrier, expected)
    sent_picks = push(picked.at[1 - y], picked_in, y_sems.at[0], y_sems.at[1], (p ^ 1, c))

    for j in range(3):
        q = RATE_COLS[j]
        plain = grads[:, j * m : (j + 1) * m]
        value = plain.astype(f32)
        moved[j, :, :m] = move_cols(value, -q).astype(bf16)
        moved[j, :, m : 2 * m] = plain
        moved[j, :, 2 * m :] = move_cols(value, q).astype(bf16)
    back = []
    for h in range(2):
        half = slice(h * m, (h + 1) * m)
        for j in range(3):
            s = RATE_ROWS[j] * 32
            for a in (1, 0, 2):
                if h == 0:
                    for load in loads[3 * j + a]:
                        load.wait()
                w = wide[3 * j + a, half]
                if a == 1:
                    value = lax.dot_general(moved[j], w, contract1, preferred_element_type=f32)
                    if j == 0:
                        acc[...] = value
                    else:
                        acc[...] += value
                elif a == 0:
                    acc[: pixels - s] += lax.dot_general(moved[j, s:], w, contract1, preferred_element_type=f32)
                else:
                    acc[s:] += lax.dot_general(moved[j, : pixels - s], w, contract1, preferred_element_type=f32)
        dsend[h] = acc[...].astype(bf16)
        for k in FAR_FIRST:
            back.append(
                push(
                    dsend.at[h, rows((p ^ k) * 128, 128)],
                    drecv.at[h, rows(p * 128, 128)],
                    d_sems.at[0, h, k],
                    d_sems.at[1, h, k],
                    (p ^ k, c),
                )
            )
        back.append(keep(dsend.at[h, rows(p * 128, 128)], drecv.at[h, rows(p * 128, 128)], own_sems.at[h]))

    for i, source in enumerate((trunk, other)):
        tpad[i, :64] = jnp.zeros((64, n), bf16)
        tpad[i, 64 : 64 + pixels] = source[...]
        tpad[i, 64 + pixels :] = jnp.zeros((64, n), bf16)

    def turn(i, part):
        at = slice(i * pixels, (i + 1) * pixels)
        for j in range(3):
            q = RATE_COLS[j]
            plain = part(j)
            value = plain.astype(f32)
            for b, piece in enumerate((move_cols(value, -q).astype(bf16), plain, move_cols(value, q).astype(bf16))):
                turned[j, b * 128 : (b + 1) * 128, at] = piece.T

    turn(0, lambda j: picked[y, j])
    sent_picks.wait()
    turn(1, lambda j: picked_in[j])
    for j in range(3):
        s = RATE_ROWS[j] * 32
        for a in range(3):
            if a == 1:
                low, high, start = 0, pixels, 64
            elif a == 0:
                low, high = s // 128 * 128, pixels
                start = 64 + low - s
            else:
                low, high, start = 0, -(-(pixels - s) // 128) * 128, 64 + s
            value = None
            for i in range(2):
                term = jnp.dot(
                    turned[j, :, i * pixels + low : i * pixels + high],
                    tpad[i, start : start + high - low],
                    preferred_element_type=f32,
                )
                value = term if value is None else value + term
            value = value.astype(bf16)
            for b in range(3):
                for to in range(4):
                    at = b * 128 + to * 32
                    zsend[to, (3 * j + a) * 3 + b] = value[at : at + 32]
    for copy in back:
        copy.wait()
    zcopies = [
        push(zsend.at[z ^ k], aspp_parts.at[z], z_sems.at[0, k], z_sems.at[1, k], (p ^ (2 * k), c)) for k in (3, 2, 1)
    ]
    zcopies.append(keep(zsend.at[z], aspp_parts.at[z], own_sems.at[2]))

    def norm_back(grad, norm, sums, scale, gain, v):
        return gain * scale * (grad - v * (sums[0] + norm * sums[1]) / count)

    def three(i, carry):
        at = rows(i * 32, 32)
        norm = norm3[at]
        pre = norm * affine3[0:1] + affine3[1:2] + masked[at].astype(f32)
        grad = jnp.concatenate([drecv[0, at], drecv[1, at]], axis=1).astype(f32)
        grad = grad * spread_lanes(valid[at], n) * slope(pre)
        gp3[at] = grad
        return carry[0] + fold(grad), carry[1] + fold(grad * norm)

    zero = jnp.zeros((8, n), f32)
    bias, gain = loop(pixels // 32, three, (zero, zero))
    packed_sums((total(bias), total(gain)), st3)
    pix_exchange(st3, st3r, st_sems.at[0])
    sums = unpacked_sums(st3r, n // 128, 2)
    sums3_out[0:1] = sums[0]
    sums3_out[1:2] = sums[1]

    def part3(t):
        def step(i, carry):
            at = rows(t * tile + i * 32, 32)
            v = spread_lanes(valid[at], n)
            g3[at] = norm_back(gp3[at], norm3[at], sums, stats3[1:2], affine3[0:1], v).astype(bf16)
            return carry

        loop(tile // 32, step, 0)
        return lax.dot_general(g3[t * tile : (t + 1) * tile], expand[...], contract1, preferred_element_type=f32)

    result = sum_over_ch(part3, tile, TILES, own, out, near, cross, near_sems.at[0], far_sems.at[0])
    value = lax.dot_general(full2[...], g3[...], contract0, preferred_element_type=f32).astype(bf16)
    for d in range(SPLIT):
        e_part[d] = value[d * mid : (d + 1) * mid]
    e_copies = [
        push(e_part.at[c ^ k], e_mid.at[c], ch_sems.at[0, 0, k], ch_sems.at[0, 1, k], (p, c ^ k)) for k in (2, 3, 1)
    ]
    e_copies.append(keep(e_part.at[c], e_mid.at[c], own_sems.at[3]))

    bias, gain = jnp.zeros((8, mid), f32), jnp.zeros((8, mid), f32)
    for t in range(TILES):
        hidden[t * tile : (t + 1) * tile] = result(t)

    def two(i, carry):
        at = rows(i * 128, 128)
        norm = norm2[at]
        grad = hidden[at] * valid[at] * slope(norm * affine2[0:1] + affine2[1:2])
        gp2[at] = grad
        return carry[0] + fold(grad), carry[1] + fold(grad * norm)

    bias, gain = loop(pixels // 128, two, (bias, gain))
    packed_sums((total(bias), total(gain)), st2)
    pix_exchange(st2, st2r, st_sems.at[1])
    sums2 = unpacked_sums(st2r, 1, 2)
    sums2_out[0:1] = sums2[0]
    sums2_out[1:2] = sums2[1]

    def ready2(t):
        def step(i, carry):
            at = rows(t * tile + i * 128, 128)
            value = norm_back(gp2[at], norm2[at], sums2, stats2[1:2], affine2[0:1], valid[at])
            g2[at, rows(c * mid, mid)] = value.astype(bf16)
            return carry

        loop(tile // 128, step, 0)

    gather_over_ch(g2, mid, tile, TILES, gn, gf, gh, ready2)
    for t in range(TILES):
        at = pl.ds(t * tile, tile)
        prod[at] = lax.dot_general(g2[at], dilated[...], contract1, preferred_element_type=f32)

    place = lax.broadcasted_iota(jnp.int32, (128, mid), 0) % 32

    def across(i, a):
        beta = i % COL_CLASSES
        two_on = (i - beta + (beta + 2) % 4) * 128
        here = slice(i * 128, (i + 1) * 128)
        there = slice(two_on, two_on + 128)
        lane = lambda b: slice((3 * a + b) * mid, (3 * a + b + 1) * mid)
        left, right = prod[there, lane(0)], prod[there, lane(2)]
        if beta >= 2:
            left = jnp.where(place == 31, 0.0, pltpu.roll(left, 127, 0))
        else:
            right = jnp.where(place == 0, 0.0, pltpu.roll(right, 1, 0))
        return prod[here, lane(1)] + left + right

    for i in range(PHASES):
        at = slice(i * 128, (i + 1) * 128)
        up, same, down = across(i, 0), across(i, 1), across(i, 2)
        zero = jnp.zeros((32, mid), f32)
        hidden[at] = same + jnp.concatenate([up[32:], zero]) + jnp.concatenate([zero, down[:96]])
        edges[0, i] = up[:32].astype(bf16)
        edges[1, i] = down[96:].astype(bf16)
    first, last = p == 0, p == PHASES - 1
    to_next = lambda: pltpu.make_async_remote_copy(
        src_ref=edges.at[1], dst_ref=edges.at[2], send_sem=edge_sems.at[0, 0], recv_sem=edge_sems.at[1, 0],
        device_id=(p + 1, c), device_id_type=MESH,
    )
    to_last = lambda: pltpu.make_async_remote_copy(
        src_ref=edges.at[0], dst_ref=edges.at[3], send_sem=edge_sems.at[0, 1], recv_sem=edge_sems.at[1, 1],
        device_id=(p - 1, c), device_id_type=MESH,
    )

    @pl.when(jnp.logical_not(last))
    def _():
        to_next().start()

    @pl.when(jnp.logical_not(first))
    def _():
        to_last().start()

    @pl.when(first)
    def _():
        edges[2] = jnp.zeros((PHASES, 32, mid), bf16)

    @pl.when(last)
    def _():
        edges[3] = jnp.zeros((PHASES, 32, mid), bf16)

    value = lax.dot_general(g2[...], taps[...], contract0, preferred_element_type=f32).astype(bf16)
    out_rows = SPLIT * mid // PHASES
    for d in range(PHASES):
        d_part[d] = value[d * out_rows : (d + 1) * out_rows]

    @pl.when(jnp.logical_not(last))
    def _():
        to_next().wait_send()
        to_last().wait_recv()

    @pl.when(jnp.logical_not(first))
    def _():
        to_last().wait_send()
        to_next().wait_recv()

    bias, gain = jnp.zeros((8, mid), f32), jnp.zeros((8, mid), f32)
    for i in range(PHASES):
        at = slice(i * 128, (i + 1) * 128)
        zero = jnp.zeros((64, mid), f32)
        edge = jnp.concatenate([edges[2, i].astype(f32), zero, edges[3, i].astype(f32)])
        norm = norm1[at]
        grad = (hidden[at] + edge) * valid[at] * slope(norm * affine1[0:1] + affine1[1:2])
        gp1[at] = grad
        bias, gain = bias + fold(grad), gain + fold(grad * norm)
    packed_sums((total(bias), total(gain)), st1)
    pix_exchange(st1, st1r, st_sems.at[2])
    sums1 = unpacked_sums(st1r, 1, 2)
    sums1_out[0:1] = sums1[0]
    sums1_out[1:2] = sums1[1]

    def ready1(t):
        def step(i, carry):
            at = rows(t * tile + i * 128, 128)
            value = norm_back(gp1[at], norm1[at], sums1, stats1[1:2], affine1[0:1], valid[at])
            g1[at, rows(c * mid, mid)] = value.astype(bf16)
            return carry

        loop(tile // 128, step, 0)

    gather_over_ch(g1, mid, tile, TILES, gn1, gf1, gh1, ready1)
    value = lax.dot_general(masked[...], g1[...], contract0, preferred_element_type=f32).astype(bf16)
    for d in range(SPLIT):
        r_part[d] = value[:, d * mid : (d + 1) * mid]
    r_copies = [
        push(r_part.at[c ^ k], r_mid.at[rows(c * n, n)], ch_sems.at[1, 0, k], ch_sems.at[1, 1, k], (p, c ^ k))
        for k in (2, 3, 1)
    ]
    r_copies.append(keep(r_part.at[c], r_mid.at[rows(c * n, n)], own_sems.at[4]))
    for copy in e_copies:
        copy.wait()

    def wanted(to):
        return e_mid.at[to // 2, :, rows(lax.rem(to, 2) * 256, 256)]

    pix_copies = [
        push(wanted(p ^ k), e_sum.at[p], pix_sems.at[0, 0, k], pix_sems.at[0, 1, k], (p ^ k, c)) for k in FAR_FIRST
    ]
    pix_copies.append(keep(wanted(p), e_sum.at[p], own_sems.at[5]))
    pix_copies += [
        push(d_part.at[p ^ k], d_sum.at[p], pix_sems.at[1, 0, k], pix_sems.at[1, 1, k], (p ^ k, c)) for k in FAR_FIRST
    ]
    pix_copies.append(keep(d_part.at[p], d_sum.at[p], own_sems.at[6]))
    for copy in r_copies:
        copy.wait()
    pix_copies += [
        push(r_mid.at[rows((p ^ k) * 256, 256)], r_sum.at[p], pix_sems.at[2, 0, k], pix_sems.at[2, 1, k], (p ^ k, c))
        for k in FAR_FIRST
    ]
    pix_copies.append(keep(r_mid.at[rows(p * 256, 256)], r_sum.at[p], own_sems.at[7]))

    for i in range(PHASES):
        at = slice(i * 128, (i + 1) * 128)
        value = lax.dot_general(g1[at], reduce_rows[...], contract1, preferred_element_type=f32) + gp3[at]
        value = value * spread_lanes(valid[at], n)
        for g in range(n // 128):
            for r in range(4):
                start = (2 * r + i // COL_CLASSES) * 128 + i % COL_CLASSES
                lanes[g, pl.ds(start, 32, stride=COL_CLASSES), :] = value[r * 32 : (r + 1) * 32, g * 128 : (g + 1) * 128]
    for g in range(n // 128):
        features_grad[:, g * 128 : (g + 1) * 128] = lanes[g].astype(bf16)
    for copy in pix_copies:
        copy.wait()

    def gathered(parts):
        value = parts[0].astype(f32)
        for d in range(1, PHASES):
            value = value + parts[d].astype(f32)
        return value

    expand_grad[...] = gathered(e_sum)
    reduce_grad[...] = gathered(r_sum)
    dilated_grad[...] = gathered(d_sum)
    for copy in zcopies:
        copy.wait()
    del zown


def run_backward(cid, arrays):
    (grads, trunk, other, weight, norm3, masked, valid, expand, affine3, norm2, affine2, full2, taps, dilated,
     norm1, affine1, reduce_rows, stats1, stats2, stats3) = arrays
    pixels, n = norm3.shape
    m = weight.shape[4]
    mid = norm2.shape[1]
    all_mid = SPLIT * mid
    outs = [
        shape((pixels, n), bf16),
        shape((4, 27, 32, n), bf16),
        shape((all_mid // PHASES, 9 * mid), f32),
        shape((mid, 256), f32),
        shape((256, mid), f32),
        shape((8, n), f32),
        shape((8, mid), f32),
        shape((8, mid), f32),
    ]
    sums = sum_scratch(pixels, mid, TILES)
    scratch = [
        pltpu.VMEM((9, n, 3 * m), bf16),
        pltpu.VMEM((3, pixels, 3 * m), bf16),
        pltpu.VMEM((pixels, m), f32),
        pltpu.VMEM((2, pixels, m), bf16),
        pltpu.VMEM((2, pixels, m), bf16),
        pltpu.VMEM((2, pixels + 128, n), bf16),
        pltpu.VMEM((2, 3, pixels, 128), bf16),
        pltpu.VMEM((3, pixels, 128), bf16),
        pltpu.VMEM((3, 384, 2 * pixels), bf16),
        pltpu.VMEM((4, 27, 32, n), bf16),
        pltpu.VMEM((8, 128), f32),
        pltpu.VMEM((pixels, n), f32),
        pltpu.VMEM((pixels, n), bf16),
        *sums[:4],
        pltpu.VMEM((pixels, mid), f32),
        pltpu.VMEM((pixels, mid), f32),
        pltpu.VMEM((pixels, all_mid), bf16),
        pltpu.VMEM((pixels, 9 * mid), f32),
        pltpu.VMEM((4, PHASES, 32, mid), bf16),
        pltpu.VMEM((pixels, all_mid), bf16),
        pltpu.VMEM((8, 128), f32),
        pltpu.VMEM((PHASES, 8, 128), f32),
        pltpu.VMEM((8, 128), f32),
        pltpu.VMEM((PHASES, 8, 128), f32),
        pltpu.VMEM((8, 128), f32),
        pltpu.VMEM((PHASES, 8, 128), f32),
        pltpu.VMEM((SPLIT, mid, n), bf16),
        pltpu.VMEM((SPLIT, mid, n), bf16),
        pltpu.VMEM((PHASES, mid, 256), bf16),
        pltpu.VMEM((PHASES, all_mid // PHASES, 9 * mid), bf16),
        pltpu.VMEM((PHASES, all_mid // PHASES, 9 * mid), bf16),
        pltpu.VMEM((SPLIT, n, mid), bf16),
        pltpu.VMEM((SPLIT * n, mid), bf16),
        pltpu.VMEM((PHASES, 256, mid), bf16),
        dma(9, 3),
        dma(2, 2, PHASES),
        dma(2),
        dma(2, 4),
        dma(1, 2, TILES, 2),
        dma(1, 2, TILES),
        dma(3, 2, PHASES),
        *gather_scratch(TILES),
        *gather_scratch(TILES),
        dma(2, 2),
        dma(2, 2, SPLIT),
        dma(3, 2, PHASES),
        dma(8),
    ]
    vmem = pl.BlockSpec(memory_space=pltpu.VMEM)
    specs = [vmem] * len(arrays)
    specs[3] = pl.BlockSpec(memory_space=pl.ANY)
    return pl.pallas_call(
        backward,
        out_shape=outs,
        in_specs=specs,
        out_specs=[vmem, pl.BlockSpec(memory_space=pl.ANY)] + [vmem] * (len(outs) - 2),
        scratch_shapes=scratch,
        compiler_params=pltpu.CompilerParams(
            collective_id=cid, has_side_effects=True, vmem_limit_bytes=VMEM_BYTES
        ),
        name="backward",
    )(*arrays)


def finish_pyramid(parts, result):
    value = parts[0, 0].astype(f32)
    for i in range(1, 4):
        value = value + parts[i, 0].astype(f32)
    result[0] = value.T


def run_finish(parts):
    steps, n = parts.shape[1], parts.shape[3]
    return pl.pallas_call(
        finish_pyramid,
        grid=(steps,),
        out_shape=shape((steps, n, 32), f32),
        in_specs=[pl.BlockSpec((4, 1, 32, n), lambda i: (0, i, 0, 0))],
        out_specs=pl.BlockSpec((1, n, 32), lambda i: (i, 0, 0)),
        name="finish_pyramid",
    )(parts)


def fast_device(
    features,
    pixel_mask,
    reduce_weight,
    reduce_gain,
    reduce_bias,
    dilated_weight,
    dilated_gain,
    dilated_bias,
    expand_weight,
    expand_gain,
    expand_bias,
    aspp_weight,
    aspp_gain,
    aspp_bias,
    task_weight,
    cotangent,
):
    rows_here, width, local_in = features.shape
    pixels = rows_here * width
    local_mid = reduce_weight.shape[1]
    full_mid = dilated_weight.shape[3]
    branch_width = aspp_weight.shape[4]
    own_branch = task_weight.shape[1]
    outs_count = task_weight.shape[2]
    me_ch = lax.axis_index("ch")
    quarter = pixels // 4
    valid = to_classes(pixel_mask.astype(f32).reshape(rows_here, width, 1)).reshape(pixels, 1)
    valid_wide = jnp.broadcast_to(valid, (pixels, 128))
    heads = jnp.concatenate(
        [
            task_weight.astype(f32).transpose(2, 0, 1).reshape(outs_count, -1),
            jnp.zeros((32 - outs_count, 3 * own_branch), f32),
            aspp_gain.reshape(1, -1),
            aspp_bias.reshape(1, -1),
            jnp.zeros((6, 3 * own_branch), f32),
        ]
    )
    heads = jnp.pad(heads, ((0, 0), (0, 256 - 3 * own_branch)))
    target_here = jnp.concatenate(
        [
            to_classes(cotangent).reshape(pixels, outs_count) * valid,
            jnp.zeros((pixels, 32 - outs_count), f32),
            valid_wide[:, :96],
        ],
        axis=1,
    )
    square = jnp.einsum("po,pq->oq", target_here[:, :32], target_here[:, :32], precision=highest)
    square = jnp.pad(square, ((0, 0), (0, 96)))

    def affine(gain, bias):
        return jnp.concatenate([gain[None], bias[None], jnp.zeros((6, gain.shape[0]), f32)])

    masked, reduce_rows, expand_cols, heads_all, target_class, square_all, norm_one, padded_one, stat_one = run_stage_one(
        1,
        features.reshape(pixels, local_in),
        valid_wide,
        reduce_weight,
        expand_weight,
        affine(reduce_gain, reduce_bias),
        heads,
        target_here.reshape(PHASES, -1, 128),
        square,
    )
    heads_all = (
        heads_all[:, :, : 3 * own_branch]
        .reshape(4, heads.shape[0], 3, own_branch)
        .transpose(1, 2, 0, 3)
        .reshape(heads.shape[0], 3 * branch_width)
    )
    head_weight, branch_gain, branch_bias = heads_all[:32], heads_all[32:33], heads_all[33:34]
    target_class = target_class.reshape(pixels, 128)

    norm_two, act_two_full, taps_one, stat_two = run_stage_two(
        2, padded_one, valid_wide, dilated_weight.reshape(9 * local_mid, full_mid), affine(dilated_gain, dilated_bias)
    )
    norm_three, trunk_class, stat_three = run_stage_three(
        3, act_two_full, expand_cols, masked, valid_wide, affine(expand_gain, expand_bias)
    )
    grad_full, predictions, head_grad, branch_sums, trunk_other = run_pyramid(
        4, trunk_class, aspp_weight, heads_all[32:40], head_weight, target_class, square_all
    )
    predictions = from_classes(predictions.transpose(0, 2, 1), rows_here, width)[:, :, :outs_count]
    head_grad = head_grad.reshape(32, 3, 4, own_branch).transpose(2, 1, 3, 0)
    task_weight_grad = lax.dynamic_index_in_dim(head_grad, me_ch, keepdims=False)[:, :, :outs_count]
    own_sums = lax.dynamic_slice_in_dim(
        branch_sums[:6].reshape(2, 3, branch_width), me_ch * own_branch, own_branch, axis=2
    )
    aspp_bias_grad, aspp_gain_grad = own_sums[0], own_sums[1]
    dilated_rows = dilated_weight.reshape(9 * local_mid, full_mid)
    features_grad, aspp_parts, dilated_sum, expand_weight_grad, reduce_weight_grad, sums3, sums2, sums1 = run_backward(
        5,
        [
            grad_full, trunk_class, trunk_other, aspp_weight, norm_three, masked, valid_wide, expand_cols,
            affine(expand_gain, expand_bias), norm_two, affine(dilated_gain, dilated_bias), act_two_full, taps_one,
            dilated_rows, norm_one, affine(reduce_gain, reduce_bias), reduce_rows, stat_one, stat_two, stat_three,
        ],
    )
    features_grad = features_grad.reshape(rows_here, width, local_in)
    aspp_weight_grad = run_finish(aspp_parts).reshape(3, 3, 3, local_in, -1)
    dilated_weight_grad = dilated_sum.transpose(1, 0).reshape(3, 3, local_mid, -1)
    expand_bias_grad, expand_gain_grad = sums3[0], sums3[1]
    dilated_bias_grad, dilated_gain_grad = sums2[0], sums2[1]
    reduce_bias_grad, reduce_gain_grad = sums1[0], sums1[1]

    return (
        predictions,
        features_grad,
        reduce_weight_grad,
        reduce_gain_grad,
        reduce_bias_grad,
        dilated_weight_grad,
        dilated_gain_grad,
        dilated_bias_grad,
        expand_weight_grad,
        expand_gain_grad,
        expand_bias_grad,
        aspp_weight_grad,
        aspp_gain_grad,
        aspp_bias_grad,
        task_weight_grad,
    )


def solution(mesh):
    placed = (
        P("pix", None, "ch"),
        P("pix", None),
        P(None, "ch"),
        P("ch"),
        P("ch"),
        P(None, None, "ch", None),
        P("ch"),
        P("ch"),
        P("ch", None),
        P("ch"),
        P("ch"),
        P(None, None, None, "ch", None),
        P(None, "ch"),
        P(None, "ch"),
        P(None, "ch", None),
        P("pix", None, None),
    )
    return jax.shard_map(
        fast_device if (mesh.shape["pix"], mesh.shape["ch"]) == (PHASES, 4) else on_device,
        mesh=mesh,
        in_specs=placed,
        out_specs=(
            P("pix", None, None),
            P("pix", None, "ch"),
            P("pix", "ch"),
            P("ch"),
            P("ch"),
            P(None, None, "ch", "pix"),
            P("ch"),
            P("ch"),
            P("ch", "pix"),
            P("ch"),
            P("ch"),
            P(None, None, None, "ch", "pix"),
            P(None, "ch"),
            P(None, "ch"),
            P(None, "ch", None),
        ),
        check_vma=False,
    )
```

```python
import jax
import jax.numpy as jnp
from jax import lax
from jax.experimental import pallas as pl
from jax.experimental.pallas import tpu as pltpu
from jax.sharding import PartitionSpec as P

CLS = 19


epsilon = 1e-05
highest = lax.Precision.HIGHEST
aspp_rates = (12, 24, 36)
inner_rate = 2


def from_behind(value, axis, steps):
    count = lax.axis_size(axis)
    first, last = (max(0, -steps), min(count, count - steps))
    return lax.ppermute(value, axis, [(source, source + steps) for source in range(first, last)])


def with_halo(shard, sides, width):
    for axis, dim in sides:
        devices, length = (lax.axis_size(axis), shard.shape[dim])
        up = [(i, (i + 1) % devices) for i in range(devices - 1)]
        down = [(j, i) for i, j in up]
        last = lax.slice_in_dim(shard, length - width, length, axis=dim)
        first = lax.slice_in_dim(shard, 0, width, axis=dim)
        before = lax.ppermute(last, axis, up)
        after = lax.ppermute(first, axis, down)
        shard = jnp.concatenate([before, shard, after], axis=dim)
    return shard


def silu_slope(value):
    sigma = jax.nn.sigmoid(value)
    return sigma * (1.0 + value * (1.0 - sigma))


def shift_cols(value, offset):
    if offset == 0:
        return value
    margin = abs(offset)
    widths = [(0, 0)] * value.ndim
    widths[1] = (margin, margin)
    padded = jnp.pad(value, widths)
    return lax.slice_in_dim(padded, margin + offset, margin + offset + value.shape[1], axis=1)


def moved(piece, distance):
    return from_behind(piece, "pix", -distance)


def shift_rows(value, offset):
    if offset == 0:
        return value
    steps_over, inner = divmod(offset, value.shape[0])
    first = moved(value, steps_over)[inner:]
    if inner == 0:
        return first
    second = moved(value, steps_over + 1)[:inner]
    return jnp.concatenate([first, second], axis=0)


def halo_rows(value):
    return with_halo(value, (("pix", 0),), inner_rate)


def gather_channels(value):
    return lax.all_gather(value, "ch", axis=1, tiled=True)


def sum_channels(value):
    return lax.psum_scatter(
        value.astype(jnp.bfloat16), "ch", scatter_dimension=1, tiled=True
    ).astype(jnp.float32)


def normalized(hidden, valid, axes):
    total, count = lax.psum(
        (jnp.sum(hidden * valid, axis=axes, keepdims=True), jnp.sum(valid)), "pix"
    )
    center = total / count
    spread_sum = lax.psum(jnp.sum(valid * (hidden - center) ** 2, axis=axes, keepdims=True), "pix")
    variance = spread_sum / count
    scale = lax.rsqrt(variance + epsilon)
    return ((hidden - center) * scale, scale, count)


def norm_grad(grad_out, centered, scale, gain, count, valid, axes):
    sum_out, sum_cross = lax.psum(
        (
            jnp.sum(grad_out, axis=axes, keepdims=True),
            jnp.sum(grad_out * centered, axis=axes, keepdims=True),
        ),
        "pix",
    )
    grad_in = gain * scale * (grad_out - valid * (sum_out + centered * sum_cross) / count)
    return (grad_in, sum_cross, sum_out)


def task_scales(gram):
    norms = jnp.sqrt(jnp.diagonal(gram) + 1e-06)
    proj = gram / norms[None, :]
    vector = proj[0, 0] - proj[0, 1:]
    matrix = proj[0, 0] - proj[0, 1:][None, :] - proj[1:, 0][:, None] + proj[1:, 1:]
    determinant = matrix[0, 0] * matrix[1, 1] - matrix[0, 1] * matrix[1, 0]
    second = (vector[0] * matrix[1, 1] - vector[1] * matrix[1, 0]) / determinant
    third = (vector[1] * matrix[0, 0] - vector[0] * matrix[0, 1]) / determinant
    return jnp.stack([1.0 - second - third, second, third])


def on_device(
    features,
    pixel_mask,
    reduce_weight,
    reduce_gain,
    reduce_bias,
    dilated_weight,
    dilated_gain,
    dilated_bias,
    expand_weight,
    expand_gain,
    expand_bias,
    aspp_weight,
    aspp_gain,
    aspp_bias,
    task_weight,
    cotangent,
):
    rows_here, width, local_in = features.shape
    pixels = rows_here * width
    local_mid = reduce_weight.shape[1]
    full_mid = dilated_weight.shape[3]
    branch_width = aspp_weight.shape[4]
    outs_count = task_weight.shape[2]
    valid = pixel_mask.astype(jnp.float32).reshape(pixels, 1)
    valid_branch = valid[None]
    masked = features.reshape(pixels, local_in) * valid.astype(jnp.bfloat16)
    inputs_full = gather_channels(masked)
    hidden_one = jnp.dot(inputs_full, reduce_weight, preferred_element_type=jnp.float32)
    norm_one, scale_one, count = normalized(hidden_one, valid, (0,))
    pre_one = norm_one * reduce_gain + reduce_bias
    act_one = (jax.nn.silu(pre_one) * valid).astype(jnp.bfloat16)
    padded_one = halo_rows(act_one.reshape(rows_here, width, local_mid))
    partial_value = jnp.zeros((pixels, full_mid), jnp.float32)
    for a in range(3):
        for b in range(3):
            shifted = shift_cols(padded_one[2 * a : 2 * a + rows_here], (b - 1) * inner_rate)
            partial_value = partial_value + jnp.dot(
                shifted.reshape(pixels, local_mid),
                dilated_weight[a, b],
                preferred_element_type=jnp.float32,
            )
    hidden_two = sum_channels(partial_value)
    norm_two, scale_two, _ = normalized(hidden_two, valid, (0,))
    pre_two = norm_two * dilated_gain + dilated_bias
    act_two = (jax.nn.silu(pre_two) * valid).astype(jnp.bfloat16)
    hidden_three = sum_channels(jnp.dot(act_two, expand_weight, preferred_element_type=jnp.float32))
    norm_three, scale_three, _ = normalized(hidden_three, valid, (0,))
    pre_three = norm_three * expand_gain + expand_bias + masked.astype(jnp.float32)
    trunk_out = (
        (jax.nn.silu(pre_three) * valid).astype(jnp.bfloat16).reshape(rows_here, width, local_in)
    )
    kept_rows = []
    partials = []
    for j in range(3):
        rate = aspp_rates[j]
        running = jnp.zeros((pixels, branch_width), jnp.float32)
        shifted_rows = []
        for a in range(3):
            row_shift = shift_rows(trunk_out, (a - 1) * rate)
            shifted_rows.append(row_shift)
            for b in range(3):
                shifted = shift_cols(row_shift, (b - 1) * rate)
                running = running + jnp.dot(
                    shifted.reshape(pixels, local_in),
                    aspp_weight[j, a, b],
                    preferred_element_type=jnp.float32,
                )
        kept_rows.append(shifted_rows)
        partials.append(running)
    branch_sum = sum_channels(jnp.stack(partials).reshape(3 * pixels, branch_width)).reshape(
        3, pixels, -1
    )
    branch_gain = aspp_gain[:, None, :]
    norm_branch, scale_branch, _ = normalized(branch_sum, valid_branch, (1,))
    pre_branch = norm_branch * branch_gain + aspp_bias[:, None, :]
    branch_out = (jax.nn.silu(pre_branch) * valid_branch).astype(jnp.bfloat16)
    predictions = lax.psum(
        jnp.einsum(
            "jpc,jco->po", branch_out, task_weight, preferred_element_type=jnp.float32
        ).astype(jnp.bfloat16),
        "ch",
    ).astype(jnp.float32)
    columns = jnp.arange(outs_count)
    task_of = (columns >= CLS).astype(jnp.int32) + (columns >= CLS + 1).astype(jnp.int32)
    select = (task_of[:, None] == jnp.arange(3)[None, :]).astype(jnp.float32)
    target = cotangent.reshape(pixels, outs_count) * valid
    task_float = task_weight.astype(jnp.float32)
    task_grads = jnp.einsum("po,ot,jco->tjpc", target, select, task_float, precision=highest)
    gram = lax.psum(
        jnp.einsum("tjpc,sjpc->ts", task_grads, task_grads, precision=highest), ("pix", "ch")
    )
    scales = task_scales(gram)
    branch_grad = jnp.einsum("t,tjpc->jpc", scales, task_grads, precision=highest)
    task_weight_grad = lax.psum(
        jnp.einsum("jpc,po->jco", branch_out.astype(jnp.float32), target, precision=highest), "pix"
    )
    grad_pre_branch = branch_grad * valid_branch * silu_slope(pre_branch)
    grad_branch, aspp_gain_grad, aspp_bias_grad = norm_grad(
        grad_pre_branch, norm_branch, scale_branch, branch_gain, count, valid_branch, (1,)
    )
    grad_full = gather_channels(grad_branch.astype(jnp.bfloat16).reshape(3 * pixels, -1)).reshape(
        3, rows_here, width, -1
    )
    grad_trunk = jnp.zeros((pixels, local_in), jnp.float32)
    aspp_list = []
    for j in range(3):
        rate = aspp_rates[j]
        grad_flat = grad_full[j].reshape(pixels, -1)
        per_row = []
        for a in range(3):
            back_rows = shift_rows(grad_full[j], -(a - 1) * rate)
            per_col = []
            for b in range(3):
                shifted = shift_cols(back_rows, -(b - 1) * rate)
                grad_trunk = grad_trunk + jnp.einsum(
                    "pa,ca->pc",
                    shifted.reshape(pixels, -1),
                    aspp_weight[j, a, b],
                    preferred_element_type=jnp.float32,
                )
                forward_tap = shift_cols(kept_rows[j][a], (b - 1) * rate).reshape(pixels, local_in)
                per_col.append(
                    jnp.einsum(
                        "pc,pa->ca", forward_tap, grad_flat, preferred_element_type=jnp.float32
                    )
                )
            per_row.append(jnp.stack(per_col))
        aspp_list.append(jnp.stack(per_row))
    aspp_weight_local = jnp.stack(aspp_list)
    grad_pre_three = grad_trunk * valid * silu_slope(pre_three)
    grad_three, expand_gain_grad, expand_bias_grad = norm_grad(
        grad_pre_three, norm_three, scale_three, expand_gain, count, valid, (0,)
    )
    grad_three_full = gather_channels(grad_three.astype(jnp.bfloat16))
    grad_act_two = jnp.einsum(
        "pc,dc->pd", grad_three_full, expand_weight, preferred_element_type=jnp.float32
    )
    expand_weight_local = jnp.einsum(
        "pd,pc->dc", act_two, grad_three_full, preferred_element_type=jnp.float32
    )
    grad_pre_two = grad_act_two * valid * silu_slope(pre_two)
    grad_two, dilated_gain_grad, dilated_bias_grad = norm_grad(
        grad_pre_two, norm_two, scale_two, dilated_gain, count, valid, (0,)
    )
    grad_two_full = gather_channels(grad_two.astype(jnp.bfloat16))
    padded_grad = halo_rows(grad_two_full.reshape(rows_here, width, full_mid))
    grad_act_one = jnp.zeros((pixels, local_mid), jnp.float32)
    dilated_rows = []
    for a in range(3):
        dilated_cols = []
        for b in range(3):
            shifted = shift_cols(
                padded_grad[4 - 2 * a : 4 - 2 * a + rows_here], -(b - 1) * inner_rate
            )
            grad_act_one = grad_act_one + jnp.einsum(
                "pe,de->pd",
                shifted.reshape(pixels, full_mid),
                dilated_weight[a, b],
                preferred_element_type=jnp.float32,
            )
            forward_tap = shift_cols(
                padded_one[2 * a : 2 * a + rows_here], (b - 1) * inner_rate
            ).reshape(pixels, local_mid)
            dilated_cols.append(
                jnp.einsum(
                    "pd,pe->de", forward_tap, grad_two_full, preferred_element_type=jnp.float32
                )
            )
        dilated_rows.append(jnp.stack(dilated_cols))
    dilated_weight_local = jnp.stack(dilated_rows)
    grad_pre_one = grad_act_one * valid * silu_slope(pre_one)
    grad_one, reduce_gain_grad, reduce_bias_grad = norm_grad(
        grad_pre_one, norm_one, scale_one, reduce_gain, count, valid, (0,)
    )
    grad_one_low = grad_one.astype(jnp.bfloat16)
    input_sum = sum_channels(
        jnp.einsum("pd,cd->pc", grad_one_low, reduce_weight, preferred_element_type=jnp.float32)
    )
    features_grad = (
        ((input_sum + grad_pre_three) * valid)
        .astype(jnp.bfloat16)
        .reshape(rows_here, width, local_in)
    )
    reduce_weight_local = jnp.einsum(
        "pc,pd->cd", inputs_full, grad_one_low, preferred_element_type=jnp.float32
    )
    reduce_weight_grad, dilated_weight_grad, expand_weight_grad, aspp_weight_grad = (
        lax.psum_scatter(reduce_weight_local, "pix", scatter_dimension=0, tiled=True),
        lax.psum_scatter(dilated_weight_local, "pix", scatter_dimension=3, tiled=True),
        lax.psum_scatter(expand_weight_local, "pix", scatter_dimension=1, tiled=True),
        lax.psum_scatter(aspp_weight_local, "pix", scatter_dimension=4, tiled=True),
    )
    return (
        predictions.reshape(rows_here, width, outs_count),
        features_grad,
        reduce_weight_grad,
        reduce_gain_grad.reshape(-1),
        reduce_bias_grad.reshape(-1),
        dilated_weight_grad,
        dilated_gain_grad.reshape(-1),
        dilated_bias_grad.reshape(-1),
        expand_weight_grad,
        expand_gain_grad.reshape(-1),
        expand_bias_grad.reshape(-1),
        aspp_weight_grad,
        aspp_gain_grad.reshape(3, -1),
        aspp_bias_grad.reshape(3, -1),
        task_weight_grad,
    )


MESH = pl.DeviceIdType.MESH
ROW_CLASSES, COL_CLASSES = 2, 4
PHASES = ROW_CLASSES * COL_CLASSES
SPLIT = 4
FAR_FIRST = (6, 7, 4, 5, 2, 3, 1)
f32, bf16 = jnp.float32, jnp.bfloat16
VMEM_BYTES = 60 << 20


def shape(dims, dtype):
    return jax.ShapeDtypeStruct(dims, dtype)


def call(name, cid, kernel, arrays, outs, scratch, hbm_ins=(), hbm_outs=()):
    vmem, hbm = pl.BlockSpec(memory_space=pltpu.VMEM), pl.BlockSpec(memory_space=pl.ANY)
    return pl.pallas_call(
        kernel,
        out_shape=outs,
        in_specs=[hbm if i in hbm_ins else vmem for i in range(len(arrays))],
        out_specs=[hbm if i in hbm_outs else vmem for i in range(len(outs))],
        scratch_shapes=scratch,
        compiler_params=pltpu.CompilerParams(
            collective_id=cid, has_side_effects=True, vmem_limit_bytes=VMEM_BYTES
        ),
        name=name,
    )(*arrays)


def dma(*dims):
    return pltpu.SemaphoreType.DMA(dims)


def greet(ch, pix):
    p, c = lax.axis_index("pix"), lax.axis_index("ch")
    barrier = pltpu.get_barrier_semaphore()
    for k in ch:
        pl.semaphore_signal(barrier, inc=1, device_id=(p, c ^ k), device_id_type=MESH)
    for k in pix:
        pl.semaphore_signal(barrier, inc=1, device_id=(p ^ k, c), device_id_type=MESH)
    return barrier, len(ch) + len(pix)


def push(src, dst, send, recv, device):
    copy = pltpu.make_async_remote_copy(
        src_ref=src,
        dst_ref=dst,
        send_sem=send,
        recv_sem=recv,
        device_id=device,
        device_id_type=MESH,
    )
    copy.start()
    return copy


def keep(src, dst, sem):
    copy = pltpu.make_async_copy(src, dst, sem)
    copy.start()
    return copy


def rows(start, size):
    return pl.ds(pl.multiple_of(start, size), size)


def fold(x):
    return jnp.sum(x.reshape(x.shape[0] // 8, 8, x.shape[1]), axis=0)


def total(x):
    return jnp.sum(x, axis=0, keepdims=True)


def loop(steps, body, init):
    return lax.fori_loop(0, steps, body, init)


def sum_over_ch(part, tile, tiles, own, out, near, cross, near_sems, far_sems):
    p, c = lax.axis_index("pix"), lax.axis_index("ch")
    k, x = lax.rem(c, 2), c // 2
    n = own.shape[2]
    copies = []
    for t in range(tiles):
        at = pl.ds(t * tile, tile)
        value = part(t)
        for d in range(SPLIT):
            block = value[:, d * n : (d + 1) * n]
            own[d, at] = block
            out[d, at] = block.astype(bf16)
        copies.append(
            [
                push(
                    out.at[2 * h + 1 - k, at],
                    near.at[h, at],
                    near_sems.at[0, t, h],
                    near_sems.at[1, t, h],
                    (p, c ^ 1),
                )
                for h in range(2)
            ]
        )
    crossing = []
    for t in range(tiles):
        at = pl.ds(t * tile, tile)
        for copy in copies[t]:
            copy.wait()
        cross[0, at] = (own[2 * (1 - x) + k, at] + near[1 - x, at].astype(f32)).astype(bf16)
        crossing.append(
            push(cross.at[0, at], cross.at[1, at], far_sems.at[0, t], far_sems.at[1, t], (p, c ^ 2))
        )

    def result(t):
        at = pl.ds(t * tile, tile)
        crossing[t].wait()
        return own[2 * x + k, at] + near[x, at].astype(f32) + cross[1, at].astype(f32)

    return result


def sum_scratch(pixels, n, tiles):
    return [
        pltpu.VMEM((SPLIT, pixels, n), f32),
        pltpu.VMEM((SPLIT, pixels, n), bf16),
        pltpu.VMEM((2, pixels, n), bf16),
        pltpu.VMEM((2, pixels, n), bf16),
        dma(2, tiles, 2),
        dma(2, tiles),
    ]


def pix_exchange(send, recv, sems):
    p, c = lax.axis_index("pix"), lax.axis_index("ch")
    copies = [
        push(send, recv.at[p], sems.at[0, k], sems.at[1, k], (p ^ k, c)) for k in FAR_FIRST
    ]
    recv[p] = send[...]
    for copy in copies:
        copy.wait()


def norm_stats(hidden, valid, pixels, send, recv, sems):
    n = hidden.shape[1]
    tile = 128
    repeat = n // 128

    def mask(at):
        v = valid[at]
        return v if repeat == 1 else jnp.concatenate([v] * repeat, axis=1)

    def first(i, carry):
        at = rows(i * tile, tile)
        v = mask(at)
        return carry[0] + fold(hidden[at] * v), carry[1] + fold(v)

    zero = jnp.zeros((8, n), f32)
    sums, count = loop(pixels // tile, first, (zero, zero))
    sums, count = total(sums), total(count)
    center = sums / jnp.maximum(count, 1.0)

    def second(i, carry):
        at = rows(i * tile, tile)
        apart = hidden[at] - center
        return carry + fold(mask(at) * apart * apart)

    spread = total(loop(pixels // tile, second, zero))
    send[0:1] = sums
    send[1:2] = spread
    send[2:3] = count
    pix_exchange(send, recv, sems)
    return join(recv, PHASES)


def join(recv, parts):
    sums, count = recv[0, 0:1], recv[0, 2:3]
    for i in range(1, parts):
        sums, count = sums + recv[i, 0:1], count + recv[i, 2:3]
    center = sums / count
    spread = jnp.zeros_like(sums)
    for i in range(parts):
        n = recv[i, 2:3]
        apart = recv[i, 0:1] / jnp.maximum(n, 1.0) - center
        spread = spread + recv[i, 1:2] + n * apart * apart
    return center, lax.rsqrt(spread / count + epsilon), count


def stat_scratch(n):
    return [pltpu.VMEM((8, n), f32), pltpu.VMEM((PHASES, 8, n), f32), dma(2, PHASES)]


def silu(x):
    return x / (1.0 + jnp.exp(-x))


def gather_over_ch(full, n, tile, tiles, near_sems, far_sems, hop_sems, ready, between=None):
    p, c = lax.axis_index("pix"), lax.axis_index("ch")

    def part(owner, t):
        return full.at[pl.ds(t * tile, tile), rows(owner * n, n)]

    near, far, hops = [], [], []
    for t in range(tiles):
        ready(t)
        src = part(c, t)
        far.append(push(src, src, far_sems.at[0, t], far_sems.at[1, t], (p, c ^ 2)))
        near.append(push(src, src, near_sems.at[0, t], near_sems.at[1, t], (p, c ^ 1)))
    if between is not None:
        between()
    for t in range(tiles):
        far[t].wait_recv()
        src = part(c ^ 2, t)
        hops.append(push(src, src, hop_sems.at[0, t], hop_sems.at[1, t], (p, c ^ 1)))
    for t in range(tiles):
        far[t].wait_send()
        near[t].wait()
        hops[t].wait()


def gather_scratch(tiles):
    return [dma(2, tiles), dma(2, tiles), dma(2, tiles)]


def to_classes(x):
    rows, cols, n = x.shape
    x = x.reshape(rows // ROW_CLASSES, ROW_CLASSES, cols // COL_CLASSES, COL_CLASSES, n)
    return x.transpose(1, 3, 0, 2, 4).reshape(PHASES, -1, n)


def from_classes(x, rows, cols):
    n = x.shape[-1]
    x = x.reshape(ROW_CLASSES, COL_CLASSES, rows // ROW_CLASSES, cols // COL_CLASSES, n)
    return x.transpose(2, 0, 3, 1, 4).reshape(rows, cols, n)


TILES = 4


def stage_one(feat, valid, weight, expand, affine, heads, targets, square, *refs):
    (masked, reduce_rows, expand_cols, heads_all, targets_all, square_all, norm, padded, stat) = refs[:9]
    (wide, hidden, own, out, near, cross, near_sems, far_sems, send, recv, stat_sems) = refs[9:20]
    (weight_sems, pix_sems, local_sems, halo_sems) = refs[20:]
    p, c = lax.axis_index("pix"), lax.axis_index("ch")
    pixels, local_in = feat.shape
    local_mid = weight.shape[1]
    tile = pixels // TILES
    barrier, expected = greet((1, 2, 3), FAR_FIRST)
    for r in range(8):
        for g in range(local_in // 128):
            lanes = slice(g * 128, (g + 1) * 128)
            wide[g] = feat[r * 128 : (r + 1) * 128, lanes].astype(f32)
            for b in range(COL_CLASSES):
                block = ((r % ROW_CLASSES) * COL_CLASSES + b) * 128 + (r // ROW_CLASSES) * 32
                value = wide[g, pl.ds(b, 32, stride=COL_CLASSES), :] * valid[block : block + 32]
                masked[block : block + 32, lanes] = value.astype(bf16)
    pl.semaphore_wait(barrier, expected)

    def pieces(to):
        return (
            (weight.at[rows(to * local_in, local_in), :], reduce_rows.at[:, rows(c * local_mid, local_mid)]),
            (expand.at[:, rows(to * local_in, local_in)], expand_cols.at[rows(c * local_mid, local_mid), :]),
            (heads, heads_all.at[c]),
        )

    copies = [
        [push(*pieces(c ^ k)[i], weight_sems.at[0, k, i], weight_sems.at[1, k, i], (p, c ^ k)) for k in (2, 3, 1)]
        for i in range(3)
    ]
    local = [keep(*pieces(c)[i], local_sems.at[i]) for i in range(3)]
    local.append(keep(targets.at[p], targets_all.at[p], local_sems.at[3]))
    local.append(keep(square, square_all.at[p], local_sems.at[4]))
    routed = [
        push(targets.at[p ^ k], targets_all.at[p], pix_sems.at[0, k, 0], pix_sems.at[1, k, 0], (p ^ k, c))
        for k in FAR_FIRST
    ] + [push(square, square_all.at[p], pix_sems.at[0, k, 1], pix_sems.at[1, k, 1], (p ^ k, c)) for k in FAR_FIRST]
    for copy in copies[0]:
        copy.wait()
    local[0].wait()

    def part(t):
        return jnp.dot(masked[t * tile : (t + 1) * tile], reduce_rows[...], preferred_element_type=f32)

    result = sum_over_ch(part, tile, TILES, own, out, near, cross, near_sems, far_sems)
    for t in range(TILES):
        hidden[t * tile : (t + 1) * tile] = result(t)
    for copy in routed + copies[1] + copies[2] + local[1:]:
        copy.wait()
    center, scale, count = norm_stats(hidden, valid, pixels, send, recv, stat_sems)
    stat[0:1] = center
    stat[1:2] = scale
    stat[2:3] = count
    for i in range(PHASES):
        at = pl.ds(i * 128, 128)
        value = (hidden[at] - center) * scale
        norm[at] = value
        act = silu(value * affine[0:1] + affine[1:2]) * valid[at]
        padded[i, 1:5] = act.astype(bf16).reshape(4, 32, local_mid)
    up = lambda: pltpu.make_async_remote_copy(
        src_ref=padded.at[:, 4],
        dst_ref=padded.at[:, 0],
        send_sem=halo_sems.at[0, 0],
        recv_sem=halo_sems.at[1, 0],
        device_id=(p + 1, c),
        device_id_type=MESH,
    )
    down = lambda: pltpu.make_async_remote_copy(
        src_ref=padded.at[:, 1],
        dst_ref=padded.at[:, 5],
        send_sem=halo_sems.at[0, 1],
        recv_sem=halo_sems.at[1, 1],
        device_id=(p - 1, c),
        device_id_type=MESH,
    )
    first, last = p == 0, p == PHASES - 1

    @pl.when(jnp.logical_not(last))
    def _():
        up().start()

    @pl.when(jnp.logical_not(first))
    def _():
        down().start()

    @pl.when(last)
    def _():
        padded[:, 5] = jnp.zeros((PHASES, 32, local_mid), bf16)

    @pl.when(first)
    def _():
        padded[:, 0] = jnp.zeros((PHASES, 32, local_mid), bf16)

    @pl.when(jnp.logical_not(last))
    def _():
        up().wait_send()
        down().wait_recv()

    @pl.when(jnp.logical_not(first))
    def _():
        down().wait_send()
        up().wait_recv()


def run_stage_one(cid, feat, valid, weight, expand, affine, heads, targets, square):
    pixels, local_in = feat.shape
    local_mid = weight.shape[1]
    mid = SPLIT * local_mid
    outs = [
        shape((pixels, local_in), bf16),
        shape((local_in, mid), bf16),
        shape((mid, local_in), bf16),
        shape((SPLIT,) + heads.shape, f32),
        shape(targets.shape, f32),
        shape((PHASES,) + square.shape, f32),
        shape((pixels, local_mid), f32),
        shape((PHASES, 6, 32, local_mid), bf16),
        shape((8, local_mid), f32),
    ]
    scratch = (
        [pltpu.VMEM((local_in // 128, 128, 128), f32), pltpu.VMEM((pixels, local_mid), f32)]
        + sum_scratch(pixels, local_mid, TILES)
        + stat_scratch(local_mid)
        + [dma(2, SPLIT, 3), dma(2, PHASES, 2), dma(5), dma(2, 2)]
    )
    return call("stage_one", cid, stage_one, [feat, valid, weight, expand, affine, heads, targets, square], outs, scratch)


def stage_two(padded, valid, weight, affine, *refs):
    (norm, full, taps, stat) = refs[:4]
    (hidden, own, out, near, cross, near_sems, far_sems, send, recv, stat_sems) = refs[4:14]
    (g_near, g_far, g_hop) = refs[14:]
    p, c = lax.axis_index("pix"), lax.axis_index("ch")
    pixels = valid.shape[0]
    local_mid = padded.shape[3]
    tile = pixels // TILES
    barrier, expected = greet((1, 2), FAR_FIRST)
    place = lax.broadcasted_iota(jnp.int32, (192, local_mid), 0) % 32
    for i in range(PHASES):
        beta = i % COL_CLASSES
        plain = padded[i].reshape(192, local_mid)
        wide = plain.astype(f32)
        if beta >= 2:
            moved_by = jnp.where(place == 0, 0.0, pltpu.roll(wide, 1, 0)).astype(bf16)
        else:
            moved_by = jnp.where(place == 31, 0.0, pltpu.roll(wide, 191, 0)).astype(bf16)
        for a in range(3):
            at = slice(a * 32, a * 32 + 128)
            for b, other, value in (
                (1, beta, plain),
                (0, (beta + 2) % 4, moved_by if beta >= 2 else plain),
                (2, (beta + 2) % 4, plain if beta >= 2 else moved_by),
            ):
                to = (i - beta + other) * 128
                col = (a * 3 + b) * local_mid
                taps[to : to + 128, col : col + local_mid] = value[at]
    pl.semaphore_wait(barrier, expected)

    def part(t):
        return jnp.dot(taps[t * tile : (t + 1) * tile], weight[...], preferred_element_type=f32)

    result = sum_over_ch(part, tile, TILES, own, out, near, cross, near_sems, far_sems)
    for t in range(TILES):
        hidden[t * tile : (t + 1) * tile] = result(t)
    center, scale, count = norm_stats(hidden, valid, pixels, send, recv, stat_sems)
    stat[0:1] = center
    stat[1:2] = scale
    stat[2:3] = count

    def ready(t):
        for i in range(tile // 128):
            at = pl.ds(t * tile + i * 128, 128)
            value = (hidden[at] - center) * scale
            norm[at] = value
            act = silu(value * affine[0:1] + affine[1:2]) * valid[at]
            full[at, rows(c * local_mid, local_mid)] = act.astype(bf16)

    gather_over_ch(full, local_mid, tile, TILES, g_near, g_far, g_hop, ready)


def run_stage_two(cid, padded, valid, weight, affine):
    pixels, local_mid = valid.shape[0], padded.shape[3]
    outs = [
        shape((pixels, local_mid), f32),
        shape((pixels, SPLIT * local_mid), bf16),
        shape((pixels, 9 * local_mid), bf16),
        shape((8, local_mid), f32),
    ]
    scratch = (
        [pltpu.VMEM((pixels, local_mid), f32)]
        + sum_scratch(pixels, local_mid, TILES)
        + stat_scratch(local_mid)
        + gather_scratch(TILES)
    )
    return call("stage_two", cid, stage_two, [padded, valid, weight, affine], outs, scratch)


def stage_three(full, weight, masked, valid, affine, *refs):
    (norm, classes, stat, inputs) = refs[:4]
    (hidden, trunk, send, recv, stat_sems, class_sems, own_sem, in_sems) = refs[4:]
    p, c = lax.axis_index("pix"), lax.axis_index("ch")
    pixels, n = masked.shape
    barrier, expected = greet((1, 2), FAR_FIRST)
    tile = pixels // TILES
    for t in range(TILES):
        at = pl.ds(t * tile, tile)
        hidden[at] = jnp.dot(full[at], weight[...], preferred_element_type=f32)
    pl.semaphore_wait(barrier, expected)
    far = push(masked, inputs.at[c], in_sems.at[0, 0], in_sems.at[1, 0], (p, c ^ 2))
    near = push(masked, inputs.at[c], in_sems.at[0, 1], in_sems.at[1, 1], (p, c ^ 1))
    mine = keep(masked, inputs.at[c], own_sem.at[1])
    center, scale, count = norm_stats(hidden, valid, pixels, send, recv, stat_sems)
    stat[0:1] = center
    stat[1:2] = scale
    stat[2:3] = count

    def finish(to):
        def half(i, carry):
            at = rows(to * 128 + i * 32, 32)
            value = (hidden[at] - center) * scale
            norm[at] = value
            pre = value * affine[0:1] + affine[1:2] + masked[at].astype(f32)
            v = valid[at]
            trunk[at] = (silu(pre) * jnp.concatenate([v] * (n // 128), axis=1)).astype(bf16)
            return carry

        loop(4, half, 0)

    copies = []
    for k in FAR_FIRST:
        to = p ^ k
        finish(to)
        copies.append(
            push(
                trunk.at[rows(to * 128, 128)],
                classes.at[rows(p * 128, 128)],
                class_sems.at[0, k],
                class_sems.at[1, k],
                (to, c),
            )
        )
    finish(p)
    copies.append(keep(trunk.at[rows(p * 128, 128)], classes.at[rows(p * 128, 128)], own_sem.at[0]))
    far.wait_recv()
    hop = push(inputs.at[c ^ 2], inputs.at[c ^ 2], in_sems.at[0, 2], in_sems.at[1, 2], (p, c ^ 1))
    far.wait_send()
    near.wait()
    mine.wait()
    hop.wait()
    for copy in copies:
        copy.wait()


def run_stage_three(cid, full, weight, masked, valid, affine):
    pixels, n = masked.shape
    outs = [
        shape((pixels, n), f32),
        shape((pixels, n), bf16),
        shape((8, n), f32),
        shape((SPLIT, pixels, n), bf16),
    ]
    scratch = (
        [pltpu.VMEM((pixels, n), f32), pltpu.VMEM((pixels, n), bf16)]
        + stat_scratch(n)
        + [dma(2, PHASES), dma(2), dma(2, 3)]
    )
    return call("stage_three", cid, stage_three, [full, weight, masked, valid, affine], outs, scratch, hbm_outs=(3,))


RATE_ROWS = tuple(rate // ROW_CLASSES for rate in aspp_rates)
RATE_COLS = tuple(rate // COL_CLASSES for rate in aspp_rates)


def load_pyramid(weight, wide, sems):
    m = weight.shape[4]
    return [
        [keep(weight.at[j, a, b], wide.at[3 * j + a, :, b * m : (b + 1) * m], sems.at[3 * j + a, b]) for b in range(3)]
        for j in range(3)
        for a in range(3)
    ]


def move_cols(x, by):
    place = lax.broadcasted_iota(jnp.int32, x.shape, 0) % 32
    rolled = pltpu.roll(x, by % x.shape[0], 0)
    return jnp.where(place < by, 0.0, rolled) if by > 0 else jnp.where(place >= 32 + by, 0.0, rolled)


def ch_exchange(send, recv, sems):
    p, c = lax.axis_index("pix"), lax.axis_index("ch")
    copies = [push(send, recv.at[c], sems.at[0, k], sems.at[1, k], (p, c ^ k)) for k in (2, 3, 1)]
    recv[c] = send[...]
    for copy in copies:
        copy.wait()


def add_up(recv, parts):
    value = recv[0]
    for i in range(1, parts):
        value = value + recv[i]
    return value


def task_vector(square, weights):
    product = square * weights
    row = lax.broadcasted_iota(jnp.int32, (32, 32), 0)
    col = lax.broadcasted_iota(jnp.int32, (32, 32), 1)

    def task(i):
        return (i >= CLS).astype(jnp.int32) + (i >= CLS + 1).astype(jnp.int32)

    def entry(t, s):
        return jnp.sum(
            jnp.sum(jnp.where((task(row) == t) & (task(col) == s), product, 0.0), axis=1, keepdims=True),
            axis=0,
            keepdims=True,
        )

    gram = [[entry(t, s) for s in range(3)] for t in range(3)]
    norms = [jnp.sqrt(gram[k][k] + 1e-06) for k in range(3)]
    proj = [[gram[i][k] / norms[k] for k in range(3)] for i in range(3)]
    vector = [proj[0][0] - proj[0][b] for b in (1, 2)]
    matrix = [[proj[0][0] - proj[0][b] - proj[a][0] + proj[a][b] for b in (1, 2)] for a in (1, 2)]
    determinant = matrix[0][0] * matrix[1][1] - matrix[0][1] * matrix[1][0]
    second = (vector[0] * matrix[1][1] - vector[1] * matrix[1][0]) / determinant
    third = (vector[1] * matrix[0][0] - vector[0] * matrix[0][1]) / determinant
    which = task(lax.broadcasted_iota(jnp.int32, (32, 1), 0))
    return jnp.where(which == 0, 1.0 - second - third, jnp.where(which == 1, second, third))


def slope(x):
    s = 1.0 / (1.0 + jnp.exp(-x))
    return s * (1.0 + x * (1.0 - s))


def pyramid(trunk, weight, affine, heads, targets, square, *refs):
    (full, predictions, head_grad, sums, others, picks) = refs[:6]
    refs = refs[2:]
    (wide, sides, own, out, near, cross, hidden, pre, grad, branch) = refs[4:14]
    (s_send, s_ch, s_mid, s_pix, b_send, b_ch, b_mid, b_pix) = refs[14:22]
    (h_send, h_ch, h_mid, h_pix, h_sum, p_send, p_ch) = refs[22:29]
    (w_sems, near_sems, far_sems, ch_sems, pix_sems, g_near, g_far, g_hop, y_sems, picked, pick_sems) = refs[29:]
    p, c = lax.axis_index("pix"), lax.axis_index("ch")
    k, x = lax.rem(c, 2), c // 2
    m = weight.shape[4]
    quarter = targets.shape[0] // SPLIT
    barrier, expected = greet((1, 2, 3), FAR_FIRST)
    loads = load_pyramid(weight, wide, w_sems)
    contract0 = (((0,), (0,)), ((), ()))
    contract1 = (((1,), (1,)), ((), ()))
    head = heads[...]
    scaled = head * task_vector(
        add_up(square, PHASES)[:, :32], lax.dot_general(head, head, contract1, precision=highest)
    )
    mine = rows(c * quarter, quarter)
    target, mask = targets[mine, :32], targets[mine, 32:33]
    grad[...] = jnp.dot(target, scaled, precision=highest) * mask
    pl.semaphore_wait(barrier, expected)
    halves = [pl.ds(0, trunk.shape[0] // 2), pl.ds(trunk.shape[0] // 2, trunk.shape[0] // 2)]
    to_y, to_z = [None, None], [None, None]
    for i in range(2):
        to_y[i] = push(trunk.at[halves[i]], others.at[0, halves[i]], y_sems.at[0, i], y_sems.at[1, i], (p ^ 1, c))
        h = 1 - i
        to_z[h] = push(
            trunk.at[halves[h]], others.at[1, halves[h]], y_sems.at[0, 2 + i], y_sems.at[1, 2 + i], (p ^ 2, c)
        )

    copies = []
    for j in range(3):
        s, q = RATE_ROWS[j] * 32, RATE_COLS[j]
        for a in (1, 0, 2):
            for load in loads[3 * j + a]:
                load.wait()
            if a == 1:
                sides[...] = jnp.dot(trunk[...], wide[3 * j + 1], preferred_element_type=f32)
            elif a == 0:
                sides[s:] += jnp.dot(trunk[: 1024 - s], wide[3 * j], preferred_element_type=f32)
            else:
                sides[: 1024 - s] += jnp.dot(trunk[s:], wide[3 * j + 2], preferred_element_type=f32)
        for d in range(SPLIT):
            at = slice(d * quarter, (d + 1) * quarter)
            value = (
                sides[at, m : 2 * m]
                + move_cols(sides[at, :m], q)
                + move_cols(sides[at, 2 * m :], -q)
            )
            own[d, j] = value
            out[d, j] = value.astype(bf16)
        copies.append(
            [
                push(out.at[2 * h + 1 - k, j], near.at[h, j], near_sems.at[0, j, h], near_sems.at[1, j, h], (p, c ^ 1))
                for h in range(2)
            ]
        )
        if j == 1:
            to_y[0].wait_recv()
            on_z = push(others.at[0, halves[0]], others.at[2, halves[0]], y_sems.at[0, 4], y_sems.at[1, 4], (p ^ 2, c))
            to_z[1].wait_recv()
            on_y = push(others.at[1, halves[1]], others.at[2, halves[1]], y_sems.at[0, 5], y_sems.at[1, 5], (p ^ 1, c))
        if j > 0:
            copies[j - 1] = cross_chips(copies[j - 1], j - 1, own, near, cross, far_sems)
    copies[2] = cross_chips(copies[2], 2, own, near, cross, far_sems)
    count = total(jnp.broadcast_to(mask, (quarter, 128)))[:, :1]
    for j in range(3):
        copies[j].wait()
        value = own[2 * x + k, j] + near[x, j].astype(f32) + cross[1, j].astype(f32)
        at = slice(j * m, (j + 1) * m)
        hidden[:, at] = value
        first = total(value * mask)
        apart = value - first / jnp.maximum(count, 1.0)
        s_send[j : j + 1] = first
        s_send[3 + j : 4 + j] = total(apart * apart * mask)
    s_send[6:7] = jnp.broadcast_to(count, (1, m))
    s_send[7:8] = jnp.zeros((1, m), f32)

    def merge(recv, parts):
        number = recv[0, 6:7]
        for i in range(1, parts):
            number = number + recv[i, 6:7]
        whole, spread = recv[0, 0:3], recv[0, 3:6]
        for i in range(1, parts):
            whole, spread = whole + recv[i, 0:3], spread + recv[i, 3:6]
        center = whole / jnp.maximum(number, 1.0)
        for i in range(parts):
            n = recv[i, 6:7]
            apart = recv[i, 0:3] / jnp.maximum(n, 1.0) - center
            spread = spread + n * apart * apart
        return whole, spread, number

    ch_exchange(s_send, s_ch, ch_sems.at[0])
    whole, spread, number = merge(s_ch, SPLIT)
    s_mid[0:3] = whole
    s_mid[3:6] = spread
    s_mid[6:7] = number
    s_mid[7:8] = jnp.zeros((1, m), f32)
    pix_exchange(s_mid, s_pix, pix_sems.at[0])
    whole, spread, number = merge(s_pix, PHASES)
    center, scale = whole / number, lax.rsqrt(spread / number + epsilon)
    for j in range(3):
        at = slice(j * m, (j + 1) * m)
        norm = (hidden[:, at] - center[j : j + 1]) * scale[j : j + 1]
        hidden[:, at] = norm
        value = norm * affine[0:1, at] + affine[1:2, at]
        branch[:, at] = (silu(value) * mask).astype(bf16)
        back = grad[:, at] * slope(value)
        grad[:, at] = back
        b_send[j : j + 1] = total(back)
        b_send[3 + j : 4 + j] = total(back * norm)
    b_send[6:8] = jnp.zeros((2, m), f32)
    p_send[...] = lax.dot_general(
        head.astype(bf16), branch[...], contract1, preferred_element_type=f32
    )
    h_send[...] = lax.dot_general(
        target, branch[...].astype(f32), contract0, precision=highest, preferred_element_type=f32
    )
    background = [
        [push(p_send, p_ch.at[c], ch_sems.at[1, 0, i], ch_sems.at[1, 1, i], (p, c ^ i)) for i in (2, 3, 1)],
        [
            push(h_send.at[rows((c ^ i) * 8, 8)], h_ch.at[c], ch_sems.at[2, 0, i], ch_sems.at[2, 1, i], (p, c ^ i))
            for i in (2, 3, 1)
        ],
    ]
    p_ch[c] = p_send[...]
    h_ch[c] = h_send[rows(c * 8, 8)]
    ch_exchange(b_send, b_ch, ch_sems.at[3])
    b_mid[...] = add_up(b_ch, SPLIT)
    for copy in background[0] + background[1]:
        copy.wait()
    h_mid[...] = add_up(h_ch, SPLIT)
    sending = [
        push(b_mid, b_pix.at[p], pix_sems.at[1, 0, i], pix_sems.at[1, 1, i], (p ^ i, c)) for i in FAR_FIRST
    ]
    b_pix[p] = b_mid[...]

    def half(to):
        return p_ch.at[to // 2, :, rows(lax.rem(to, 2) * 128, 128)]

    background = [
        push(half(p ^ i), predictions.at[p], pix_sems.at[2, 0, i], pix_sems.at[2, 1, i], (p ^ i, c)) for i in FAR_FIRST
    ] + [push(h_mid, h_pix.at[p], pix_sems.at[3, 0, i], pix_sems.at[3, 1, i], (p ^ i, c)) for i in FAR_FIRST]
    predictions[p] = half(p)[...]
    h_pix[p] = h_mid[...]
    for copy in sending:
        copy.wait()
    summed = add_up(b_pix, PHASES)
    sums[...] = summed
    for j in range(3):
        at = slice(j * m, (j + 1) * m)
        value = grad[:, at] - mask * (summed[j : j + 1] + hidden[:, at] * summed[3 + j : 4 + j]) / number
        full[mine, at] = (affine[0:1, at] * scale[j : j + 1] * value).astype(bf16)
    far = push(full.at[mine], full.at[mine], g_far.at[0], g_far.at[1], (p, c ^ 2))
    by = push(full.at[mine], full.at[mine], g_near.at[0], g_near.at[1], (p, c ^ 1))
    group = lax.rem(p, 4)
    pick = pick_rows(m, m, 0)
    for j in range(3):
        value = lax.dot_general(
            pick, full[mine, j * m : (j + 1) * m], contract1, preferred_element_type=f32
        ).astype(bf16)
        for g in range(4):
            picked[g, j * 64 : (j + 1) * 64] = value[g * 64 : (g + 1) * 64]
    sent_picks = [
        push(picked.at[group ^ i], picks.at[i - 1], pick_sems.at[0, i], pick_sems.at[1, i], (p ^ i, c)) for i in (3, 1, 2)
    ]
    for copy in background:
        copy.wait()
    own_rows = add_up(h_pix, PHASES)
    h_sum[...] = own_rows
    head_grad[rows(c * 8, 8)] = own_rows
    last = [
        push(h_sum, head_grad.at[rows(c * 8, 8)], ch_sems.at[4, 0, i], ch_sems.at[4, 1, i], (p, c ^ i))
        for i in (2, 3, 1)
    ]
    far.wait_recv()
    theirs = rows((c ^ 2) * quarter, quarter)
    hop = push(full.at[theirs], full.at[theirs], g_hop.at[0], g_hop.at[1], (p, c ^ 1))
    far.wait_send()
    by.wait()
    hop.wait()
    for copy in last:
        copy.wait()
    to_y[0].wait_send()
    to_z[1].wait_send()
    for copy in [to_y[1], to_z[0], on_y, on_z] + sent_picks:
        copy.wait()


def pick_rows(m, count, first):
    row = lax.broadcasted_iota(jnp.int32, (count, m), 0)
    col = lax.broadcasted_iota(jnp.int32, (count, m), 1)
    source = (4 * (row % 64 // 32) + row // 64 + first) * 32 + row % 32
    return jnp.where(col == source, 1.0, 0.0).astype(bf16)


def cross_chips(near_copies, j, own, near, cross, sems):
    p, c = lax.axis_index("pix"), lax.axis_index("ch")
    k, x = lax.rem(c, 2), c // 2
    for copy in near_copies:
        copy.wait()
    cross[0, j] = (own[2 * (1 - x) + k, j] + near[1 - x, j].astype(f32)).astype(bf16)
    return push(cross.at[0, j], cross.at[1, j], sems.at[0, j], sems.at[1, j], (p, c ^ 2))


def run_pyramid(cid, trunk, weight, affine, heads, targets, square):
    pixels, n = trunk.shape
    m = weight.shape[4]
    quarter = pixels // SPLIT
    outs = [
        shape((pixels, 3 * m), bf16),
        shape((PHASES, 32, 128), f32),
        shape((32, 3 * m), f32),
        shape((8, m), f32),
        shape((3, pixels, n), bf16),
        shape((3, 192, quarter), bf16),
    ]
    small = [pltpu.VMEM((8, m), f32), pltpu.VMEM((SPLIT, 8, m), f32), pltpu.VMEM((8, m), f32), pltpu.VMEM((PHASES, 8, m), f32)]
    scratch = (
        [
            pltpu.VMEM((9, n, 3 * m), bf16),
            pltpu.VMEM((pixels, 3 * m), f32),
            pltpu.VMEM((SPLIT, 3, quarter, m), f32),
            pltpu.VMEM((SPLIT, 3, quarter, m), bf16),
            pltpu.VMEM((2, 3, quarter, m), bf16),
            pltpu.VMEM((2, 3, quarter, m), bf16),
            pltpu.VMEM((quarter, 3 * m), f32),
            pltpu.VMEM((8, 128), f32),
            pltpu.VMEM((quarter, 3 * m), f32),
            pltpu.VMEM((quarter, 3 * m), bf16),
        ]
        + small
        + small
        + [
            pltpu.VMEM((32, 3 * m), f32),
            pltpu.VMEM((SPLIT, 8, 3 * m), f32),
            pltpu.VMEM((8, 3 * m), f32),
            pltpu.VMEM((PHASES, 8, 3 * m), f32),
            pltpu.VMEM((8, 3 * m), f32),
            pltpu.VMEM((32, quarter), f32),
            pltpu.VMEM((SPLIT, 32, quarter), f32),
        ]
        + [dma(9, 3), dma(2, 3, 2), dma(2, 3), dma(5, 2, SPLIT), dma(4, 2, PHASES), dma(2), dma(2), dma(2), dma(2, 6)]
        + [pltpu.VMEM((4, 192, quarter), bf16), dma(2, 4)]
    )
    vmem = pl.BlockSpec(memory_space=pltpu.VMEM)
    specs = [vmem] * 6
    specs[1] = pl.BlockSpec(memory_space=pl.ANY)
    return pl.pallas_call(
        pyramid,
        out_shape=outs,
        in_specs=specs,
        out_specs=[vmem] * 4 + [pl.BlockSpec(memory_space=pl.ANY), vmem],
        scratch_shapes=scratch,
        compiler_params=pltpu.CompilerParams(
            collective_id=cid, has_side_effects=True, vmem_limit_bytes=VMEM_BYTES
        ),
        name="pyramid",
    )(trunk, weight, affine, heads, targets, square)


PACE = (2, 10, 16, 18)


def packed_sums(values, send):
    i = 0
    for value in values:
        for g in range(value.shape[1] // 128):
            send[i : i + 1] = value[:, g * 128 : (g + 1) * 128]
            i += 1


def unpacked_sums(recv, rows_each, count):
    out, i = [], 0
    for _ in range(count):
        parts = []
        for _ in range(rows_each):
            value = recv[0, i : i + 1]
            for d in range(1, PHASES):
                value = value + recv[d, i : i + 1]
            parts.append(value)
            i += 1
        out.append(parts[0] if rows_each == 1 else jnp.concatenate(parts, axis=1))
    return out


def spread_lanes(v, n):
    return v if n == 128 else jnp.concatenate([v] * (n // 128), axis=1)


def backward(
    grads, trunk, others, weight, norm3, masked, valid, expand, affine3, norm2, affine2, full2, taps, dilated,
    norm1, affine1, reduce_rows, stats1, stats2, stats3, picks, inputs, *refs
):
    outs, scratch = refs[:8], refs[8:]
    (features_grad, aspp_parts, dilated_grad, expand_grad, reduce_grad, sums3_out, sums2_out, sums1_out) = outs
    (wide, moved, acc, dsend, drecv, tpad, r_in, picked_in, turned, zsend, r_y) = scratch[:11]
    (gp3, g3, own, out, near, cross, hidden, gp2, g2, prod, edges, g1) = scratch[11:23]
    gp1, lanes = gp2, own
    (st3, st3r, st2, st2r, st1, st1r, e_part, e_mid, e_in, e_y, e_sum, d_part, d_in, d_y, d_sum, r_mid, r_sum) = scratch[23:40]
    (w_sems, d_sems, y_sems, z_sems, near_sems, far_sems, st_sems, gn, gf, gh, gn1, gf1, gh1, edge_sems, ch_sems, pix_sems, pair_sems, own_sems, tap_sems, in_sems) = scratch[40:]
    p, c = lax.axis_index("pix"), lax.axis_index("ch")
    y, z = lax.rem(p, 2), p // 2
    pixels, n = norm3.shape
    m = weight.shape[4]
    mid = norm2.shape[1]
    tile = pixels // TILES
    contract0 = (((0,), (0,)), ((), ()))
    contract1 = (((1,), (1,)), ((), ()))
    count = stats1[2:3, :1]
    barrier, expected = greet((1, 2, 3), FAR_FIRST)
    loads = load_pyramid(weight, wide, w_sems)

    group, upper = lax.rem(p, 4), p // 4
    quarter = picks.shape[2]
    pl.semaphore_wait(barrier, expected)
    mine = rows(c * quarter, quarter)
    sent_picks = [
        push(picks, picked_in.at[:, :, mine], y_sems.at[0, k], y_sems.at[1, k], (p, c ^ k)) for k in (2, 3, 1)
    ] + [keep(picks, picked_in.at[:, :, mine], y_sems.at[0, 0])]
    filled = [keep(trunk, tpad.at[0, 64 : 64 + pixels], y_sems.at[2, 0])] + [
        keep(others.at[k - 1], tpad.at[k, 64 : 64 + pixels], y_sems.at[2, k]) for k in (1, 2, 3)
    ]
    for i in range(4):
        tpad[i, :64] = jnp.zeros((64, n), bf16)
        tpad[i, 64 + pixels :] = jnp.zeros((64, n), bf16)

    for j in range(3):
        q = RATE_COLS[j]
        plain = grads[:, j * m : (j + 1) * m]
        value = plain.astype(f32)
        moved[j, :, :m] = move_cols(value, -q).astype(bf16)
        moved[j, :, m : 2 * m] = plain
        moved[j, :, 2 * m :] = move_cols(value, q).astype(bf16)
    back = []
    for h in range(2):
        half = slice(h * m, (h + 1) * m)
        for j in range(3):
            s = RATE_ROWS[j] * 32
            for a in (1, 0, 2):
                if h == 0:
                    for load in loads[3 * j + a]:
                        load.wait()
                w = wide[3 * j + a, half]
                if a == 1:
                    value = lax.dot_general(moved[j], w, contract1, preferred_element_type=f32)
                    if j == 0:
                        acc[...] = value
                    else:
                        acc[...] += value
                elif a == 0:
                    acc[: pixels - s] += lax.dot_general(moved[j, s:], w, contract1, preferred_element_type=f32)
                else:
                    acc[s:] += lax.dot_general(moved[j, : pixels - s], w, contract1, preferred_element_type=f32)
        dsend[h] = acc[...].astype(bf16)
        for k in FAR_FIRST:
            back.append(
                push(
                    dsend.at[h, rows((p ^ k) * 128, 128)],
                    drecv.at[h, rows(p * 128, 128)],
                    d_sems.at[0, h, k],
                    d_sems.at[1, h, k],
                    (p ^ k, c),
                )
            )
        back.append(keep(dsend.at[h, rows(p * 128, 128)], drecv.at[h, rows(p * 128, 128)], own_sems.at[h]))

    all_inputs = [
        keep(inputs.at[i // 2, pl.ds(i % 2 * n, n)], wide.at[i, :, :n], in_sems.at[i]) for i in range(8)
    ]
    cut = moved.shape[2]
    own_taps = [
        keep(taps.at[:, :cut], moved.at[0], tap_sems.at[0]),
        keep(taps.at[:, cut:], moved.at[1, :, : taps.shape[1] - cut], tap_sems.at[1]),
    ]

    place = lax.broadcasted_iota(jnp.int32, (64, pixels), 1) % 32

    def turn(i, part):
        at = slice(i * pixels, (i + 1) * pixels)
        for j in range(3):
            q = RATE_COLS[j]
            plain = part(j)
            value = plain.astype(f32)
            turned[j, :64, at] = jnp.where(place >= 32 - q, 0.0, pltpu.roll(value, pixels - q, 1)).astype(bf16)
            turned[j, 64:128, at] = plain
            turned[j, 128:, at] = jnp.where(place < q, 0.0, pltpu.roll(value, q, 1)).astype(bf16)

    pick = pick_rows(m, 64, group)
    turn(
        0,
        lambda j: lax.dot_general(
            pick, grads[:, j * m : (j + 1) * m], contract1, preferred_element_type=f32
        ).astype(bf16),
    )
    for copy in sent_picks:
        copy.wait()
    for k in (1, 2, 3):
        turn(k, lambda j: picked_in[k - 1, j * 64 : (j + 1) * 64])
    for copy in filled:
        copy.wait()
    for j in range(3):
        s = RATE_ROWS[j] * 32
        for a in range(3):
            if a == 1:
                low, high, start = 0, pixels, 64
            elif a == 0:
                low, high = s // 128 * 128, pixels
                start = 64 + low - s
            else:
                low, high, start = 0, -(-(pixels - s) // 128) * 128, 64 + s
            value = None
            for i in range(4):
                term = jnp.dot(
                    turned[j, :, i * pixels + low : i * pixels + high],
                    tpad[i, start : start + high - low],
                    preferred_element_type=f32,
                )
                value = term if value is None else value + term
            value = value.astype(bf16)
            for b in range(3):
                for to in range(2):
                    at = b * 64 + to * 32
                    zsend[to, (3 * j + a) * 3 + b] = value[at : at + 32]
    for copy in back:
        copy.wait()
    zcopies = [keep(zsend.at[upper], aspp_parts.at[0], own_sems.at[2])]

    def send_parts(first, end):
        for i in range(first, end):
            zcopies.append(
                push(zsend.at[1 - upper, i], aspp_parts.at[1, i], z_sems.at[0, i], z_sems.at[1, i], (p ^ 4, c))
            )

    send_parts(0, PACE[0])

    def over_z(blocks, sums, sems, own_sem):
        return [
            push(blocks.at[z ^ k], sums.at[z], sems.at[0, k], sems.at[1, k], (p ^ (2 * k), c)) for k in (3, 2, 1)
        ] + [keep(blocks.at[z], sums.at[z], own_sem)]

    def norm_back(grad, norm, sums, scale, gain, v):
        return gain * scale * (grad - v * (sums[0] + norm * sums[1]) / count)

    def three(i, carry):
        at = rows(i * 32, 32)
        norm = norm3[at]
        pre = norm * affine3[0:1] + affine3[1:2] + masked[at].astype(f32)
        grad = jnp.concatenate([drecv[0, at], drecv[1, at]], axis=1).astype(f32)
        grad = grad * spread_lanes(valid[at], n) * slope(pre)
        gp3[at] = grad
        return carry[0] + fold(grad), carry[1] + fold(grad * norm)

    zero = jnp.zeros((8, n), f32)
    bias, gain = loop(pixels // 32, three, (zero, zero))
    packed_sums((total(bias), total(gain)), st3)
    pix_exchange(st3, st3r, st_sems.at[0])
    send_parts(PACE[0], PACE[1])
    sums = unpacked_sums(st3r, n // 128, 2)
    sums3_out[0:1] = sums[0]
    sums3_out[1:2] = sums[1]

    def part3(t):
        def step(i, carry):
            at = rows(t * tile + i * 32, 32)
            v = spread_lanes(valid[at], n)
            g3[at] = norm_back(gp3[at], norm3[at], sums, stats3[1:2], affine3[0:1], v).astype(bf16)
            return carry

        loop(tile // 32, step, 0)
        return lax.dot_general(g3[t * tile : (t + 1) * tile], expand[...], contract1, preferred_element_type=f32)

    result = sum_over_ch(part3, tile, TILES, own, out, near, cross, near_sems.at[0], far_sems.at[0])
    value = lax.dot_general(full2[...], g3[...], contract0, preferred_element_type=f32).astype(bf16)
    for d in range(SPLIT):
        e_part[d] = value[d * mid : (d + 1) * mid]
    e_copies = [
        push(e_part.at[c ^ k], e_mid.at[c], ch_sems.at[0, 0, k], ch_sems.at[0, 1, k], (p, c ^ k)) for k in (2, 3, 1)
    ]
    e_copies.append(keep(e_part.at[c], e_mid.at[c], own_sems.at[3]))

    bias, gain = jnp.zeros((8, mid), f32), jnp.zeros((8, mid), f32)
    for t in range(TILES):
        hidden[t * tile : (t + 1) * tile] = result(t)

    def two(i, carry):
        at = rows(i * 128, 128)
        norm = norm2[at]
        grad = hidden[at] * valid[at] * slope(norm * affine2[0:1] + affine2[1:2])
        gp2[at] = grad
        return carry[0] + fold(grad), carry[1] + fold(grad * norm)

    bias, gain = loop(pixels // 128, two, (bias, gain))
    packed_sums((total(bias), total(gain)), st2)
    pix_exchange(st2, st2r, st_sems.at[1])
    send_parts(PACE[1], PACE[2])
    for copy in e_copies:
        copy.wait()
    e_to_y = push(
        e_mid.at[:, :, rows((1 - y) * 256, 256)], e_in, pair_sems.at[0, 0], pair_sems.at[1, 0], (p ^ 1, c)
    )
    sums2 = unpacked_sums(st2r, 1, 2)
    sums2_out[0:1] = sums2[0]
    sums2_out[1:2] = sums2[1]

    def ready2(t):
        def step(i, carry):
            at = rows(t * tile + i * 128, 128)
            value = norm_back(gp2[at], norm2[at], sums2, stats2[1:2], affine2[0:1], valid[at])
            g2[at, rows(c * mid, mid)] = value.astype(bf16)
            return carry

        loop(tile // 128, step, 0)

    gather_over_ch(g2, mid, tile, TILES, gn, gf, gh, ready2)

    e_to_y.wait()
    for d in range(4):
        e_y[d] = (e_mid[d, :, rows(y * 256, 256)].astype(f32) + e_in[d].astype(f32)).astype(bf16)
    pix_copies = over_z(e_y, e_sum, pix_sems.at[0], own_sems.at[5])

    place = lax.broadcasted_iota(jnp.int32, (128, mid), 0) % 32

    def across(i, a):
        beta = i % COL_CLASSES
        two_on = (beta + 2) % 4 * 128
        here = slice(beta * 128, (beta + 1) * 128)
        there = slice(two_on, two_on + 128)
        lane = lambda b: slice((3 * a + b) * mid, (3 * a + b + 1) * mid)
        left, right = prod[there, lane(0)], prod[there, lane(2)]
        if beta >= 2:
            left = jnp.where(place == 31, 0.0, pltpu.roll(left, 127, 0))
        else:
            right = jnp.where(place == 0, 0.0, pltpu.roll(right, 1, 0))
        return prod[here, lane(1)] + left + right

    for i in range(PHASES):
        at = slice(i * 128, (i + 1) * 128)
        if i % COL_CLASSES == 0:
            prod[...] = lax.dot_general(
                g2[i * 128 : (i + COL_CLASSES) * 128], dilated[...], contract1, preferred_element_type=f32
            )
        up, same, down = across(i, 0), across(i, 1), across(i, 2)
        zero = jnp.zeros((32, mid), f32)
        hidden[at] = same + jnp.concatenate([up[32:], zero]) + jnp.concatenate([zero, down[:96]])
        edges[0, i] = up[:32].astype(bf16)
        edges[1, i] = down[96:].astype(bf16)
    first, last = p == 0, p == PHASES - 1
    to_next = lambda: pltpu.make_async_remote_copy(
        src_ref=edges.at[1], dst_ref=edges.at[2], send_sem=edge_sems.at[0, 0], recv_sem=edge_sems.at[1, 0],
        device_id=(p + 1, c), device_id_type=MESH,
    )
    to_last = lambda: pltpu.make_async_remote_copy(
        src_ref=edges.at[0], dst_ref=edges.at[3], send_sem=edge_sems.at[0, 1], recv_sem=edge_sems.at[1, 1],
        device_id=(p - 1, c), device_id_type=MESH,
    )

    @pl.when(jnp.logical_not(last))
    def _():
        to_next().start()

    @pl.when(jnp.logical_not(first))
    def _():
        to_last().start()

    @pl.when(first)
    def _():
        edges[2] = jnp.zeros((PHASES, 32, mid), bf16)

    @pl.when(last)
    def _():
        edges[3] = jnp.zeros((PHASES, 32, mid), bf16)

    for copy in own_taps:
        copy.wait()
    value = jnp.concatenate(
        [
            lax.dot_general(g2[...], moved[0], contract0, preferred_element_type=f32).astype(bf16),
            lax.dot_general(
                g2[...], moved[1, :, : taps.shape[1] - cut], contract0, preferred_element_type=f32
            ).astype(bf16),
        ],
        axis=1,
    )
    out_rows = SPLIT * mid // PHASES
    for d in range(PHASES):
        d_part[d % 2, d // 2] = value[d * out_rows : (d + 1) * out_rows]
    d_to_y = push(d_part.at[1 - y], d_in, pair_sems.at[0, 1], pair_sems.at[1, 1], (p ^ 1, c))

    @pl.when(jnp.logical_not(last))
    def _():
        to_next().wait_send()
        to_last().wait_recv()

    @pl.when(jnp.logical_not(first))
    def _():
        to_last().wait_send()
        to_next().wait_recv()

    send_parts(PACE[2], PACE[3])

    bias, gain = jnp.zeros((8, mid), f32), jnp.zeros((8, mid), f32)
    for i in range(PHASES):
        at = slice(i * 128, (i + 1) * 128)
        zero = jnp.zeros((64, mid), f32)
        edge = jnp.concatenate([edges[2, i].astype(f32), zero, edges[3, i].astype(f32)])
        norm = norm1[at]
        grad = (hidden[at] + edge) * valid[at] * slope(norm * affine1[0:1] + affine1[1:2])
        gp1[at] = grad
        bias, gain = bias + fold(grad), gain + fold(grad * norm)
    packed_sums((total(bias), total(gain)), st1)
    pix_exchange(st1, st1r, st_sems.at[2])
    send_parts(PACE[3], 27)
    sums1 = unpacked_sums(st1r, 1, 2)
    sums1_out[0:1] = sums1[0]
    sums1_out[1:2] = sums1[1]

    def ready1(t):
        def step(i, carry):
            at = rows(t * tile + i * 128, 128)
            value = norm_back(gp1[at], norm1[at], sums1, stats1[1:2], affine1[0:1], valid[at])
            g1[at, rows(c * mid, mid)] = value.astype(bf16)
            return carry

        loop(tile // 128, step, 0)

    late = []

    def between():
        for copy in all_inputs:
            copy.wait()
        own_g1 = g1[:, rows(c * mid, mid)]
        for i in range(SPLIT):
            value = lax.dot_general(wide[2 * i, :, :n], own_g1[:n], contract0, preferred_element_type=f32)
            value = value + lax.dot_general(wide[2 * i + 1, :, :n], own_g1[n:], contract0, preferred_element_type=f32)
            r_mid[i] = value.astype(bf16).reshape(2, 256, mid)
        late.append(push(r_mid.at[:, 1 - y], r_in, pair_sems.at[0, 2], pair_sems.at[1, 2], (p ^ 1, c)))
        d_to_y.wait()
        for d in range(4):
            d_y[d] = (d_part[y, d].astype(f32) + d_in[d].astype(f32)).astype(bf16)
        pix_copies.extend(over_z(d_y, d_sum, pix_sems.at[1], own_sems.at[6]))

    gather_over_ch(g1, mid, tile, TILES, gn1, gf1, gh1, ready1, between)
    late[0].wait()
    for d in range(4):
        r_y[d] = (r_mid[d, y].astype(f32) + r_in[d].astype(f32)).astype(bf16)
    pix_copies += over_z(r_y, r_sum, pix_sems.at[2], own_sems.at[7])

    for i in range(PHASES):
        at = slice(i * 128, (i + 1) * 128)
        value = lax.dot_general(g1[at], reduce_rows[...], contract1, preferred_element_type=f32) + gp3[at]
        value = value * spread_lanes(valid[at], n)
        for g in range(n // 128):
            for r in range(4):
                start = (2 * r + i // COL_CLASSES) * 128 + i % COL_CLASSES
                lanes[g, pl.ds(start, 32, stride=COL_CLASSES), :] = value[r * 32 : (r + 1) * 32, g * 128 : (g + 1) * 128]
    for g in range(n // 128):
        features_grad[:, g * 128 : (g + 1) * 128] = lanes[g].astype(bf16)
    for copy in pix_copies:
        copy.wait()

    def gathered(parts):
        value = parts[0].astype(f32)
        for d in range(1, parts.shape[0]):
            value = value + parts[d].astype(f32)
        return value

    expand_grad[...] = gathered(e_sum)
    reduce_grad[...] = gathered(r_sum)
    dilated_grad[...] = gathered(d_sum)
    for copy in zcopies:
        copy.wait()


def run_backward(cid, arrays):
    (grads, trunk, others, weight, norm3, masked, valid, expand, affine3, norm2, affine2, full2, taps, dilated,
     norm1, affine1, reduce_rows, stats1, stats2, stats3, picks, inputs) = arrays
    pixels, n = norm3.shape
    m = weight.shape[4]
    mid = norm2.shape[1]
    all_mid = SPLIT * mid
    outs = [
        shape((pixels, n), bf16),
        shape((2, 27, 32, n), bf16),
        shape((all_mid // PHASES, 9 * mid), f32),
        shape((mid, 256), f32),
        shape((256, mid), f32),
        shape((8, n), f32),
        shape((8, mid), f32),
        shape((8, mid), f32),
    ]
    sums = sum_scratch(pixels, mid, TILES)
    scratch = [
        pltpu.VMEM((9, n, 3 * m), bf16),
        pltpu.VMEM((3, pixels, 3 * m), bf16),
        pltpu.VMEM((pixels, m), f32),
        pltpu.VMEM((2, pixels, m), bf16),
        pltpu.VMEM((2, pixels, m), bf16),
        pltpu.VMEM((4, pixels + 128, n), bf16),
        pltpu.VMEM((4, 256, mid), bf16),
        pltpu.VMEM((3, 192, pixels), bf16),
        pltpu.VMEM((3, 192, 4 * pixels), bf16),
        pltpu.VMEM((2, 27, 32, n), bf16),
        pltpu.VMEM((4, 256, mid), bf16),
        pltpu.VMEM((pixels, n), f32),
        pltpu.VMEM((pixels, n), bf16),
        *sums[:4],
        pltpu.VMEM((pixels, mid), f32),
        pltpu.VMEM((pixels, mid), f32),
        pltpu.VMEM((pixels, all_mid), bf16),
        pltpu.VMEM((pixels // ROW_CLASSES, 9 * mid), f32),
        pltpu.VMEM((4, PHASES, 32, mid), bf16),
        pltpu.VMEM((pixels, all_mid), bf16),
        pltpu.VMEM((8, 128), f32),
        pltpu.VMEM((PHASES, 8, 128), f32),
        pltpu.VMEM((8, 128), f32),
        pltpu.VMEM((PHASES, 8, 128), f32),
        pltpu.VMEM((8, 128), f32),
        pltpu.VMEM((PHASES, 8, 128), f32),
        pltpu.VMEM((SPLIT, mid, n), bf16),
        pltpu.VMEM((SPLIT, mid, n), bf16),
        pltpu.VMEM((4, mid, 256), bf16),
        pltpu.VMEM((4, mid, 256), bf16),
        pltpu.VMEM((4, mid, 256), bf16),
        pltpu.VMEM((2, 4, all_mid // PHASES, 9 * mid), bf16),
        pltpu.VMEM((4, all_mid // PHASES, 9 * mid), bf16),
        pltpu.VMEM((4, all_mid // PHASES, 9 * mid), bf16),
        pltpu.VMEM((4, all_mid // PHASES, 9 * mid), bf16),
        pltpu.VMEM((4, 2, 256, mid), bf16),
        pltpu.VMEM((4, 256, mid), bf16),
        dma(9, 3),
        dma(2, 2, PHASES),
        dma(3, 4),
        dma(2, 27),
        dma(1, 2, TILES, 2),
        dma(1, 2, TILES),
        dma(3, 2, PHASES),
        *gather_scratch(TILES),
        *gather_scratch(TILES),
        dma(2, 2),
        dma(2, 2, SPLIT),
        dma(3, 2, PHASES),
        dma(2, 3),
        dma(8),
        dma(2),
        dma(8),
    ]
    vmem = pl.BlockSpec(memory_space=pltpu.VMEM)
    specs = [vmem] * len(arrays)
    specs[1] = specs[2] = specs[3] = specs[12] = specs[21] = pl.BlockSpec(memory_space=pl.ANY)
    return pl.pallas_call(
        backward,
        out_shape=outs,
        in_specs=specs,
        out_specs=[vmem, pl.BlockSpec(memory_space=pl.ANY)] + [vmem] * (len(outs) - 2),
        scratch_shapes=scratch,
        compiler_params=pltpu.CompilerParams(
            collective_id=cid, has_side_effects=True, vmem_limit_bytes=VMEM_BYTES
        ),
        name="backward",
    )(*arrays)


def finish_pyramid(parts, result):
    for i in range(parts.shape[1]):
        result[i] = (parts[0, i].astype(f32) + parts[1, i].astype(f32)).T


def run_finish(parts):
    steps, n = parts.shape[1], parts.shape[3]
    each = 9
    return pl.pallas_call(
        finish_pyramid,
        grid=(steps // each,),
        out_shape=shape((steps, n, 32), f32),
        in_specs=[pl.BlockSpec((2, each, 32, n), lambda i: (0, i, 0, 0))],
        out_specs=pl.BlockSpec((each, n, 32), lambda i: (i, 0, 0)),
        name="finish_pyramid",
    )(parts)


def fast_device(
    features,
    pixel_mask,
    reduce_weight,
    reduce_gain,
    reduce_bias,
    dilated_weight,
    dilated_gain,
    dilated_bias,
    expand_weight,
    expand_gain,
    expand_bias,
    aspp_weight,
    aspp_gain,
    aspp_bias,
    task_weight,
    cotangent,
):
    rows_here, width, local_in = features.shape
    pixels = rows_here * width
    local_mid = reduce_weight.shape[1]
    full_mid = dilated_weight.shape[3]
    branch_width = aspp_weight.shape[4]
    own_branch = task_weight.shape[1]
    outs_count = task_weight.shape[2]
    me_ch = lax.axis_index("ch")
    quarter = pixels // 4
    valid = to_classes(pixel_mask.astype(f32).reshape(rows_here, width, 1)).reshape(pixels, 1)
    valid_wide = jnp.broadcast_to(valid, (pixels, 128))
    heads = jnp.concatenate(
        [
            task_weight.astype(f32).transpose(2, 0, 1).reshape(outs_count, -1),
            jnp.zeros((32 - outs_count, 3 * own_branch), f32),
            aspp_gain.reshape(1, -1),
            aspp_bias.reshape(1, -1),
            jnp.zeros((6, 3 * own_branch), f32),
        ]
    )
    heads = jnp.pad(heads, ((0, 0), (0, 256 - 3 * own_branch)))
    target_here = jnp.concatenate(
        [
            to_classes(cotangent).reshape(pixels, outs_count) * valid,
            jnp.zeros((pixels, 32 - outs_count), f32),
            valid_wide[:, :96],
        ],
        axis=1,
    )
    square = jnp.einsum("po,pq->oq", target_here[:, :32], target_here[:, :32], precision=highest)
    square = jnp.pad(square, ((0, 0), (0, 96)))

    def affine(gain, bias):
        return jnp.concatenate([gain[None], bias[None], jnp.zeros((6, gain.shape[0]), f32)])

    masked, reduce_rows, expand_cols, heads_all, target_class, square_all, norm_one, padded_one, stat_one = run_stage_one(
        1,
        features.reshape(pixels, local_in),
        valid_wide,
        reduce_weight,
        expand_weight,
        affine(reduce_gain, reduce_bias),
        heads,
        target_here.reshape(PHASES, -1, 128),
        square,
    )
    heads_all = (
        heads_all[:, :, : 3 * own_branch]
        .reshape(4, heads.shape[0], 3, own_branch)
        .transpose(1, 2, 0, 3)
        .reshape(heads.shape[0], 3 * branch_width)
    )
    head_weight, branch_gain, branch_bias = heads_all[:32], heads_all[32:33], heads_all[33:34]
    target_class = target_class.reshape(pixels, 128)

    norm_two, act_two_full, taps_one, stat_two = run_stage_two(
        2, padded_one, valid_wide, dilated_weight.reshape(9 * local_mid, full_mid), affine(dilated_gain, dilated_bias)
    )
    norm_three, trunk_class, stat_three, inputs_all = run_stage_three(
        3, act_two_full, expand_cols, masked, valid_wide, affine(expand_gain, expand_bias)
    )
    grad_full, predictions, head_grad, branch_sums, trunk_other, picks = run_pyramid(
        4, trunk_class, aspp_weight, heads_all[32:40], head_weight, target_class, square_all
    )
    predictions = from_classes(predictions.transpose(0, 2, 1), rows_here, width)[:, :, :outs_count]
    head_grad = head_grad.reshape(32, 3, 4, own_branch).transpose(2, 1, 3, 0)
    task_weight_grad = lax.dynamic_index_in_dim(head_grad, me_ch, keepdims=False)[:, :, :outs_count]
    own_sums = lax.dynamic_slice_in_dim(
        branch_sums[:6].reshape(2, 3, branch_width), me_ch * own_branch, own_branch, axis=2
    )
    aspp_bias_grad, aspp_gain_grad = own_sums[0], own_sums[1]
    dilated_rows = dilated_weight.reshape(9 * local_mid, full_mid)
    features_grad, aspp_parts, dilated_sum, expand_weight_grad, reduce_weight_grad, sums3, sums2, sums1 = run_backward(
        5,
        [
            grad_full, trunk_class, trunk_other, aspp_weight, norm_three, masked, valid_wide, expand_cols,
            affine(expand_gain, expand_bias), norm_two, affine(dilated_gain, dilated_bias), act_two_full, taps_one,
            dilated_rows, norm_one, affine(reduce_gain, reduce_bias), reduce_rows, stat_one, stat_two, stat_three, picks, inputs_all,
        ],
    )
    features_grad = features_grad.reshape(rows_here, width, local_in)
    aspp_weight_grad = run_finish(aspp_parts).reshape(3, 3, 3, local_in, -1)
    dilated_weight_grad = dilated_sum.transpose(1, 0).reshape(3, 3, local_mid, -1)
    expand_bias_grad, expand_gain_grad = sums3[0], sums3[1]
    dilated_bias_grad, dilated_gain_grad = sums2[0], sums2[1]
    reduce_bias_grad, reduce_gain_grad = sums1[0], sums1[1]

    return (
        predictions,
        features_grad,
        reduce_weight_grad,
        reduce_gain_grad,
        reduce_bias_grad,
        dilated_weight_grad,
        dilated_gain_grad,
        dilated_bias_grad,
        expand_weight_grad,
        expand_gain_grad,
        expand_bias_grad,
        aspp_weight_grad,
        aspp_gain_grad,
        aspp_bias_grad,
        task_weight_grad,
    )


def solution(mesh):
    placed = (
        P("pix", None, "ch"),
        P("pix", None),
        P(None, "ch"),
        P("ch"),
        P("ch"),
        P(None, None, "ch", None),
        P("ch"),
        P("ch"),
        P("ch", None),
        P("ch"),
        P("ch"),
        P(None, None, None, "ch", None),
        P(None, "ch"),
        P(None, "ch"),
        P(None, "ch", None),
        P("pix", None, None),
    )
    return jax.shard_map(
        fast_device if (mesh.shape["pix"], mesh.shape["ch"]) == (PHASES, 4) else on_device,
        mesh=mesh,
        in_specs=placed,
        out_specs=(
            P("pix", None, None),
            P("pix", None, "ch"),
            P("pix", "ch"),
            P("ch"),
            P("ch"),
            P(None, None, "ch", "pix"),
            P("ch"),
            P("ch"),
            P("ch", "pix"),
            P("ch"),
            P("ch"),
            P(None, None, None, "ch", "pix"),
            P(None, "ch"),
            P(None, "ch"),
            P(None, "ch", None),
        ),
        check_vma=False,
    )
```

```python
import jax
import jax.numpy as jnp
from jax import lax
from jax.experimental import pallas as pl
from jax.experimental.pallas import tpu as pltpu
from jax.sharding import PartitionSpec as P

CLS = 19


epsilon = 1e-05
highest = lax.Precision.HIGHEST
aspp_rates = (12, 24, 36)
inner_rate = 2


def from_behind(value, axis, steps):
    count = lax.axis_size(axis)
    first, last = (max(0, -steps), min(count, count - steps))
    return lax.ppermute(value, axis, [(source, source + steps) for source in range(first, last)])


def with_halo(shard, sides, width):
    for axis, dim in sides:
        devices, length = (lax.axis_size(axis), shard.shape[dim])
        up = [(i, (i + 1) % devices) for i in range(devices - 1)]
        down = [(j, i) for i, j in up]
        last = lax.slice_in_dim(shard, length - width, length, axis=dim)
        first = lax.slice_in_dim(shard, 0, width, axis=dim)
        before = lax.ppermute(last, axis, up)
        after = lax.ppermute(first, axis, down)
        shard = jnp.concatenate([before, shard, after], axis=dim)
    return shard


def silu_slope(value):
    sigma = jax.nn.sigmoid(value)
    return sigma * (1.0 + value * (1.0 - sigma))


def shift_cols(value, offset):
    if offset == 0:
        return value
    margin = abs(offset)
    widths = [(0, 0)] * value.ndim
    widths[1] = (margin, margin)
    padded = jnp.pad(value, widths)
    return lax.slice_in_dim(padded, margin + offset, margin + offset + value.shape[1], axis=1)


def moved(piece, distance):
    return from_behind(piece, "pix", -distance)


def shift_rows(value, offset):
    if offset == 0:
        return value
    steps_over, inner = divmod(offset, value.shape[0])
    first = moved(value, steps_over)[inner:]
    if inner == 0:
        return first
    second = moved(value, steps_over + 1)[:inner]
    return jnp.concatenate([first, second], axis=0)


def halo_rows(value):
    return with_halo(value, (("pix", 0),), inner_rate)


def gather_channels(value):
    return lax.all_gather(value, "ch", axis=1, tiled=True)


def sum_channels(value):
    return lax.psum_scatter(
        value.astype(jnp.bfloat16), "ch", scatter_dimension=1, tiled=True
    ).astype(jnp.float32)


def normalized(hidden, valid, axes):
    total, count = lax.psum(
        (jnp.sum(hidden * valid, axis=axes, keepdims=True), jnp.sum(valid)), "pix"
    )
    center = total / count
    spread_sum = lax.psum(jnp.sum(valid * (hidden - center) ** 2, axis=axes, keepdims=True), "pix")
    variance = spread_sum / count
    scale = lax.rsqrt(variance + epsilon)
    return ((hidden - center) * scale, scale, count)


def norm_grad(grad_out, centered, scale, gain, count, valid, axes):
    sum_out, sum_cross = lax.psum(
        (
            jnp.sum(grad_out, axis=axes, keepdims=True),
            jnp.sum(grad_out * centered, axis=axes, keepdims=True),
        ),
        "pix",
    )
    grad_in = gain * scale * (grad_out - valid * (sum_out + centered * sum_cross) / count)
    return (grad_in, sum_cross, sum_out)


def task_scales(gram):
    norms = jnp.sqrt(jnp.diagonal(gram) + 1e-06)
    proj = gram / norms[None, :]
    vector = proj[0, 0] - proj[0, 1:]
    matrix = proj[0, 0] - proj[0, 1:][None, :] - proj[1:, 0][:, None] + proj[1:, 1:]
    determinant = matrix[0, 0] * matrix[1, 1] - matrix[0, 1] * matrix[1, 0]
    second = (vector[0] * matrix[1, 1] - vector[1] * matrix[1, 0]) / determinant
    third = (vector[1] * matrix[0, 0] - vector[0] * matrix[0, 1]) / determinant
    return jnp.stack([1.0 - second - third, second, third])


def on_device(
    features,
    pixel_mask,
    reduce_weight,
    reduce_gain,
    reduce_bias,
    dilated_weight,
    dilated_gain,
    dilated_bias,
    expand_weight,
    expand_gain,
    expand_bias,
    aspp_weight,
    aspp_gain,
    aspp_bias,
    task_weight,
    cotangent,
):
    rows_here, width, local_in = features.shape
    pixels = rows_here * width
    local_mid = reduce_weight.shape[1]
    full_mid = dilated_weight.shape[3]
    branch_width = aspp_weight.shape[4]
    outs_count = task_weight.shape[2]
    valid = pixel_mask.astype(jnp.float32).reshape(pixels, 1)
    valid_branch = valid[None]
    masked = features.reshape(pixels, local_in) * valid.astype(jnp.bfloat16)
    inputs_full = gather_channels(masked)
    hidden_one = jnp.dot(inputs_full, reduce_weight, preferred_element_type=jnp.float32)
    norm_one, scale_one, count = normalized(hidden_one, valid, (0,))
    pre_one = norm_one * reduce_gain + reduce_bias
    act_one = (jax.nn.silu(pre_one) * valid).astype(jnp.bfloat16)
    padded_one = halo_rows(act_one.reshape(rows_here, width, local_mid))
    partial_value = jnp.zeros((pixels, full_mid), jnp.float32)
    for a in range(3):
        for b in range(3):
            shifted = shift_cols(padded_one[2 * a : 2 * a + rows_here], (b - 1) * inner_rate)
            partial_value = partial_value + jnp.dot(
                shifted.reshape(pixels, local_mid),
                dilated_weight[a, b],
                preferred_element_type=jnp.float32,
            )
    hidden_two = sum_channels(partial_value)
    norm_two, scale_two, _ = normalized(hidden_two, valid, (0,))
    pre_two = norm_two * dilated_gain + dilated_bias
    act_two = (jax.nn.silu(pre_two) * valid).astype(jnp.bfloat16)
    hidden_three = sum_channels(jnp.dot(act_two, expand_weight, preferred_element_type=jnp.float32))
    norm_three, scale_three, _ = normalized(hidden_three, valid, (0,))
    pre_three = norm_three * expand_gain + expand_bias + masked.astype(jnp.float32)
    trunk_out = (
        (jax.nn.silu(pre_three) * valid).astype(jnp.bfloat16).reshape(rows_here, width, local_in)
    )
    kept_rows = []
    partials = []
    for j in range(3):
        rate = aspp_rates[j]
        running = jnp.zeros((pixels, branch_width), jnp.float32)
        shifted_rows = []
        for a in range(3):
            row_shift = shift_rows(trunk_out, (a - 1) * rate)
            shifted_rows.append(row_shift)
            for b in range(3):
                shifted = shift_cols(row_shift, (b - 1) * rate)
                running = running + jnp.dot(
                    shifted.reshape(pixels, local_in),
                    aspp_weight[j, a, b],
                    preferred_element_type=jnp.float32,
                )
        kept_rows.append(shifted_rows)
        partials.append(running)
    branch_sum = sum_channels(jnp.stack(partials).reshape(3 * pixels, branch_width)).reshape(
        3, pixels, -1
    )
    branch_gain = aspp_gain[:, None, :]
    norm_branch, scale_branch, _ = normalized(branch_sum, valid_branch, (1,))
    pre_branch = norm_branch * branch_gain + aspp_bias[:, None, :]
    branch_out = (jax.nn.silu(pre_branch) * valid_branch).astype(jnp.bfloat16)
    predictions = lax.psum(
        jnp.einsum(
            "jpc,jco->po", branch_out, task_weight, preferred_element_type=jnp.float32
        ).astype(jnp.bfloat16),
        "ch",
    ).astype(jnp.float32)
    columns = jnp.arange(outs_count)
    task_of = (columns >= CLS).astype(jnp.int32) + (columns >= CLS + 1).astype(jnp.int32)
    select = (task_of[:, None] == jnp.arange(3)[None, :]).astype(jnp.float32)
    target = cotangent.reshape(pixels, outs_count) * valid
    task_float = task_weight.astype(jnp.float32)
    task_grads = jnp.einsum("po,ot,jco->tjpc", target, select, task_float, precision=highest)
    gram = lax.psum(
        jnp.einsum("tjpc,sjpc->ts", task_grads, task_grads, precision=highest), ("pix", "ch")
    )
    scales = task_scales(gram)
    branch_grad = jnp.einsum("t,tjpc->jpc", scales, task_grads, precision=highest)
    task_weight_grad = lax.psum(
        jnp.einsum("jpc,po->jco", branch_out.astype(jnp.float32), target, precision=highest), "pix"
    )
    grad_pre_branch = branch_grad * valid_branch * silu_slope(pre_branch)
    grad_branch, aspp_gain_grad, aspp_bias_grad = norm_grad(
        grad_pre_branch, norm_branch, scale_branch, branch_gain, count, valid_branch, (1,)
    )
    grad_full = gather_channels(grad_branch.astype(jnp.bfloat16).reshape(3 * pixels, -1)).reshape(
        3, rows_here, width, -1
    )
    grad_trunk = jnp.zeros((pixels, local_in), jnp.float32)
    aspp_list = []
    for j in range(3):
        rate = aspp_rates[j]
        grad_flat = grad_full[j].reshape(pixels, -1)
        per_row = []
        for a in range(3):
            back_rows = shift_rows(grad_full[j], -(a - 1) * rate)
            per_col = []
            for b in range(3):
                shifted = shift_cols(back_rows, -(b - 1) * rate)
                grad_trunk = grad_trunk + jnp.einsum(
                    "pa,ca->pc",
                    shifted.reshape(pixels, -1),
                    aspp_weight[j, a, b],
                    preferred_element_type=jnp.float32,
                )
                forward_tap = shift_cols(kept_rows[j][a], (b - 1) * rate).reshape(pixels, local_in)
                per_col.append(
                    jnp.einsum(
                        "pc,pa->ca", forward_tap, grad_flat, preferred_element_type=jnp.float32
                    )
                )
            per_row.append(jnp.stack(per_col))
        aspp_list.append(jnp.stack(per_row))
    aspp_weight_local = jnp.stack(aspp_list)
    grad_pre_three = grad_trunk * valid * silu_slope(pre_three)
    grad_three, expand_gain_grad, expand_bias_grad = norm_grad(
        grad_pre_three, norm_three, scale_three, expand_gain, count, valid, (0,)
    )
    grad_three_full = gather_channels(grad_three.astype(jnp.bfloat16))
    grad_act_two = jnp.einsum(
        "pc,dc->pd", grad_three_full, expand_weight, preferred_element_type=jnp.float32
    )
    expand_weight_local = jnp.einsum(
        "pd,pc->dc", act_two, grad_three_full, preferred_element_type=jnp.float32
    )
    grad_pre_two = grad_act_two * valid * silu_slope(pre_two)
    grad_two, dilated_gain_grad, dilated_bias_grad = norm_grad(
        grad_pre_two, norm_two, scale_two, dilated_gain, count, valid, (0,)
    )
    grad_two_full = gather_channels(grad_two.astype(jnp.bfloat16))
    padded_grad = halo_rows(grad_two_full.reshape(rows_here, width, full_mid))
    grad_act_one = jnp.zeros((pixels, local_mid), jnp.float32)
    dilated_rows = []
    for a in range(3):
        dilated_cols = []
        for b in range(3):
            shifted = shift_cols(
                padded_grad[4 - 2 * a : 4 - 2 * a + rows_here], -(b - 1) * inner_rate
            )
            grad_act_one = grad_act_one + jnp.einsum(
                "pe,de->pd",
                shifted.reshape(pixels, full_mid),
                dilated_weight[a, b],
                preferred_element_type=jnp.float32,
            )
            forward_tap = shift_cols(
                padded_one[2 * a : 2 * a + rows_here], (b - 1) * inner_rate
            ).reshape(pixels, local_mid)
            dilated_cols.append(
                jnp.einsum(
                    "pd,pe->de", forward_tap, grad_two_full, preferred_element_type=jnp.float32
                )
            )
        dilated_rows.append(jnp.stack(dilated_cols))
    dilated_weight_local = jnp.stack(dilated_rows)
    grad_pre_one = grad_act_one * valid * silu_slope(pre_one)
    grad_one, reduce_gain_grad, reduce_bias_grad = norm_grad(
        grad_pre_one, norm_one, scale_one, reduce_gain, count, valid, (0,)
    )
    grad_one_low = grad_one.astype(jnp.bfloat16)
    input_sum = sum_channels(
        jnp.einsum("pd,cd->pc", grad_one_low, reduce_weight, preferred_element_type=jnp.float32)
    )
    features_grad = (
        ((input_sum + grad_pre_three) * valid)
        .astype(jnp.bfloat16)
        .reshape(rows_here, width, local_in)
    )
    reduce_weight_local = jnp.einsum(
        "pc,pd->cd", inputs_full, grad_one_low, preferred_element_type=jnp.float32
    )
    reduce_weight_grad, dilated_weight_grad, expand_weight_grad, aspp_weight_grad = (
        lax.psum_scatter(reduce_weight_local, "pix", scatter_dimension=0, tiled=True),
        lax.psum_scatter(dilated_weight_local, "pix", scatter_dimension=3, tiled=True),
        lax.psum_scatter(expand_weight_local, "pix", scatter_dimension=1, tiled=True),
        lax.psum_scatter(aspp_weight_local, "pix", scatter_dimension=4, tiled=True),
    )
    return (
        predictions.reshape(rows_here, width, outs_count),
        features_grad,
        reduce_weight_grad,
        reduce_gain_grad.reshape(-1),
        reduce_bias_grad.reshape(-1),
        dilated_weight_grad,
        dilated_gain_grad.reshape(-1),
        dilated_bias_grad.reshape(-1),
        expand_weight_grad,
        expand_gain_grad.reshape(-1),
        expand_bias_grad.reshape(-1),
        aspp_weight_grad,
        aspp_gain_grad.reshape(3, -1),
        aspp_bias_grad.reshape(3, -1),
        task_weight_grad,
    )


MESH = pl.DeviceIdType.MESH
ROW_CLASSES, COL_CLASSES = 2, 4
PHASES = ROW_CLASSES * COL_CLASSES
SPLIT = 4
FAR_FIRST = (6, 7, 4, 5, 2, 3, 1)
f32, bf16 = jnp.float32, jnp.bfloat16
VMEM_BYTES = 60 << 20


def shape(dims, dtype):
    return jax.ShapeDtypeStruct(dims, dtype)


def call(name, cid, kernel, arrays, outs, scratch, hbm_ins=(), hbm_outs=()):
    vmem, hbm = pl.BlockSpec(memory_space=pltpu.VMEM), pl.BlockSpec(memory_space=pl.ANY)
    return pl.pallas_call(
        kernel,
        out_shape=outs,
        in_specs=[hbm if i in hbm_ins else vmem for i in range(len(arrays))],
        out_specs=[hbm if i in hbm_outs else vmem for i in range(len(outs))],
        scratch_shapes=scratch,
        compiler_params=pltpu.CompilerParams(
            collective_id=cid, has_side_effects=True, vmem_limit_bytes=VMEM_BYTES
        ),
        name=name,
    )(*arrays)


def dma(*dims):
    return pltpu.SemaphoreType.DMA(dims)


def greet(ch, pix):
    p, c = lax.axis_index("pix"), lax.axis_index("ch")
    barrier = pltpu.get_barrier_semaphore()
    for k in ch:
        pl.semaphore_signal(barrier, inc=1, device_id=(p, c ^ k), device_id_type=MESH)
    for k in pix:
        pl.semaphore_signal(barrier, inc=1, device_id=(p ^ k, c), device_id_type=MESH)
    return barrier, len(ch) + len(pix)


def push(src, dst, send, recv, device):
    copy = pltpu.make_async_remote_copy(
        src_ref=src,
        dst_ref=dst,
        send_sem=send,
        recv_sem=recv,
        device_id=device,
        device_id_type=MESH,
    )
    copy.start()
    return copy


def keep(src, dst, sem):
    copy = pltpu.make_async_copy(src, dst, sem)
    copy.start()
    return copy


def rows(start, size):
    return pl.ds(pl.multiple_of(start, size), size)


def fold(x):
    return jnp.sum(x.reshape(x.shape[0] // 8, 8, x.shape[1]), axis=0)


def total(x):
    return jnp.sum(x, axis=0, keepdims=True)


def loop(steps, body, init):
    return lax.fori_loop(0, steps, body, init)


def sum_over_ch(part, tile, tiles, own, out, near, cross, near_sems, far_sems):
    p, c = lax.axis_index("pix"), lax.axis_index("ch")
    k, x = lax.rem(c, 2), c // 2
    n = own.shape[2]
    copies = []
    for t in range(tiles):
        at = pl.ds(t * tile, tile)
        value = part(t)
        for d in range(SPLIT):
            block = value[:, d * n : (d + 1) * n]
            own[d, at] = block
            out[d, at] = block.astype(bf16)
        copies.append(
            [
                push(
                    out.at[2 * h + 1 - k, at],
                    near.at[h, at],
                    near_sems.at[0, t, h],
                    near_sems.at[1, t, h],
                    (p, c ^ 1),
                )
                for h in range(2)
            ]
        )
    crossing = []
    for t in range(tiles):
        at = pl.ds(t * tile, tile)
        for copy in copies[t]:
            copy.wait()
        cross[0, at] = (own[2 * (1 - x) + k, at] + near[1 - x, at].astype(f32)).astype(bf16)
        crossing.append(
            push(cross.at[0, at], cross.at[1, at], far_sems.at[0, t], far_sems.at[1, t], (p, c ^ 2))
        )

    def result(t):
        at = pl.ds(t * tile, tile)
        crossing[t].wait()
        return own[2 * x + k, at] + near[x, at].astype(f32) + cross[1, at].astype(f32)

    return result


def sum_scratch(pixels, n, tiles):
    return [
        pltpu.VMEM((SPLIT, pixels, n), f32),
        pltpu.VMEM((SPLIT, pixels, n), bf16),
        pltpu.VMEM((2, pixels, n), bf16),
        pltpu.VMEM((2, pixels, n), bf16),
        dma(2, tiles, 2),
        dma(2, tiles),
    ]


def pix_exchange(send, recv, sems):
    p, c = lax.axis_index("pix"), lax.axis_index("ch")
    copies = [
        push(send, recv.at[p], sems.at[0, k], sems.at[1, k], (p ^ k, c)) for k in FAR_FIRST
    ]
    recv[p] = send[...]
    for copy in copies:
        copy.wait()


def norm_stats(hidden, valid, pixels, send, recv, sems):
    n = hidden.shape[1]
    tile = 128
    repeat = n // 128

    def mask(at):
        v = valid[at]
        return v if repeat == 1 else jnp.concatenate([v] * repeat, axis=1)

    def first(i, carry):
        at = rows(i * tile, tile)
        v = mask(at)
        return carry[0] + fold(hidden[at] * v), carry[1] + fold(v)

    zero = jnp.zeros((8, n), f32)
    sums, count = loop(pixels // tile, first, (zero, zero))
    sums, count = total(sums), total(count)
    center = sums / jnp.maximum(count, 1.0)

    def second(i, carry):
        at = rows(i * tile, tile)
        apart = hidden[at] - center
        return carry + fold(mask(at) * apart * apart)

    spread = total(loop(pixels // tile, second, zero))
    send[0:1] = sums
    send[1:2] = spread
    send[2:3] = count
    pix_exchange(send, recv, sems)
    return join(recv, PHASES)


def join(recv, parts):
    sums, count = recv[0, 0:1], recv[0, 2:3]
    for i in range(1, parts):
        sums, count = sums + recv[i, 0:1], count + recv[i, 2:3]
    center = sums / count
    spread = jnp.zeros_like(sums)
    for i in range(parts):
        n = recv[i, 2:3]
        apart = recv[i, 0:1] / jnp.maximum(n, 1.0) - center
        spread = spread + recv[i, 1:2] + n * apart * apart
    return center, lax.rsqrt(spread / count + epsilon), count


def stat_scratch(n):
    return [pltpu.VMEM((8, n), f32), pltpu.VMEM((PHASES, 8, n), f32), dma(2, PHASES)]


def silu(x):
    return x / (1.0 + jnp.exp(-x))


def gather_over_ch(full, n, tile, tiles, near_sems, far_sems, hop_sems, ready, between=None):
    p, c = lax.axis_index("pix"), lax.axis_index("ch")

    def part(owner, t):
        return full.at[pl.ds(t * tile, tile), rows(owner * n, n)]

    near, far, hops = [], [], []
    for t in range(tiles):
        ready(t)
        src = part(c, t)
        far.append(push(src, src, far_sems.at[0, t], far_sems.at[1, t], (p, c ^ 2)))
        near.append(push(src, src, near_sems.at[0, t], near_sems.at[1, t], (p, c ^ 1)))
    if between is not None:
        between()
    for t in range(tiles):
        far[t].wait_recv()
        src = part(c ^ 2, t)
        hops.append(push(src, src, hop_sems.at[0, t], hop_sems.at[1, t], (p, c ^ 1)))
    for t in range(tiles):
        far[t].wait_send()
        near[t].wait()
        hops[t].wait()


def gather_scratch(tiles):
    return [dma(2, tiles), dma(2, tiles), dma(2, tiles)]


def to_classes(x):
    rows, cols, n = x.shape
    x = x.reshape(rows // ROW_CLASSES, ROW_CLASSES, cols // COL_CLASSES, COL_CLASSES, n)
    return x.transpose(1, 3, 0, 2, 4).reshape(PHASES, -1, n)


def from_classes(x, rows, cols):
    n = x.shape[-1]
    x = x.reshape(ROW_CLASSES, COL_CLASSES, rows // ROW_CLASSES, cols // COL_CLASSES, n)
    return x.transpose(2, 0, 3, 1, 4).reshape(rows, cols, n)


RATE_ROWS = tuple(rate // ROW_CLASSES for rate in aspp_rates)
RATE_COLS = tuple(rate // COL_CLASSES for rate in aspp_rates)


def load_pyramid(weight, wide, sems):
    m = weight.shape[4]
    return [
        [keep(weight.at[j, a, b], wide.at[3 * j + a, :, b * m : (b + 1) * m], sems.at[3 * j + a, b]) for b in range(3)]
        for j in range(3)
        for a in range(3)
    ]


def move_cols(x, by):
    place = lax.broadcasted_iota(jnp.int32, x.shape, 0) % 32
    rolled = pltpu.roll(x, by % x.shape[0], 0)
    return jnp.where(place < by, 0.0, rolled) if by > 0 else jnp.where(place >= 32 + by, 0.0, rolled)


def ch_exchange(send, recv, sems):
    p, c = lax.axis_index("pix"), lax.axis_index("ch")
    copies = [push(send, recv.at[c], sems.at[0, k], sems.at[1, k], (p, c ^ k)) for k in (2, 3, 1)]
    recv[c] = send[...]
    for copy in copies:
        copy.wait()


def add_up(recv, parts):
    value = recv[0]
    for i in range(1, parts):
        value = value + recv[i]
    return value


def task_vector(square, weights):
    product = square * weights
    row = lax.broadcasted_iota(jnp.int32, (32, 32), 0)
    col = lax.broadcasted_iota(jnp.int32, (32, 32), 1)

    def task(i):
        return (i >= CLS).astype(jnp.int32) + (i >= CLS + 1).astype(jnp.int32)

    def entry(t, s):
        return jnp.sum(
            jnp.sum(jnp.where((task(row) == t) & (task(col) == s), product, 0.0), axis=1, keepdims=True),
            axis=0,
            keepdims=True,
        )

    gram = [[entry(t, s) for s in range(3)] for t in range(3)]
    norms = [jnp.sqrt(gram[k][k] + 1e-06) for k in range(3)]
    proj = [[gram[i][k] / norms[k] for k in range(3)] for i in range(3)]
    vector = [proj[0][0] - proj[0][b] for b in (1, 2)]
    matrix = [[proj[0][0] - proj[0][b] - proj[a][0] + proj[a][b] for b in (1, 2)] for a in (1, 2)]
    determinant = matrix[0][0] * matrix[1][1] - matrix[0][1] * matrix[1][0]
    second = (vector[0] * matrix[1][1] - vector[1] * matrix[1][0]) / determinant
    third = (vector[1] * matrix[0][0] - vector[0] * matrix[0][1]) / determinant
    which = task(lax.broadcasted_iota(jnp.int32, (32, 1), 0))
    return jnp.where(which == 0, 1.0 - second - third, jnp.where(which == 1, second, third))


def slope(x):
    s = 1.0 / (1.0 + jnp.exp(-x))
    return s * (1.0 + x * (1.0 - s))


def pyramid(trunk, loads, wide, moving, pass_inputs, heads, targets, square, *refs):
    (full, predictions, head_grad, sums, others, picks) = refs[:6]
    (sides, own, out, near, cross, hidden, grad, branch) = refs[6:14]
    (s_send, s_ch, s_mid, s_pix, b_send, b_ch, b_mid, b_pix) = refs[14:22]
    (h_send, h_ch, h_mid, h_pix, h_sum, p_send, p_ch) = refs[22:29]
    (near_sems, far_sems, ch_sems, pix_sems, g_near, g_far, g_hop, y_sems, picked, pick_sems) = refs[29:]
    p, c = lax.axis_index("pix"), lax.axis_index("ch")
    k, x = lax.rem(c, 2), c // 2
    m = wide.shape[2] // 3
    pixels, half = trunk.shape[1], trunk.shape[2]
    quarter = pixels // SPLIT
    gain, bias = heads[32:33], heads[33:34]
    contract0 = (((0,), (0,)), ((), ()))
    contract1 = (((1,), (1,)), ((), ()))
    head = heads[:32]
    scaled = head * task_vector(
        add_up(square, PHASES)[:, :32], lax.dot_general(head, head, contract1, precision=highest)
    )
    mine = rows(c * quarter, quarter)
    target = jnp.concatenate([targets[2 * c], targets[2 * c + 1]], axis=1)
    mask = lax.dot_general(
        target[24:].astype(bf16), jnp.ones((8, m), bf16), contract0, preferred_element_type=f32
    )
    grad[...] = lax.dot_general(target, scaled, contract0, precision=highest) * jnp.concatenate([mask] * 3, axis=1)
    part = pixels // SPLIT
    sharing = []

    def share(slot, quarters, own, k, first):
        for i, q in enumerate(quarters):
            at = pl.ds(q * part, part)
            src = trunk.at[:, at] if own else others.at[2 - k, :, at]
            sharing.append(
                push(src, others.at[slot, :, at], y_sems.at[0, first + i], y_sems.at[1, first + i], (p ^ k, c))
            )
        return sharing[-len(quarters) :]

    def convolve(j, h):
        s = RATE_ROWS[j] * 32
        for a in (1, 0, 2):
            if h == 0:
                for load in loads[3 * j + a]:
                    load.wait()
            w = wide[3 * j + a, h * half : (h + 1) * half]
            if a == 1:
                value = jnp.dot(trunk[h], w, preferred_element_type=f32)
                if h == 0:
                    sides[j] = value
                else:
                    sides[j] += value
            elif a == 0:
                sides[j, s:] += jnp.dot(trunk[h, : pixels - s], w, preferred_element_type=f32)
            else:
                sides[j, : pixels - s] += jnp.dot(trunk[h, s:], w, preferred_element_type=f32)

    for copy in moving[0]:
        copy.wait()
    for j in range(3):
        convolve(j, 0)
    inputs_done = pass_inputs()
    for copy in moving[1]:
        copy.wait()
    from_y = share(0, (0, 1), True, 1, 0)
    from_z = share(1, (2, 3), True, 2, 2)

    copies = []
    for j in range(3):
        q = RATE_COLS[j]
        convolve(j, 1)
        for d in range(SPLIT):
            at = slice(d * quarter, (d + 1) * quarter)
            value = (
                sides[j, at, m : 2 * m]
                + move_cols(sides[j, at, :m], q)
                + move_cols(sides[j, at, 2 * m :], -q)
            )
            own[d, j] = value
            out[d, j] = value.astype(bf16)
        copies.append(
            [
                push(out.at[2 * h + 1 - k, j], near.at[h, j], near_sems.at[0, j, h], near_sems.at[1, j, h], (p, c ^ 1))
                for h in range(2)
            ]
        )
        if j > 0:
            copies[j - 1] = cross_chips(copies[j - 1], j - 1, own, near, cross, far_sems)
    copies[2] = cross_chips(copies[2], 2, own, near, cross, far_sems)
    for i in range(2):
        from_y[i].wait_recv()
        share(2, (i,), False, 2, 4 + i)
        from_z[i].wait_recv()
        share(2, (i + 2,), False, 1, 6 + i)
    count = total(mask)
    for j in range(3):
        copies[j].wait()
        value = own[2 * x + k, j] + near[x, j].astype(f32) + cross[1, j].astype(f32)
        at = slice(j * m, (j + 1) * m)
        hidden[:, at] = value
        first = total(value * mask)
        apart = value - first / jnp.maximum(count, 1.0)
        s_send[j : j + 1] = first
        s_send[3 + j : 4 + j] = total(apart * apart * mask)
    s_send[6:7] = count
    s_send[7:8] = jnp.zeros((1, m), f32)

    def merge(recv, parts):
        number = recv[0, 6:7]
        for i in range(1, parts):
            number = number + recv[i, 6:7]
        whole, spread = recv[0, 0:3], recv[0, 3:6]
        for i in range(1, parts):
            whole, spread = whole + recv[i, 0:3], spread + recv[i, 3:6]
        center = whole / jnp.maximum(number, 1.0)
        for i in range(parts):
            n = recv[i, 6:7]
            apart = recv[i, 0:3] / jnp.maximum(n, 1.0) - center
            spread = spread + n * apart * apart
        return whole, spread, number

    ch_exchange(s_send, s_ch, ch_sems.at[0])
    whole, spread, number = merge(s_ch, SPLIT)
    s_mid[0:3] = whole
    s_mid[3:6] = spread
    s_mid[6:7] = number
    s_mid[7:8] = jnp.zeros((1, m), f32)
    pix_exchange(s_mid, s_pix, pix_sems.at[0])
    share(0, (2,), True, 1, 8)
    share(1, (0,), True, 2, 9)
    whole, spread, number = merge(s_pix, PHASES)
    center, scale = whole / number, lax.rsqrt(spread / number + epsilon)
    for j in range(3):
        at = slice(j * m, (j + 1) * m)
        norm = (hidden[:, at] - center[j : j + 1]) * scale[j : j + 1]
        hidden[:, at] = norm
        value = norm * gain[:, at] + bias[:, at]
        branch[:, at] = (silu(value) * mask).astype(bf16)
        back = grad[:, at] * slope(value)
        grad[:, at] = back
        b_send[j : j + 1] = total(back)
        b_send[3 + j : 4 + j] = total(back * norm)
    b_send[6:8] = jnp.zeros((2, m), f32)
    to_ch = [push(b_send, b_ch.at[c], ch_sems.at[3, 0, i], ch_sems.at[3, 1, i], (p, c ^ i)) for i in (2, 3, 1)]
    b_ch[c] = b_send[...]
    p_send[...] = lax.dot_general(
        head.astype(bf16), branch[...], contract1, preferred_element_type=f32
    )
    for copy in to_ch:
        copy.wait()
    b_mid[...] = add_up(b_ch, SPLIT)
    sending = [
        push(b_mid, b_pix.at[p], pix_sems.at[1, 0, i], pix_sems.at[1, 1, i], (p ^ i, c)) for i in FAR_FIRST
    ]
    b_pix[p] = b_mid[...]
    h_send[...] = jnp.dot(
        target, branch[...].astype(f32), precision=highest, preferred_element_type=f32
    )
    background = [push(p_send, p_ch.at[c], ch_sems.at[1, 0, i], ch_sems.at[1, 1, i], (p, c ^ i)) for i in (2, 3, 1)] + [
        push(h_send.at[rows((c ^ i) * 8, 8)], h_ch.at[c], ch_sems.at[2, 0, i], ch_sems.at[2, 1, i], (p, c ^ i))
        for i in (2, 3, 1)
    ]
    p_ch[c] = p_send[...]
    h_ch[c] = h_send[rows(c * 8, 8)]
    for copy in sending:
        copy.wait()
    for copy in background:
        copy.wait()
    h_mid[...] = add_up(h_ch, SPLIT)

    def half(to):
        return p_ch.at[to // 2, :, rows(lax.rem(to, 2) * 128, 128)]

    background = [
        push(half(p ^ i), predictions.at[p], pix_sems.at[2, 0, i], pix_sems.at[2, 1, i], (p ^ i, c)) for i in FAR_FIRST
    ] + [push(h_mid, h_pix.at[p], pix_sems.at[3, 0, i], pix_sems.at[3, 1, i], (p ^ i, c)) for i in FAR_FIRST]
    predictions[p] = half(p)[...]
    h_pix[p] = h_mid[...]
    share(0, (3,), True, 1, 10)
    share(1, (1,), True, 2, 11)
    summed = add_up(b_pix, PHASES)
    sums[...] = summed
    for j in range(3):
        at = slice(j * m, (j + 1) * m)
        value = grad[:, at] - mask * (summed[j : j + 1] + hidden[:, at] * summed[3 + j : 4 + j]) / number
        full[mine, at] = (gain[:, at] * scale[j : j + 1] * value).astype(bf16)
    far = push(full.at[mine], full.at[mine], g_far.at[0], g_far.at[1], (p, c ^ 2))
    by = push(full.at[mine], full.at[mine], g_near.at[0], g_near.at[1], (p, c ^ 1))
    group = lax.rem(p, 4)
    pick = pick_rows(m, m, 0)
    for j in range(3):
        value = lax.dot_general(
            pick, full[mine, j * m : (j + 1) * m], contract1, preferred_element_type=f32
        ).astype(bf16)
        for g in range(4):
            picked[g, j * 64 : (j + 1) * 64] = value[g * 64 : (g + 1) * 64]
    sent_picks = [
        push(picked.at[group ^ i], picks.at[i - 1], pick_sems.at[0, i], pick_sems.at[1, i], (p ^ i, c)) for i in (3, 1, 2)
    ]
    for copy in background:
        copy.wait()
    own_rows = add_up(h_pix, PHASES)
    h_sum[...] = own_rows
    head_grad[rows(c * 8, 8)] = own_rows
    last = [
        push(h_sum, head_grad.at[rows(c * 8, 8)], ch_sems.at[4, 0, i], ch_sems.at[4, 1, i], (p, c ^ i))
        for i in (2, 3, 1)
    ]
    far.wait_recv()
    theirs = rows((c ^ 2) * quarter, quarter)
    hop = push(full.at[theirs], full.at[theirs], g_hop.at[0], g_hop.at[1], (p, c ^ 1))
    far.wait_send()
    by.wait()
    hop.wait()
    for copy in last:
        copy.wait()
    for copy in from_y + from_z:
        copy.wait_send()
    for copy in sharing[4:] + sent_picks:
        copy.wait()
    inputs_done()


def pick_rows(m, count, first):
    row = lax.broadcasted_iota(jnp.int32, (count, m), 0)
    col = lax.broadcasted_iota(jnp.int32, (count, m), 1)
    source = (4 * (row % 64 // 32) + row // 64 + first) * 32 + row % 32
    return jnp.where(col == source, 1.0, 0.0).astype(bf16)


def cross_chips(near_copies, j, own, near, cross, sems):
    p, c = lax.axis_index("pix"), lax.axis_index("ch")
    k, x = lax.rem(c, 2), c // 2
    for copy in near_copies:
        copy.wait()
    cross[0, j] = (own[2 * (1 - x) + k, j] + near[1 - x, j].astype(f32)).astype(bf16)
    return push(cross.at[0, j], cross.at[1, j], sems.at[0, j], sems.at[1, j], (p, c ^ 2))


def pyramid_scratch(pixels, n, m):
    quarter = pixels // SPLIT
    small = [
        pltpu.VMEM((8, m), f32),
        pltpu.VMEM((SPLIT, 8, m), f32),
        pltpu.VMEM((8, m), f32),
        pltpu.VMEM((PHASES, 8, m), f32),
    ]
    return [
        pltpu.VMEM((3, pixels, 3 * m), f32),
        pltpu.VMEM((SPLIT, 3, quarter, m), f32),
        pltpu.VMEM((SPLIT, 3, quarter, m), bf16),
        pltpu.VMEM((2, 3, quarter, m), bf16),
        pltpu.VMEM((2, 3, quarter, m), bf16),
        pltpu.VMEM((quarter, 3 * m), f32),
        pltpu.VMEM((quarter, 3 * m), f32),
        pltpu.VMEM((quarter, 3 * m), bf16),
        *small,
        *small,
        pltpu.VMEM((32, 3 * m), f32),
        pltpu.VMEM((SPLIT, 8, 3 * m), f32),
        pltpu.VMEM((8, 3 * m), f32),
        pltpu.VMEM((PHASES, 8, 3 * m), f32),
        pltpu.VMEM((8, 3 * m), f32),
        pltpu.VMEM((32, quarter), f32),
        pltpu.VMEM((SPLIT, 32, quarter), f32),
        dma(2, 3, 2),
        dma(2, 3),
        dma(5, 2, SPLIT),
        dma(4, 2, PHASES),
        dma(2),
        dma(2),
        dma(2),
        dma(2, 12),
        pltpu.VMEM((4, 192, quarter), bf16),
        dma(2, 4),
    ]


TILES = 4


def one_hot(rows_count, cols_count, source):
    row = lax.broadcasted_iota(jnp.int32, (rows_count, cols_count), 0)
    col = lax.broadcasted_iota(jnp.int32, (rows_count, cols_count), 1)
    return col == source(row)


def stage_one(feat, mask, weight, expand, gain, bias, head_weight, head_gain, head_bias, cotangent, *refs):
    (masked, reduce_rows, expand_cols, heads_full, targets_all, square_all, norm, padded, stat, valid) = refs[:10]
    (wide, hidden, own, out, near, cross, near_sems, far_sems, send, recv, stat_sems) = refs[10:21]
    (weight_sems, pix_sems, local_sems, halo_sems, heads, heads_all, targets, square, image) = refs[21:]
    p, c = lax.axis_index("pix"), lax.axis_index("ch")
    pixels, local_in = feat.shape
    local_mid = weight.shape[1]
    tile = pixels // TILES
    contract1 = (((1,), (1,)), ((), ()))

    def piece(i, to):
        return (
            (weight.at[rows(to * local_in, local_in), :], reduce_rows.at[:, rows(c * local_mid, local_mid)]),
            (expand.at[:, rows(to * local_in, local_in)], expand_cols.at[rows(c * local_mid, local_mid), :]),
            (heads, heads_all.at[c]),
        )[i]

    def to_ch(i):
        return [
            push(*piece(i, c ^ k), weight_sems.at[0, k, i], weight_sems.at[1, k, i], (p, c ^ k)) for k in (2, 3, 1)
        ] + [keep(*piece(i, c), local_sems.at[i])]

    reduce_copies = to_ch(0)

    present = mask[...].astype(f32)
    order = one_hot(128, 128, lambda i: 4 * (i % 32) + i // 32)
    ones = jnp.ones((128, 128), bf16)
    for r in range(8):
        column = jnp.dot(
            jnp.where(order, present[r : r + 1], 0.0).astype(bf16), ones, preferred_element_type=f32
        )
        for b in range(COL_CLASSES):
            block = ((r % ROW_CLASSES) * COL_CLASSES + b) * 128 + (r // ROW_CLASSES) * 32
            valid[block : block + 32] = column[b * 32 : (b + 1) * 32]
    for r in range(8):
        for g in range(local_in // 128):
            lanes = slice(g * 128, (g + 1) * 128)
            wide[g] = feat[r * 128 : (r + 1) * 128, lanes].astype(f32)
            for b in range(COL_CLASSES):
                block = ((r % ROW_CLASSES) * COL_CLASSES + b) * 128 + (r // ROW_CLASSES) * 32
                value = wide[g, pl.ds(b, 32, stride=COL_CLASSES), :] * valid[block : block + 32]
                masked[block : block + 32, lanes] = value.astype(bf16)

    columns, m = head_weight.shape[1], head_weight.shape[2]
    heads[...] = jnp.zeros(heads.shape, f32)
    for j in range(3):
        heads[:columns, j * m : (j + 1) * m] = head_weight[j].astype(f32)
        heads[32:33, j * m : (j + 1) * m] = head_gain[j : j + 1]
        heads[33:34, j * m : (j + 1) * m] = head_bias[j : j + 1]

    image[...] = jnp.zeros(image.shape, f32)
    for r in range(8):
        at = slice(r * 128, (r + 1) * 128)
        image[:columns, at] = cotangent[:, at] * present[r : r + 1]
        image[31:32, at] = present[r : r + 1]
    square[...] = jnp.zeros(square.shape, f32)
    square[:, :32] = lax.dot_general(
        image[...], image[...], contract1, precision=highest, preferred_element_type=f32
    )
    place = jnp.where(
        one_hot(512, 512, lambda i: i % 4 * 128 + i // 128 * 32 + i % 128 // 4), 1.0, 0.0
    )
    for a in range(ROW_CLASSES):
        some = jnp.concatenate([image[:, (2 * r + a) * 128 : (2 * r + a + 1) * 128] for r in range(4)], axis=1)
        value = jnp.dot(some, place, precision=highest, preferred_element_type=f32)
        for b in range(COL_CLASSES):
            targets[a * COL_CLASSES + b] = value[:, b * 128 : (b + 1) * 128]
    routed = [
        push(targets.at[p ^ k], targets_all.at[p], pix_sems.at[0, k, 0], pix_sems.at[1, k, 0], (p ^ k, c))
        for k in FAR_FIRST
    ] + [push(square, square_all.at[p], pix_sems.at[0, k, 1], pix_sems.at[1, k, 1], (p ^ k, c)) for k in FAR_FIRST]
    routed.append(keep(targets.at[p], targets_all.at[p], local_sems.at[3]))
    routed.append(keep(square, square_all.at[p], local_sems.at[4]))
    for copy in reduce_copies:
        copy.wait()

    def part(t):
        return jnp.dot(masked[t * tile : (t + 1) * tile], reduce_rows[...], preferred_element_type=f32)

    result = sum_over_ch(part, tile, TILES, own, out, near, cross, near_sems, far_sems)
    for t in range(TILES):
        hidden[t * tile : (t + 1) * tile] = result(t)
    for copy in routed:
        copy.wait()
    later = to_ch(1) + to_ch(2)
    center, scale, count = norm_stats(hidden, valid, pixels, send, recv, stat_sems)
    stat[0:1] = center
    stat[1:2] = scale
    stat[2:3] = count
    for i in range(PHASES):
        at = pl.ds(i * 128, 128)
        value = (hidden[at] - center) * scale
        norm[at] = value
        act = silu(value * gain[...] + bias[...]) * valid[at]
        padded[i, 1:5] = act.astype(bf16).reshape(4, 32, local_mid)
    up = lambda: pltpu.make_async_remote_copy(
        src_ref=padded.at[:, 4],
        dst_ref=padded.at[:, 0],
        send_sem=halo_sems.at[0, 0],
        recv_sem=halo_sems.at[1, 0],
        device_id=(p + 1, c),
        device_id_type=MESH,
    )
    down = lambda: pltpu.make_async_remote_copy(
        src_ref=padded.at[:, 1],
        dst_ref=padded.at[:, 5],
        send_sem=halo_sems.at[0, 1],
        recv_sem=halo_sems.at[1, 1],
        device_id=(p - 1, c),
        device_id_type=MESH,
    )
    first, last = p == 0, p == PHASES - 1

    @pl.when(jnp.logical_not(last))
    def _():
        up().start()

    @pl.when(jnp.logical_not(first))
    def _():
        down().start()

    @pl.when(last)
    def _():
        padded[:, 5] = jnp.zeros((PHASES, 32, local_mid), bf16)

    @pl.when(first)
    def _():
        padded[:, 0] = jnp.zeros((PHASES, 32, local_mid), bf16)

    for copy in later:
        copy.wait()
    for j in range(3):
        for d in range(SPLIT):
            heads_full[:, (j * SPLIT + d) * m : (j * SPLIT + d + 1) * m] = heads_all[d, :, j * m : (j + 1) * m]

    @pl.when(jnp.logical_not(last))
    def _():
        up().wait_send()
        down().wait_recv()

    @pl.when(jnp.logical_not(first))
    def _():
        down().wait_send()
        up().wait_recv()


def stage_two(padded, valid, weight, gain, bias, *refs):
    (norm, full, taps, stat) = refs[:4]
    (hidden, own, out, near, cross, near_sems, far_sems, send, recv, stat_sems) = refs[4:14]
    (g_near, g_far, g_hop) = refs[14:]
    p, c = lax.axis_index("pix"), lax.axis_index("ch")
    pixels = valid.shape[0]
    local_mid = padded.shape[3]
    tile = pixels // TILES
    place = lax.broadcasted_iota(jnp.int32, (192, local_mid), 0) % 32
    for i in range(PHASES):
        beta = i % COL_CLASSES
        plain = padded[i].reshape(192, local_mid)
        wide = plain.astype(f32)
        if beta >= 2:
            moved_by = jnp.where(place == 0, 0.0, pltpu.roll(wide, 1, 0)).astype(bf16)
        else:
            moved_by = jnp.where(place == 31, 0.0, pltpu.roll(wide, 191, 0)).astype(bf16)
        for a in range(3):
            at = slice(a * 32, a * 32 + 128)
            for b, other, value in (
                (1, beta, plain),
                (0, (beta + 2) % 4, moved_by if beta >= 2 else plain),
                (2, (beta + 2) % 4, plain if beta >= 2 else moved_by),
            ):
                to = (i - beta + other) * 128
                col = (a * 3 + b) * local_mid
                taps[to : to + 128, col : col + local_mid] = value[at]

    def part(t):
        return jnp.dot(taps[t * tile : (t + 1) * tile], weight[...], preferred_element_type=f32)

    result = sum_over_ch(part, tile, TILES, own, out, near, cross, near_sems, far_sems)
    for t in range(TILES):
        hidden[t * tile : (t + 1) * tile] = result(t)
    center, scale, count = norm_stats(hidden, valid, pixels, send, recv, stat_sems)
    stat[0:1] = center
    stat[1:2] = scale
    stat[2:3] = count

    def ready(t):
        for i in range(tile // 128):
            at = pl.ds(t * tile + i * 128, 128)
            value = (hidden[at] - center) * scale
            norm[at] = value
            act = silu(value * gain[...] + bias[...]) * valid[at]
            full[at, rows(c * local_mid, local_mid)] = act.astype(bf16)

    gather_over_ch(full, local_mid, tile, TILES, g_near, g_far, g_hop, ready)


def stage_three(full, weight, masked, valid, gain, bias, *refs):
    (norm, classes, stat, inputs) = refs[:4]
    (hidden, trunk, send, recv, stat_sems, class_sems, own_sem, in_sems) = refs[4:]
    p, c = lax.axis_index("pix"), lax.axis_index("ch")
    pixels, n = masked.shape
    tile = pixels // TILES
    for t in range(TILES):
        at = pl.ds(t * tile, tile)
        hidden[at] = jnp.dot(full[at], weight[...], preferred_element_type=f32)
    far = push(masked, inputs.at[c], in_sems.at[0, 0], in_sems.at[1, 0], (p, c ^ 2))
    near = push(masked, inputs.at[c], in_sems.at[0, 1], in_sems.at[1, 1], (p, c ^ 1))
    mine = keep(masked, inputs.at[c], own_sem.at[2])
    center, scale, count = norm_stats(hidden, valid, pixels, send, recv, stat_sems)
    stat[0:1] = center
    stat[1:2] = scale
    stat[2:3] = count

    half = n // 2

    def finish(to, h):
        lanes = slice(h * half, (h + 1) * half)

        def step(i, carry):
            at = rows(to * 128 + i * 64, 64)
            value = (hidden[at, lanes] - center[:, lanes]) * scale[:, lanes]
            norm[at, lanes] = value
            pre = value * gain[:, lanes] + bias[:, lanes] + masked[at, lanes].astype(f32)
            v = valid[at]
            trunk[h, at] = (silu(pre) * jnp.concatenate([v] * (half // 128), axis=1)).astype(bf16)
            return carry

        loop(2, step, 0)

    copies = []
    for h in range(2):
        some = []
        for k in FAR_FIRST:
            to = p ^ k
            finish(to, h)
            some.append(
                push(
                    trunk.at[h, rows(to * 128, 128)],
                    classes.at[h, rows(p * 128, 128)],
                    class_sems.at[0, h, k],
                    class_sems.at[1, h, k],
                    (to, c),
                )
            )
        finish(p, h)
        some.append(keep(trunk.at[h, rows(p * 128, 128)], classes.at[h, rows(p * 128, 128)], own_sem.at[h]))
        copies.append(some)

    def pass_inputs():
        far.wait_recv()
        hop = push(inputs.at[c ^ 2], inputs.at[c ^ 2], in_sems.at[0, 2], in_sems.at[1, 2], (p, c ^ 1))

        def done():
            far.wait_send()
            near.wait()
            mine.wait()
            hop.wait()

        return done

    return copies, pass_inputs


def forward(
    feat, mask, weight, expand, gain1, bias1, head_weight, head_gain, head_bias, cotangent, dilated, gain2, bias2,
    gain3, bias3, pyramid_weight, *refs
):
    (masked, reduce_rows, expand_cols, norm1, stat1, valid, norm2, full2, taps, stat2, norm3, classes, stat3, inputs,
     grads, predictions, head_grad, branch_sums, others, picks) = refs[:20]
    heads_full, targets_all, square_all, padded, wide, w_sems = refs[20:26]
    own = refs[26:]
    one, two, three = 20, 13, 8
    barrier, expected = greet((1, 2, 3), FAR_FIRST)
    loads = load_pyramid(pyramid_weight, wide, w_sems)
    pl.semaphore_wait(barrier, expected)
    stage_one(
        feat, mask, weight, expand, gain1, bias1, head_weight, head_gain, head_bias, cotangent,
        masked, reduce_rows, expand_cols, heads_full, targets_all, square_all, norm1, padded, stat1, valid, *own[:one],
    )
    own = own[one:]
    stage_two(padded, valid, dilated, gain2, bias2, norm2, full2, taps, stat2, *own[:two])
    own = own[two:]
    moving, pass_inputs = stage_three(
        full2, expand_cols, masked, valid, gain3, bias3, norm3, classes, stat3, inputs, *own[:three]
    )
    own = own[three:]
    pyramid(
        classes, loads, wide, moving, pass_inputs, heads_full, targets_all, square_all,
        grads, predictions, head_grad, branch_sums, others, picks, *own,
    )


def run_forward(
    cid, feat, mask, weight, expand, gain1, bias1, head_weight, head_gain, head_bias, cotangent, dilated, gain2, bias2,
    gain3, bias3, pyramid_weight
):
    pixels, n = feat.shape
    mid = weight.shape[1]
    all_mid = SPLIT * mid
    m = pyramid_weight.shape[4]
    quarter = pixels // SPLIT
    outs = [
        shape((pixels, n), bf16),
        shape((n, all_mid), bf16),
        shape((all_mid, n), bf16),
        shape((pixels, mid), f32),
        shape((8, mid), f32),
        shape((pixels, 128), f32),
        shape((pixels, mid), f32),
        shape((pixels, all_mid), bf16),
        shape((pixels, 9 * mid), bf16),
        shape((8, mid), f32),
        shape((pixels, n), f32),
        shape((2, pixels, n // 2), bf16),
        shape((8, n), f32),
        shape((SPLIT, pixels, n), bf16),
        shape((pixels, 3 * m), bf16),
        shape((PHASES, 32, 128), f32),
        shape((32, 3 * m), f32),
        shape((8, m), f32),
        shape((3, 2, pixels, n // 2), bf16),
        shape((3, 192, quarter), bf16),
    ]
    scratch = [
        pltpu.VMEM((40, 3 * m), f32),
        pltpu.VMEM((PHASES, 32, 128), f32),
        pltpu.VMEM((PHASES, 32, 128), f32),
        pltpu.VMEM((PHASES, 6, 32, mid), bf16),
        pltpu.VMEM((9, n, 3 * m), bf16),
        dma(9, 3),
        pltpu.VMEM((n // 128, 128, 128), f32),
        pltpu.VMEM((pixels, mid), f32),
        *sum_scratch(pixels, mid, TILES),
        *stat_scratch(mid),
        dma(2, SPLIT, 3),
        dma(2, PHASES, 2),
        dma(5),
        dma(2, 2),
        pltpu.VMEM((40, 256), f32),
        pltpu.VMEM((SPLIT, 40, 256), f32),
        pltpu.VMEM((PHASES, 32, 128), f32),
        pltpu.VMEM((32, 128), f32),
        pltpu.VMEM((32, pixels), f32),
        pltpu.VMEM((pixels, mid), f32),
        *sum_scratch(pixels, mid, TILES),
        *stat_scratch(mid),
        *gather_scratch(TILES),
        pltpu.VMEM((pixels, n), f32),
        pltpu.VMEM((2, pixels, n // 2), bf16),
        *stat_scratch(n),
        dma(2, 2, PHASES),
        dma(4),
        dma(2, 3),
        *pyramid_scratch(pixels, n, m),
    ]
    arrays = [
        feat, mask, weight, expand, gain1, bias1, head_weight, head_gain, head_bias, cotangent, dilated, gain2, bias2,
        gain3, bias3, pyramid_weight,
    ]
    return call("forward", cid, forward, arrays, outs, scratch, hbm_ins=(15,), hbm_outs=(13, 18))


PACE = (2, 14, 22, 24)


def packed_sums(values, send):
    i = 0
    for value in values:
        for g in range(value.shape[1] // 128):
            send[i : i + 1] = value[:, g * 128 : (g + 1) * 128]
            i += 1


def unpacked_sums(recv, rows_each, count):
    out, i = [], 0
    for _ in range(count):
        parts = []
        for _ in range(rows_each):
            value = recv[0, i : i + 1]
            for d in range(1, PHASES):
                value = value + recv[d, i : i + 1]
            parts.append(value)
            i += 1
        out.append(parts[0] if rows_each == 1 else jnp.concatenate(parts, axis=1))
    return out


def spread_lanes(v, n):
    return v if n == 128 else jnp.concatenate([v] * (n // 128), axis=1)


def backward(
    grads, trunk, others, weight, norm3, masked, valid, expand, gain3, bias3, norm2, gain2, bias2, full2, taps, dilated,
    norm1, gain1, bias1, reduce_rows, stats1, stats2, stats3, picks, inputs, *refs
):
    outs, scratch = refs[:6], refs[6:]
    (features_grad, aspp_parts, dilated_grad, expand_grad, reduce_grad, sums_out) = outs
    (wide, moved, acc, dsend, drecv, tpad, r_in, picked_in, turned, zsend, r_y) = scratch[:11]
    (gp3, g3, own, out, near, cross, hidden, gp2, g2, prod, edges, g1) = scratch[11:23]
    gp1, lanes = gp2, own
    (st3, st3r, st2, st2r, st1, st1r, e_part, e_mid, e_in, e_y, e_sum, d_part, d_in, d_y, d_sum, r_mid, r_sum) = scratch[23:40]
    (w_sems, d_sems, y_sems, z_sems, near_sems, far_sems, st_sems, gn, gf, gh, gn1, gf1, gh1, edge_sems, ch_sems, pix_sems, pair_sems, own_sems, tap_sems, in_sems, fill_sems) = scratch[40:]
    p, c = lax.axis_index("pix"), lax.axis_index("ch")
    y, z = lax.rem(p, 2), p // 2
    pixels, n = norm3.shape
    m = weight.shape[4]
    mid = norm2.shape[1]
    tile = pixels // TILES
    contract0 = (((0,), (0,)), ((), ()))
    contract1 = (((1,), (1,)), ((), ()))
    count = stats1[2:3, :1]
    barrier, expected = greet((1, 2, 3), FAR_FIRST)
    loads = load_pyramid(weight, wide, w_sems)

    group, upper = lax.rem(p, 4), p // 4
    quarter = picks.shape[2]
    pl.semaphore_wait(barrier, expected)
    mine = rows(c * quarter, quarter)
    sent_picks = [
        push(picks, picked_in.at[:, :, mine], y_sems.at[0, k], y_sems.at[1, k], (p, c ^ k)) for k in (2, 3, 1)
    ] + [keep(picks, picked_in.at[:, :, mine], y_sems.at[0, 0])]
    filled = [
        keep(
            (others.at[k - 1] if k else trunk).at[h],
            tpad.at[k, 64 : 64 + pixels, h * m : (h + 1) * m],
            fill_sems.at[k, h],
        )
        for k in range(4)
        for h in range(2)
    ]
    for i in range(4):
        tpad[i, :64] = jnp.zeros((64, n), bf16)
        tpad[i, 64 + pixels :] = jnp.zeros((64, n), bf16)

    for j in range(3):
        q = RATE_COLS[j]
        plain = grads[:, j * m : (j + 1) * m]
        value = plain.astype(f32)
        moved[j, :, :m] = move_cols(value, -q).astype(bf16)
        moved[j, :, m : 2 * m] = plain
        moved[j, :, 2 * m :] = move_cols(value, q).astype(bf16)
    back = []
    for h in range(2):
        half = slice(h * m, (h + 1) * m)
        for j in range(3):
            s = RATE_ROWS[j] * 32
            for a in (1, 0, 2):
                if h == 0:
                    for load in loads[3 * j + a]:
                        load.wait()
                w = wide[3 * j + a, half]
                if a == 1:
                    value = lax.dot_general(moved[j], w, contract1, preferred_element_type=f32)
                    if j == 0:
                        acc[...] = value
                    else:
                        acc[...] += value
                elif a == 0:
                    acc[: pixels - s] += lax.dot_general(moved[j, s:], w, contract1, preferred_element_type=f32)
                else:
                    acc[s:] += lax.dot_general(moved[j, : pixels - s], w, contract1, preferred_element_type=f32)
        dsend[h] = acc[...].astype(bf16)
        for k in FAR_FIRST:
            back.append(
                push(
                    dsend.at[h, rows((p ^ k) * 128, 128)],
                    drecv.at[h, rows(p * 128, 128)],
                    d_sems.at[0, h, k],
                    d_sems.at[1, h, k],
                    (p ^ k, c),
                )
            )
        back.append(keep(dsend.at[h, rows(p * 128, 128)], drecv.at[h, rows(p * 128, 128)], own_sems.at[h]))

    all_inputs = [
        keep(inputs.at[i // 2, pl.ds(i % 2 * n, n)], wide.at[i, :, :n], in_sems.at[i]) for i in range(8)
    ]
    cut = moved.shape[2]
    own_taps = [
        keep(taps.at[:, :cut], moved.at[0], tap_sems.at[0]),
        keep(taps.at[:, cut:], moved.at[1, :, : taps.shape[1] - cut], tap_sems.at[1]),
    ]

    place = lax.broadcasted_iota(jnp.int32, (64, pixels), 1) % 32

    def turn(i, part):
        at = slice(i * pixels, (i + 1) * pixels)
        for j in range(3):
            q = RATE_COLS[j]
            plain = part(j)
            value = plain.astype(f32)
            turned[j, :64, at] = jnp.where(place >= 32 - q, 0.0, pltpu.roll(value, pixels - q, 1)).astype(bf16)
            turned[j, 64:128, at] = plain
            turned[j, 128:, at] = jnp.where(place < q, 0.0, pltpu.roll(value, q, 1)).astype(bf16)

    pick = pick_rows(m, 64, group)
    turn(
        0,
        lambda j: lax.dot_general(
            pick, grads[:, j * m : (j + 1) * m], contract1, preferred_element_type=f32
        ).astype(bf16),
    )
    for copy in sent_picks:
        copy.wait()
    for k in (1, 2, 3):
        turn(k, lambda j: picked_in[k - 1, j * 64 : (j + 1) * 64])
    for copy in filled:
        copy.wait()
    for j in range(3):
        s = RATE_ROWS[j] * 32
        for a in range(3):
            if a == 1:
                low, high, start = 0, pixels, 64
            elif a == 0:
                low, high = s // 128 * 128, pixels
                start = 64 + low - s
            else:
                low, high, start = 0, -(-(pixels - s) // 128) * 128, 64 + s
            value = None
            for i in range(4):
                term = jnp.dot(
                    turned[j, :, i * pixels + low : i * pixels + high],
                    tpad[i, start : start + high - low],
                    preferred_element_type=f32,
                )
                value = term if value is None else value + term
            value = value.astype(bf16)
            for b in range(3):
                for to in range(2):
                    at = b * 64 + to * 32
                    zsend[to, (3 * j + a) * 3 + b] = value[at : at + 32]
    for copy in back:
        copy.wait()
    zcopies = [keep(zsend.at[upper], aspp_parts.at[0], own_sems.at[2])]

    def send_parts(first, end):
        for i in range(first, end):
            zcopies.append(
                push(zsend.at[1 - upper, i], aspp_parts.at[1, i], z_sems.at[0, i], z_sems.at[1, i], (p ^ 4, c))
            )

    send_parts(0, PACE[0])

    def over_z(blocks, sums, sems, own_sem):
        return [
            push(blocks.at[z ^ k], sums.at[z], sems.at[0, k], sems.at[1, k], (p ^ (2 * k), c)) for k in (3, 2, 1)
        ] + [keep(blocks.at[z], sums.at[z], own_sem)]

    def norm_back(grad, norm, sums, scale, gain, v):
        return gain * scale * (grad - v * (sums[0] + norm * sums[1]) / count)

    def three(i, carry):
        at = rows(i * 32, 32)
        norm = norm3[at]
        pre = norm * gain3[...] + bias3[...] + masked[at].astype(f32)
        grad = jnp.concatenate([drecv[0, at], drecv[1, at]], axis=1).astype(f32)
        grad = grad * spread_lanes(valid[at], n) * slope(pre)
        gp3[at] = grad
        return carry[0] + fold(grad), carry[1] + fold(grad * norm)

    zero = jnp.zeros((8, n), f32)
    bias, gain = loop(pixels // 32, three, (zero, zero))
    packed_sums((total(bias), total(gain)), st3)
    pix_exchange(st3, st3r, st_sems.at[0])
    send_parts(PACE[0], PACE[1])
    sums = unpacked_sums(st3r, n // 128, 2)
    sums_out[0:1] = sums[0]
    sums_out[1:2] = sums[1]

    def part3(t):
        def step(i, carry):
            at = rows(t * tile + i * 32, 32)
            v = spread_lanes(valid[at], n)
            g3[at] = norm_back(gp3[at], norm3[at], sums, stats3[1:2], gain3[...], v).astype(bf16)
            return carry

        loop(tile // 32, step, 0)
        return lax.dot_general(g3[t * tile : (t + 1) * tile], expand[...], contract1, preferred_element_type=f32)

    result = sum_over_ch(part3, tile, TILES, own, out, near, cross, near_sems.at[0], far_sems.at[0])
    value = lax.dot_general(full2[...], g3[...], contract0, preferred_element_type=f32).astype(bf16)
    for d in range(SPLIT):
        e_part[d] = value[d * mid : (d + 1) * mid]
    e_copies = [
        push(e_part.at[c ^ k], e_mid.at[c], ch_sems.at[0, 0, k], ch_sems.at[0, 1, k], (p, c ^ k)) for k in (2, 3, 1)
    ]
    e_copies.append(keep(e_part.at[c], e_mid.at[c], own_sems.at[3]))

    bias, gain = jnp.zeros((8, mid), f32), jnp.zeros((8, mid), f32)
    for t in range(TILES):
        hidden[t * tile : (t + 1) * tile] = result(t)

    def two(i, carry):
        at = rows(i * 128, 128)
        norm = norm2[at]
        grad = hidden[at] * valid[at] * slope(norm * gain2[...] + bias2[...])
        gp2[at] = grad
        return carry[0] + fold(grad), carry[1] + fold(grad * norm)

    bias, gain = loop(pixels // 128, two, (bias, gain))
    packed_sums((total(bias), total(gain)), st2)
    pix_exchange(st2, st2r, st_sems.at[1])
    send_parts(PACE[1], PACE[2])
    for copy in e_copies:
        copy.wait()
    e_to_y = push(
        e_mid.at[:, :, rows((1 - y) * 256, 256)], e_in, pair_sems.at[0, 0], pair_sems.at[1, 0], (p ^ 1, c)
    )
    sums2 = unpacked_sums(st2r, 1, 2)
    sums_out[2:3, :mid] = sums2[0]
    sums_out[3:4, :mid] = sums2[1]

    def ready2(t):
        def step(i, carry):
            at = rows(t * tile + i * 128, 128)
            value = norm_back(gp2[at], norm2[at], sums2, stats2[1:2], gain2[...], valid[at])
            g2[at, rows(c * mid, mid)] = value.astype(bf16)
            return carry

        loop(tile // 128, step, 0)

    gather_over_ch(g2, mid, tile, TILES, gn, gf, gh, ready2)

    e_to_y.wait()
    for d in range(4):
        e_y[d] = (e_mid[d, :, rows(y * 256, 256)].astype(f32) + e_in[d].astype(f32)).astype(bf16)
    pix_copies = over_z(e_y, e_sum, pix_sems.at[0], own_sems.at[5])

    place = lax.broadcasted_iota(jnp.int32, (128, mid), 0) % 32

    def across(i, a):
        beta = i % COL_CLASSES
        two_on = (beta + 2) % 4 * 128
        here = slice(beta * 128, (beta + 1) * 128)
        there = slice(two_on, two_on + 128)
        lane = lambda b: slice((3 * a + b) * mid, (3 * a + b + 1) * mid)
        left, right = prod[there, lane(0)], prod[there, lane(2)]
        if beta >= 2:
            left = jnp.where(place == 31, 0.0, pltpu.roll(left, 127, 0))
        else:
            right = jnp.where(place == 0, 0.0, pltpu.roll(right, 1, 0))
        return prod[here, lane(1)] + left + right

    for i in range(PHASES):
        at = slice(i * 128, (i + 1) * 128)
        if i % COL_CLASSES == 0:
            prod[...] = lax.dot_general(
                g2[i * 128 : (i + COL_CLASSES) * 128], dilated[...], contract1, preferred_element_type=f32
            )
        up, same, down = across(i, 0), across(i, 1), across(i, 2)
        zero = jnp.zeros((32, mid), f32)
        hidden[at] = same + jnp.concatenate([up[32:], zero]) + jnp.concatenate([zero, down[:96]])
        edges[0, i] = up[:32].astype(bf16)
        edges[1, i] = down[96:].astype(bf16)
    first, last = p == 0, p == PHASES - 1
    to_next = lambda: pltpu.make_async_remote_copy(
        src_ref=edges.at[1], dst_ref=edges.at[2], send_sem=edge_sems.at[0, 0], recv_sem=edge_sems.at[1, 0],
        device_id=(p + 1, c), device_id_type=MESH,
    )
    to_last = lambda: pltpu.make_async_remote_copy(
        src_ref=edges.at[0], dst_ref=edges.at[3], send_sem=edge_sems.at[0, 1], recv_sem=edge_sems.at[1, 1],
        device_id=(p - 1, c), device_id_type=MESH,
    )

    @pl.when(jnp.logical_not(last))
    def _():
        to_next().start()

    @pl.when(jnp.logical_not(first))
    def _():
        to_last().start()

    @pl.when(first)
    def _():
        edges[2] = jnp.zeros((PHASES, 32, mid), bf16)

    @pl.when(last)
    def _():
        edges[3] = jnp.zeros((PHASES, 32, mid), bf16)

    for copy in own_taps:
        copy.wait()
    value = jnp.concatenate(
        [
            lax.dot_general(g2[...], moved[0], contract0, preferred_element_type=f32).astype(bf16),
            lax.dot_general(
                g2[...], moved[1, :, : taps.shape[1] - cut], contract0, preferred_element_type=f32
            ).astype(bf16),
        ],
        axis=1,
    )
    out_rows = SPLIT * mid // PHASES
    for d in range(PHASES):
        d_part[d % 2, d // 2] = value[d * out_rows : (d + 1) * out_rows]
    d_to_y = push(d_part.at[1 - y], d_in, pair_sems.at[0, 1], pair_sems.at[1, 1], (p ^ 1, c))

    @pl.when(jnp.logical_not(last))
    def _():
        to_next().wait_send()
        to_last().wait_recv()

    @pl.when(jnp.logical_not(first))
    def _():
        to_last().wait_send()
        to_next().wait_recv()

    send_parts(PACE[2], PACE[3])

    bias, gain = jnp.zeros((8, mid), f32), jnp.zeros((8, mid), f32)
    for i in range(PHASES):
        at = slice(i * 128, (i + 1) * 128)
        zero = jnp.zeros((64, mid), f32)
        edge = jnp.concatenate([edges[2, i].astype(f32), zero, edges[3, i].astype(f32)])
        norm = norm1[at]
        grad = (hidden[at] + edge) * valid[at] * slope(norm * gain1[...] + bias1[...])
        gp1[at] = grad
        bias, gain = bias + fold(grad), gain + fold(grad * norm)
    packed_sums((total(bias), total(gain)), st1)
    pix_exchange(st1, st1r, st_sems.at[2])
    send_parts(PACE[3], 27)
    sums1 = unpacked_sums(st1r, 1, 2)
    sums_out[4:5, :mid] = sums1[0]
    sums_out[5:6, :mid] = sums1[1]

    def ready1(t):
        def step(i, carry):
            at = rows(t * tile + i * 128, 128)
            value = norm_back(gp1[at], norm1[at], sums1, stats1[1:2], gain1[...], valid[at])
            g1[at, rows(c * mid, mid)] = value.astype(bf16)
            return carry

        loop(tile // 128, step, 0)

    late = []

    def between():
        for copy in all_inputs:
            copy.wait()
        own_g1 = g1[:, rows(c * mid, mid)]
        for i in range(SPLIT):
            value = lax.dot_general(wide[2 * i, :, :n], own_g1[:n], contract0, preferred_element_type=f32)
            value = value + lax.dot_general(wide[2 * i + 1, :, :n], own_g1[n:], contract0, preferred_element_type=f32)
            r_mid[i] = value.astype(bf16).reshape(2, 256, mid)
        late.append(push(r_mid.at[:, 1 - y], r_in, pair_sems.at[0, 2], pair_sems.at[1, 2], (p ^ 1, c)))
        d_to_y.wait()
        for d in range(4):
            d_y[d] = (d_part[y, d].astype(f32) + d_in[d].astype(f32)).astype(bf16)
        pix_copies.extend(over_z(d_y, d_sum, pix_sems.at[1], own_sems.at[6]))

    gather_over_ch(g1, mid, tile, TILES, gn1, gf1, gh1, ready1, between)
    late[0].wait()
    for d in range(4):
        r_y[d] = (r_mid[d, y].astype(f32) + r_in[d].astype(f32)).astype(bf16)
    pix_copies += over_z(r_y, r_sum, pix_sems.at[2], own_sems.at[7])

    for i in range(PHASES):
        at = slice(i * 128, (i + 1) * 128)
        value = lax.dot_general(g1[at], reduce_rows[...], contract1, preferred_element_type=f32) + gp3[at]
        value = value * spread_lanes(valid[at], n)
        for g in range(n // 128):
            for r in range(4):
                start = (2 * r + i // COL_CLASSES) * 128 + i % COL_CLASSES
                lanes[g, pl.ds(start, 32, stride=COL_CLASSES), :] = value[r * 32 : (r + 1) * 32, g * 128 : (g + 1) * 128]
    for g in range(n // 128):
        features_grad[:, g * 128 : (g + 1) * 128] = lanes[g].astype(bf16)
    for copy in pix_copies:
        copy.wait()

    def gathered(parts):
        value = parts[0].astype(f32)
        for d in range(1, parts.shape[0]):
            value = value + parts[d].astype(f32)
        return value

    expand_grad[...] = gathered(e_sum)
    reduce_grad[...] = gathered(r_sum)
    value = gathered(d_sum)
    for i in range(9):
        dilated_grad[i] = value[:, i * mid : (i + 1) * mid]
    for copy in zcopies:
        copy.wait()


def run_backward(cid, arrays):
    (grads, trunk, others, weight, norm3, masked, valid, expand, gain3, bias3, norm2, gain2, bias2, full2, taps, dilated,
     norm1, gain1, bias1, reduce_rows, stats1, stats2, stats3, picks, inputs) = arrays
    pixels, n = norm3.shape
    m = weight.shape[4]
    mid = norm2.shape[1]
    all_mid = SPLIT * mid
    outs = [
        shape((pixels, n), bf16),
        shape((2, 27, 32, n), bf16),
        shape((9, all_mid // PHASES, mid), f32),
        shape((mid, 256), f32),
        shape((256, mid), f32),
        shape((8, n), f32),
    ]
    sums = sum_scratch(pixels, mid, TILES)
    scratch = [
        pltpu.VMEM((9, n, 3 * m), bf16),
        pltpu.VMEM((3, pixels, 3 * m), bf16),
        pltpu.VMEM((pixels, m), f32),
        pltpu.VMEM((2, pixels, m), bf16),
        pltpu.VMEM((2, pixels, m), bf16),
        pltpu.VMEM((4, pixels + 128, n), bf16),
        pltpu.VMEM((4, 256, mid), bf16),
        pltpu.VMEM((3, 192, pixels), bf16),
        pltpu.VMEM((3, 192, 4 * pixels), bf16),
        pltpu.VMEM((2, 27, 32, n), bf16),
        pltpu.VMEM((4, 256, mid), bf16),
        pltpu.VMEM((pixels, n), f32),
        pltpu.VMEM((pixels, n), bf16),
        *sums[:4],
        pltpu.VMEM((pixels, mid), f32),
        pltpu.VMEM((pixels, mid), f32),
        pltpu.VMEM((pixels, all_mid), bf16),
        pltpu.VMEM((pixels // ROW_CLASSES, 9 * mid), f32),
        pltpu.VMEM((4, PHASES, 32, mid), bf16),
        pltpu.VMEM((pixels, all_mid), bf16),
        pltpu.VMEM((8, 128), f32),
        pltpu.VMEM((PHASES, 8, 128), f32),
        pltpu.VMEM((8, 128), f32),
        pltpu.VMEM((PHASES, 8, 128), f32),
        pltpu.VMEM((8, 128), f32),
        pltpu.VMEM((PHASES, 8, 128), f32),
        pltpu.VMEM((SPLIT, mid, n), bf16),
        pltpu.VMEM((SPLIT, mid, n), bf16),
        pltpu.VMEM((4, mid, 256), bf16),
        pltpu.VMEM((4, mid, 256), bf16),
        pltpu.VMEM((4, mid, 256), bf16),
        pltpu.VMEM((2, 4, all_mid // PHASES, 9 * mid), bf16),
        pltpu.VMEM((4, all_mid // PHASES, 9 * mid), bf16),
        pltpu.VMEM((4, all_mid // PHASES, 9 * mid), bf16),
        pltpu.VMEM((4, all_mid // PHASES, 9 * mid), bf16),
        pltpu.VMEM((4, 2, 256, mid), bf16),
        pltpu.VMEM((4, 256, mid), bf16),
        dma(9, 3),
        dma(2, 2, PHASES),
        dma(3, 4),
        dma(2, 27),
        dma(1, 2, TILES, 2),
        dma(1, 2, TILES),
        dma(3, 2, PHASES),
        *gather_scratch(TILES),
        *gather_scratch(TILES),
        dma(2, 2),
        dma(2, 2, SPLIT),
        dma(3, 2, PHASES),
        dma(2, 3),
        dma(8),
        dma(2),
        dma(8),
        dma(4, 2),
    ]
    vmem = pl.BlockSpec(memory_space=pltpu.VMEM)
    specs = [vmem] * len(arrays)
    specs[1] = specs[2] = specs[3] = specs[14] = specs[24] = pl.BlockSpec(memory_space=pl.ANY)
    return pl.pallas_call(
        backward,
        out_shape=outs,
        in_specs=specs,
        out_specs=[vmem, pl.BlockSpec(memory_space=pl.ANY)] + [vmem] * (len(outs) - 2),
        scratch_shapes=scratch,
        compiler_params=pltpu.CompilerParams(
            collective_id=cid, has_side_effects=True, vmem_limit_bytes=VMEM_BYTES
        ),
        name="backward",
    )(*arrays)


def fast_device(
    features,
    pixel_mask,
    reduce_weight,
    reduce_gain,
    reduce_bias,
    dilated_weight,
    dilated_gain,
    dilated_bias,
    expand_weight,
    expand_gain,
    expand_bias,
    aspp_weight,
    aspp_gain,
    aspp_bias,
    task_weight,
    cotangent,
):
    rows_here, width, local_in = features.shape
    pixels = rows_here * width
    local_mid = reduce_weight.shape[1]
    full_mid = dilated_weight.shape[3]
    branch_width = aspp_weight.shape[4]
    own_branch = task_weight.shape[1]
    outs_count = task_weight.shape[2]
    me_ch = lax.axis_index("ch")
    line = lambda v: v.reshape(1, -1)
    dilated_rows = dilated_weight.reshape(9 * local_mid, full_mid)
    (
        masked, reduce_rows, expand_cols, norm_one, stat_one, valid, norm_two, act_two_full, taps_one, stat_two, norm_three,
        trunk_class, stat_three, inputs_all, grad_full, predictions, head_grad, branch_sums, trunk_others, picks,
    ) = run_forward(
        1,
        features.reshape(pixels, local_in),
        pixel_mask,
        reduce_weight,
        expand_weight,
        line(reduce_gain),
        line(reduce_bias),
        task_weight.transpose(0, 2, 1),
        aspp_gain,
        aspp_bias,
        cotangent.transpose(2, 0, 1).reshape(outs_count, pixels),
        dilated_rows,
        line(dilated_gain),
        line(dilated_bias),
        line(expand_gain),
        line(expand_bias),
        aspp_weight,
    )
    features_grad, aspp_parts, dilated_sum, expand_weight_grad, reduce_weight_grad, norm_sums = run_backward(
        2,
        [
            grad_full, trunk_class, trunk_others, aspp_weight, norm_three, masked, valid, expand_cols,
            line(expand_gain), line(expand_bias), norm_two, line(dilated_gain), line(dilated_bias), act_two_full,
            taps_one, dilated_rows, norm_one, line(reduce_gain), line(reduce_bias), reduce_rows, stat_one, stat_two,
            stat_three, picks, inputs_all,
        ],
    )
    features_grad = features_grad.reshape(rows_here, width, local_in)
    aspp_weight_grad = (aspp_parts[0].astype(f32) + aspp_parts[1].astype(f32)).reshape(
        3, 3, 3, -1, local_in
    ).transpose(0, 1, 2, 4, 3)
    dilated_weight_grad = dilated_sum.reshape(3, 3, -1, local_mid).transpose(0, 1, 3, 2)
    expand_bias_grad, expand_gain_grad = norm_sums[0], norm_sums[1]
    dilated_bias_grad, dilated_gain_grad = norm_sums[2, :local_mid], norm_sums[3, :local_mid]
    reduce_bias_grad, reduce_gain_grad = norm_sums[4, :local_mid], norm_sums[5, :local_mid]
    predictions = from_classes(predictions.transpose(0, 2, 1), rows_here, width)[:, :, :outs_count]
    head_grad = head_grad.reshape(32, 3, 4, own_branch).transpose(2, 1, 3, 0)
    task_weight_grad = lax.dynamic_index_in_dim(head_grad, me_ch, keepdims=False)[:, :, :outs_count]
    own_sums = lax.dynamic_slice_in_dim(
        branch_sums[:6].reshape(2, 3, branch_width), me_ch * own_branch, own_branch, axis=2
    )
    aspp_bias_grad, aspp_gain_grad = own_sums[0], own_sums[1]

    return (
        predictions,
        features_grad,
        reduce_weight_grad,
        reduce_gain_grad,
        reduce_bias_grad,
        dilated_weight_grad,
        dilated_gain_grad,
        dilated_bias_grad,
        expand_weight_grad,
        expand_gain_grad,
        expand_bias_grad,
        aspp_weight_grad,
        aspp_gain_grad,
        aspp_bias_grad,
        task_weight_grad,
    )


def solution(mesh):
    placed = (
        P("pix", None, "ch"),
        P("pix", None),
        P(None, "ch"),
        P("ch"),
        P("ch"),
        P(None, None, "ch", None),
        P("ch"),
        P("ch"),
        P("ch", None),
        P("ch"),
        P("ch"),
        P(None, None, None, "ch", None),
        P(None, "ch"),
        P(None, "ch"),
        P(None, "ch", None),
        P("pix", None, None),
    )
    return jax.shard_map(
        fast_device if (mesh.shape["pix"], mesh.shape["ch"]) == (PHASES, 4) else on_device,
        mesh=mesh,
        in_specs=placed,
        out_specs=(
            P("pix", None, None),
            P("pix", None, "ch"),
            P("pix", "ch"),
            P("ch"),
            P("ch"),
            P(None, None, "ch", "pix"),
            P("ch"),
            P("ch"),
            P("ch", "pix"),
            P("ch"),
            P("ch"),
            P(None, None, None, "ch", "pix"),
            P(None, "ch"),
            P(None, "ch"),
            P(None, "ch", None),
        ),
        check_vma=False,
    )
```

```python
import jax
import jax.numpy as jnp
from jax import lax
from jax.experimental import pallas as pl
from jax.experimental.pallas import tpu as pltpu
from jax.sharding import PartitionSpec as P

CLS = 19


epsilon = 1e-05
highest = lax.Precision.HIGHEST
aspp_rates = (12, 24, 36)
inner_rate = 2


def from_behind(value, axis, steps):
    count = lax.axis_size(axis)
    first, last = (max(0, -steps), min(count, count - steps))
    return lax.ppermute(value, axis, [(source, source + steps) for source in range(first, last)])


def with_halo(shard, sides, width):
    for axis, dim in sides:
        devices, length = (lax.axis_size(axis), shard.shape[dim])
        up = [(i, (i + 1) % devices) for i in range(devices - 1)]
        down = [(j, i) for i, j in up]
        last = lax.slice_in_dim(shard, length - width, length, axis=dim)
        first = lax.slice_in_dim(shard, 0, width, axis=dim)
        before = lax.ppermute(last, axis, up)
        after = lax.ppermute(first, axis, down)
        shard = jnp.concatenate([before, shard, after], axis=dim)
    return shard


def silu_slope(value):
    sigma = jax.nn.sigmoid(value)
    return sigma * (1.0 + value * (1.0 - sigma))


def shift_cols(value, offset):
    if offset == 0:
        return value
    margin = abs(offset)
    widths = [(0, 0)] * value.ndim
    widths[1] = (margin, margin)
    padded = jnp.pad(value, widths)
    return lax.slice_in_dim(padded, margin + offset, margin + offset + value.shape[1], axis=1)


def moved(piece, distance):
    return from_behind(piece, "pix", -distance)


def shift_rows(value, offset):
    if offset == 0:
        return value
    steps_over, inner = divmod(offset, value.shape[0])
    first = moved(value, steps_over)[inner:]
    if inner == 0:
        return first
    second = moved(value, steps_over + 1)[:inner]
    return jnp.concatenate([first, second], axis=0)


def halo_rows(value):
    return with_halo(value, (("pix", 0),), inner_rate)


def gather_channels(value):
    return lax.all_gather(value, "ch", axis=1, tiled=True)


def sum_channels(value):
    return lax.psum_scatter(
        value.astype(jnp.bfloat16), "ch", scatter_dimension=1, tiled=True
    ).astype(jnp.float32)


def normalized(hidden, valid, axes):
    total, count = lax.psum(
        (jnp.sum(hidden * valid, axis=axes, keepdims=True), jnp.sum(valid)), "pix"
    )
    center = total / count
    spread_sum = lax.psum(jnp.sum(valid * (hidden - center) ** 2, axis=axes, keepdims=True), "pix")
    variance = spread_sum / count
    scale = lax.rsqrt(variance + epsilon)
    return ((hidden - center) * scale, scale, count)


def norm_grad(grad_out, centered, scale, gain, count, valid, axes):
    sum_out, sum_cross = lax.psum(
        (
            jnp.sum(grad_out, axis=axes, keepdims=True),
            jnp.sum(grad_out * centered, axis=axes, keepdims=True),
        ),
        "pix",
    )
    grad_in = gain * scale * (grad_out - valid * (sum_out + centered * sum_cross) / count)
    return (grad_in, sum_cross, sum_out)


def task_scales(gram):
    norms = jnp.sqrt(jnp.diagonal(gram) + 1e-06)
    proj = gram / norms[None, :]
    vector = proj[0, 0] - proj[0, 1:]
    matrix = proj[0, 0] - proj[0, 1:][None, :] - proj[1:, 0][:, None] + proj[1:, 1:]
    determinant = matrix[0, 0] * matrix[1, 1] - matrix[0, 1] * matrix[1, 0]
    second = (vector[0] * matrix[1, 1] - vector[1] * matrix[1, 0]) / determinant
    third = (vector[1] * matrix[0, 0] - vector[0] * matrix[0, 1]) / determinant
    return jnp.stack([1.0 - second - third, second, third])


def on_device(
    features,
    pixel_mask,
    reduce_weight,
    reduce_gain,
    reduce_bias,
    dilated_weight,
    dilated_gain,
    dilated_bias,
    expand_weight,
    expand_gain,
    expand_bias,
    aspp_weight,
    aspp_gain,
    aspp_bias,
    task_weight,
    cotangent,
):
    rows_here, width, local_in = features.shape
    pixels = rows_here * width
    local_mid = reduce_weight.shape[1]
    full_mid = dilated_weight.shape[3]
    branch_width = aspp_weight.shape[4]
    outs_count = task_weight.shape[2]
    valid = pixel_mask.astype(jnp.float32).reshape(pixels, 1)
    valid_branch = valid[None]
    masked = features.reshape(pixels, local_in) * valid.astype(jnp.bfloat16)
    inputs_full = gather_channels(masked)
    hidden_one = jnp.dot(inputs_full, reduce_weight, preferred_element_type=jnp.float32)
    norm_one, scale_one, count = normalized(hidden_one, valid, (0,))
    pre_one = norm_one * reduce_gain + reduce_bias
    act_one = (jax.nn.silu(pre_one) * valid).astype(jnp.bfloat16)
    padded_one = halo_rows(act_one.reshape(rows_here, width, local_mid))
    partial_value = jnp.zeros((pixels, full_mid), jnp.float32)
    for a in range(3):
        for b in range(3):
            shifted = shift_cols(padded_one[2 * a : 2 * a + rows_here], (b - 1) * inner_rate)
            partial_value = partial_value + jnp.dot(
                shifted.reshape(pixels, local_mid),
                dilated_weight[a, b],
                preferred_element_type=jnp.float32,
            )
    hidden_two = sum_channels(partial_value)
    norm_two, scale_two, _ = normalized(hidden_two, valid, (0,))
    pre_two = norm_two * dilated_gain + dilated_bias
    act_two = (jax.nn.silu(pre_two) * valid).astype(jnp.bfloat16)
    hidden_three = sum_channels(jnp.dot(act_two, expand_weight, preferred_element_type=jnp.float32))
    norm_three, scale_three, _ = normalized(hidden_three, valid, (0,))
    pre_three = norm_three * expand_gain + expand_bias + masked.astype(jnp.float32)
    trunk_out = (
        (jax.nn.silu(pre_three) * valid).astype(jnp.bfloat16).reshape(rows_here, width, local_in)
    )
    kept_rows = []
    partials = []
    for j in range(3):
        rate = aspp_rates[j]
        running = jnp.zeros((pixels, branch_width), jnp.float32)
        shifted_rows = []
        for a in range(3):
            row_shift = shift_rows(trunk_out, (a - 1) * rate)
            shifted_rows.append(row_shift)
            for b in range(3):
                shifted = shift_cols(row_shift, (b - 1) * rate)
                running = running + jnp.dot(
                    shifted.reshape(pixels, local_in),
                    aspp_weight[j, a, b],
                    preferred_element_type=jnp.float32,
                )
        kept_rows.append(shifted_rows)
        partials.append(running)
    branch_sum = sum_channels(jnp.stack(partials).reshape(3 * pixels, branch_width)).reshape(
        3, pixels, -1
    )
    branch_gain = aspp_gain[:, None, :]
    norm_branch, scale_branch, _ = normalized(branch_sum, valid_branch, (1,))
    pre_branch = norm_branch * branch_gain + aspp_bias[:, None, :]
    branch_out = (jax.nn.silu(pre_branch) * valid_branch).astype(jnp.bfloat16)
    predictions = lax.psum(
        jnp.einsum(
            "jpc,jco->po", branch_out, task_weight, preferred_element_type=jnp.float32
        ).astype(jnp.bfloat16),
        "ch",
    ).astype(jnp.float32)
    columns = jnp.arange(outs_count)
    task_of = (columns >= CLS).astype(jnp.int32) + (columns >= CLS + 1).astype(jnp.int32)
    select = (task_of[:, None] == jnp.arange(3)[None, :]).astype(jnp.float32)
    target = cotangent.reshape(pixels, outs_count) * valid
    task_float = task_weight.astype(jnp.float32)
    task_grads = jnp.einsum("po,ot,jco->tjpc", target, select, task_float, precision=highest)
    gram = lax.psum(
        jnp.einsum("tjpc,sjpc->ts", task_grads, task_grads, precision=highest), ("pix", "ch")
    )
    scales = task_scales(gram)
    branch_grad = jnp.einsum("t,tjpc->jpc", scales, task_grads, precision=highest)
    task_weight_grad = lax.psum(
        jnp.einsum("jpc,po->jco", branch_out.astype(jnp.float32), target, precision=highest), "pix"
    )
    grad_pre_branch = branch_grad * valid_branch * silu_slope(pre_branch)
    grad_branch, aspp_gain_grad, aspp_bias_grad = norm_grad(
        grad_pre_branch, norm_branch, scale_branch, branch_gain, count, valid_branch, (1,)
    )
    grad_full = gather_channels(grad_branch.astype(jnp.bfloat16).reshape(3 * pixels, -1)).reshape(
        3, rows_here, width, -1
    )
    grad_trunk = jnp.zeros((pixels, local_in), jnp.float32)
    aspp_list = []
    for j in range(3):
        rate = aspp_rates[j]
        grad_flat = grad_full[j].reshape(pixels, -1)
        per_row = []
        for a in range(3):
            back_rows = shift_rows(grad_full[j], -(a - 1) * rate)
            per_col = []
            for b in range(3):
                shifted = shift_cols(back_rows, -(b - 1) * rate)
                grad_trunk = grad_trunk + jnp.einsum(
                    "pa,ca->pc",
                    shifted.reshape(pixels, -1),
                    aspp_weight[j, a, b],
                    preferred_element_type=jnp.float32,
                )
                forward_tap = shift_cols(kept_rows[j][a], (b - 1) * rate).reshape(pixels, local_in)
                per_col.append(
                    jnp.einsum(
                        "pc,pa->ca", forward_tap, grad_flat, preferred_element_type=jnp.float32
                    )
                )
            per_row.append(jnp.stack(per_col))
        aspp_list.append(jnp.stack(per_row))
    aspp_weight_local = jnp.stack(aspp_list)
    grad_pre_three = grad_trunk * valid * silu_slope(pre_three)
    grad_three, expand_gain_grad, expand_bias_grad = norm_grad(
        grad_pre_three, norm_three, scale_three, expand_gain, count, valid, (0,)
    )
    grad_three_full = gather_channels(grad_three.astype(jnp.bfloat16))
    grad_act_two = jnp.einsum(
        "pc,dc->pd", grad_three_full, expand_weight, preferred_element_type=jnp.float32
    )
    expand_weight_local = jnp.einsum(
        "pd,pc->dc", act_two, grad_three_full, preferred_element_type=jnp.float32
    )
    grad_pre_two = grad_act_two * valid * silu_slope(pre_two)
    grad_two, dilated_gain_grad, dilated_bias_grad = norm_grad(
        grad_pre_two, norm_two, scale_two, dilated_gain, count, valid, (0,)
    )
    grad_two_full = gather_channels(grad_two.astype(jnp.bfloat16))
    padded_grad = halo_rows(grad_two_full.reshape(rows_here, width, full_mid))
    grad_act_one = jnp.zeros((pixels, local_mid), jnp.float32)
    dilated_rows = []
    for a in range(3):
        dilated_cols = []
        for b in range(3):
            shifted = shift_cols(
                padded_grad[4 - 2 * a : 4 - 2 * a + rows_here], -(b - 1) * inner_rate
            )
            grad_act_one = grad_act_one + jnp.einsum(
                "pe,de->pd",
                shifted.reshape(pixels, full_mid),
                dilated_weight[a, b],
                preferred_element_type=jnp.float32,
            )
            forward_tap = shift_cols(
                padded_one[2 * a : 2 * a + rows_here], (b - 1) * inner_rate
            ).reshape(pixels, local_mid)
            dilated_cols.append(
                jnp.einsum(
                    "pd,pe->de", forward_tap, grad_two_full, preferred_element_type=jnp.float32
                )
            )
        dilated_rows.append(jnp.stack(dilated_cols))
    dilated_weight_local = jnp.stack(dilated_rows)
    grad_pre_one = grad_act_one * valid * silu_slope(pre_one)
    grad_one, reduce_gain_grad, reduce_bias_grad = norm_grad(
        grad_pre_one, norm_one, scale_one, reduce_gain, count, valid, (0,)
    )
    grad_one_low = grad_one.astype(jnp.bfloat16)
    input_sum = sum_channels(
        jnp.einsum("pd,cd->pc", grad_one_low, reduce_weight, preferred_element_type=jnp.float32)
    )
    features_grad = (
        ((input_sum + grad_pre_three) * valid)
        .astype(jnp.bfloat16)
        .reshape(rows_here, width, local_in)
    )
    reduce_weight_local = jnp.einsum(
        "pc,pd->cd", inputs_full, grad_one_low, preferred_element_type=jnp.float32
    )
    reduce_weight_grad, dilated_weight_grad, expand_weight_grad, aspp_weight_grad = (
        lax.psum_scatter(reduce_weight_local, "pix", scatter_dimension=0, tiled=True),
        lax.psum_scatter(dilated_weight_local, "pix", scatter_dimension=3, tiled=True),
        lax.psum_scatter(expand_weight_local, "pix", scatter_dimension=1, tiled=True),
        lax.psum_scatter(aspp_weight_local, "pix", scatter_dimension=4, tiled=True),
    )
    return (
        predictions.reshape(rows_here, width, outs_count),
        features_grad,
        reduce_weight_grad,
        reduce_gain_grad.reshape(-1),
        reduce_bias_grad.reshape(-1),
        dilated_weight_grad,
        dilated_gain_grad.reshape(-1),
        dilated_bias_grad.reshape(-1),
        expand_weight_grad,
        expand_gain_grad.reshape(-1),
        expand_bias_grad.reshape(-1),
        aspp_weight_grad,
        aspp_gain_grad.reshape(3, -1),
        aspp_bias_grad.reshape(3, -1),
        task_weight_grad,
    )


MESH = pl.DeviceIdType.MESH
ROW_CLASSES, COL_CLASSES = 2, 4
PHASES = ROW_CLASSES * COL_CLASSES
SPLIT = 4
FAR_FIRST = (6, 7, 4, 5, 2, 3, 1)
f32, bf16 = jnp.float32, jnp.bfloat16
VMEM_BYTES = 60 << 20


def shape(dims, dtype):
    return jax.ShapeDtypeStruct(dims, dtype)


def call(name, cid, kernel, arrays, outs, scratch, hbm_ins=(), hbm_outs=()):
    vmem, hbm = pl.BlockSpec(memory_space=pltpu.VMEM), pl.BlockSpec(memory_space=pl.ANY)
    return pl.pallas_call(
        kernel,
        out_shape=outs,
        in_specs=[hbm if i in hbm_ins else vmem for i in range(len(arrays))],
        out_specs=[hbm if i in hbm_outs else vmem for i in range(len(outs))],
        scratch_shapes=scratch,
        compiler_params=pltpu.CompilerParams(
            collective_id=cid, has_side_effects=True, vmem_limit_bytes=VMEM_BYTES
        ),
        name=name,
    )(*arrays)


def dma(*dims):
    return pltpu.SemaphoreType.DMA(dims)


def greet(ch, pix):
    p, c = lax.axis_index("pix"), lax.axis_index("ch")
    barrier = pltpu.get_barrier_semaphore()
    for k in ch:
        pl.semaphore_signal(barrier, inc=1, device_id=(p, c ^ k), device_id_type=MESH)
    for k in pix:
        pl.semaphore_signal(barrier, inc=1, device_id=(p ^ k, c), device_id_type=MESH)
    return barrier, len(ch) + len(pix)


def push(src, dst, send, recv, device):
    copy = pltpu.make_async_remote_copy(
        src_ref=src,
        dst_ref=dst,
        send_sem=send,
        recv_sem=recv,
        device_id=device,
        device_id_type=MESH,
    )
    copy.start()
    return copy


def keep(src, dst, sem):
    copy = pltpu.make_async_copy(src, dst, sem)
    copy.start()
    return copy


def rows(start, size):
    return pl.ds(pl.multiple_of(start, size), size)


def fold(x):
    return jnp.sum(x.reshape(x.shape[0] // 8, 8, x.shape[1]), axis=0)


def total(x):
    return jnp.sum(x, axis=0, keepdims=True)


def loop(steps, body, init):
    return lax.fori_loop(0, steps, body, init)


def sum_over_ch(part, tile, tiles, own, out, near, cross, near_sems, far_sems):
    p, c = lax.axis_index("pix"), lax.axis_index("ch")
    k, x = lax.rem(c, 2), c // 2
    n = own.shape[2]
    copies = []
    for t in range(tiles):
        at = pl.ds(t * tile, tile)
        value = part(t)
        for d in range(SPLIT):
            block = value[:, d * n : (d + 1) * n]
            own[d, at] = block
            out[d, at] = block.astype(bf16)
        copies.append(
            [
                push(
                    out.at[2 * h + 1 - k, at],
                    near.at[h, at],
                    near_sems.at[0, t, h],
                    near_sems.at[1, t, h],
                    (p, c ^ 1),
                )
                for h in range(2)
            ]
        )
    crossing = []
    for t in range(tiles):
        at = pl.ds(t * tile, tile)
        for copy in copies[t]:
            copy.wait()
        cross[0, at] = (own[2 * (1 - x) + k, at] + near[1 - x, at].astype(f32)).astype(bf16)
        crossing.append(
            push(cross.at[0, at], cross.at[1, at], far_sems.at[0, t], far_sems.at[1, t], (p, c ^ 2))
        )

    def result(t):
        at = pl.ds(t * tile, tile)
        crossing[t].wait()
        return own[2 * x + k, at] + near[x, at].astype(f32) + cross[1, at].astype(f32)

    return result


def sum_scratch(pixels, n, tiles):
    return [
        pltpu.VMEM((SPLIT, pixels, n), f32),
        pltpu.VMEM((SPLIT, pixels, n), bf16),
        pltpu.VMEM((2, pixels, n), bf16),
        pltpu.VMEM((2, pixels, n), bf16),
        dma(2, tiles, 2),
        dma(2, tiles),
    ]


def pix_exchange(send, recv, sems):
    p, c = lax.axis_index("pix"), lax.axis_index("ch")
    copies = [
        push(send, recv.at[p], sems.at[0, k], sems.at[1, k], (p ^ k, c)) for k in FAR_FIRST
    ]
    recv[p] = send[...]
    for copy in copies:
        copy.wait()


def norm_stats(hidden, valid, pixels, send, recv, sems):
    n = hidden.shape[1]
    tile = 128
    repeat = n // 128

    def mask(at):
        v = valid[at]
        return v if repeat == 1 else jnp.concatenate([v] * repeat, axis=1)

    def first(i, carry):
        at = rows(i * tile, tile)
        v = mask(at)
        return carry[0] + fold(hidden[at] * v), carry[1] + fold(v)

    zero = jnp.zeros((8, n), f32)
    sums, count = loop(pixels // tile, first, (zero, zero))
    sums, count = total(sums), total(count)
    center = sums / jnp.maximum(count, 1.0)

    def second(i, carry):
        at = rows(i * tile, tile)
        apart = hidden[at] - center
        return carry + fold(mask(at) * apart * apart)

    spread = total(loop(pixels // tile, second, zero))
    send[0:1] = sums
    send[1:2] = spread
    send[2:3] = count
    pix_exchange(send, recv, sems)
    return join(recv, PHASES)


def join(recv, parts):
    sums, count = recv[0, 0:1], recv[0, 2:3]
    for i in range(1, parts):
        sums, count = sums + recv[i, 0:1], count + recv[i, 2:3]
    center = sums / count
    spread = jnp.zeros_like(sums)
    for i in range(parts):
        n = recv[i, 2:3]
        apart = recv[i, 0:1] / jnp.maximum(n, 1.0) - center
        spread = spread + recv[i, 1:2] + n * apart * apart
    return center, lax.rsqrt(spread / count + epsilon), count


def stat_scratch(n):
    return [pltpu.VMEM((8, n), f32), pltpu.VMEM((PHASES, 8, n), f32), dma(2, PHASES)]


def silu(x):
    return x / (1.0 + jnp.exp(-x))


def gather_over_ch(full, n, tile, tiles, near_sems, far_sems, hop_sems, ready, between=None):
    p, c = lax.axis_index("pix"), lax.axis_index("ch")

    def part(owner, t):
        return full.at[pl.ds(t * tile, tile), rows(owner * n, n)]

    near, far, hops = [], [], []
    for t in range(tiles):
        ready(t)
        src = part(c, t)
        far.append(push(src, src, far_sems.at[0, t], far_sems.at[1, t], (p, c ^ 2)))
        near.append(push(src, src, near_sems.at[0, t], near_sems.at[1, t], (p, c ^ 1)))
    if between is not None:
        between()
    for t in range(tiles):
        far[t].wait_recv()
        src = part(c ^ 2, t)
        hops.append(push(src, src, hop_sems.at[0, t], hop_sems.at[1, t], (p, c ^ 1)))
    for t in range(tiles):
        far[t].wait_send()
        near[t].wait()
        hops[t].wait()


def gather_scratch(tiles):
    return [dma(2, tiles), dma(2, tiles), dma(2, tiles)]


def to_classes(x):
    rows, cols, n = x.shape
    x = x.reshape(rows // ROW_CLASSES, ROW_CLASSES, cols // COL_CLASSES, COL_CLASSES, n)
    return x.transpose(1, 3, 0, 2, 4).reshape(PHASES, -1, n)


def from_classes(x, rows, cols):
    n = x.shape[-1]
    x = x.reshape(ROW_CLASSES, COL_CLASSES, rows // ROW_CLASSES, cols // COL_CLASSES, n)
    return x.transpose(2, 0, 3, 1, 4).reshape(rows, cols, n)


RATE_ROWS = tuple(rate // ROW_CLASSES for rate in aspp_rates)
RATE_COLS = tuple(rate // COL_CLASSES for rate in aspp_rates)


def load_pyramid(weight, wide, sems):
    m = weight.shape[4]
    return [
        [keep(weight.at[j, a, b], wide.at[3 * j + a, :, b * m : (b + 1) * m], sems.at[3 * j + a, b]) for b in range(3)]
        for j in range(3)
        for a in range(3)
    ]


def move_cols(x, by):
    place = lax.broadcasted_iota(jnp.int32, x.shape, 0) % 32
    rolled = pltpu.roll(x, by % x.shape[0], 0)
    return jnp.where(place < by, 0.0, rolled) if by > 0 else jnp.where(place >= 32 + by, 0.0, rolled)


def ch_exchange(send, recv, sems):
    p, c = lax.axis_index("pix"), lax.axis_index("ch")
    copies = [push(send, recv.at[c], sems.at[0, k], sems.at[1, k], (p, c ^ k)) for k in (2, 3, 1)]
    recv[c] = send[...]
    for copy in copies:
        copy.wait()


def add_up(recv, parts):
    value = recv[0]
    for i in range(1, parts):
        value = value + recv[i]
    return value


def task_vector(square, weights):
    product = square * weights
    row = lax.broadcasted_iota(jnp.int32, (32, 32), 0)
    col = lax.broadcasted_iota(jnp.int32, (32, 32), 1)

    def task(i):
        return (i >= CLS).astype(jnp.int32) + (i >= CLS + 1).astype(jnp.int32)

    def entry(t, s):
        return jnp.sum(
            jnp.sum(jnp.where((task(row) == t) & (task(col) == s), product, 0.0), axis=1, keepdims=True),
            axis=0,
            keepdims=True,
        )

    gram = [[entry(t, s) for s in range(3)] for t in range(3)]
    norms = [jnp.sqrt(gram[k][k] + 1e-06) for k in range(3)]
    proj = [[gram[i][k] / norms[k] for k in range(3)] for i in range(3)]
    vector = [proj[0][0] - proj[0][b] for b in (1, 2)]
    matrix = [[proj[0][0] - proj[0][b] - proj[a][0] + proj[a][b] for b in (1, 2)] for a in (1, 2)]
    determinant = matrix[0][0] * matrix[1][1] - matrix[0][1] * matrix[1][0]
    second = (vector[0] * matrix[1][1] - vector[1] * matrix[1][0]) / determinant
    third = (vector[1] * matrix[0][0] - vector[0] * matrix[0][1]) / determinant
    which = task(lax.broadcasted_iota(jnp.int32, (32, 1), 0))
    return jnp.where(which == 0, 1.0 - second - third, jnp.where(which == 1, second, third))


def slope(x):
    s = 1.0 / (1.0 + jnp.exp(-x))
    return s * (1.0 + x * (1.0 - s))


def pyramid(trunk, loads, wide, moving, pass_inputs, head_copies, heads, heads_all, targets, square, *refs):
    (full, predictions, head_grad, sums, others, picks) = refs[:6]
    (sides, own, out, near, cross, hidden, grad, branch) = refs[6:14]
    (s_send, s_ch, s_mid, s_pix, b_send, b_ch, b_mid, b_pix) = refs[14:22]
    (h_send, h_ch, h_mid, h_pix, h_sum, p_send, p_ch) = refs[22:29]
    (near_sems, far_sems, ch_sems, pix_sems, g_near, g_far, g_hop, y_sems, picked, pick_sems) = refs[29:]
    p, c = lax.axis_index("pix"), lax.axis_index("ch")
    k, x = lax.rem(c, 2), c // 2
    m = wide.shape[2] // 3
    pixels, half = trunk.shape[1], trunk.shape[2]
    quarter = pixels // SPLIT
    contract0 = (((0,), (0,)), ((), ()))
    contract1 = (((1,), (1,)), ((), ()))
    mine = rows(c * quarter, quarter)
    part = pixels // SPLIT
    sharing = []

    def share(slot, quarters, own, k, first):
        for i, q in enumerate(quarters):
            at = pl.ds(q * part, part)
            src = trunk.at[:, at] if own else others.at[2 - k, :, at]
            sharing.append(
                push(src, others.at[slot, :, at], y_sems.at[0, first + i], y_sems.at[1, first + i], (p ^ k, c))
            )
        return sharing[-len(quarters) :]

    def convolve(j, h):
        s = RATE_ROWS[j] * 32
        for a in (1, 0, 2):
            if h == 0:
                for load in loads[3 * j + a]:
                    load.wait()
            w = wide[3 * j + a, h * half : (h + 1) * half]
            if a == 1:
                value = jnp.dot(trunk[h], w, preferred_element_type=f32)
                if h == 0:
                    sides[j] = value
                else:
                    sides[j] += value
            elif a == 0:
                sides[j, s:] += jnp.dot(trunk[h, : pixels - s], w, preferred_element_type=f32)
            else:
                sides[j, : pixels - s] += jnp.dot(trunk[h, s:], w, preferred_element_type=f32)

    for copy in moving[0]:
        copy.wait()
    for j in range(3):
        convolve(j, 0)
    inputs_done = pass_inputs()
    for copy in moving[1]:
        copy.wait()
    from_y = share(0, (0, 1), True, 1, 0)
    from_z = share(1, (2, 3), True, 2, 2)

    def pass_on(i):
        from_y[i].wait_recv()
        share(2, (i,), False, 2, 4 + i)
        from_z[i].wait_recv()
        share(2, (i + 2,), False, 1, 6 + i)

    copies = []
    for j in range(3):
        q = RATE_COLS[j]
        convolve(j, 1)
        if j == 2:
            pass_on(0)
        for d in range(SPLIT):
            at = slice(d * quarter, (d + 1) * quarter)
            value = (
                sides[j, at, m : 2 * m]
                + move_cols(sides[j, at, :m], q)
                + move_cols(sides[j, at, 2 * m :], -q)
            )
            own[d, j] = value
            out[d, j] = value.astype(bf16)
        copies.append(
            [
                push(out.at[2 * h + 1 - k, j], near.at[h, j], near_sems.at[0, j, h], near_sems.at[1, j, h], (p, c ^ 1))
                for h in range(2)
            ]
        )
        if j > 0:
            copies[j - 1] = cross_chips(copies[j - 1], j - 1, own, near, cross, far_sems)
    copies[2] = cross_chips(copies[2], 2, own, near, cross, far_sems)
    for copy in head_copies:
        copy.wait()
    each = m // SPLIT
    for j in range(3):
        for d in range(SPLIT):
            heads[:, (j * SPLIT + d) * each : (j * SPLIT + d + 1) * each] = heads_all[d, :, j * each : (j + 1) * each]
    gain, bias = heads[32:33], heads[33:34]
    head = heads[:32]
    scaled = head * task_vector(
        add_up(square, PHASES)[:, :32], lax.dot_general(head, head, contract1, precision=highest)
    )
    target = jnp.concatenate([targets[2 * c], targets[2 * c + 1]], axis=1)
    mask = lax.dot_general(
        target[24:].astype(bf16), jnp.ones((8, m), bf16), contract0, preferred_element_type=f32
    )
    grad[...] = lax.dot_general(target, scaled, contract0, precision=highest) * jnp.concatenate([mask] * 3, axis=1)
    pass_on(1)
    count = total(mask)
    for j in range(3):
        copies[j].wait()
        value = own[2 * x + k, j] + near[x, j].astype(f32) + cross[1, j].astype(f32)
        at = slice(j * m, (j + 1) * m)
        hidden[:, at] = value
        first = total(value * mask)
        apart = value - first / jnp.maximum(count, 1.0)
        s_send[j : j + 1] = first
        s_send[3 + j : 4 + j] = total(apart * apart * mask)
    s_send[6:7] = count
    s_send[7:8] = jnp.zeros((1, m), f32)

    def merge(recv, parts):
        number = recv[0, 6:7]
        for i in range(1, parts):
            number = number + recv[i, 6:7]
        whole, spread = recv[0, 0:3], recv[0, 3:6]
        for i in range(1, parts):
            whole, spread = whole + recv[i, 0:3], spread + recv[i, 3:6]
        center = whole / jnp.maximum(number, 1.0)
        for i in range(parts):
            n = recv[i, 6:7]
            apart = recv[i, 0:3] / jnp.maximum(n, 1.0) - center
            spread = spread + n * apart * apart
        return whole, spread, number

    ch_exchange(s_send, s_ch, ch_sems.at[0])
    whole, spread, number = merge(s_ch, SPLIT)
    s_mid[0:3] = whole
    s_mid[3:6] = spread
    s_mid[6:7] = number
    s_mid[7:8] = jnp.zeros((1, m), f32)
    pix_exchange(s_mid, s_pix, pix_sems.at[0])
    share(0, (2,), True, 1, 8)
    share(1, (0,), True, 2, 9)
    whole, spread, number = merge(s_pix, PHASES)
    center, scale = whole / number, lax.rsqrt(spread / number + epsilon)
    for j in range(3):
        at = slice(j * m, (j + 1) * m)
        norm = (hidden[:, at] - center[j : j + 1]) * scale[j : j + 1]
        hidden[:, at] = norm
        value = norm * gain[:, at] + bias[:, at]
        branch[:, at] = (silu(value) * mask).astype(bf16)
        back = grad[:, at] * slope(value)
        grad[:, at] = back
        b_send[j : j + 1] = total(back)
        b_send[3 + j : 4 + j] = total(back * norm)
    b_send[6:8] = jnp.zeros((2, m), f32)
    to_ch = [push(b_send, b_ch.at[c], ch_sems.at[3, 0, i], ch_sems.at[3, 1, i], (p, c ^ i)) for i in (2, 3, 1)]
    b_ch[c] = b_send[...]
    high = target.astype(bf16)
    rest = target - high.astype(f32)
    middle = rest.astype(bf16)
    low = (rest - middle.astype(f32)).astype(bf16)
    p_send[...] = lax.dot_general(
        head.astype(bf16), branch[...], contract1, preferred_element_type=f32
    )
    value = jnp.dot(jnp.concatenate([high, middle, low]), branch[...], preferred_element_type=f32)
    h_send[...] = value[:32] + (value[32:64] + value[64:])
    background = [push(p_send, p_ch.at[c], ch_sems.at[1, 0, i], ch_sems.at[1, 1, i], (p, c ^ i)) for i in (2, 3, 1)] + [
        push(h_send.at[rows((c ^ i) * 8, 8)], h_ch.at[c], ch_sems.at[2, 0, i], ch_sems.at[2, 1, i], (p, c ^ i))
        for i in (2, 3, 1)
    ]
    p_ch[c] = p_send[...]
    h_ch[c] = h_send[rows(c * 8, 8)]
    for copy in to_ch:
        copy.wait()
    b_mid[...] = add_up(b_ch, SPLIT)
    sending = [
        push(b_mid, b_pix.at[p], pix_sems.at[1, 0, i], pix_sems.at[1, 1, i], (p ^ i, c)) for i in FAR_FIRST
    ]
    b_pix[p] = b_mid[...]
    for copy in background:
        copy.wait()
    h_mid[...] = add_up(h_ch, SPLIT)

    def block(to):
        return p_ch.at[to // 2, :, rows(lax.rem(to, 2) * 128, 128)]

    background = [
        push(block(p ^ i), predictions.at[p], pix_sems.at[2, 0, i], pix_sems.at[2, 1, i], (p ^ i, c)) for i in FAR_FIRST
    ] + [push(h_mid, h_pix.at[p], pix_sems.at[3, 0, i], pix_sems.at[3, 1, i], (p ^ i, c)) for i in FAR_FIRST]
    predictions[p] = block(p)[...]
    h_pix[p] = h_mid[...]
    for copy in sending:
        copy.wait()
    summed = add_up(b_pix, PHASES)
    sums[...] = summed
    for j in range(3):
        at = slice(j * m, (j + 1) * m)
        value = grad[:, at] - mask * (summed[j : j + 1] + hidden[:, at] * summed[3 + j : 4 + j]) / number
        full[mine, at] = (gain[:, at] * scale[j : j + 1] * value).astype(bf16)
    far = push(full.at[mine], full.at[mine], g_far.at[0], g_far.at[1], (p, c ^ 2))
    by = push(full.at[mine], full.at[mine], g_near.at[0], g_near.at[1], (p, c ^ 1))
    group = lax.rem(p, 4)
    pick = pick_rows(m, m, 0)
    for j in range(3):
        value = lax.dot_general(
            pick, full[mine, j * m : (j + 1) * m], contract1, preferred_element_type=f32
        ).astype(bf16)
        for g in range(4):
            picked[g, j * 64 : (j + 1) * 64] = value[g * 64 : (g + 1) * 64]
    sent_picks = [
        push(picked.at[group ^ i], picks.at[i - 1], pick_sems.at[0, i], pick_sems.at[1, i], (p ^ i, c)) for i in (3, 1, 2)
    ]
    for copy in background:
        copy.wait()
    own_rows = add_up(h_pix, PHASES)
    h_sum[...] = own_rows
    head_grad[rows(c * 8, 8)] = own_rows
    last = [
        push(h_sum, head_grad.at[rows(c * 8, 8)], ch_sems.at[4, 0, i], ch_sems.at[4, 1, i], (p, c ^ i))
        for i in (2, 3, 1)
    ]
    far.wait_recv()
    theirs = rows((c ^ 2) * quarter, quarter)
    hop = push(full.at[theirs], full.at[theirs], g_hop.at[0], g_hop.at[1], (p, c ^ 1))
    far.wait_send()
    by.wait()
    hop.wait()
    for copy in last:
        copy.wait()
    for copy in from_y + from_z:
        copy.wait_send()
    for copy in sharing[4:] + sent_picks:
        copy.wait()
    inputs_done()


def pick_rows(m, count, first):
    row = lax.broadcasted_iota(jnp.int32, (count, m), 0)
    col = lax.broadcasted_iota(jnp.int32, (count, m), 1)
    source = (4 * (row % 64 // 32) + row // 64 + first) * 32 + row % 32
    return jnp.where(col == source, 1.0, 0.0).astype(bf16)


def cross_chips(near_copies, j, own, near, cross, sems):
    p, c = lax.axis_index("pix"), lax.axis_index("ch")
    k, x = lax.rem(c, 2), c // 2
    for copy in near_copies:
        copy.wait()
    cross[0, j] = (own[2 * (1 - x) + k, j] + near[1 - x, j].astype(f32)).astype(bf16)
    return push(cross.at[0, j], cross.at[1, j], sems.at[0, j], sems.at[1, j], (p, c ^ 2))


def pyramid_scratch(pixels, n, m):
    quarter = pixels // SPLIT
    small = [
        pltpu.VMEM((8, m), f32),
        pltpu.VMEM((SPLIT, 8, m), f32),
        pltpu.VMEM((8, m), f32),
        pltpu.VMEM((PHASES, 8, m), f32),
    ]
    return [
        pltpu.VMEM((3, pixels, 3 * m), f32),
        pltpu.VMEM((SPLIT, 3, quarter, m), f32),
        pltpu.VMEM((SPLIT, 3, quarter, m), bf16),
        pltpu.VMEM((2, 3, quarter, m), bf16),
        pltpu.VMEM((2, 3, quarter, m), bf16),
        pltpu.VMEM((quarter, 3 * m), f32),
        pltpu.VMEM((quarter, 3 * m), f32),
        pltpu.VMEM((quarter, 3 * m), bf16),
        *small,
        *small,
        pltpu.VMEM((32, 3 * m), f32),
        pltpu.VMEM((SPLIT, 8, 3 * m), f32),
        pltpu.VMEM((8, 3 * m), f32),
        pltpu.VMEM((PHASES, 8, 3 * m), f32),
        pltpu.VMEM((8, 3 * m), f32),
        pltpu.VMEM((32, quarter), f32),
        pltpu.VMEM((SPLIT, 32, quarter), f32),
        dma(2, 3, 2),
        dma(2, 3),
        dma(5, 2, SPLIT),
        dma(4, 2, PHASES),
        dma(2),
        dma(2),
        dma(2),
        dma(2, 10),
        pltpu.VMEM((4, 192, quarter), bf16),
        dma(2, 4),
    ]


TILES = 4


def one_hot(rows_count, cols_count, source):
    row = lax.broadcasted_iota(jnp.int32, (rows_count, cols_count), 0)
    col = lax.broadcasted_iota(jnp.int32, (rows_count, cols_count), 1)
    return col == source(row)


def stage_one(feat, mask, weight, expand, gain, bias, *refs):
    (masked, reduce_rows, expand_cols, norm, padded, stat, valid) = refs[:7]
    (wide, hidden, own, out, near, cross, near_sems, far_sems, send, recv, stat_sems) = refs[7:18]
    (weight_sems, local_sems, halo_sems) = refs[18:]
    p, c = lax.axis_index("pix"), lax.axis_index("ch")
    pixels, local_in = feat.shape
    local_mid = weight.shape[1]
    tile = pixels // TILES

    def piece(i, to):
        return (
            (weight.at[rows(to * local_in, local_in), :], reduce_rows.at[:, rows(c * local_mid, local_mid)]),
            (expand.at[:, rows(to * local_in, local_in)], expand_cols.at[rows(c * local_mid, local_mid), :]),
        )[i]

    def to_ch(i):
        return [
            push(*piece(i, c ^ k), weight_sems.at[0, k, i], weight_sems.at[1, k, i], (p, c ^ k)) for k in (2, 3, 1)
        ] + [keep(*piece(i, c), local_sems.at[i])]

    reduce_copies = to_ch(0)

    present = mask[...].astype(f32)
    order = one_hot(128, 128, lambda i: 4 * (i % 32) + i // 32)
    ones = jnp.ones((128, 128), bf16)
    for r in range(8):
        column = jnp.dot(
            jnp.where(order, present[r : r + 1], 0.0).astype(bf16), ones, preferred_element_type=f32
        )
        for b in range(COL_CLASSES):
            block = ((r % ROW_CLASSES) * COL_CLASSES + b) * 128 + (r // ROW_CLASSES) * 32
            valid[block : block + 32] = column[b * 32 : (b + 1) * 32]
    for r in range(8):
        for g in range(local_in // 128):
            lanes = slice(g * 128, (g + 1) * 128)
            wide[g] = feat[r * 128 : (r + 1) * 128, lanes].astype(f32)
            for b in range(COL_CLASSES):
                block = ((r % ROW_CLASSES) * COL_CLASSES + b) * 128 + (r // ROW_CLASSES) * 32
                value = wide[g, pl.ds(b, 32, stride=COL_CLASSES), :] * valid[block : block + 32]
                masked[block : block + 32, lanes] = value.astype(bf16)

    for copy in reduce_copies:
        copy.wait()

    def part(t):
        return jnp.dot(masked[t * tile : (t + 1) * tile], reduce_rows[...], preferred_element_type=f32)

    result = sum_over_ch(part, tile, TILES, own, out, near, cross, near_sems, far_sems)
    for t in range(TILES):
        hidden[t * tile : (t + 1) * tile] = result(t)
    later = to_ch(1)
    center, scale, count = norm_stats(hidden, valid, pixels, send, recv, stat_sems)
    stat[0:1] = center
    stat[1:2] = scale
    stat[2:3] = count
    for i in range(PHASES):
        at = pl.ds(i * 128, 128)
        value = (hidden[at] - center) * scale
        norm[at] = value
        act = silu(value * gain[...] + bias[...]) * valid[at]
        padded[i, 1:5] = act.astype(bf16).reshape(4, 32, local_mid)
    up = lambda: pltpu.make_async_remote_copy(
        src_ref=padded.at[:, 4],
        dst_ref=padded.at[:, 0],
        send_sem=halo_sems.at[0, 0],
        recv_sem=halo_sems.at[1, 0],
        device_id=(p + 1, c),
        device_id_type=MESH,
    )
    down = lambda: pltpu.make_async_remote_copy(
        src_ref=padded.at[:, 1],
        dst_ref=padded.at[:, 5],
        send_sem=halo_sems.at[0, 1],
        recv_sem=halo_sems.at[1, 1],
        device_id=(p - 1, c),
        device_id_type=MESH,
    )
    first, last = p == 0, p == PHASES - 1

    @pl.when(jnp.logical_not(last))
    def _():
        up().start()

    @pl.when(jnp.logical_not(first))
    def _():
        down().start()

    @pl.when(last)
    def _():
        padded[:, 5] = jnp.zeros((PHASES, 32, local_mid), bf16)

    @pl.when(first)
    def _():
        padded[:, 0] = jnp.zeros((PHASES, 32, local_mid), bf16)

    @pl.when(jnp.logical_not(last))
    def _():
        up().wait_send()
        down().wait_recv()

    @pl.when(jnp.logical_not(first))
    def _():
        down().wait_send()
        up().wait_recv()

    return later


def prepare_heads(mask, head_weight, head_gain, head_bias, cotangent, *refs):
    (heads_all, targets_all, square_all, heads, targets, square, image, head_sems, pix_sems, local_sems) = refs
    p, c = lax.axis_index("pix"), lax.axis_index("ch")
    contract1 = (((1,), (1,)), ((), ()))
    present = mask[...].astype(f32)
    columns, m = head_weight.shape[1], head_weight.shape[2]
    heads[...] = jnp.zeros(heads.shape, f32)
    for j in range(3):
        heads[:columns, j * m : (j + 1) * m] = head_weight[j].astype(f32)
        heads[32:33, j * m : (j + 1) * m] = head_gain[j : j + 1]
        heads[33:34, j * m : (j + 1) * m] = head_bias[j : j + 1]

    image[...] = jnp.zeros(image.shape, f32)
    for r in range(8):
        at = slice(r * 128, (r + 1) * 128)
        image[:columns, at] = cotangent[:, at] * present[r : r + 1]
        image[31:32, at] = present[r : r + 1]
    square[...] = jnp.zeros(square.shape, f32)
    square[:, :32] = lax.dot_general(
        image[...], image[...], contract1, precision=highest, preferred_element_type=f32
    )
    place = jnp.where(
        one_hot(512, 512, lambda i: i % 4 * 128 + i // 128 * 32 + i % 128 // 4), 1.0, 0.0
    )
    for a in range(ROW_CLASSES):
        some = jnp.concatenate([image[:, (2 * r + a) * 128 : (2 * r + a + 1) * 128] for r in range(4)], axis=1)
        value = jnp.dot(some, place, precision=highest, preferred_element_type=f32)
        for b in range(COL_CLASSES):
            targets[a * COL_CLASSES + b] = value[:, b * 128 : (b + 1) * 128]
    copies = [push(heads, heads_all.at[c], head_sems.at[0, k], head_sems.at[1, k], (p, c ^ k)) for k in (2, 3, 1)]
    copies += [
        push(targets.at[p ^ k], targets_all.at[p], pix_sems.at[0, k, 0], pix_sems.at[1, k, 0], (p ^ k, c))
        for k in FAR_FIRST
    ] + [push(square, square_all.at[p], pix_sems.at[0, k, 1], pix_sems.at[1, k, 1], (p ^ k, c)) for k in FAR_FIRST]
    copies.append(keep(heads, heads_all.at[c], local_sems.at[0]))
    copies.append(keep(targets.at[p], targets_all.at[p], local_sems.at[1]))
    copies.append(keep(square, square_all.at[p], local_sems.at[2]))
    return copies


def stage_two(padded, valid, weight, gain, bias, *refs):
    (norm, full, taps, stat) = refs[:4]
    (hidden, own, out, near, cross, near_sems, far_sems, send, recv, stat_sems) = refs[4:14]
    (g_near, g_far, g_hop) = refs[14:]
    p, c = lax.axis_index("pix"), lax.axis_index("ch")
    pixels = valid.shape[0]
    local_mid = padded.shape[3]
    tile = pixels // TILES
    place = lax.broadcasted_iota(jnp.int32, (192, local_mid), 0) % 32
    for i in range(PHASES):
        beta = i % COL_CLASSES
        plain = padded[i].reshape(192, local_mid)
        wide = plain.astype(f32)
        if beta >= 2:
            moved_by = jnp.where(place == 0, 0.0, pltpu.roll(wide, 1, 0)).astype(bf16)
        else:
            moved_by = jnp.where(place == 31, 0.0, pltpu.roll(wide, 191, 0)).astype(bf16)
        for a in range(3):
            at = slice(a * 32, a * 32 + 128)
            for b, other, value in (
                (1, beta, plain),
                (0, (beta + 2) % 4, moved_by if beta >= 2 else plain),
                (2, (beta + 2) % 4, plain if beta >= 2 else moved_by),
            ):
                to = (i - beta + other) * 128
                col = (a * 3 + b) * local_mid
                taps[to : to + 128, col : col + local_mid] = value[at]

    def part(t):
        return jnp.dot(taps[t * tile : (t + 1) * tile], weight[...], preferred_element_type=f32)

    result = sum_over_ch(part, tile, TILES, own, out, near, cross, near_sems, far_sems)
    for t in range(TILES):
        hidden[t * tile : (t + 1) * tile] = result(t)
    center, scale, count = norm_stats(hidden, valid, pixels, send, recv, stat_sems)
    stat[0:1] = center
    stat[1:2] = scale
    stat[2:3] = count

    def ready(t):
        for i in range(tile // 128):
            at = pl.ds(t * tile + i * 128, 128)
            value = (hidden[at] - center) * scale
            norm[at] = value
            act = silu(value * gain[...] + bias[...]) * valid[at]
            full[at, rows(c * local_mid, local_mid)] = act.astype(bf16)

    gather_over_ch(full, local_mid, tile, TILES, g_near, g_far, g_hop, ready)


def stage_three(full, weight, masked, valid, gain, bias, *refs):
    (norm, classes, stat, inputs) = refs[:4]
    (hidden, trunk, send, recv, stat_sems, class_sems, own_sem, in_sems) = refs[4:]
    p, c = lax.axis_index("pix"), lax.axis_index("ch")
    pixels, n = masked.shape
    tile = pixels // TILES
    for t in range(TILES):
        at = pl.ds(t * tile, tile)
        hidden[at] = jnp.dot(full[at], weight[...], preferred_element_type=f32)
    far = push(masked, inputs.at[c], in_sems.at[0, 0], in_sems.at[1, 0], (p, c ^ 2))
    near = push(masked, inputs.at[c], in_sems.at[0, 1], in_sems.at[1, 1], (p, c ^ 1))
    mine = keep(masked, inputs.at[c], own_sem.at[2])
    center, scale, count = norm_stats(hidden, valid, pixels, send, recv, stat_sems)
    stat[0:1] = center
    stat[1:2] = scale
    stat[2:3] = count

    half = n // 2

    def finish(to, h):
        lanes = slice(h * half, (h + 1) * half)

        def step(i, carry):
            at = rows(to * 128 + i * 64, 64)
            value = (hidden[at, lanes] - center[:, lanes]) * scale[:, lanes]
            norm[at, lanes] = value
            pre = value * gain[:, lanes] + bias[:, lanes] + masked[at, lanes].astype(f32)
            v = valid[at]
            trunk[h, at] = (silu(pre) * jnp.concatenate([v] * (half // 128), axis=1)).astype(bf16)
            return carry

        loop(2, step, 0)

    copies = []
    for h in range(2):
        some = []
        for k in FAR_FIRST:
            to = p ^ k
            finish(to, h)
            some.append(
                push(
                    trunk.at[h, rows(to * 128, 128)],
                    classes.at[h, rows(p * 128, 128)],
                    class_sems.at[0, h, k],
                    class_sems.at[1, h, k],
                    (to, c),
                )
            )
        finish(p, h)
        some.append(keep(trunk.at[h, rows(p * 128, 128)], classes.at[h, rows(p * 128, 128)], own_sem.at[h]))
        copies.append(some)

    def pass_inputs():
        far.wait_recv()
        hop = push(inputs.at[c ^ 2], inputs.at[c ^ 2], in_sems.at[0, 2], in_sems.at[1, 2], (p, c ^ 1))

        def done():
            far.wait_send()
            near.wait()
            mine.wait()
            hop.wait()

        return done

    return copies, pass_inputs


def forward(
    feat, mask, weight, expand, gain1, bias1, head_weight, head_gain, head_bias, cotangent, dilated, gain2, bias2,
    gain3, bias3, pyramid_weight, *refs
):
    saved, stats, (inputs, grads, predictions, head_grad, branch_sums, others, picks) = refs[:10], refs[10:13], refs[13:20]
    padded, wide, w_sems, heads_full, save_sems = refs[20:25]
    masked, reduce_rows, expand_cols, norm1, valid, norm2, full2, taps, norm3, classes = refs[25:35]
    stat1, stat2, stat3 = stats
    own = refs[35:]
    saving = []

    def save(*which):
        for i in which:
            saving.append(keep(refs[25 + i], saved[i], save_sems.at[i]))

    one, two, three, heads = 14, 13, 8, 10
    barrier, expected = greet((1, 2, 3), FAR_FIRST)
    loads = load_pyramid(pyramid_weight, wide, w_sems)
    pl.semaphore_wait(barrier, expected)
    expand_copies = stage_one(
        feat, mask, weight, expand, gain1, bias1, masked, reduce_rows, expand_cols, norm1, padded, stat1, valid, *own[:one]
    )
    own = own[one:]
    save(0, 1, 3, 4)
    stage_two(padded, valid, dilated, gain2, bias2, norm2, full2, taps, stat2, *own[:two])
    own = own[two:]
    for copy in expand_copies:
        copy.wait()
    save(2, 5, 6, 7)
    moving, pass_inputs = stage_three(
        full2, expand_cols, masked, valid, gain3, bias3, norm3, classes, stat3, inputs, *own[:three]
    )
    own = own[three:]
    save(8)
    head_copies = prepare_heads(mask, head_weight, head_gain, head_bias, cotangent, *own[:heads])
    pyramid(
        classes, loads, wide, moving, pass_inputs, head_copies, heads_full, *own[:3],
        grads, predictions, head_grad, branch_sums, others, picks, *own[heads:],
    )
    save(9)
    for copy in saving:
        copy.wait()


def run_forward(
    cid, feat, mask, weight, expand, gain1, bias1, head_weight, head_gain, head_bias, cotangent, dilated, gain2, bias2,
    gain3, bias3, pyramid_weight
):
    pixels, n = feat.shape
    mid = weight.shape[1]
    all_mid = SPLIT * mid
    m = pyramid_weight.shape[4]
    quarter = pixels // SPLIT
    saved = [
        ((pixels, n), bf16),
        ((n, all_mid), bf16),
        ((all_mid, n), bf16),
        ((pixels, mid), f32),
        ((pixels, 128), f32),
        ((pixels, mid), f32),
        ((pixels, all_mid), bf16),
        ((pixels, 9 * mid), bf16),
        ((pixels, n), f32),
        ((2, pixels, n // 2), bf16),
    ]
    outs = [shape(*each) for each in saved] + [
        shape((8, mid), f32),
        shape((8, mid), f32),
        shape((8, n), f32),
        shape((SPLIT, pixels, n), bf16),
        shape((pixels, 3 * m), bf16),
        shape((PHASES, 32, 128), f32),
        shape((32, 3 * m), f32),
        shape((8, m), f32),
        shape((3, 2, pixels, n // 2), bf16),
        shape((3, 192, quarter), bf16),
    ]
    scratch = [
        pltpu.VMEM((PHASES, 6, 32, mid), bf16),
        pltpu.VMEM((9, n, 3 * m), bf16),
        dma(9, 3),
        pltpu.VMEM((40, 3 * m), f32),
        dma(10),
        *[pltpu.VMEM(*each) for each in saved],
        pltpu.VMEM((n // 128, 128, 128), f32),
        pltpu.VMEM((pixels, mid), f32),
        *sum_scratch(pixels, mid, TILES),
        *stat_scratch(mid),
        dma(2, SPLIT, 2),
        dma(2),
        dma(2, 2),
        pltpu.VMEM((pixels, mid), f32),
        *sum_scratch(pixels, mid, TILES),
        *stat_scratch(mid),
        *gather_scratch(TILES),
        pltpu.VMEM((pixels, n), f32),
        pltpu.VMEM((2, pixels, n // 2), bf16),
        *stat_scratch(n),
        dma(2, 2, PHASES),
        dma(4),
        dma(2, 3),
        pltpu.VMEM((SPLIT, 40, 256), f32),
        pltpu.VMEM((PHASES, 32, 128), f32),
        pltpu.VMEM((PHASES, 32, 128), f32),
        pltpu.VMEM((40, 256), f32),
        pltpu.VMEM((PHASES, 32, 128), f32),
        pltpu.VMEM((32, 128), f32),
        pltpu.VMEM((32, pixels), f32),
        dma(2, SPLIT),
        dma(2, PHASES, 2),
        dma(3),
        *pyramid_scratch(pixels, n, m),
    ]
    arrays = [
        feat, mask, weight, expand, gain1, bias1, head_weight, head_gain, head_bias, cotangent, dilated, gain2, bias2,
        gain3, bias3, pyramid_weight,
    ]
    return call("forward", cid, forward, arrays, outs, scratch, hbm_ins=(15,), hbm_outs=(*range(10), 13, 18))


PACE = (1, 10, 18, 21)


def packed_sums(values, send):
    i = 0
    for value in values:
        for g in range(value.shape[1] // 128):
            send[i : i + 1] = value[:, g * 128 : (g + 1) * 128]
            i += 1


def unpacked_sums(recv, rows_each, count):
    out, i = [], 0
    for _ in range(count):
        parts = []
        for _ in range(rows_each):
            value = recv[0, i : i + 1]
            for d in range(1, PHASES):
                value = value + recv[d, i : i + 1]
            parts.append(value)
            i += 1
        out.append(parts[0] if rows_each == 1 else jnp.concatenate(parts, axis=1))
    return out


def spread_lanes(v, n):
    return v if n == 128 else jnp.concatenate([v] * (n // 128), axis=1)


def backward(
    grads, trunk, others, weight, norm3, masked, valid, expand, gain3, bias3, norm2, gain2, bias2, full2, taps, dilated,
    norm1, gain1, bias1, reduce_rows, stats1, stats2, stats3, picks, inputs, *refs
):
    stored = (valid, norm3, masked, expand, norm2, full2, norm1, dilated, reduce_rows)
    valid, norm3, masked, expand, norm2, full2, norm1, dilated, reduce_rows, store_sems = refs[-10:]
    refs = refs[:-10]
    outs, scratch = refs[:6], refs[6:]
    (features_grad, aspp_parts, dilated_grad, expand_grad, reduce_grad, sums_out) = outs
    (wide, moved, acc, dsend, drecv, tpad, r_in, picked_in, turned, zsend, r_y) = scratch[:11]
    (gp3, g3, own, out, near, cross, hidden, gp2, g2, prod, edges, g1) = scratch[11:23]
    gp1, lanes = gp2, own
    (st3, st3r, st2, st2r, st1, st1r, e_part, e_mid, e_in, e_y, e_sum, d_part, d_in, d_y, d_sum, r_mid, r_sum) = scratch[23:40]
    (w_sems, d_sems, y_sems, z_sems, near_sems, far_sems, st_sems, gn, gf, gh, gn1, gf1, gh1, edge_sems, ch_sems, pix_sems, pair_sems, own_sems, tap_sems, in_sems, fill_sems, last_sems, slope1, d_near, d_far, mid_sems) = scratch[40:]
    p, c = lax.axis_index("pix"), lax.axis_index("ch")
    y, z = lax.rem(p, 2), p // 2
    lower = lax.rem(z, 2)
    pixels, n = norm3.shape
    m = weight.shape[4]
    mid = norm2.shape[1]
    tile = pixels // TILES
    contract0 = (((0,), (0,)), ((), ()))
    contract1 = (((1,), (1,)), ((), ()))
    count = stats1[2:3, :1]
    barrier, expected = greet((1, 2, 3), FAR_FIRST)
    loads = load_pyramid(weight, wide, w_sems)
    arrived = dict(
        zip(
            ("valid", "norm3", "masked", "expand", "norm2", "full2", "norm1", "dilated", "reduce"),
            [keep(a, b, store_sems.at[i]) for i, (a, b) in enumerate(
                zip(stored, (valid, norm3, masked, expand, norm2, full2, norm1, dilated, reduce_rows))
            )],
        )
    )

    group, upper = lax.rem(p, 4), p // 4
    quarter = picks.shape[2]
    pl.semaphore_wait(barrier, expected)
    mine = rows(c * quarter, quarter)
    sent_picks = [
        push(picks, picked_in.at[:, :, mine], y_sems.at[0, k], y_sems.at[1, k], (p, c ^ k)) for k in (2, 3, 1)
    ] + [keep(picks, picked_in.at[:, :, mine], y_sems.at[0, 0])]
    part = pixels // SPLIT
    filled = []
    for k in range(4):
        for h in range(2):
            cols = slice(h * m, (h + 1) * m)
            source = (others.at[k - 1] if k else trunk).at[h]
            here = {0: ((0, 4),), 1: ((0, 3),), 2: ((0, 1), (2, 4)), 3: ((0, 4),)}[k]
            for i, (first, end) in enumerate(here):
                at = pl.ds(first * part, (end - first) * part)
                filled.append(
                    keep(source.at[at], tpad.at[k, pl.ds(64 + first * part, (end - first) * part), cols], fill_sems.at[k, h, i])
                )
            if k in (1, 2):
                q = 3 if k == 1 else 1
                filled.append(
                    push(
                        trunk.at[h, pl.ds(q * part, part)],
                        tpad.at[k, pl.ds(64 + q * part, part), cols],
                        last_sems.at[0, k - 1, h],
                        last_sems.at[1, k - 1, h],
                        (p ^ k, c),
                    )
                )
    for i in range(4):
        tpad[i, :64] = jnp.zeros((64, n), bf16)
        tpad[i, 64 + pixels :] = jnp.zeros((64, n), bf16)

    for j in range(3):
        q = RATE_COLS[j]
        plain = grads[:, j * m : (j + 1) * m]
        value = plain.astype(f32)
        moved[j, :, :m] = move_cols(value, -q).astype(bf16)
        moved[j, :, m : 2 * m] = plain
        moved[j, :, 2 * m :] = move_cols(value, q).astype(bf16)
    back = []
    for h in range(2):
        half = slice(h * m, (h + 1) * m)
        for j in range(3):
            s = RATE_ROWS[j] * 32
            for a in (1, 0, 2):
                if h == 0:
                    for load in loads[3 * j + a]:
                        load.wait()
                w = wide[3 * j + a, half]
                if a == 1:
                    value = lax.dot_general(moved[j], w, contract1, preferred_element_type=f32)
                    if j == 0:
                        acc[...] = value
                    else:
                        acc[...] += value
                elif a == 0:
                    acc[: pixels - s] += lax.dot_general(moved[j, s:], w, contract1, preferred_element_type=f32)
                else:
                    acc[s:] += lax.dot_general(moved[j, : pixels - s], w, contract1, preferred_element_type=f32)
        dsend[h] = acc[...].astype(bf16)
        for k in FAR_FIRST:
            back.append(
                push(
                    dsend.at[h, rows((p ^ k) * 128, 128)],
                    drecv.at[h, rows(p * 128, 128)],
                    d_sems.at[0, h, k],
                    d_sems.at[1, h, k],
                    (p ^ k, c),
                )
            )
        back.append(keep(dsend.at[h, rows(p * 128, 128)], drecv.at[h, rows(p * 128, 128)], own_sems.at[h]))

    all_inputs = [
        keep(inputs.at[i // 2, pl.ds(i % 2 * n, n)], wide.at[i, :, :n], in_sems.at[i]) for i in range(8)
    ]
    cut = moved.shape[2]
    own_taps = [
        keep(taps.at[:, :cut], moved.at[0], tap_sems.at[0]),
        keep(taps.at[:, cut:], moved.at[1, :, : taps.shape[1] - cut], tap_sems.at[1]),
    ]

    place = lax.broadcasted_iota(jnp.int32, (64, pixels), 1) % 32

    def turn(i, part):
        at = slice(i * pixels, (i + 1) * pixels)
        for j in range(3):
            q = RATE_COLS[j]
            plain = part(j)
            value = plain.astype(f32)
            turned[j, :64, at] = jnp.where(place >= 32 - q, 0.0, pltpu.roll(value, pixels - q, 1)).astype(bf16)
            turned[j, 64:128, at] = plain
            turned[j, 128:, at] = jnp.where(place < q, 0.0, pltpu.roll(value, q, 1)).astype(bf16)

    pick = pick_rows(m, 64, group)
    turn(
        0,
        lambda j: lax.dot_general(
            pick, grads[:, j * m : (j + 1) * m], contract1, preferred_element_type=f32
        ).astype(bf16),
    )
    for copy in sent_picks:
        copy.wait()
    for k in (1, 2, 3):
        turn(k, lambda j: picked_in[k - 1, j * 64 : (j + 1) * 64])
    for copy in filled:
        copy.wait()
    for j in range(3):
        s = RATE_ROWS[j] * 32
        for a in range(3):
            if a == 1:
                low, high, start = 0, pixels, 64
            elif a == 0:
                low, high = s // 128 * 128, pixels
                start = 64 + low - s
            else:
                low, high, start = 0, -(-(pixels - s) // 128) * 128, 64 + s
            value = None
            for i in range(4):
                term = jnp.dot(
                    turned[j, :, i * pixels + low : i * pixels + high],
                    tpad[i, start : start + high - low],
                    preferred_element_type=f32,
                )
                value = term if value is None else value + term
            value = value.astype(bf16)
            for b in range(3):
                for to in range(2):
                    at = b * 64 + to * 32
                    zsend[to, (3 * j + a) * 3 + b] = value[at : at + 32]
    for name in ("valid", "norm3", "masked", "norm2", "norm1"):
        arrived[name].wait()

    def slopes(i, carry):
        at = rows(i * 32, 32)
        pre = norm3[at] * gain3[...] + bias3[...] + masked[at].astype(f32)
        gp3[at] = spread_lanes(valid[at], n) * slope(pre)
        gp2[at] = valid[at] * slope(norm2[at] * gain2[...] + bias2[...])
        slope1[at] = valid[at] * slope(norm1[at] * gain1[...] + bias1[...])
        return carry

    loop(pixels // 32, slopes, 0)
    zcopies = [keep(zsend.at[upper], aspp_parts.at[0], own_sems.at[2])]

    def send_parts(first, end):
        for i in range(first, end):
            zcopies.append(
                push(zsend.at[1 - upper, i], aspp_parts.at[1, i], z_sems.at[0, i], z_sems.at[1, i], (p ^ 4, c))
            )


    def over_z(blocks, sums, sems, own_sem):
        return [
            push(blocks.at[z ^ k], sums.at[z], sems.at[0, k], sems.at[1, k], (p ^ (2 * k), c)) for k in (3, 2, 1)
        ] + [keep(blocks.at[z], sums.at[z], own_sem)]

    def norm_back(grad, norm, sums, scale, gain, v):
        return gain * scale * (grad - v * (sums[0] + norm * sums[1]) / count)

    totals = []
    for h in range(2):
        for copy in back[h * PHASES : (h + 1) * PHASES]:
            copy.wait()
        if h == 1:
            send_parts(0, PACE[0])
        cols = slice(h * m, (h + 1) * m)

        def three(i, carry):
            at = rows(i * 64, 64)
            grad = drecv[h, at].astype(f32) * gp3[at, cols]
            gp3[at, cols] = grad
            return carry[0] + fold(grad), carry[1] + fold(grad * norm3[at, cols])

        zero = jnp.zeros((8, m), f32)
        bias, gain = loop(pixels // 64, three, (zero, zero))
        totals.append((total(bias), total(gain)))
    bias, gain = (jnp.concatenate([totals[0][i], totals[1][i]], axis=1) for i in range(2))
    packed_sums((bias, gain), st3)
    pix_exchange(st3, st3r, st_sems.at[0])
    send_parts(PACE[0], PACE[1])
    sums = unpacked_sums(st3r, n // 128, 2)
    sums_out[0:1] = sums[0]
    sums_out[1:2] = sums[1]

    arrived["expand"].wait()

    def part3(t):
        def step(i, carry):
            at = rows(t * tile + i * 32, 32)
            v = spread_lanes(valid[at], n)
            g3[at] = norm_back(gp3[at], norm3[at], sums, stats3[1:2], gain3[...], v).astype(bf16)
            return carry

        loop(tile // 32, step, 0)
        return lax.dot_general(g3[t * tile : (t + 1) * tile], expand[...], contract1, preferred_element_type=f32)

    result = sum_over_ch(part3, tile, TILES, own, out, near, cross, near_sems.at[0], far_sems.at[0])
    arrived["full2"].wait()
    value = lax.dot_general(full2[...], g3[...], contract0, preferred_element_type=f32).astype(bf16)
    for d in range(SPLIT):
        e_part[d] = value[d * mid : (d + 1) * mid]
    e_copies = [
        push(e_part.at[c ^ k], e_mid.at[c], ch_sems.at[0, 0, k], ch_sems.at[0, 1, k], (p, c ^ k)) for k in (2, 3, 1)
    ]
    e_copies.append(keep(e_part.at[c], e_mid.at[c], own_sems.at[3]))

    bias, gain = jnp.zeros((8, mid), f32), jnp.zeros((8, mid), f32)
    for t in range(TILES):
        hidden[t * tile : (t + 1) * tile] = result(t)

    def two(i, carry):
        at = rows(i * 128, 128)
        grad = hidden[at] * gp2[at]
        gp2[at] = grad
        return carry[0] + fold(grad), carry[1] + fold(grad * norm2[at])

    bias, gain = loop(pixels // 128, two, (bias, gain))
    packed_sums((total(bias), total(gain)), st2)
    pix_exchange(st2, st2r, st_sems.at[1])
    send_parts(PACE[1], PACE[2])
    for copy in e_copies:
        copy.wait()
    e_to_y = push(
        e_mid.at[:, :, rows((1 - y) * 256, 256)], e_in, pair_sems.at[0, 0], pair_sems.at[1, 0], (p ^ 1, c)
    )
    sums2 = unpacked_sums(st2r, 1, 2)
    sums_out[2:3, :mid] = sums2[0]
    sums_out[3:4, :mid] = sums2[1]

    def ready2(t):
        def step(i, carry):
            at = rows(t * tile + i * 128, 128)
            value = norm_back(gp2[at], norm2[at], sums2, stats2[1:2], gain2[...], valid[at])
            g2[at, rows(c * mid, mid)] = value.astype(bf16)
            return carry

        loop(tile // 128, step, 0)

    gather_over_ch(g2, mid, tile, TILES, gn, gf, gh, ready2)

    e_to_y.wait()
    for d in range(4):
        e_y[d] = (e_mid[d, :, rows(y * 256, 256)].astype(f32) + e_in[d].astype(f32)).astype(bf16)
    pix_copies = over_z(e_y, e_sum, pix_sems.at[0], own_sems.at[5])

    place = lax.broadcasted_iota(jnp.int32, (128, mid), 0) % 32

    def across(i, a):
        beta = i % COL_CLASSES
        two_on = (beta + 2) % 4 * 128
        here = slice(beta * 128, (beta + 1) * 128)
        there = slice(two_on, two_on + 128)
        lane = lambda b: slice((3 * a + b) * mid, (3 * a + b + 1) * mid)
        left, right = prod[there, lane(0)], prod[there, lane(2)]
        if beta >= 2:
            left = jnp.where(place == 31, 0.0, pltpu.roll(left, 127, 0))
        else:
            right = jnp.where(place == 0, 0.0, pltpu.roll(right, 1, 0))
        return prod[here, lane(1)] + left + right

    arrived["dilated"].wait()
    for i in range(PHASES):
        at = slice(i * 128, (i + 1) * 128)
        if i % COL_CLASSES == 0:
            prod[...] = lax.dot_general(
                g2[i * 128 : (i + COL_CLASSES) * 128], dilated[...], contract1, preferred_element_type=f32
            )
        up, same, down = across(i, 0), across(i, 1), across(i, 2)
        zero = jnp.zeros((32, mid), f32)
        hidden[at] = same + jnp.concatenate([up[32:], zero]) + jnp.concatenate([zero, down[:96]])
        edges[0, i] = up[:32].astype(bf16)
        edges[1, i] = down[96:].astype(bf16)
    first, last = p == 0, p == PHASES - 1
    to_next = lambda: pltpu.make_async_remote_copy(
        src_ref=edges.at[1], dst_ref=edges.at[2], send_sem=edge_sems.at[0, 0], recv_sem=edge_sems.at[1, 0],
        device_id=(p + 1, c), device_id_type=MESH,
    )
    to_last = lambda: pltpu.make_async_remote_copy(
        src_ref=edges.at[0], dst_ref=edges.at[3], send_sem=edge_sems.at[0, 1], recv_sem=edge_sems.at[1, 1],
        device_id=(p - 1, c), device_id_type=MESH,
    )

    @pl.when(jnp.logical_not(last))
    def _():
        to_next().start()

    @pl.when(jnp.logical_not(first))
    def _():
        to_last().start()

    @pl.when(first)
    def _():
        edges[2] = jnp.zeros((PHASES, 32, mid), bf16)

    @pl.when(last)
    def _():
        edges[3] = jnp.zeros((PHASES, 32, mid), bf16)

    for copy in own_taps:
        copy.wait()
    value = jnp.concatenate(
        [
            lax.dot_general(g2[...], moved[0], contract0, preferred_element_type=f32).astype(bf16),
            lax.dot_general(
                g2[...], moved[1, :, : taps.shape[1] - cut], contract0, preferred_element_type=f32
            ).astype(bf16),
        ],
        axis=1,
    )
    out_rows = SPLIT * mid // PHASES
    for d in range(PHASES):
        d_part[d % 2, d // 2] = value[d * out_rows : (d + 1) * out_rows]
    d_to_y = push(d_part.at[1 - y], d_in, pair_sems.at[0, 1], pair_sems.at[1, 1], (p ^ 1, c))

    @pl.when(jnp.logical_not(last))
    def _():
        to_next().wait_send()
        to_last().wait_recv()

    @pl.when(jnp.logical_not(first))
    def _():
        to_last().wait_send()
        to_next().wait_recv()

    send_parts(PACE[2], PACE[3])

    bias, gain = jnp.zeros((8, mid), f32), jnp.zeros((8, mid), f32)
    for i in range(PHASES):
        at = slice(i * 128, (i + 1) * 128)
        zero = jnp.zeros((64, mid), f32)
        edge = jnp.concatenate([edges[2, i].astype(f32), zero, edges[3, i].astype(f32)])
        grad = (hidden[at] + edge) * slope1[at]
        gp1[at] = grad
        bias, gain = bias + fold(grad), gain + fold(grad * norm1[at])
    packed_sums((total(bias), total(gain)), st1)
    pix_exchange(st1, st1r, st_sems.at[2])
    send_parts(PACE[3], 27)
    sums1 = unpacked_sums(st1r, 1, 2)
    sums_out[4:5, :mid] = sums1[0]
    sums_out[5:6, :mid] = sums1[1]

    def ready1(t):
        def step(i, carry):
            at = rows(t * tile + i * 128, 128)
            value = norm_back(gp1[at], norm1[at], sums1, stats1[1:2], gain1[...], valid[at])
            g1[at, rows(c * mid, mid)] = value.astype(bf16)
            return carry

        loop(tile // 128, step, 0)

    late = []

    def between():
        for copy in all_inputs:
            copy.wait()
        own_g1 = g1[:, rows(c * mid, mid)]
        for i in range(SPLIT):
            value = lax.dot_general(wide[2 * i, :, :n], own_g1[:n], contract0, preferred_element_type=f32)
            value = value + lax.dot_general(wide[2 * i + 1, :, :n], own_g1[n:], contract0, preferred_element_type=f32)
            r_mid[i] = value.astype(bf16).reshape(2, 256, mid)
        late.append(push(r_mid.at[:, 1 - y], r_in, pair_sems.at[0, 2], pair_sems.at[1, 2], (p ^ 1, c)))
        d_to_y.wait()
        for d in range(4):
            d_y[d // 2, d % 2] = (d_part[y, d].astype(f32) + d_in[d].astype(f32)).astype(bf16)
        late.append(push(d_y.at[:, 1 - lower], d_near, mid_sems.at[0, 0], mid_sems.at[1, 0], (p ^ 2, c)))

    gather_over_ch(g1, mid, tile, TILES, gn1, gf1, gh1, ready1, between)
    late[0].wait()
    for d in range(4):
        r_y[d] = (r_mid[d, y].astype(f32) + r_in[d].astype(f32)).astype(bf16)
    pix_copies += over_z(r_y, r_sum, pix_sems.at[2], own_sems.at[7])

    arrived["reduce"].wait()
    for i in range(PHASES):
        at = slice(i * 128, (i + 1) * 128)
        value = lax.dot_general(g1[at], reduce_rows[...], contract1, preferred_element_type=f32) + gp3[at]
        value = value * spread_lanes(valid[at], n)
        for g in range(n // 128):
            for r in range(4):
                start = (2 * r + i // COL_CLASSES) * 128 + i % COL_CLASSES
                lanes[g, pl.ds(start, 32, stride=COL_CLASSES), :] = value[r * 32 : (r + 1) * 32, g * 128 : (g + 1) * 128]
    for g in range(n // 128):
        features_grad[:, g * 128 : (g + 1) * 128] = lanes[g].astype(bf16)
    late[1].wait()
    for d in range(2):
        d_sum[d] = (d_y[d, lower].astype(f32) + d_near[d].astype(f32)).astype(bf16)
    d_last = push(d_sum.at[1 - upper], d_far, mid_sems.at[0, 1], mid_sems.at[1, 1], (p ^ 4, c))
    for copy in pix_copies:
        copy.wait()

    def gathered(parts):
        value = parts[0].astype(f32)
        for d in range(1, parts.shape[0]):
            value = value + parts[d].astype(f32)
        return value

    expand_grad[...] = gathered(e_sum)
    reduce_grad[...] = gathered(r_sum)
    d_last.wait()
    value = d_sum[upper].astype(f32) + d_far[...].astype(f32)
    for i in range(9):
        dilated_grad[i] = value[:, i * mid : (i + 1) * mid]
    for copy in zcopies:
        copy.wait()


def run_backward(cid, arrays):
    (grads, trunk, others, weight, norm3, masked, valid, expand, gain3, bias3, norm2, gain2, bias2, full2, taps, dilated,
     norm1, gain1, bias1, reduce_rows, stats1, stats2, stats3, picks, inputs) = arrays
    pixels, n = norm3.shape
    m = weight.shape[4]
    mid = norm2.shape[1]
    all_mid = SPLIT * mid
    outs = [
        shape((pixels, n), bf16),
        shape((2, 27, 32, n), bf16),
        shape((9, all_mid // PHASES, mid), f32),
        shape((mid, 256), f32),
        shape((256, mid), f32),
        shape((8, n), f32),
    ]
    sums = sum_scratch(pixels, mid, TILES)
    scratch = [
        pltpu.VMEM((9, n, 3 * m), bf16),
        pltpu.VMEM((3, pixels, 3 * m), bf16),
        pltpu.VMEM((pixels, m), f32),
        pltpu.VMEM((2, pixels, m), bf16),
        pltpu.VMEM((2, pixels, m), bf16),
        pltpu.VMEM((4, pixels + 128, n), bf16),
        pltpu.VMEM((4, 256, mid), bf16),
        pltpu.VMEM((3, 192, pixels), bf16),
        pltpu.VMEM((3, 192, 4 * pixels), bf16),
        pltpu.VMEM((2, 27, 32, n), bf16),
        pltpu.VMEM((4, 256, mid), bf16),
        pltpu.VMEM((pixels, n), f32),
        pltpu.VMEM((pixels, n), bf16),
        *sums[:4],
        pltpu.VMEM((pixels, mid), f32),
        pltpu.VMEM((pixels, mid), f32),
        pltpu.VMEM((pixels, all_mid), bf16),
        pltpu.VMEM((pixels // ROW_CLASSES, 9 * mid), f32),
        pltpu.VMEM((4, PHASES, 32, mid), bf16),
        pltpu.VMEM((pixels, all_mid), bf16),
        pltpu.VMEM((8, 128), f32),
        pltpu.VMEM((PHASES, 8, 128), f32),
        pltpu.VMEM((8, 128), f32),
        pltpu.VMEM((PHASES, 8, 128), f32),
        pltpu.VMEM((8, 128), f32),
        pltpu.VMEM((PHASES, 8, 128), f32),
        pltpu.VMEM((SPLIT, mid, n), bf16),
        pltpu.VMEM((SPLIT, mid, n), bf16),
        pltpu.VMEM((4, mid, 256), bf16),
        pltpu.VMEM((4, mid, 256), bf16),
        pltpu.VMEM((4, mid, 256), bf16),
        pltpu.VMEM((2, 4, all_mid // PHASES, 9 * mid), bf16),
        pltpu.VMEM((4, all_mid // PHASES, 9 * mid), bf16),
        pltpu.VMEM((2, 2, all_mid // PHASES, 9 * mid), bf16),
        pltpu.VMEM((2, all_mid // PHASES, 9 * mid), bf16),
        pltpu.VMEM((4, 2, 256, mid), bf16),
        pltpu.VMEM((4, 256, mid), bf16),
        dma(9, 3),
        dma(2, 2, PHASES),
        dma(3, 4),
        dma(2, 27),
        dma(1, 2, TILES, 2),
        dma(1, 2, TILES),
        dma(3, 2, PHASES),
        *gather_scratch(TILES),
        *gather_scratch(TILES),
        dma(2, 2),
        dma(2, 2, SPLIT),
        dma(3, 2, PHASES),
        dma(2, 3),
        dma(8),
        dma(2),
        dma(8),
        dma(4, 2, 2),
        dma(2, 2, 2),
        pltpu.VMEM((pixels, mid), f32),
        pltpu.VMEM((2, all_mid // PHASES, 9 * mid), bf16),
        pltpu.VMEM((all_mid // PHASES, 9 * mid), bf16),
        dma(2, 2),
        pltpu.VMEM((pixels, 128), f32),
        pltpu.VMEM((pixels, n), f32),
        pltpu.VMEM((pixels, n), bf16),
        pltpu.VMEM((all_mid, n), bf16),
        pltpu.VMEM((pixels, mid), f32),
        pltpu.VMEM((pixels, all_mid), bf16),
        pltpu.VMEM((pixels, mid), f32),
        pltpu.VMEM((9 * mid, all_mid), bf16),
        pltpu.VMEM((n, all_mid), bf16),
        dma(9),
    ]
    vmem = pl.BlockSpec(memory_space=pltpu.VMEM)
    specs = [vmem] * len(arrays)
    for i in (1, 2, 3, 4, 5, 6, 7, 10, 13, 14, 15, 16, 19, 24):
        specs[i] = pl.BlockSpec(memory_space=pl.ANY)
    return pl.pallas_call(
        backward,
        out_shape=outs,
        in_specs=specs,
        out_specs=[vmem, pl.BlockSpec(memory_space=pl.ANY)] + [vmem] * (len(outs) - 2),
        scratch_shapes=scratch,
        compiler_params=pltpu.CompilerParams(
            collective_id=cid, has_side_effects=True, vmem_limit_bytes=VMEM_BYTES
        ),
        name="backward",
    )(*arrays)


def fast_device(
    features,
    pixel_mask,
    reduce_weight,
    reduce_gain,
    reduce_bias,
    dilated_weight,
    dilated_gain,
    dilated_bias,
    expand_weight,
    expand_gain,
    expand_bias,
    aspp_weight,
    aspp_gain,
    aspp_bias,
    task_weight,
    cotangent,
):
    rows_here, width, local_in = features.shape
    pixels = rows_here * width
    local_mid = reduce_weight.shape[1]
    full_mid = dilated_weight.shape[3]
    branch_width = aspp_weight.shape[4]
    own_branch = task_weight.shape[1]
    outs_count = task_weight.shape[2]
    me_ch = lax.axis_index("ch")
    line = lambda v: v.reshape(1, -1)
    dilated_rows = dilated_weight.reshape(9 * local_mid, full_mid)
    (
        masked, reduce_rows, expand_cols, norm_one, valid, norm_two, act_two_full, taps_one, norm_three, trunk_class,
        stat_one, stat_two, stat_three, inputs_all, grad_full, predictions, head_grad, branch_sums, trunk_others, picks,
    ) = run_forward(
        1,
        features.reshape(pixels, local_in),
        pixel_mask,
        reduce_weight,
        expand_weight,
        line(reduce_gain),
        line(reduce_bias),
        task_weight.transpose(0, 2, 1),
        aspp_gain,
        aspp_bias,
        cotangent.transpose(2, 0, 1).reshape(outs_count, pixels),
        dilated_rows,
        line(dilated_gain),
        line(dilated_bias),
        line(expand_gain),
        line(expand_bias),
        aspp_weight,
    )
    features_grad, aspp_parts, dilated_sum, expand_weight_grad, reduce_weight_grad, norm_sums = run_backward(
        2,
        [
            grad_full, trunk_class, trunk_others, aspp_weight, norm_three, masked, valid, expand_cols,
            line(expand_gain), line(expand_bias), norm_two, line(dilated_gain), line(dilated_bias), act_two_full,
            taps_one, dilated_rows, norm_one, line(reduce_gain), line(reduce_bias), reduce_rows, stat_one, stat_two,
            stat_three, picks, inputs_all,
        ],
    )
    features_grad = features_grad.reshape(rows_here, width, local_in)
    aspp_weight_grad = (aspp_parts[0].astype(f32) + aspp_parts[1].astype(f32)).reshape(
        3, 3, 3, -1, local_in
    ).transpose(0, 1, 2, 4, 3)
    dilated_weight_grad = dilated_sum.reshape(3, 3, -1, local_mid).transpose(0, 1, 3, 2)
    expand_bias_grad, expand_gain_grad = norm_sums[0], norm_sums[1]
    dilated_bias_grad, dilated_gain_grad = norm_sums[2, :local_mid], norm_sums[3, :local_mid]
    reduce_bias_grad, reduce_gain_grad = norm_sums[4, :local_mid], norm_sums[5, :local_mid]
    predictions = from_classes(predictions.transpose(0, 2, 1), rows_here, width)[:, :, :outs_count]
    head_grad = head_grad.reshape(32, 3, 4, own_branch).transpose(2, 1, 3, 0)
    task_weight_grad = lax.dynamic_index_in_dim(head_grad, me_ch, keepdims=False)[:, :, :outs_count]
    own_sums = lax.dynamic_slice_in_dim(
        branch_sums[:6].reshape(2, 3, branch_width), me_ch * own_branch, own_branch, axis=2
    )
    aspp_bias_grad, aspp_gain_grad = own_sums[0], own_sums[1]

    return (
        predictions,
        features_grad,
        reduce_weight_grad,
        reduce_gain_grad,
        reduce_bias_grad,
        dilated_weight_grad,
        dilated_gain_grad,
        dilated_bias_grad,
        expand_weight_grad,
        expand_gain_grad,
        expand_bias_grad,
        aspp_weight_grad,
        aspp_gain_grad,
        aspp_bias_grad,
        task_weight_grad,
    )


def solution(mesh):
    placed = (
        P("pix", None, "ch"),
        P("pix", None),
        P(None, "ch"),
        P("ch"),
        P("ch"),
        P(None, None, "ch", None),
        P("ch"),
        P("ch"),
        P("ch", None),
        P("ch"),
        P("ch"),
        P(None, None, None, "ch", None),
        P(None, "ch"),
        P(None, "ch"),
        P(None, "ch", None),
        P("pix", None, None),
    )
    return jax.shard_map(
        fast_device if (mesh.shape["pix"], mesh.shape["ch"]) == (PHASES, 4) else on_device,
        mesh=mesh,
        in_specs=placed,
        out_specs=(
            P("pix", None, None),
            P("pix", None, "ch"),
            P("pix", "ch"),
            P("ch"),
            P("ch"),
            P(None, None, "ch", "pix"),
            P("ch"),
            P("ch"),
            P("ch", "pix"),
            P("ch"),
            P("ch"),
            P(None, None, None, "ch", "pix"),
            P(None, "ch"),
            P(None, "ch"),
            P(None, "ch", None),
        ),
        check_vma=False,
    )
```

```python
import jax
import jax.numpy as jnp
from jax import lax
from jax.experimental import pallas as pl
from jax.experimental.pallas import tpu as pltpu
from jax.sharding import PartitionSpec as P

CLS = 19


epsilon = 1e-05
highest = lax.Precision.HIGHEST
aspp_rates = (12, 24, 36)
inner_rate = 2


def from_behind(value, axis, steps):
    count = lax.axis_size(axis)
    first, last = (max(0, -steps), min(count, count - steps))
    return lax.ppermute(value, axis, [(source, source + steps) for source in range(first, last)])


def with_halo(shard, sides, width):
    for axis, dim in sides:
        devices, length = (lax.axis_size(axis), shard.shape[dim])
        up = [(i, (i + 1) % devices) for i in range(devices - 1)]
        down = [(j, i) for i, j in up]
        last = lax.slice_in_dim(shard, length - width, length, axis=dim)
        first = lax.slice_in_dim(shard, 0, width, axis=dim)
        before = lax.ppermute(last, axis, up)
        after = lax.ppermute(first, axis, down)
        shard = jnp.concatenate([before, shard, after], axis=dim)
    return shard


def silu_slope(value):
    sigma = jax.nn.sigmoid(value)
    return sigma * (1.0 + value * (1.0 - sigma))


def shift_cols(value, offset):
    if offset == 0:
        return value
    margin = abs(offset)
    widths = [(0, 0)] * value.ndim
    widths[1] = (margin, margin)
    padded = jnp.pad(value, widths)
    return lax.slice_in_dim(padded, margin + offset, margin + offset + value.shape[1], axis=1)


def moved(piece, distance):
    return from_behind(piece, "pix", -distance)


def shift_rows(value, offset):
    if offset == 0:
        return value
    steps_over, inner = divmod(offset, value.shape[0])
    first = moved(value, steps_over)[inner:]
    if inner == 0:
        return first
    second = moved(value, steps_over + 1)[:inner]
    return jnp.concatenate([first, second], axis=0)


def halo_rows(value):
    return with_halo(value, (("pix", 0),), inner_rate)


def gather_channels(value):
    return lax.all_gather(value, "ch", axis=1, tiled=True)


def sum_channels(value):
    return lax.psum_scatter(
        value.astype(jnp.bfloat16), "ch", scatter_dimension=1, tiled=True
    ).astype(jnp.float32)


def normalized(hidden, valid, axes):
    total, count = lax.psum(
        (jnp.sum(hidden * valid, axis=axes, keepdims=True), jnp.sum(valid)), "pix"
    )
    center = total / count
    spread_sum = lax.psum(jnp.sum(valid * (hidden - center) ** 2, axis=axes, keepdims=True), "pix")
    variance = spread_sum / count
    scale = lax.rsqrt(variance + epsilon)
    return ((hidden - center) * scale, scale, count)


def norm_grad(grad_out, centered, scale, gain, count, valid, axes):
    sum_out, sum_cross = lax.psum(
        (
            jnp.sum(grad_out, axis=axes, keepdims=True),
            jnp.sum(grad_out * centered, axis=axes, keepdims=True),
        ),
        "pix",
    )
    grad_in = gain * scale * (grad_out - valid * (sum_out + centered * sum_cross) / count)
    return (grad_in, sum_cross, sum_out)


def task_scales(gram):
    norms = jnp.sqrt(jnp.diagonal(gram) + 1e-06)
    proj = gram / norms[None, :]
    vector = proj[0, 0] - proj[0, 1:]
    matrix = proj[0, 0] - proj[0, 1:][None, :] - proj[1:, 0][:, None] + proj[1:, 1:]
    determinant = matrix[0, 0] * matrix[1, 1] - matrix[0, 1] * matrix[1, 0]
    second = (vector[0] * matrix[1, 1] - vector[1] * matrix[1, 0]) / determinant
    third = (vector[1] * matrix[0, 0] - vector[0] * matrix[0, 1]) / determinant
    return jnp.stack([1.0 - second - third, second, third])


def on_device(
    features,
    pixel_mask,
    reduce_weight,
    reduce_gain,
    reduce_bias,
    dilated_weight,
    dilated_gain,
    dilated_bias,
    expand_weight,
    expand_gain,
    expand_bias,
    aspp_weight,
    aspp_gain,
    aspp_bias,
    task_weight,
    cotangent,
):
    rows_here, width, local_in = features.shape
    pixels = rows_here * width
    local_mid = reduce_weight.shape[1]
    full_mid = dilated_weight.shape[3]
    branch_width = aspp_weight.shape[4]
    outs_count = task_weight.shape[2]
    valid = pixel_mask.astype(jnp.float32).reshape(pixels, 1)
    valid_branch = valid[None]
    masked = features.reshape(pixels, local_in) * valid.astype(jnp.bfloat16)
    inputs_full = gather_channels(masked)
    hidden_one = jnp.dot(inputs_full, reduce_weight, preferred_element_type=jnp.float32)
    norm_one, scale_one, count = normalized(hidden_one, valid, (0,))
    pre_one = norm_one * reduce_gain + reduce_bias
    act_one = (jax.nn.silu(pre_one) * valid).astype(jnp.bfloat16)
    padded_one = halo_rows(act_one.reshape(rows_here, width, local_mid))
    partial_value = jnp.zeros((pixels, full_mid), jnp.float32)
    for a in range(3):
        for b in range(3):
            shifted = shift_cols(padded_one[2 * a : 2 * a + rows_here], (b - 1) * inner_rate)
            partial_value = partial_value + jnp.dot(
                shifted.reshape(pixels, local_mid),
                dilated_weight[a, b],
                preferred_element_type=jnp.float32,
            )
    hidden_two = sum_channels(partial_value)
    norm_two, scale_two, _ = normalized(hidden_two, valid, (0,))
    pre_two = norm_two * dilated_gain + dilated_bias
    act_two = (jax.nn.silu(pre_two) * valid).astype(jnp.bfloat16)
    hidden_three = sum_channels(jnp.dot(act_two, expand_weight, preferred_element_type=jnp.float32))
    norm_three, scale_three, _ = normalized(hidden_three, valid, (0,))
    pre_three = norm_three * expand_gain + expand_bias + masked.astype(jnp.float32)
    trunk_out = (
        (jax.nn.silu(pre_three) * valid).astype(jnp.bfloat16).reshape(rows_here, width, local_in)
    )
    kept_rows = []
    partials = []
    for j in range(3):
        rate = aspp_rates[j]
        running = jnp.zeros((pixels, branch_width), jnp.float32)
        shifted_rows = []
        for a in range(3):
            row_shift = shift_rows(trunk_out, (a - 1) * rate)
            shifted_rows.append(row_shift)
            for b in range(3):
                shifted = shift_cols(row_shift, (b - 1) * rate)
                running = running + jnp.dot(
                    shifted.reshape(pixels, local_in),
                    aspp_weight[j, a, b],
                    preferred_element_type=jnp.float32,
                )
        kept_rows.append(shifted_rows)
        partials.append(running)
    branch_sum = sum_channels(jnp.stack(partials).reshape(3 * pixels, branch_width)).reshape(
        3, pixels, -1
    )
    branch_gain = aspp_gain[:, None, :]
    norm_branch, scale_branch, _ = normalized(branch_sum, valid_branch, (1,))
    pre_branch = norm_branch * branch_gain + aspp_bias[:, None, :]
    branch_out = (jax.nn.silu(pre_branch) * valid_branch).astype(jnp.bfloat16)
    predictions = lax.psum(
        jnp.einsum(
            "jpc,jco->po", branch_out, task_weight, preferred_element_type=jnp.float32
        ).astype(jnp.bfloat16),
        "ch",
    ).astype(jnp.float32)
    columns = jnp.arange(outs_count)
    task_of = (columns >= CLS).astype(jnp.int32) + (columns >= CLS + 1).astype(jnp.int32)
    select = (task_of[:, None] == jnp.arange(3)[None, :]).astype(jnp.float32)
    target = cotangent.reshape(pixels, outs_count) * valid
    task_float = task_weight.astype(jnp.float32)
    task_grads = jnp.einsum("po,ot,jco->tjpc", target, select, task_float, precision=highest)
    gram = lax.psum(
        jnp.einsum("tjpc,sjpc->ts", task_grads, task_grads, precision=highest), ("pix", "ch")
    )
    scales = task_scales(gram)
    branch_grad = jnp.einsum("t,tjpc->jpc", scales, task_grads, precision=highest)
    task_weight_grad = lax.psum(
        jnp.einsum("jpc,po->jco", branch_out.astype(jnp.float32), target, precision=highest), "pix"
    )
    grad_pre_branch = branch_grad * valid_branch * silu_slope(pre_branch)
    grad_branch, aspp_gain_grad, aspp_bias_grad = norm_grad(
        grad_pre_branch, norm_branch, scale_branch, branch_gain, count, valid_branch, (1,)
    )
    grad_full = gather_channels(grad_branch.astype(jnp.bfloat16).reshape(3 * pixels, -1)).reshape(
        3, rows_here, width, -1
    )
    grad_trunk = jnp.zeros((pixels, local_in), jnp.float32)
    aspp_list = []
    for j in range(3):
        rate = aspp_rates[j]
        grad_flat = grad_full[j].reshape(pixels, -1)
        per_row = []
        for a in range(3):
            back_rows = shift_rows(grad_full[j], -(a - 1) * rate)
            per_col = []
            for b in range(3):
                shifted = shift_cols(back_rows, -(b - 1) * rate)
                grad_trunk = grad_trunk + jnp.einsum(
                    "pa,ca->pc",
                    shifted.reshape(pixels, -1),
                    aspp_weight[j, a, b],
                    preferred_element_type=jnp.float32,
                )
                forward_tap = shift_cols(kept_rows[j][a], (b - 1) * rate).reshape(pixels, local_in)
                per_col.append(
                    jnp.einsum(
                        "pc,pa->ca", forward_tap, grad_flat, preferred_element_type=jnp.float32
                    )
                )
            per_row.append(jnp.stack(per_col))
        aspp_list.append(jnp.stack(per_row))
    aspp_weight_local = jnp.stack(aspp_list)
    grad_pre_three = grad_trunk * valid * silu_slope(pre_three)
    grad_three, expand_gain_grad, expand_bias_grad = norm_grad(
        grad_pre_three, norm_three, scale_three, expand_gain, count, valid, (0,)
    )
    grad_three_full = gather_channels(grad_three.astype(jnp.bfloat16))
    grad_act_two = jnp.einsum(
        "pc,dc->pd", grad_three_full, expand_weight, preferred_element_type=jnp.float32
    )
    expand_weight_local = jnp.einsum(
        "pd,pc->dc", act_two, grad_three_full, preferred_element_type=jnp.float32
    )
    grad_pre_two = grad_act_two * valid * silu_slope(pre_two)
    grad_two, dilated_gain_grad, dilated_bias_grad = norm_grad(
        grad_pre_two, norm_two, scale_two, dilated_gain, count, valid, (0,)
    )
    grad_two_full = gather_channels(grad_two.astype(jnp.bfloat16))
    padded_grad = halo_rows(grad_two_full.reshape(rows_here, width, full_mid))
    grad_act_one = jnp.zeros((pixels, local_mid), jnp.float32)
    dilated_rows = []
    for a in range(3):
        dilated_cols = []
        for b in range(3):
            shifted = shift_cols(
                padded_grad[4 - 2 * a : 4 - 2 * a + rows_here], -(b - 1) * inner_rate
            )
            grad_act_one = grad_act_one + jnp.einsum(
                "pe,de->pd",
                shifted.reshape(pixels, full_mid),
                dilated_weight[a, b],
                preferred_element_type=jnp.float32,
            )
            forward_tap = shift_cols(
                padded_one[2 * a : 2 * a + rows_here], (b - 1) * inner_rate
            ).reshape(pixels, local_mid)
            dilated_cols.append(
                jnp.einsum(
                    "pd,pe->de", forward_tap, grad_two_full, preferred_element_type=jnp.float32
                )
            )
        dilated_rows.append(jnp.stack(dilated_cols))
    dilated_weight_local = jnp.stack(dilated_rows)
    grad_pre_one = grad_act_one * valid * silu_slope(pre_one)
    grad_one, reduce_gain_grad, reduce_bias_grad = norm_grad(
        grad_pre_one, norm_one, scale_one, reduce_gain, count, valid, (0,)
    )
    grad_one_low = grad_one.astype(jnp.bfloat16)
    input_sum = sum_channels(
        jnp.einsum("pd,cd->pc", grad_one_low, reduce_weight, preferred_element_type=jnp.float32)
    )
    features_grad = (
        ((input_sum + grad_pre_three) * valid)
        .astype(jnp.bfloat16)
        .reshape(rows_here, width, local_in)
    )
    reduce_weight_local = jnp.einsum(
        "pc,pd->cd", inputs_full, grad_one_low, preferred_element_type=jnp.float32
    )
    reduce_weight_grad, dilated_weight_grad, expand_weight_grad, aspp_weight_grad = (
        lax.psum_scatter(reduce_weight_local, "pix", scatter_dimension=0, tiled=True),
        lax.psum_scatter(dilated_weight_local, "pix", scatter_dimension=3, tiled=True),
        lax.psum_scatter(expand_weight_local, "pix", scatter_dimension=1, tiled=True),
        lax.psum_scatter(aspp_weight_local, "pix", scatter_dimension=4, tiled=True),
    )
    return (
        predictions.reshape(rows_here, width, outs_count),
        features_grad,
        reduce_weight_grad,
        reduce_gain_grad.reshape(-1),
        reduce_bias_grad.reshape(-1),
        dilated_weight_grad,
        dilated_gain_grad.reshape(-1),
        dilated_bias_grad.reshape(-1),
        expand_weight_grad,
        expand_gain_grad.reshape(-1),
        expand_bias_grad.reshape(-1),
        aspp_weight_grad,
        aspp_gain_grad.reshape(3, -1),
        aspp_bias_grad.reshape(3, -1),
        task_weight_grad,
    )


MESH = pl.DeviceIdType.MESH
ROW_CLASSES, COL_CLASSES = 2, 4
PHASES = ROW_CLASSES * COL_CLASSES
SPLIT = 4
FAR_FIRST = (1, 2, 3, 4, 5, 6, 7)
f32, bf16 = jnp.float32, jnp.bfloat16
VMEM_BYTES = 60 << 20


def shape(dims, dtype):
    return jax.ShapeDtypeStruct(dims, dtype)


def call(name, cid, kernel, arrays, outs, scratch, hbm_ins=(), hbm_outs=()):
    vmem, hbm = pl.BlockSpec(memory_space=pltpu.VMEM), pl.BlockSpec(memory_space=pl.ANY)
    return pl.pallas_call(
        kernel,
        out_shape=outs,
        in_specs=[hbm if i in hbm_ins else vmem for i in range(len(arrays))],
        out_specs=[hbm if i in hbm_outs else vmem for i in range(len(outs))],
        scratch_shapes=scratch,
        compiler_params=pltpu.CompilerParams(
            collective_id=cid, has_side_effects=True, vmem_limit_bytes=VMEM_BYTES
        ),
        name=name,
    )(*arrays)


def dma(*dims):
    return pltpu.SemaphoreType.DMA(dims)


def greet(ch, pix):
    p, c = lax.axis_index("pix"), lax.axis_index("ch")
    barrier = pltpu.get_barrier_semaphore()
    for k in ch:
        pl.semaphore_signal(barrier, inc=1, device_id=(p, c ^ k), device_id_type=MESH)
    for k in pix:
        pl.semaphore_signal(barrier, inc=1, device_id=(p ^ k, c), device_id_type=MESH)
    return barrier, len(ch) + len(pix)


def push(src, dst, send, recv, device):
    copy = pltpu.make_async_remote_copy(
        src_ref=src,
        dst_ref=dst,
        send_sem=send,
        recv_sem=recv,
        device_id=device,
        device_id_type=MESH,
    )
    copy.start()
    return copy


def keep(src, dst, sem):
    copy = pltpu.make_async_copy(src, dst, sem)
    copy.start()
    return copy


def rows(start, size):
    return pl.ds(pl.multiple_of(start, size), size)


def fold(x):
    return jnp.sum(x.reshape(x.shape[0] // 8, 8, x.shape[1]), axis=0)


def total(x):
    return jnp.sum(x, axis=0, keepdims=True)


def loop(steps, body, init):
    return lax.fori_loop(0, steps, body, init)


def sum_over_ch(part, tile, tiles, own, out, near, cross, near_sems, far_sems):
    p, c = lax.axis_index("pix"), lax.axis_index("ch")
    k, x = lax.rem(c, 2), c // 2
    n = own.shape[2]
    copies = []
    for t in range(tiles):
        at = pl.ds(t * tile, tile)
        value = part(t)
        for d in range(SPLIT):
            block = value[:, d * n : (d + 1) * n]
            own[d, at] = block
            out[d, at] = block.astype(bf16)
        copies.append(
            [
                push(
                    out.at[2 * h + 1 - k, at],
                    near.at[h, at],
                    near_sems.at[0, t, h],
                    near_sems.at[1, t, h],
                    (p, c ^ 1),
                )
                for h in range(2)
            ]
        )
    crossing = []
    for t in range(tiles):
        at = pl.ds(t * tile, tile)
        for copy in copies[t]:
            copy.wait()
        cross[0, at] = (own[2 * (1 - x) + k, at] + near[1 - x, at].astype(f32)).astype(bf16)
        crossing.append(
            push(cross.at[0, at], cross.at[1, at], far_sems.at[0, t], far_sems.at[1, t], (p, c ^ 2))
        )

    def result(t):
        at = pl.ds(t * tile, tile)
        crossing[t].wait()
        return own[2 * x + k, at] + near[x, at].astype(f32) + cross[1, at].astype(f32)

    return result


def sum_scratch(pixels, n, tiles):
    return [
        pltpu.VMEM((SPLIT, pixels, n), f32),
        pltpu.VMEM((SPLIT, pixels, n), bf16),
        pltpu.VMEM((2, pixels, n), bf16),
        pltpu.VMEM((2, pixels, n), bf16),
        dma(2, tiles, 2),
        dma(2, tiles),
    ]


def pix_exchange(send, recv, sems):
    p, c = lax.axis_index("pix"), lax.axis_index("ch")
    copies = [
        push(send, recv.at[p], sems.at[0, k], sems.at[1, k], (p ^ k, c)) for k in FAR_FIRST
    ]
    recv[p] = send[...]
    for copy in copies:
        copy.wait()


def norm_stats(hidden, valid, pixels, send, recv, sems, counted=None):
    n = hidden.shape[1]
    tile = 128
    repeat = n // 128

    def mask(at):
        v = valid[at]
        return v if repeat == 1 else jnp.concatenate([v] * repeat, axis=1)

    def first(i, carry):
        at = rows(i * tile, tile)
        v = mask(at)
        return carry[0] + fold(hidden[at] * v), carry[1] + fold(v)

    zero = jnp.zeros((8, n), f32)
    sums, count = loop(pixels // tile, first, (zero, zero))
    sums, count = total(sums), total(count)
    center = sums / jnp.maximum(count, 1.0)

    def second(i, carry):
        at = rows(i * tile, tile)
        apart = hidden[at] - center
        return carry + fold(mask(at) * apart * apart)

    spread = total(loop(pixels // tile, second, zero))
    if counted is not None:
        groups = n // 128
        for i in range(groups):
            send[i : i + 1] = sums[:, i * 128 : (i + 1) * 128]
            send[groups + i : groups + i + 1] = spread[:, i * 128 : (i + 1) * 128]
        pix_exchange(send, recv, sems)
        sums = [
            jnp.concatenate([recv[d, i : i + 1] for i in range(groups)], axis=1) for d in range(PHASES)
        ]
        spreads = [
            jnp.concatenate([recv[d, groups + i : groups + i + 1] for i in range(groups)], axis=1)
            for d in range(PHASES)
        ]
        counts = [spread_lanes(counted[d, 2:3], n) for d in range(PHASES)]
        return join_parts(sums, spreads, counts)
    send[0:1] = sums
    send[1:2] = spread
    send[2:3] = count
    pix_exchange(send, recv, sems)
    return join(recv, PHASES)


def spread_lanes(v, n):
    return v if n == 128 else jnp.concatenate([v] * (n // 128), axis=1)


def join_parts(sums, spreads, counts):
    whole, count = sums[0], counts[0]
    for i in range(1, len(sums)):
        whole, count = whole + sums[i], count + counts[i]
    center = whole / count
    spread = jnp.zeros_like(whole)
    for i in range(len(sums)):
        apart = sums[i] / jnp.maximum(counts[i], 1.0) - center
        spread = spread + spreads[i] + counts[i] * apart * apart
    return center, lax.rsqrt(spread / count + epsilon), count


def join(recv, parts):
    return join_parts(*[[recv[i, row : row + 1] for i in range(parts)] for row in range(3)])


def stat_scratch(n):
    return [pltpu.VMEM((8, n), f32), pltpu.VMEM((PHASES, 8, n), f32), dma(2, PHASES)]


def silu(x):
    return x / (1.0 + jnp.exp(-x))


def gather_over_ch(full, n, tile, tiles, near_sems, far_sems, hop_sems, ready, between=None):
    p, c = lax.axis_index("pix"), lax.axis_index("ch")

    def part(owner, t):
        return full.at[pl.ds(t * tile, tile), rows(owner * n, n)]

    near, far, hops = [], [], []
    for t in range(tiles):
        ready(t)
        src = part(c, t)
        far.append(push(src, src, far_sems.at[0, t], far_sems.at[1, t], (p, c ^ 2)))
        near.append(push(src, src, near_sems.at[0, t], near_sems.at[1, t], (p, c ^ 1)))
    if between is not None:
        between()
    for t in range(tiles):
        far[t].wait_recv()
        src = part(c ^ 2, t)
        hops.append(push(src, src, hop_sems.at[0, t], hop_sems.at[1, t], (p, c ^ 1)))
    for t in range(tiles):
        far[t].wait_send()
        near[t].wait()
        hops[t].wait()


def gather_scratch(tiles):
    return [dma(2, tiles), dma(2, tiles), dma(2, tiles)]


def to_classes(x):
    rows, cols, n = x.shape
    x = x.reshape(rows // ROW_CLASSES, ROW_CLASSES, cols // COL_CLASSES, COL_CLASSES, n)
    return x.transpose(1, 3, 0, 2, 4).reshape(PHASES, -1, n)


def from_classes(x, rows, cols):
    n = x.shape[-1]
    x = x.reshape(ROW_CLASSES, COL_CLASSES, rows // ROW_CLASSES, cols // COL_CLASSES, n)
    return x.transpose(2, 0, 3, 1, 4).reshape(rows, cols, n)


RATE_ROWS = tuple(rate // ROW_CLASSES for rate in aspp_rates)
RATE_COLS = tuple(rate // COL_CLASSES for rate in aspp_rates)


def load_pyramid(weight, wide, sems):
    m = weight.shape[4]
    return [
        [keep(weight.at[j, a, b], wide.at[3 * j + a, :, b * m : (b + 1) * m], sems.at[3 * j + a, b]) for b in range(3)]
        for j in range(3)
        for a in range(3)
    ]


def move_cols(x, by):
    place = lax.broadcasted_iota(jnp.int32, x.shape, 0) % 32
    rolled = pltpu.roll(x, by % x.shape[0], 0)
    return jnp.where(place < by, 0.0, rolled) if by > 0 else jnp.where(place >= 32 + by, 0.0, rolled)


def ch_exchange(send, recv, sems):
    p, c = lax.axis_index("pix"), lax.axis_index("ch")
    copies = [push(send, recv.at[c], sems.at[0, k], sems.at[1, k], (p, c ^ k)) for k in (2, 3, 1)]
    recv[c] = send[...]
    for copy in copies:
        copy.wait()


def add_up(recv, parts):
    value = recv[0]
    for i in range(1, parts):
        value = value + recv[i]
    return value


def task_vector(square, weights):
    product = square * weights
    row = lax.broadcasted_iota(jnp.int32, (32, 32), 0)
    col = lax.broadcasted_iota(jnp.int32, (32, 32), 1)

    def task(i):
        return (i >= CLS).astype(jnp.int32) + (i >= CLS + 1).astype(jnp.int32)

    def entry(t, s):
        return jnp.sum(
            jnp.sum(jnp.where((task(row) == t) & (task(col) == s), product, 0.0), axis=1, keepdims=True),
            axis=0,
            keepdims=True,
        )

    gram = [[entry(t, s) for s in range(3)] for t in range(3)]
    norms = [jnp.sqrt(gram[k][k] + 1e-06) for k in range(3)]
    proj = [[gram[i][k] / norms[k] for k in range(3)] for i in range(3)]
    vector = [proj[0][0] - proj[0][b] for b in (1, 2)]
    matrix = [[proj[0][0] - proj[0][b] - proj[a][0] + proj[a][b] for b in (1, 2)] for a in (1, 2)]
    determinant = matrix[0][0] * matrix[1][1] - matrix[0][1] * matrix[1][0]
    second = (vector[0] * matrix[1][1] - vector[1] * matrix[1][0]) / determinant
    third = (vector[1] * matrix[0][0] - vector[0] * matrix[0][1]) / determinant
    which = task(lax.broadcasted_iota(jnp.int32, (32, 1), 0))
    return jnp.where(which == 0, 1.0 - second - third, jnp.where(which == 1, second, third))


def slope(x):
    s = 1.0 / (1.0 + jnp.exp(-x))
    return s * (1.0 + x * (1.0 - s))


def pyramid(trunk, loads, wide, moving, pass_inputs, head_copies, heads, heads_all, targets, square, *refs):
    (full, predictions, head_grad, sums, others, picks) = refs[:6]
    (sides, own, out, near, cross, hidden, grad, branch) = refs[6:14]
    (s_send, s_ch, s_mid, s_pix, b_send, b_ch, b_mid, b_pix) = refs[14:22]
    (h_send, h_ch, h_mid, h_pix, h_sum, p_send, p_ch) = refs[22:29]
    (near_sems, far_sems, ch_sems, pix_sems, g_near, g_far, g_hop, y_sems, picked, pick_sems) = refs[29:]
    p, c = lax.axis_index("pix"), lax.axis_index("ch")
    k, x = lax.rem(c, 2), c // 2
    m = wide.shape[2] // 3
    pixels, half = trunk.shape[1], trunk.shape[2]
    quarter = pixels // SPLIT
    contract0 = (((0,), (0,)), ((), ()))
    contract1 = (((1,), (1,)), ((), ()))
    mine = rows(c * quarter, quarter)
    part = pixels // SPLIT
    sharing = []

    def share(slot, quarters, own, k, first):
        for i, q in enumerate(quarters):
            at = pl.ds(q * part, part)
            src = trunk.at[:, at] if own else others.at[2 - k, :, at]
            sharing.append(
                push(src, others.at[slot, :, at], y_sems.at[0, first + i], y_sems.at[1, first + i], (p ^ k, c))
            )
        return sharing[-len(quarters) :]

    def convolve(j, h):
        s = RATE_ROWS[j] * 32
        for a in (1, 0, 2):
            if h == 0:
                for load in loads[3 * j + a]:
                    load.wait()
            w = wide[3 * j + a, h * half : (h + 1) * half]
            if a == 1:
                value = jnp.dot(trunk[h], w, preferred_element_type=f32)
                if h == 0:
                    sides[j] = value
                else:
                    sides[j] += value
            elif a == 0:
                sides[j, s:] += jnp.dot(trunk[h, : pixels - s], w, preferred_element_type=f32)
            else:
                sides[j, : pixels - s] += jnp.dot(trunk[h, s:], w, preferred_element_type=f32)

    for copy in moving[0]:
        copy.wait()
    for j in range(3):
        convolve(j, 0)
    inputs_done = pass_inputs()
    for copy in moving[1]:
        copy.wait()
    from_y = share(0, (0, 1), True, 1, 0)
    from_z = share(1, (2, 3), True, 2, 2)

    def pass_on(i):
        from_y[i].wait_recv()
        share(2, (i,), False, 2, 4 + i)
        from_z[i].wait_recv()
        share(2, (i + 2,), False, 1, 6 + i)

    copies = []
    for j in range(3):
        q = RATE_COLS[j]
        convolve(j, 1)
        if j == 2:
            pass_on(0)
        for d in range(SPLIT):
            at = slice(d * quarter, (d + 1) * quarter)
            value = (
                sides[j, at, m : 2 * m]
                + move_cols(sides[j, at, :m], q)
                + move_cols(sides[j, at, 2 * m :], -q)
            )
            own[d, j] = value
            out[d, j] = value.astype(bf16)
        copies.append(
            [
                push(out.at[2 * h + 1 - k, j], near.at[h, j], near_sems.at[0, j, h], near_sems.at[1, j, h], (p, c ^ 1))
                for h in range(2)
            ]
        )
        if j > 0:
            copies[j - 1] = cross_chips(copies[j - 1], j - 1, own, near, cross, far_sems)
    copies[2] = cross_chips(copies[2], 2, own, near, cross, far_sems)
    for copy in head_copies:
        copy.wait()
    each = m // SPLIT
    for j in range(3):
        for d in range(SPLIT):
            heads[:, (j * SPLIT + d) * each : (j * SPLIT + d + 1) * each] = heads_all[d, :, j * each : (j + 1) * each]
    gain, bias = heads[32:33], heads[33:34]
    head = heads[:32]
    scaled = head * task_vector(
        add_up(square, PHASES)[:, :32], lax.dot_general(head, head, contract1, precision=highest)
    )
    target = jnp.concatenate([targets[2 * c], targets[2 * c + 1]], axis=1)
    mask = lax.dot_general(
        target[24:].astype(bf16), jnp.ones((8, m), bf16), contract0, preferred_element_type=f32
    )
    grad[...] = lax.dot_general(target, scaled, contract0, precision=highest) * jnp.concatenate([mask] * 3, axis=1)
    pass_on(1)
    count = total(mask)
    for j in range(3):
        copies[j].wait()
        value = own[2 * x + k, j] + near[x, j].astype(f32) + cross[1, j].astype(f32)
        at = slice(j * m, (j + 1) * m)
        hidden[:, at] = value
        first = total(value * mask)
        apart = value - first / jnp.maximum(count, 1.0)
        s_send[j : j + 1] = first
        s_send[3 + j : 4 + j] = total(apart * apart * mask)
    s_send[6:7] = count
    s_send[7:8] = jnp.zeros((1, m), f32)

    def merge(recv, parts):
        number = recv[0, 6:7]
        for i in range(1, parts):
            number = number + recv[i, 6:7]
        whole, spread = recv[0, 0:3], recv[0, 3:6]
        for i in range(1, parts):
            whole, spread = whole + recv[i, 0:3], spread + recv[i, 3:6]
        center = whole / jnp.maximum(number, 1.0)
        for i in range(parts):
            n = recv[i, 6:7]
            apart = recv[i, 0:3] / jnp.maximum(n, 1.0) - center
            spread = spread + n * apart * apart
        return whole, spread, number

    ch_exchange(s_send, s_ch, ch_sems.at[0])
    whole, spread, number = merge(s_ch, SPLIT)
    s_mid[0:3] = whole
    s_mid[3:6] = spread
    s_mid[6:7] = number
    s_mid[7:8] = jnp.zeros((1, m), f32)
    pix_exchange(s_mid, s_pix, pix_sems.at[0])
    share(0, (2,), True, 1, 8)
    share(1, (0,), True, 2, 9)
    whole, spread, number = merge(s_pix, PHASES)
    center, scale = whole / number, lax.rsqrt(spread / number + epsilon)
    for j in range(3):
        at = slice(j * m, (j + 1) * m)
        norm = (hidden[:, at] - center[j : j + 1]) * scale[j : j + 1]
        hidden[:, at] = norm
        value = norm * gain[:, at] + bias[:, at]
        branch[:, at] = (silu(value) * mask).astype(bf16)
        back = grad[:, at] * slope(value)
        grad[:, at] = back
        b_send[j : j + 1] = total(back)
        b_send[3 + j : 4 + j] = total(back * norm)
    b_send[6:8] = jnp.zeros((2, m), f32)
    to_ch = [push(b_send, b_ch.at[c], ch_sems.at[3, 0, i], ch_sems.at[3, 1, i], (p, c ^ i)) for i in (2, 3, 1)]
    b_ch[c] = b_send[...]
    high = target.astype(bf16)
    rest = target - high.astype(f32)
    middle = rest.astype(bf16)
    low = (rest - middle.astype(f32)).astype(bf16)
    p_send[...] = lax.dot_general(
        head.astype(bf16), branch[...], contract1, preferred_element_type=f32
    )
    value = jnp.dot(jnp.concatenate([high, middle, low]), branch[...], preferred_element_type=f32)
    h_send[...] = value[:32] + (value[32:64] + value[64:])
    background = [push(p_send, p_ch.at[c], ch_sems.at[1, 0, i], ch_sems.at[1, 1, i], (p, c ^ i)) for i in (2, 3, 1)] + [
        push(h_send.at[rows((c ^ i) * 8, 8)], h_ch.at[c], ch_sems.at[2, 0, i], ch_sems.at[2, 1, i], (p, c ^ i))
        for i in (2, 3, 1)
    ]
    p_ch[c] = p_send[...]
    h_ch[c] = h_send[rows(c * 8, 8)]
    for copy in to_ch:
        copy.wait()
    b_mid[...] = add_up(b_ch, SPLIT)
    sending = [
        push(b_mid, b_pix.at[p], pix_sems.at[1, 0, i], pix_sems.at[1, 1, i], (p ^ i, c)) for i in FAR_FIRST
    ]
    b_pix[p] = b_mid[...]
    for copy in background:
        copy.wait()
    h_mid[...] = add_up(h_ch, SPLIT)

    def block(to):
        return p_ch.at[to // 2, :, rows(lax.rem(to, 2) * 128, 128)]

    background = [
        push(block(p ^ i), predictions.at[p], pix_sems.at[2, 0, i], pix_sems.at[2, 1, i], (p ^ i, c)) for i in FAR_FIRST
    ] + [push(h_mid, h_pix.at[p], pix_sems.at[3, 0, i], pix_sems.at[3, 1, i], (p ^ i, c)) for i in FAR_FIRST]
    predictions[p] = block(p)[...]
    h_pix[p] = h_mid[...]
    for copy in sending:
        copy.wait()
    summed = add_up(b_pix, PHASES)
    sums[...] = summed
    for j in range(3):
        at = slice(j * m, (j + 1) * m)
        value = grad[:, at] - mask * (summed[j : j + 1] + hidden[:, at] * summed[3 + j : 4 + j]) / number
        full[mine, at] = (gain[:, at] * scale[j : j + 1] * value).astype(bf16)
    far = push(full.at[mine], full.at[mine], g_far.at[0], g_far.at[1], (p, c ^ 2))
    by = push(full.at[mine], full.at[mine], g_near.at[0], g_near.at[1], (p, c ^ 1))
    group = lax.rem(p, 4)
    pick = pick_rows(m, m, 0)
    for j in range(3):
        value = lax.dot_general(
            pick, full[mine, j * m : (j + 1) * m], contract1, preferred_element_type=f32
        ).astype(bf16)
        for g in range(4):
            picked[g, j * 64 : (j + 1) * 64] = value[g * 64 : (g + 1) * 64]
    sent_picks = [
        push(picked.at[group ^ i], picks.at[i - 1], pick_sems.at[0, i], pick_sems.at[1, i], (p ^ i, c)) for i in (3, 1, 2)
    ]
    for copy in background:
        copy.wait()
    own_rows = add_up(h_pix, PHASES)
    h_sum[...] = own_rows
    head_grad[rows(c * 8, 8)] = own_rows
    last = [
        push(h_sum, head_grad.at[rows(c * 8, 8)], ch_sems.at[4, 0, i], ch_sems.at[4, 1, i], (p, c ^ i))
        for i in (2, 3, 1)
    ]
    far.wait_recv()
    theirs = rows((c ^ 2) * quarter, quarter)
    hop = push(full.at[theirs], full.at[theirs], g_hop.at[0], g_hop.at[1], (p, c ^ 1))
    far.wait_send()
    by.wait()
    hop.wait()
    for copy in last:
        copy.wait()
    for copy in from_y + from_z:
        copy.wait_send()
    for copy in sharing[4:] + sent_picks:
        copy.wait()
    inputs_done()


def pick_rows(m, count, first):
    row = lax.broadcasted_iota(jnp.int32, (count, m), 0)
    col = lax.broadcasted_iota(jnp.int32, (count, m), 1)
    source = (4 * (row % 64 // 32) + row // 64 + first) * 32 + row % 32
    return jnp.where(col == source, 1.0, 0.0).astype(bf16)


def cross_chips(near_copies, j, own, near, cross, sems):
    p, c = lax.axis_index("pix"), lax.axis_index("ch")
    k, x = lax.rem(c, 2), c // 2
    for copy in near_copies:
        copy.wait()
    cross[0, j] = (own[2 * (1 - x) + k, j] + near[1 - x, j].astype(f32)).astype(bf16)
    return push(cross.at[0, j], cross.at[1, j], sems.at[0, j], sems.at[1, j], (p, c ^ 2))


def pyramid_scratch(pixels, n, m):
    quarter = pixels // SPLIT
    small = [
        pltpu.VMEM((8, m), f32),
        pltpu.VMEM((SPLIT, 8, m), f32),
        pltpu.VMEM((8, m), f32),
        pltpu.VMEM((PHASES, 8, m), f32),
    ]
    return [
        pltpu.VMEM((3, pixels, 3 * m), f32),
        pltpu.VMEM((SPLIT, 3, quarter, m), f32),
        pltpu.VMEM((SPLIT, 3, quarter, m), bf16),
        pltpu.VMEM((2, 3, quarter, m), bf16),
        pltpu.VMEM((2, 3, quarter, m), bf16),
        pltpu.VMEM((quarter, 3 * m), f32),
        pltpu.VMEM((quarter, 3 * m), f32),
        pltpu.VMEM((quarter, 3 * m), bf16),
        *small,
        *small,
        pltpu.VMEM((32, 3 * m), f32),
        pltpu.VMEM((SPLIT, 8, 3 * m), f32),
        pltpu.VMEM((8, 3 * m), f32),
        pltpu.VMEM((PHASES, 8, 3 * m), f32),
        pltpu.VMEM((8, 3 * m), f32),
        pltpu.VMEM((32, quarter), f32),
        pltpu.VMEM((SPLIT, 32, quarter), f32),
        dma(2, 3, 2),
        dma(2, 3),
        dma(5, 2, SPLIT),
        dma(4, 2, PHASES),
        dma(2),
        dma(2),
        dma(2),
        dma(2, 10),
        pltpu.VMEM((4, 192, quarter), bf16),
        dma(2, 4),
    ]


TILES = 4


def one_hot(rows_count, cols_count, source):
    row = lax.broadcasted_iota(jnp.int32, (rows_count, cols_count), 0)
    col = lax.broadcasted_iota(jnp.int32, (rows_count, cols_count), 1)
    return col == source(row)


def stage_one(feat, mask, weight, expand, gain, bias, *refs):
    (masked, reduce_rows, expand_cols, norm, padded, stat, valid) = refs[:7]
    (wide, hidden, own, out, near, cross, near_sems, far_sems, send, recv, stat_sems) = refs[7:18]
    (weight_sems, local_sems, halo_sems) = refs[18:]
    p, c = lax.axis_index("pix"), lax.axis_index("ch")
    pixels, local_in = feat.shape
    local_mid = weight.shape[1]
    tile = pixels // TILES

    def piece(i, to):
        return (
            (weight.at[rows(to * local_in, local_in), :], reduce_rows.at[:, rows(c * local_mid, local_mid)]),
            (expand.at[:, rows(to * local_in, local_in)], expand_cols.at[rows(c * local_mid, local_mid), :]),
        )[i]

    def to_ch(i):
        return [
            push(*piece(i, c ^ k), weight_sems.at[0, k, i], weight_sems.at[1, k, i], (p, c ^ k)) for k in (2, 3, 1)
        ] + [keep(*piece(i, c), local_sems.at[i])]

    reduce_copies = to_ch(0)

    present = mask[...].astype(f32)
    order = one_hot(128, 128, lambda i: 4 * (i % 32) + i // 32)
    ones = jnp.ones((128, 128), bf16)
    for r in range(8):
        column = jnp.dot(
            jnp.where(order, present[r : r + 1], 0.0).astype(bf16), ones, preferred_element_type=f32
        )
        for b in range(COL_CLASSES):
            block = ((r % ROW_CLASSES) * COL_CLASSES + b) * 128 + (r // ROW_CLASSES) * 32
            valid[block : block + 32] = column[b * 32 : (b + 1) * 32]
    for r in range(8):
        for g in range(local_in // 128):
            lanes = slice(g * 128, (g + 1) * 128)
            wide[g] = feat[r * 128 : (r + 1) * 128, lanes].astype(f32)
            for b in range(COL_CLASSES):
                block = ((r % ROW_CLASSES) * COL_CLASSES + b) * 128 + (r // ROW_CLASSES) * 32
                value = wide[g, pl.ds(b, 32, stride=COL_CLASSES), :] * valid[block : block + 32]
                masked[block : block + 32, lanes] = value.astype(bf16)

    for copy in reduce_copies:
        copy.wait()

    def part(t):
        return jnp.dot(masked[t * tile : (t + 1) * tile], reduce_rows[...], preferred_element_type=f32)

    result = sum_over_ch(part, tile, TILES, own, out, near, cross, near_sems, far_sems)
    for t in range(TILES):
        hidden[t * tile : (t + 1) * tile] = result(t)
    later = to_ch(1)
    center, scale, count = norm_stats(hidden, valid, pixels, send, recv, stat_sems)
    stat[0:1] = center
    stat[1:2] = scale
    stat[2:3] = count
    for i in range(PHASES):
        at = pl.ds(i * 128, 128)
        value = (hidden[at] - center) * scale
        norm[at] = value
        act = silu(value * gain[...] + bias[...]) * valid[at]
        padded[i, 1:5] = act.astype(bf16).reshape(4, 32, local_mid)
    up = lambda: pltpu.make_async_remote_copy(
        src_ref=padded.at[:, 4],
        dst_ref=padded.at[:, 0],
        send_sem=halo_sems.at[0, 0],
        recv_sem=halo_sems.at[1, 0],
        device_id=(p + 1, c),
        device_id_type=MESH,
    )
    down = lambda: pltpu.make_async_remote_copy(
        src_ref=padded.at[:, 1],
        dst_ref=padded.at[:, 5],
        send_sem=halo_sems.at[0, 1],
        recv_sem=halo_sems.at[1, 1],
        device_id=(p - 1, c),
        device_id_type=MESH,
    )
    first, last = p == 0, p == PHASES - 1

    @pl.when(jnp.logical_not(last))
    def _():
        up().start()

    @pl.when(jnp.logical_not(first))
    def _():
        down().start()

    @pl.when(last)
    def _():
        padded[:, 5] = jnp.zeros((PHASES, 32, local_mid), bf16)

    @pl.when(first)
    def _():
        padded[:, 0] = jnp.zeros((PHASES, 32, local_mid), bf16)

    @pl.when(jnp.logical_not(last))
    def _():
        up().wait_send()
        down().wait_recv()

    @pl.when(jnp.logical_not(first))
    def _():
        down().wait_send()
        up().wait_recv()

    return later


def prepare_heads(mask, head_weight, head_gain, head_bias, cotangent, *refs):
    (heads_all, targets_all, square_all, heads, targets, square, image, head_sems, pix_sems, local_sems) = refs
    p, c = lax.axis_index("pix"), lax.axis_index("ch")
    contract1 = (((1,), (1,)), ((), ()))
    present = mask[...].astype(f32)
    columns, m = head_weight.shape[1], head_weight.shape[2]
    heads[...] = jnp.zeros(heads.shape, f32)
    for j in range(3):
        heads[:columns, j * m : (j + 1) * m] = head_weight[j].astype(f32)
        heads[32:33, j * m : (j + 1) * m] = head_gain[j : j + 1]
        heads[33:34, j * m : (j + 1) * m] = head_bias[j : j + 1]

    image[...] = jnp.zeros(image.shape, f32)
    for r in range(8):
        at = slice(r * 128, (r + 1) * 128)
        image[:columns, at] = cotangent[:, at] * present[r : r + 1]
        image[31:32, at] = present[r : r + 1]
    square[...] = jnp.zeros(square.shape, f32)
    square[:, :32] = lax.dot_general(
        image[...], image[...], contract1, precision=highest, preferred_element_type=f32
    )
    place = jnp.where(
        one_hot(512, 512, lambda i: i % 4 * 128 + i // 128 * 32 + i % 128 // 4), 1.0, 0.0
    )
    for a in range(ROW_CLASSES):
        some = jnp.concatenate([image[:, (2 * r + a) * 128 : (2 * r + a + 1) * 128] for r in range(4)], axis=1)
        value = jnp.dot(some, place, precision=highest, preferred_element_type=f32)
        for b in range(COL_CLASSES):
            targets[a * COL_CLASSES + b] = value[:, b * 128 : (b + 1) * 128]
    copies = [push(heads, heads_all.at[c], head_sems.at[0, k], head_sems.at[1, k], (p, c ^ k)) for k in (2, 3, 1)]
    copies += [
        push(targets.at[p ^ k], targets_all.at[p], pix_sems.at[0, k, 0], pix_sems.at[1, k, 0], (p ^ k, c))
        for k in FAR_FIRST
    ] + [push(square, square_all.at[p], pix_sems.at[0, k, 1], pix_sems.at[1, k, 1], (p ^ k, c)) for k in FAR_FIRST]
    copies.append(keep(heads, heads_all.at[c], local_sems.at[0]))
    copies.append(keep(targets.at[p], targets_all.at[p], local_sems.at[1]))
    copies.append(keep(square, square_all.at[p], local_sems.at[2]))
    return copies


def stage_two(padded, valid, weight, gain, bias, *refs):
    (norm, full, taps, stat) = refs[:4]
    (hidden, own, out, near, cross, near_sems, far_sems, send, recv, stat_sems) = refs[4:14]
    (g_near, g_far, g_hop) = refs[14:]
    p, c = lax.axis_index("pix"), lax.axis_index("ch")
    pixels = valid.shape[0]
    local_mid = padded.shape[3]
    tile = pixels // TILES
    place = lax.broadcasted_iota(jnp.int32, (192, local_mid), 0) % 32
    for i in range(PHASES):
        beta = i % COL_CLASSES
        plain = padded[i].reshape(192, local_mid)
        wide = plain.astype(f32)
        if beta >= 2:
            moved_by = jnp.where(place == 0, 0.0, pltpu.roll(wide, 1, 0)).astype(bf16)
        else:
            moved_by = jnp.where(place == 31, 0.0, pltpu.roll(wide, 191, 0)).astype(bf16)
        for a in range(3):
            at = slice(a * 32, a * 32 + 128)
            for b, other, value in (
                (1, beta, plain),
                (0, (beta + 2) % 4, moved_by if beta >= 2 else plain),
                (2, (beta + 2) % 4, plain if beta >= 2 else moved_by),
            ):
                to = (i - beta + other) * 128
                col = (a * 3 + b) * local_mid
                taps[to : to + 128, col : col + local_mid] = value[at]

    def part(t):
        return jnp.dot(taps[t * tile : (t + 1) * tile], weight[...], preferred_element_type=f32)

    result = sum_over_ch(part, tile, TILES, own, out, near, cross, near_sems, far_sems)
    for t in range(TILES):
        hidden[t * tile : (t + 1) * tile] = result(t)
    center, scale, count = norm_stats(hidden, valid, pixels, send, recv, stat_sems)
    stat[0:1] = center
    stat[1:2] = scale
    stat[2:3] = count

    def ready(t):
        for i in range(tile // 128):
            at = pl.ds(t * tile + i * 128, 128)
            value = (hidden[at] - center) * scale
            norm[at] = value
            act = silu(value * gain[...] + bias[...]) * valid[at]
            full[at, rows(c * local_mid, local_mid)] = act.astype(bf16)

    gather_over_ch(full, local_mid, tile, TILES, g_near, g_far, g_hop, ready)


def stage_three(full, weight, masked, valid, gain, bias, counted, *refs):
    (norm, classes, stat, inputs) = refs[:4]
    (hidden, trunk, send, recv, stat_sems, class_sems, own_sem, in_sems) = refs[4:]
    p, c = lax.axis_index("pix"), lax.axis_index("ch")
    pixels, n = masked.shape
    tile = pixels // TILES
    for t in range(TILES):
        at = pl.ds(t * tile, tile)
        hidden[at] = jnp.dot(full[at], weight[...], preferred_element_type=f32)
    far = push(masked, inputs.at[c], in_sems.at[0, 0], in_sems.at[1, 0], (p, c ^ 2))
    near = push(masked, inputs.at[c], in_sems.at[0, 1], in_sems.at[1, 1], (p, c ^ 1))
    mine = keep(masked, inputs.at[c], own_sem.at[2])
    center, scale, count = norm_stats(hidden, valid, pixels, send, recv, stat_sems, counted)
    stat[0:1] = center
    stat[1:2] = scale
    stat[2:3] = count

    half = n // 2

    def finish(to, h):
        lanes = slice(h * half, (h + 1) * half)

        def step(i, carry):
            at = rows(to * 128 + i * 64, 64)
            value = (hidden[at, lanes] - center[:, lanes]) * scale[:, lanes]
            norm[at, lanes] = value
            pre = value * gain[:, lanes] + bias[:, lanes] + masked[at, lanes].astype(f32)
            v = valid[at]
            trunk[h, at] = (silu(pre) * jnp.concatenate([v] * (half // 128), axis=1)).astype(bf16)
            return carry

        loop(2, step, 0)

    copies = []
    for h in range(2):
        some = []
        for k in FAR_FIRST:
            to = p ^ k
            finish(to, h)
            some.append(
                push(
                    trunk.at[h, rows(to * 128, 128)],
                    classes.at[h, rows(p * 128, 128)],
                    class_sems.at[0, h, k],
                    class_sems.at[1, h, k],
                    (to, c),
                )
            )
        finish(p, h)
        some.append(keep(trunk.at[h, rows(p * 128, 128)], classes.at[h, rows(p * 128, 128)], own_sem.at[h]))
        copies.append(some)

    def pass_inputs():
        far.wait_recv()
        hop = push(inputs.at[c ^ 2], inputs.at[c ^ 2], in_sems.at[0, 2], in_sems.at[1, 2], (p, c ^ 1))

        def done():
            far.wait_send()
            near.wait()
            mine.wait()
            hop.wait()

        return done

    return copies, pass_inputs


def forward(
    feat, mask, weight, expand, gain1, bias1, head_weight, head_gain, head_bias, cotangent, dilated, gain2, bias2,
    gain3, bias3, pyramid_weight, *refs
):
    saved, stats, (inputs, grads, predictions, head_grad, branch_sums, others, picks) = refs[:10], refs[10:13], refs[13:20]
    padded, wide, w_sems, heads_full, save_sems = refs[20:25]
    masked, reduce_rows, expand_cols, norm1, valid, norm2, full2, taps, norm3, classes = refs[25:35]
    stat1, stat2, stat3 = stats
    own = refs[35:]
    saving = []

    def save(*which):
        for i in which:
            saving.append(keep(refs[25 + i], saved[i], save_sems.at[i]))

    one, two, three, heads = 14, 13, 8, 10
    barrier, expected = greet((1, 2, 3), FAR_FIRST)
    loads = load_pyramid(pyramid_weight, wide, w_sems)
    pl.semaphore_wait(barrier, expected)
    expand_copies = stage_one(
        feat, mask, weight, expand, gain1, bias1, masked, reduce_rows, expand_cols, norm1, padded, stat1, valid, *own[:one]
    )
    counted = own[9]
    own = own[one:]
    save(0, 1, 3, 4)
    stage_two(padded, valid, dilated, gain2, bias2, norm2, full2, taps, stat2, *own[:two])
    own = own[two:]
    for copy in expand_copies:
        copy.wait()
    save(2, 5, 6, 7)
    moving, pass_inputs = stage_three(
        full2, expand_cols, masked, valid, gain3, bias3, counted, norm3, classes, stat3, inputs, *own[:three]
    )
    own = own[three:]
    save(8)
    head_copies = prepare_heads(mask, head_weight, head_gain, head_bias, cotangent, *own[:heads])
    pyramid(
        classes, loads, wide, moving, pass_inputs, head_copies, heads_full, *own[:3],
        grads, predictions, head_grad, branch_sums, others, picks, *own[heads:],
    )
    save(9)
    for copy in saving:
        copy.wait()


def run_forward(
    cid, feat, mask, weight, expand, gain1, bias1, head_weight, head_gain, head_bias, cotangent, dilated, gain2, bias2,
    gain3, bias3, pyramid_weight
):
    pixels, n = feat.shape
    mid = weight.shape[1]
    all_mid = SPLIT * mid
    m = pyramid_weight.shape[4]
    quarter = pixels // SPLIT
    saved = [
        ((pixels, n), bf16),
        ((n, all_mid), bf16),
        ((all_mid, n), bf16),
        ((pixels, mid), f32),
        ((pixels, 128), f32),
        ((pixels, mid), f32),
        ((pixels, all_mid), bf16),
        ((pixels, 9 * mid), bf16),
        ((pixels, n), f32),
        ((2, pixels, n // 2), bf16),
    ]
    outs = [shape(*each) for each in saved] + [
        shape((8, mid), f32),
        shape((8, mid), f32),
        shape((8, n), f32),
        shape((SPLIT, pixels, n), bf16),
        shape((pixels, 3 * m), bf16),
        shape((PHASES, 32, 128), f32),
        shape((32, 3 * m), f32),
        shape((8, m), f32),
        shape((3, 2, pixels, n // 2), bf16),
        shape((3, 192, quarter), bf16),
    ]
    scratch = [
        pltpu.VMEM((PHASES, 6, 32, mid), bf16),
        pltpu.VMEM((9, n, 3 * m), bf16),
        dma(9, 3),
        pltpu.VMEM((40, 3 * m), f32),
        dma(10),
        *[pltpu.VMEM(*each) for each in saved],
        pltpu.VMEM((n // 128, 128, 128), f32),
        pltpu.VMEM((pixels, mid), f32),
        *sum_scratch(pixels, mid, TILES),
        *stat_scratch(mid),
        dma(2, SPLIT, 2),
        dma(2),
        dma(2, 2),
        pltpu.VMEM((pixels, mid), f32),
        *sum_scratch(pixels, mid, TILES),
        *stat_scratch(mid),
        *gather_scratch(TILES),
        pltpu.VMEM((pixels, n), f32),
        pltpu.VMEM((2, pixels, n // 2), bf16),
        *stat_scratch(128),
        dma(2, 2, PHASES),
        dma(4),
        dma(2, 3),
        pltpu.VMEM((SPLIT, 40, 256), f32),
        pltpu.VMEM((PHASES, 32, 128), f32),
        pltpu.VMEM((PHASES, 32, 128), f32),
        pltpu.VMEM((40, 256), f32),
        pltpu.VMEM((PHASES, 32, 128), f32),
        pltpu.VMEM((32, 128), f32),
        pltpu.VMEM((32, pixels), f32),
        dma(2, SPLIT),
        dma(2, PHASES, 2),
        dma(3),
        *pyramid_scratch(pixels, n, m),
    ]
    arrays = [
        feat, mask, weight, expand, gain1, bias1, head_weight, head_gain, head_bias, cotangent, dilated, gain2, bias2,
        gain3, bias3, pyramid_weight,
    ]
    return call("forward", cid, forward, arrays, outs, scratch, hbm_ins=(15,), hbm_outs=(*range(10), 13, 18))


PACE = (1, 10, 18, 21)


def packed_sums(values, send):
    i = 0
    for value in values:
        for g in range(value.shape[1] // 128):
            send[i : i + 1] = value[:, g * 128 : (g + 1) * 128]
            i += 1


def unpacked_sums(recv, rows_each, count):
    out, i = [], 0
    for _ in range(count):
        parts = []
        for _ in range(rows_each):
            value = recv[0, i : i + 1]
            for d in range(1, PHASES):
                value = value + recv[d, i : i + 1]
            parts.append(value)
            i += 1
        out.append(parts[0] if rows_each == 1 else jnp.concatenate(parts, axis=1))
    return out


def backward(
    grads, trunk, others, weight, norm3, masked, valid, expand, gain3, bias3, norm2, gain2, bias2, full2, taps, dilated,
    norm1, gain1, bias1, reduce_rows, stats1, stats2, stats3, picks, inputs, *refs
):
    stored = (valid, norm3, masked, expand, norm2, full2, norm1, dilated, reduce_rows)
    valid, norm3, masked, expand, norm2, full2, norm1, dilated, reduce_rows, store_sems = refs[-10:]
    refs = refs[:-10]
    outs, scratch = refs[:6], refs[6:]
    (features_grad, aspp_parts, dilated_grad, expand_grad, reduce_grad, sums_out) = outs
    (wide, moved, acc, dsend, drecv, tpad, r_in, picked_in, turned, zsend, r_y) = scratch[:11]
    (gp3, g3, own, out, near, cross, hidden, gp2, g2, prod, edges, g1) = scratch[11:23]
    gp1, lanes = gp2, own
    (st3, st3r, st2, st2r, st1, st1r, e_part, e_mid, e_in, e_y, e_sum, d_part, d_in, d_y, d_sum, r_mid, r_sum) = scratch[23:40]
    (w_sems, d_sems, y_sems, z_sems, near_sems, far_sems, st_sems, gn, gf, gh, gn1, gf1, gh1, edge_sems, ch_sems, pix_sems, pair_sems, own_sems, tap_sems, in_sems, fill_sems, last_sems, slope1, d_near, d_far, mid_sems) = scratch[40:]
    p, c = lax.axis_index("pix"), lax.axis_index("ch")
    y, z = lax.rem(p, 2), p // 2
    lower = lax.rem(z, 2)
    pixels, n = norm3.shape
    m = weight.shape[4]
    mid = norm2.shape[1]
    tile = pixels // TILES
    contract0 = (((0,), (0,)), ((), ()))
    contract1 = (((1,), (1,)), ((), ()))
    count = stats1[2:3, :1]
    barrier, expected = greet((1, 2, 3), FAR_FIRST)
    loads = load_pyramid(weight, wide, w_sems)
    arrived = dict(
        zip(
            ("valid", "norm3", "masked", "expand", "norm2", "full2", "norm1", "dilated", "reduce"),
            [keep(a, b, store_sems.at[i]) for i, (a, b) in enumerate(
                zip(stored, (valid, norm3, masked, expand, norm2, full2, norm1, dilated, reduce_rows))
            )],
        )
    )

    group, upper = lax.rem(p, 4), p // 4
    quarter = picks.shape[2]
    pl.semaphore_wait(barrier, expected)
    mine = rows(c * quarter, quarter)
    sent_picks = [
        push(picks, picked_in.at[:, :, mine], y_sems.at[0, k], y_sems.at[1, k], (p, c ^ k)) for k in (2, 3, 1)
    ] + [keep(picks, picked_in.at[:, :, mine], y_sems.at[0, 0])]
    part = pixels // SPLIT
    filled = []
    for k in range(4):
        for h in range(2):
            cols = slice(h * m, (h + 1) * m)
            source = (others.at[k - 1] if k else trunk).at[h]
            here = {0: ((0, 4),), 1: ((0, 3),), 2: ((0, 1), (2, 4)), 3: ((0, 4),)}[k]
            for i, (first, end) in enumerate(here):
                at = pl.ds(first * part, (end - first) * part)
                filled.append(
                    keep(source.at[at], tpad.at[k, pl.ds(64 + first * part, (end - first) * part), cols], fill_sems.at[k, h, i])
                )
            if k in (1, 2):
                q = 3 if k == 1 else 1
                filled.append(
                    push(
                        trunk.at[h, pl.ds(q * part, part)],
                        tpad.at[k, pl.ds(64 + q * part, part), cols],
                        last_sems.at[0, k - 1, h],
                        last_sems.at[1, k - 1, h],
                        (p ^ k, c),
                    )
                )
    for i in range(4):
        tpad[i, :64] = jnp.zeros((64, n), bf16)
        tpad[i, 64 + pixels :] = jnp.zeros((64, n), bf16)

    for j in range(3):
        q = RATE_COLS[j]
        plain = grads[:, j * m : (j + 1) * m]
        value = plain.astype(f32)
        moved[j, :, :m] = move_cols(value, -q).astype(bf16)
        moved[j, :, m : 2 * m] = plain
        moved[j, :, 2 * m :] = move_cols(value, q).astype(bf16)
    back = []
    for h in range(2):
        half = slice(h * m, (h + 1) * m)
        for j in range(3):
            s = RATE_ROWS[j] * 32
            for a in (1, 0, 2):
                if h == 0:
                    for load in loads[3 * j + a]:
                        load.wait()
                w = wide[3 * j + a, half]
                if a == 1:
                    value = lax.dot_general(moved[j], w, contract1, preferred_element_type=f32)
                    if j == 0:
                        acc[...] = value
                    else:
                        acc[...] += value
                elif a == 0:
                    acc[: pixels - s] += lax.dot_general(moved[j, s:], w, contract1, preferred_element_type=f32)
                else:
                    acc[s:] += lax.dot_general(moved[j, : pixels - s], w, contract1, preferred_element_type=f32)
        dsend[h] = acc[...].astype(bf16)
        for k in FAR_FIRST:
            back.append(
                push(
                    dsend.at[h, rows((p ^ k) * 128, 128)],
                    drecv.at[h, rows(p * 128, 128)],
                    d_sems.at[0, h, k],
                    d_sems.at[1, h, k],
                    (p ^ k, c),
                )
            )
        back.append(keep(dsend.at[h, rows(p * 128, 128)], drecv.at[h, rows(p * 128, 128)], own_sems.at[h]))

    all_inputs = [
        keep(inputs.at[i // 2, pl.ds(i % 2 * n, n)], wide.at[i, :, :n], in_sems.at[i]) for i in range(8)
    ]
    cut = moved.shape[2]
    own_taps = [
        keep(taps.at[:, :cut], moved.at[0], tap_sems.at[0]),
        keep(taps.at[:, cut:], moved.at[1, :, : taps.shape[1] - cut], tap_sems.at[1]),
    ]

    place = lax.broadcasted_iota(jnp.int32, (64, pixels), 1) % 32

    def turn(i, part):
        at = slice(i * pixels, (i + 1) * pixels)
        for j in range(3):
            q = RATE_COLS[j]
            plain = part(j)
            value = plain.astype(f32)
            turned[j, :64, at] = jnp.where(place >= 32 - q, 0.0, pltpu.roll(value, pixels - q, 1)).astype(bf16)
            turned[j, 64:128, at] = plain
            turned[j, 128:, at] = jnp.where(place < q, 0.0, pltpu.roll(value, q, 1)).astype(bf16)

    pick = pick_rows(m, 64, group)
    turn(
        0,
        lambda j: lax.dot_general(
            pick, grads[:, j * m : (j + 1) * m], contract1, preferred_element_type=f32
        ).astype(bf16),
    )
    for copy in sent_picks:
        copy.wait()
    for k in (1, 2, 3):
        turn(k, lambda j: picked_in[k - 1, j * 64 : (j + 1) * 64])
    for copy in filled:
        copy.wait()
    for j in range(3):
        s = RATE_ROWS[j] * 32
        for a in range(3):
            if a == 1:
                low, high, start = 0, pixels, 64
            elif a == 0:
                low, high = s // 128 * 128, pixels
                start = 64 + low - s
            else:
                low, high, start = 0, -(-(pixels - s) // 128) * 128, 64 + s
            value = None
            for i in range(4):
                term = jnp.dot(
                    turned[j, :, i * pixels + low : i * pixels + high],
                    tpad[i, start : start + high - low],
                    preferred_element_type=f32,
                )
                value = term if value is None else value + term
            value = value.astype(bf16)
            for b in range(3):
                for to in range(2):
                    at = b * 64 + to * 32
                    zsend[to, (3 * j + a) * 3 + b] = value[at : at + 32]
    for name in ("valid", "norm3", "masked", "norm2", "norm1"):
        arrived[name].wait()

    def slopes(i, carry):
        at = rows(i * 32, 32)
        pre = norm3[at] * gain3[...] + bias3[...] + masked[at].astype(f32)
        gp3[at] = spread_lanes(valid[at], n) * slope(pre)
        gp2[at] = valid[at] * slope(norm2[at] * gain2[...] + bias2[...])
        slope1[at] = valid[at] * slope(norm1[at] * gain1[...] + bias1[...])
        return carry

    loop(pixels // 32, slopes, 0)
    zcopies = [keep(zsend.at[upper], aspp_parts.at[0], own_sems.at[2])]

    def send_parts(first, end):
        for i in range(first, end):
            zcopies.append(
                push(zsend.at[1 - upper, i], aspp_parts.at[1, i], z_sems.at[0, i], z_sems.at[1, i], (p ^ 4, c))
            )


    def over_z(blocks, sums, sems, own_sem):
        return [
            push(blocks.at[z ^ k], sums.at[z], sems.at[0, k], sems.at[1, k], (p ^ (2 * k), c)) for k in (3, 2, 1)
        ] + [keep(blocks.at[z], sums.at[z], own_sem)]

    def norm_back(grad, norm, sums, scale, gain, v):
        return gain * scale * (grad - v * (sums[0] + norm * sums[1]) / count)

    totals = []
    for h in range(2):
        for copy in back[h * PHASES : (h + 1) * PHASES]:
            copy.wait()
        if h == 1:
            send_parts(0, PACE[0])
        cols = slice(h * m, (h + 1) * m)

        def three(i, carry):
            at = rows(i * 64, 64)
            grad = drecv[h, at].astype(f32) * gp3[at, cols]
            gp3[at, cols] = grad
            return carry[0] + fold(grad), carry[1] + fold(grad * norm3[at, cols])

        zero = jnp.zeros((8, m), f32)
        bias, gain = loop(pixels // 64, three, (zero, zero))
        totals.append((total(bias), total(gain)))
    bias, gain = (jnp.concatenate([totals[0][i], totals[1][i]], axis=1) for i in range(2))
    packed_sums((bias, gain), st3)
    pix_exchange(st3, st3r, st_sems.at[0])
    send_parts(PACE[0], PACE[1])
    sums = unpacked_sums(st3r, n // 128, 2)
    sums_out[0:1] = sums[0]
    sums_out[1:2] = sums[1]

    arrived["expand"].wait()

    def part3(t):
        def step(i, carry):
            at = rows(t * tile + i * 32, 32)
            v = spread_lanes(valid[at], n)
            g3[at] = norm_back(gp3[at], norm3[at], sums, stats3[1:2], gain3[...], v).astype(bf16)
            return carry

        loop(tile // 32, step, 0)
        return lax.dot_general(g3[t * tile : (t + 1) * tile], expand[...], contract1, preferred_element_type=f32)

    result = sum_over_ch(part3, tile, TILES, own, out, near, cross, near_sems.at[0], far_sems.at[0])
    arrived["full2"].wait()
    value = lax.dot_general(full2[...], g3[...], contract0, preferred_element_type=f32).astype(bf16)
    for d in range(SPLIT):
        e_part[d] = value[d * mid : (d + 1) * mid]
    e_copies = [
        push(e_part.at[c ^ k], e_mid.at[c], ch_sems.at[0, 0, k], ch_sems.at[0, 1, k], (p, c ^ k)) for k in (2, 3, 1)
    ]
    e_copies.append(keep(e_part.at[c], e_mid.at[c], own_sems.at[3]))

    bias, gain = jnp.zeros((8, mid), f32), jnp.zeros((8, mid), f32)
    for t in range(TILES):
        hidden[t * tile : (t + 1) * tile] = result(t)

    def two(i, carry):
        at = rows(i * 128, 128)
        grad = hidden[at] * gp2[at]
        gp2[at] = grad
        return carry[0] + fold(grad), carry[1] + fold(grad * norm2[at])

    bias, gain = loop(pixels // 128, two, (bias, gain))
    packed_sums((total(bias), total(gain)), st2)
    pix_exchange(st2, st2r, st_sems.at[1])
    send_parts(PACE[1], PACE[2])
    for copy in e_copies:
        copy.wait()
    e_to_y = push(
        e_mid.at[:, :, rows((1 - y) * 256, 256)], e_in, pair_sems.at[0, 0], pair_sems.at[1, 0], (p ^ 1, c)
    )
    sums2 = unpacked_sums(st2r, 1, 2)
    sums_out[2:3, :mid] = sums2[0]
    sums_out[3:4, :mid] = sums2[1]

    def ready2(t):
        def step(i, carry):
            at = rows(t * tile + i * 128, 128)
            value = norm_back(gp2[at], norm2[at], sums2, stats2[1:2], gain2[...], valid[at])
            g2[at, rows(c * mid, mid)] = value.astype(bf16)
            return carry

        loop(tile // 128, step, 0)

    gather_over_ch(g2, mid, tile, TILES, gn, gf, gh, ready2)

    e_to_y.wait()
    for d in range(4):
        e_y[d] = (e_mid[d, :, rows(y * 256, 256)].astype(f32) + e_in[d].astype(f32)).astype(bf16)
    pix_copies = over_z(e_y, e_sum, pix_sems.at[0], own_sems.at[5])

    place = lax.broadcasted_iota(jnp.int32, (128, mid), 0) % 32

    def across(i, a):
        beta = i % COL_CLASSES
        two_on = (beta + 2) % 4 * 128
        here = slice(beta * 128, (beta + 1) * 128)
        there = slice(two_on, two_on + 128)
        lane = lambda b: slice((3 * a + b) * mid, (3 * a + b + 1) * mid)
        left, right = prod[there, lane(0)], prod[there, lane(2)]
        if beta >= 2:
            left = jnp.where(place == 31, 0.0, pltpu.roll(left, 127, 0))
        else:
            right = jnp.where(place == 0, 0.0, pltpu.roll(right, 1, 0))
        return prod[here, lane(1)] + left + right

    arrived["dilated"].wait()
    for i in range(PHASES):
        at = slice(i * 128, (i + 1) * 128)
        if i % COL_CLASSES == 0:
            prod[...] = lax.dot_general(
                g2[i * 128 : (i + COL_CLASSES) * 128], dilated[...], contract1, preferred_element_type=f32
            )
        up, same, down = across(i, 0), across(i, 1), across(i, 2)
        zero = jnp.zeros((32, mid), f32)
        hidden[at] = same + jnp.concatenate([up[32:], zero]) + jnp.concatenate([zero, down[:96]])
        edges[0, i] = up[:32].astype(bf16)
        edges[1, i] = down[96:].astype(bf16)
    first, last = p == 0, p == PHASES - 1
    to_next = lambda: pltpu.make_async_remote_copy(
        src_ref=edges.at[1], dst_ref=edges.at[2], send_sem=edge_sems.at[0, 0], recv_sem=edge_sems.at[1, 0],
        device_id=(p + 1, c), device_id_type=MESH,
    )
    to_last = lambda: pltpu.make_async_remote_copy(
        src_ref=edges.at[0], dst_ref=edges.at[3], send_sem=edge_sems.at[0, 1], recv_sem=edge_sems.at[1, 1],
        device_id=(p - 1, c), device_id_type=MESH,
    )

    @pl.when(jnp.logical_not(last))
    def _():
        to_next().start()

    @pl.when(jnp.logical_not(first))
    def _():
        to_last().start()

    @pl.when(first)
    def _():
        edges[2] = jnp.zeros((PHASES, 32, mid), bf16)

    @pl.when(last)
    def _():
        edges[3] = jnp.zeros((PHASES, 32, mid), bf16)

    for copy in own_taps:
        copy.wait()
    value = jnp.concatenate(
        [
            lax.dot_general(g2[...], moved[0], contract0, preferred_element_type=f32).astype(bf16),
            lax.dot_general(
                g2[...], moved[1, :, : taps.shape[1] - cut], contract0, preferred_element_type=f32
            ).astype(bf16),
        ],
        axis=1,
    )
    out_rows = SPLIT * mid // PHASES
    for d in range(PHASES):
        d_part[d % 2, d // 2] = value[d * out_rows : (d + 1) * out_rows]
    d_to_y = push(d_part.at[1 - y], d_in, pair_sems.at[0, 1], pair_sems.at[1, 1], (p ^ 1, c))

    @pl.when(jnp.logical_not(last))
    def _():
        to_next().wait_send()
        to_last().wait_recv()

    @pl.when(jnp.logical_not(first))
    def _():
        to_last().wait_send()
        to_next().wait_recv()

    send_parts(PACE[2], PACE[3])

    bias, gain = jnp.zeros((8, mid), f32), jnp.zeros((8, mid), f32)
    for i in range(PHASES):
        at = slice(i * 128, (i + 1) * 128)
        zero = jnp.zeros((64, mid), f32)
        edge = jnp.concatenate([edges[2, i].astype(f32), zero, edges[3, i].astype(f32)])
        grad = (hidden[at] + edge) * slope1[at]
        gp1[at] = grad
        bias, gain = bias + fold(grad), gain + fold(grad * norm1[at])
    packed_sums((total(bias), total(gain)), st1)
    pix_exchange(st1, st1r, st_sems.at[2])
    send_parts(PACE[3], 27)
    sums1 = unpacked_sums(st1r, 1, 2)
    sums_out[4:5, :mid] = sums1[0]
    sums_out[5:6, :mid] = sums1[1]

    def ready1(t):
        def step(i, carry):
            at = rows(t * tile + i * 128, 128)
            value = norm_back(gp1[at], norm1[at], sums1, stats1[1:2], gain1[...], valid[at])
            g1[at, rows(c * mid, mid)] = value.astype(bf16)
            return carry

        loop(tile // 128, step, 0)

    late = []

    def between():
        for copy in all_inputs:
            copy.wait()
        own_g1 = g1[:, rows(c * mid, mid)]
        for i in range(SPLIT):
            value = lax.dot_general(wide[2 * i, :, :n], own_g1[:n], contract0, preferred_element_type=f32)
            value = value + lax.dot_general(wide[2 * i + 1, :, :n], own_g1[n:], contract0, preferred_element_type=f32)
            r_mid[i] = value.astype(bf16).reshape(2, 256, mid)
        late.append(push(r_mid.at[:, 1 - y], r_in, pair_sems.at[0, 2], pair_sems.at[1, 2], (p ^ 1, c)))
        d_to_y.wait()
        for d in range(4):
            d_y[d // 2, d % 2] = (d_part[y, d].astype(f32) + d_in[d].astype(f32)).astype(bf16)
        late.append(push(d_y.at[:, 1 - lower], d_near, mid_sems.at[0, 0], mid_sems.at[1, 0], (p ^ 2, c)))

    gather_over_ch(g1, mid, tile, TILES, gn1, gf1, gh1, ready1, between)
    late[0].wait()
    for d in range(4):
        r_y[d] = (r_mid[d, y].astype(f32) + r_in[d].astype(f32)).astype(bf16)
    pix_copies += over_z(r_y, r_sum, pix_sems.at[2], own_sems.at[7])

    arrived["reduce"].wait()
    for i in range(PHASES):
        at = slice(i * 128, (i + 1) * 128)
        value = lax.dot_general(g1[at], reduce_rows[...], contract1, preferred_element_type=f32) + gp3[at]
        value = value * spread_lanes(valid[at], n)
        for g in range(n // 128):
            for r in range(4):
                start = (2 * r + i // COL_CLASSES) * 128 + i % COL_CLASSES
                lanes[g, pl.ds(start, 32, stride=COL_CLASSES), :] = value[r * 32 : (r + 1) * 32, g * 128 : (g + 1) * 128]
    for g in range(n // 128):
        features_grad[:, g * 128 : (g + 1) * 128] = lanes[g].astype(bf16)
    late[1].wait()
    for d in range(2):
        d_sum[d] = (d_y[d, lower].astype(f32) + d_near[d].astype(f32)).astype(bf16)
    d_last = push(d_sum.at[1 - upper], d_far, mid_sems.at[0, 1], mid_sems.at[1, 1], (p ^ 4, c))
    for copy in pix_copies:
        copy.wait()

    def gathered(parts):
        value = parts[0].astype(f32)
        for d in range(1, parts.shape[0]):
            value = value + parts[d].astype(f32)
        return value

    expand_grad[...] = gathered(e_sum)
    reduce_grad[...] = gathered(r_sum)
    d_last.wait()
    value = d_sum[upper].astype(f32) + d_far[...].astype(f32)
    for i in range(9):
        dilated_grad[i] = value[:, i * mid : (i + 1) * mid]
    for copy in zcopies:
        copy.wait()


def run_backward(cid, arrays):
    (grads, trunk, others, weight, norm3, masked, valid, expand, gain3, bias3, norm2, gain2, bias2, full2, taps, dilated,
     norm1, gain1, bias1, reduce_rows, stats1, stats2, stats3, picks, inputs) = arrays
    pixels, n = norm3.shape
    m = weight.shape[4]
    mid = norm2.shape[1]
    all_mid = SPLIT * mid
    outs = [
        shape((pixels, n), bf16),
        shape((2, 27, 32, n), bf16),
        shape((9, all_mid // PHASES, mid), f32),
        shape((mid, 256), f32),
        shape((256, mid), f32),
        shape((8, n), f32),
    ]
    sums = sum_scratch(pixels, mid, TILES)
    scratch = [
        pltpu.VMEM((9, n, 3 * m), bf16),
        pltpu.VMEM((3, pixels, 3 * m), bf16),
        pltpu.VMEM((pixels, m), f32),
        pltpu.VMEM((2, pixels, m), bf16),
        pltpu.VMEM((2, pixels, m), bf16),
        pltpu.VMEM((4, pixels + 128, n), bf16),
        pltpu.VMEM((4, 256, mid), bf16),
        pltpu.VMEM((3, 192, pixels), bf16),
        pltpu.VMEM((3, 192, 4 * pixels), bf16),
        pltpu.VMEM((2, 27, 32, n), bf16),
        pltpu.VMEM((4, 256, mid), bf16),
        pltpu.VMEM((pixels, n), f32),
        pltpu.VMEM((pixels, n), bf16),
        *sums[:4],
        pltpu.VMEM((pixels, mid), f32),
        pltpu.VMEM((pixels, mid), f32),
        pltpu.VMEM((pixels, all_mid), bf16),
        pltpu.VMEM((pixels // ROW_CLASSES, 9 * mid), f32),
        pltpu.VMEM((4, PHASES, 32, mid), bf16),
        pltpu.VMEM((pixels, all_mid), bf16),
        pltpu.VMEM((8, 128), f32),
        pltpu.VMEM((PHASES, 8, 128), f32),
        pltpu.VMEM((8, 128), f32),
        pltpu.VMEM((PHASES, 8, 128), f32),
        pltpu.VMEM((8, 128), f32),
        pltpu.VMEM((PHASES, 8, 128), f32),
        pltpu.VMEM((SPLIT, mid, n), bf16),
        pltpu.VMEM((SPLIT, mid, n), bf16),
        pltpu.VMEM((4, mid, 256), bf16),
        pltpu.VMEM((4, mid, 256), bf16),
        pltpu.VMEM((4, mid, 256), bf16),
        pltpu.VMEM((2, 4, all_mid // PHASES, 9 * mid), bf16),
        pltpu.VMEM((4, all_mid // PHASES, 9 * mid), bf16),
        pltpu.VMEM((2, 2, all_mid // PHASES, 9 * mid), bf16),
        pltpu.VMEM((2, all_mid // PHASES, 9 * mid), bf16),
        pltpu.VMEM((4, 2, 256, mid), bf16),
        pltpu.VMEM((4, 256, mid), bf16),
        dma(9, 3),
        dma(2, 2, PHASES),
        dma(3, 4),
        dma(2, 27),
        dma(1, 2, TILES, 2),
        dma(1, 2, TILES),
        dma(3, 2, PHASES),
        *gather_scratch(TILES),
        *gather_scratch(TILES),
        dma(2, 2),
        dma(2, 2, SPLIT),
        dma(3, 2, PHASES),
        dma(2, 3),
        dma(8),
        dma(2),
        dma(8),
        dma(4, 2, 2),
        dma(2, 2, 2),
        pltpu.VMEM((pixels, mid), f32),
        pltpu.VMEM((2, all_mid // PHASES, 9 * mid), bf16),
        pltpu.VMEM((all_mid // PHASES, 9 * mid), bf16),
        dma(2, 2),
        pltpu.VMEM((pixels, 128), f32),
        pltpu.VMEM((pixels, n), f32),
        pltpu.VMEM((pixels, n), bf16),
        pltpu.VMEM((all_mid, n), bf16),
        pltpu.VMEM((pixels, mid), f32),
        pltpu.VMEM((pixels, all_mid), bf16),
        pltpu.VMEM((pixels, mid), f32),
        pltpu.VMEM((9 * mid, all_mid), bf16),
        pltpu.VMEM((n, all_mid), bf16),
        dma(9),
    ]
    vmem = pl.BlockSpec(memory_space=pltpu.VMEM)
    specs = [vmem] * len(arrays)
    for i in (1, 2, 3, 4, 5, 6, 7, 10, 13, 14, 15, 16, 19, 24):
        specs[i] = pl.BlockSpec(memory_space=pl.ANY)
    return pl.pallas_call(
        backward,
        out_shape=outs,
        in_specs=specs,
        out_specs=[vmem, pl.BlockSpec(memory_space=pl.ANY)] + [vmem] * (len(outs) - 2),
        scratch_shapes=scratch,
        compiler_params=pltpu.CompilerParams(
            collective_id=cid, has_side_effects=True, vmem_limit_bytes=VMEM_BYTES
        ),
        name="backward",
    )(*arrays)


def publish(features, parts, dilated, expand, reduce, norm_sums, predictions, head_grad, branch_sums, *outs):
    (o_predictions, o_features, o_reduce, o_gain1, o_bias1, o_dilated, o_gain2, o_bias2, o_expand, o_gain3, o_bias3,
     o_parts, o_branch_gain, o_branch_bias, o_heads) = outs
    c = lax.axis_index("ch")
    columns, mid = o_predictions.shape[0], o_gain1.shape[1]
    m = o_heads.shape[2]
    o_features[...] = features[...]
    o_reduce[...] = reduce[...]
    o_expand[...] = expand[...]
    o_dilated[...] = dilated[...]
    for i in range(parts.shape[1]):
        o_parts[i] = parts[0, i].astype(f32) + parts[1, i].astype(f32)
    o_bias3[...] = norm_sums[0:1]
    o_gain3[...] = norm_sums[1:2]
    o_bias2[...] = norm_sums[2:3, :mid]
    o_gain2[...] = norm_sums[3:4, :mid]
    o_bias1[...] = norm_sums[4:5, :mid]
    o_gain1[...] = norm_sums[5:6, :mid]

    def own(value):
        return jnp.where(lax.rem(c, 2) == 1, value[:, m:], value[:, :m])

    lanes = rows(c // 2 * 2 * m, 2 * m)
    value = own(branch_sums[:, lanes])
    o_branch_bias[...] = value[0:3]
    o_branch_gain[...] = value[3:6]
    for j in range(3):
        value = own(head_grad[:, rows(j * SPLIT * m + c // 2 * 2 * m, 2 * m)])
        o_heads[j] = value[:columns]
    place = jnp.where(
        one_hot(512, 512, lambda i: i % 128 // 32 * 128 + 4 * (i % 32) + i // 128), 1.0, 0.0
    ).astype(bf16)
    for a in range(ROW_CLASSES):
        value = jnp.concatenate([predictions[a * COL_CLASSES + b] for b in range(COL_CLASSES)], axis=1)
        high = value.astype(bf16)
        rest = value - high.astype(f32)
        middle = rest.astype(bf16)
        low = (rest - middle.astype(f32)).astype(bf16)
        value = jnp.dot(jnp.concatenate([high, middle, low]), place, preferred_element_type=f32)
        value = value[:32] + (value[32:64] + value[64:])
        for r in range(4):
            o_predictions[:, 2 * r + a, :] = value[:columns, r * 128 : (r + 1) * 128]


def run_publish(columns, m, arrays):
    features, parts, dilated, expand, reduce = arrays[:5]
    n, mid = features.shape[1], reduce.shape[1]
    outs = [
        shape((columns, 8, 128), f32),
        shape(features.shape, bf16),
        shape(reduce.shape, f32),
        shape((1, mid), f32),
        shape((1, mid), f32),
        shape(dilated.shape, f32),
        shape((1, mid), f32),
        shape((1, mid), f32),
        shape(expand.shape, f32),
        shape((1, n), f32),
        shape((1, n), f32),
        shape(parts.shape[1:], f32),
        shape((3, m), f32),
        shape((3, m), f32),
        shape((3, columns, m), f32),
    ]
    vmem = pl.BlockSpec(memory_space=pltpu.VMEM)
    return pl.pallas_call(
        publish,
        out_shape=outs,
        in_specs=[vmem] * len(arrays),
        out_specs=[vmem] * len(outs),
        compiler_params=pltpu.CompilerParams(vmem_limit_bytes=VMEM_BYTES),
        name="publish",
    )(*arrays)


def fast_device(
    features,
    pixel_mask,
    reduce_weight,
    reduce_gain,
    reduce_bias,
    dilated_weight,
    dilated_gain,
    dilated_bias,
    expand_weight,
    expand_gain,
    expand_bias,
    aspp_weight,
    aspp_gain,
    aspp_bias,
    task_weight,
    cotangent,
):
    rows_here, width, local_in = features.shape
    pixels = rows_here * width
    local_mid = reduce_weight.shape[1]
    full_mid = dilated_weight.shape[3]
    branch_width = aspp_weight.shape[4]
    own_branch = task_weight.shape[1]
    outs_count = task_weight.shape[2]
    line = lambda v: v.reshape(1, -1)
    dilated_rows = dilated_weight.reshape(9 * local_mid, full_mid)
    (
        masked, reduce_rows, expand_cols, norm_one, valid, norm_two, act_two_full, taps_one, norm_three, trunk_class,
        stat_one, stat_two, stat_three, inputs_all, grad_full, predictions, head_grad, branch_sums, trunk_others, picks,
    ) = run_forward(
        1,
        features.reshape(pixels, local_in),
        pixel_mask,
        reduce_weight,
        expand_weight,
        line(reduce_gain),
        line(reduce_bias),
        task_weight.transpose(0, 2, 1),
        aspp_gain,
        aspp_bias,
        cotangent.transpose(2, 0, 1).reshape(outs_count, pixels),
        dilated_rows,
        line(dilated_gain),
        line(dilated_bias),
        line(expand_gain),
        line(expand_bias),
        aspp_weight,
    )
    features_grad, aspp_parts, dilated_sum, expand_weight_grad, reduce_weight_grad, norm_sums = run_backward(
        2,
        [
            grad_full, trunk_class, trunk_others, aspp_weight, norm_three, masked, valid, expand_cols,
            line(expand_gain), line(expand_bias), norm_two, line(dilated_gain), line(dilated_bias), act_two_full,
            taps_one, dilated_rows, norm_one, line(reduce_gain), line(reduce_bias), reduce_rows, stat_one, stat_two,
            stat_three, picks, inputs_all,
        ],
    )
    (
        predictions, features_grad, reduce_weight_grad, reduce_gain_grad, reduce_bias_grad, dilated_weight_grad,
        dilated_gain_grad, dilated_bias_grad, expand_weight_grad, expand_gain_grad, expand_bias_grad, aspp_weight_grad,
        aspp_gain_grad, aspp_bias_grad, task_weight_grad,
    ) = run_publish(
        outs_count,
        own_branch,
        [
            features_grad, aspp_parts, dilated_sum, expand_weight_grad, reduce_weight_grad, norm_sums, predictions,
            head_grad, branch_sums,
        ],
    )
    return (
        predictions.transpose(1, 2, 0),
        features_grad.reshape(rows_here, width, local_in),
        reduce_weight_grad,
        reduce_gain_grad.reshape(-1),
        reduce_bias_grad.reshape(-1),
        dilated_weight_grad.reshape(3, 3, -1, local_mid).transpose(0, 1, 3, 2),
        dilated_gain_grad.reshape(-1),
        dilated_bias_grad.reshape(-1),
        expand_weight_grad,
        expand_gain_grad.reshape(-1),
        expand_bias_grad.reshape(-1),
        aspp_weight_grad.reshape(3, 3, 3, -1, local_in).transpose(0, 1, 2, 4, 3),
        aspp_gain_grad,
        aspp_bias_grad,
        task_weight_grad.transpose(0, 2, 1),
    )


def solution(mesh):
    placed = (
        P("pix", None, "ch"),
        P("pix", None),
        P(None, "ch"),
        P("ch"),
        P("ch"),
        P(None, None, "ch", None),
        P("ch"),
        P("ch"),
        P("ch", None),
        P("ch"),
        P("ch"),
        P(None, None, None, "ch", None),
        P(None, "ch"),
        P(None, "ch"),
        P(None, "ch", None),
        P("pix", None, None),
    )
    return jax.shard_map(
        fast_device if (mesh.shape["pix"], mesh.shape["ch"]) == (PHASES, 4) else on_device,
        mesh=mesh,
        in_specs=placed,
        out_specs=(
            P("pix", None, None),
            P("pix", None, "ch"),
            P("pix", "ch"),
            P("ch"),
            P("ch"),
            P(None, None, "ch", "pix"),
            P("ch"),
            P("ch"),
            P("ch", "pix"),
            P("ch"),
            P("ch"),
            P(None, None, None, "ch", "pix"),
            P(None, "ch"),
            P(None, "ch"),
            P(None, "ch", None),
        ),
        check_vma=False,
    )
```

```python
import jax
import jax.numpy as jnp
from jax import lax
from jax.experimental import pallas as pl
from jax.experimental.pallas import tpu as pltpu
from jax.sharding import PartitionSpec as P

CLS = 19


epsilon = 1e-05
highest = lax.Precision.HIGHEST
aspp_rates = (12, 24, 36)
inner_rate = 2


def from_behind(value, axis, steps):
    count = lax.axis_size(axis)
    first, last = (max(0, -steps), min(count, count - steps))
    return lax.ppermute(value, axis, [(source, source + steps) for source in range(first, last)])


def with_halo(shard, sides, width):
    for axis, dim in sides:
        devices, length = (lax.axis_size(axis), shard.shape[dim])
        up = [(i, (i + 1) % devices) for i in range(devices - 1)]
        down = [(j, i) for i, j in up]
        last = lax.slice_in_dim(shard, length - width, length, axis=dim)
        first = lax.slice_in_dim(shard, 0, width, axis=dim)
        before = lax.ppermute(last, axis, up)
        after = lax.ppermute(first, axis, down)
        shard = jnp.concatenate([before, shard, after], axis=dim)
    return shard


def silu_slope(value):
    sigma = jax.nn.sigmoid(value)
    return sigma * (1.0 + value * (1.0 - sigma))


def shift_cols(value, offset):
    if offset == 0:
        return value
    margin = abs(offset)
    widths = [(0, 0)] * value.ndim
    widths[1] = (margin, margin)
    padded = jnp.pad(value, widths)
    return lax.slice_in_dim(padded, margin + offset, margin + offset + value.shape[1], axis=1)


def moved(piece, distance):
    return from_behind(piece, "pix", -distance)


def shift_rows(value, offset):
    if offset == 0:
        return value
    steps_over, inner = divmod(offset, value.shape[0])
    first = moved(value, steps_over)[inner:]
    if inner == 0:
        return first
    second = moved(value, steps_over + 1)[:inner]
    return jnp.concatenate([first, second], axis=0)


def halo_rows(value):
    return with_halo(value, (("pix", 0),), inner_rate)


def gather_channels(value):
    return lax.all_gather(value, "ch", axis=1, tiled=True)


def sum_channels(value):
    return lax.psum_scatter(
        value.astype(jnp.bfloat16), "ch", scatter_dimension=1, tiled=True
    ).astype(jnp.float32)


def normalized(hidden, valid, axes):
    total, count = lax.psum(
        (jnp.sum(hidden * valid, axis=axes, keepdims=True), jnp.sum(valid)), "pix"
    )
    center = total / count
    spread_sum = lax.psum(jnp.sum(valid * (hidden - center) ** 2, axis=axes, keepdims=True), "pix")
    variance = spread_sum / count
    scale = lax.rsqrt(variance + epsilon)
    return ((hidden - center) * scale, scale, count)


def norm_grad(grad_out, centered, scale, gain, count, valid, axes):
    sum_out, sum_cross = lax.psum(
        (
            jnp.sum(grad_out, axis=axes, keepdims=True),
            jnp.sum(grad_out * centered, axis=axes, keepdims=True),
        ),
        "pix",
    )
    grad_in = gain * scale * (grad_out - valid * (sum_out + centered * sum_cross) / count)
    return (grad_in, sum_cross, sum_out)


def task_scales(gram):
    norms = jnp.sqrt(jnp.diagonal(gram) + 1e-06)
    proj = gram / norms[None, :]
    vector = proj[0, 0] - proj[0, 1:]
    matrix = proj[0, 0] - proj[0, 1:][None, :] - proj[1:, 0][:, None] + proj[1:, 1:]
    determinant = matrix[0, 0] * matrix[1, 1] - matrix[0, 1] * matrix[1, 0]
    second = (vector[0] * matrix[1, 1] - vector[1] * matrix[1, 0]) / determinant
    third = (vector[1] * matrix[0, 0] - vector[0] * matrix[0, 1]) / determinant
    return jnp.stack([1.0 - second - third, second, third])


def on_device(
    features,
    pixel_mask,
    reduce_weight,
    reduce_gain,
    reduce_bias,
    dilated_weight,
    dilated_gain,
    dilated_bias,
    expand_weight,
    expand_gain,
    expand_bias,
    aspp_weight,
    aspp_gain,
    aspp_bias,
    task_weight,
    cotangent,
):
    rows_here, width, local_in = features.shape
    pixels = rows_here * width
    local_mid = reduce_weight.shape[1]
    full_mid = dilated_weight.shape[3]
    branch_width = aspp_weight.shape[4]
    outs_count = task_weight.shape[2]
    valid = pixel_mask.astype(jnp.float32).reshape(pixels, 1)
    valid_branch = valid[None]
    masked = features.reshape(pixels, local_in) * valid.astype(jnp.bfloat16)
    inputs_full = gather_channels(masked)
    hidden_one = jnp.dot(inputs_full, reduce_weight, preferred_element_type=jnp.float32)
    norm_one, scale_one, count = normalized(hidden_one, valid, (0,))
    pre_one = norm_one * reduce_gain + reduce_bias
    act_one = (jax.nn.silu(pre_one) * valid).astype(jnp.bfloat16)
    padded_one = halo_rows(act_one.reshape(rows_here, width, local_mid))
    partial_value = jnp.zeros((pixels, full_mid), jnp.float32)
    for a in range(3):
        for b in range(3):
            shifted = shift_cols(padded_one[2 * a : 2 * a + rows_here], (b - 1) * inner_rate)
            partial_value = partial_value + jnp.dot(
                shifted.reshape(pixels, local_mid),
                dilated_weight[a, b],
                preferred_element_type=jnp.float32,
            )
    hidden_two = sum_channels(partial_value)
    norm_two, scale_two, _ = normalized(hidden_two, valid, (0,))
    pre_two = norm_two * dilated_gain + dilated_bias
    act_two = (jax.nn.silu(pre_two) * valid).astype(jnp.bfloat16)
    hidden_three = sum_channels(jnp.dot(act_two, expand_weight, preferred_element_type=jnp.float32))
    norm_three, scale_three, _ = normalized(hidden_three, valid, (0,))
    pre_three = norm_three * expand_gain + expand_bias + masked.astype(jnp.float32)
    trunk_out = (
        (jax.nn.silu(pre_three) * valid).astype(jnp.bfloat16).reshape(rows_here, width, local_in)
    )
    kept_rows = []
    partials = []
    for j in range(3):
        rate = aspp_rates[j]
        running = jnp.zeros((pixels, branch_width), jnp.float32)
        shifted_rows = []
        for a in range(3):
            row_shift = shift_rows(trunk_out, (a - 1) * rate)
            shifted_rows.append(row_shift)
            for b in range(3):
                shifted = shift_cols(row_shift, (b - 1) * rate)
                running = running + jnp.dot(
                    shifted.reshape(pixels, local_in),
                    aspp_weight[j, a, b],
                    preferred_element_type=jnp.float32,
                )
        kept_rows.append(shifted_rows)
        partials.append(running)
    branch_sum = sum_channels(jnp.stack(partials).reshape(3 * pixels, branch_width)).reshape(
        3, pixels, -1
    )
    branch_gain = aspp_gain[:, None, :]
    norm_branch, scale_branch, _ = normalized(branch_sum, valid_branch, (1,))
    pre_branch = norm_branch * branch_gain + aspp_bias[:, None, :]
    branch_out = (jax.nn.silu(pre_branch) * valid_branch).astype(jnp.bfloat16)
    predictions = lax.psum(
        jnp.einsum(
            "jpc,jco->po", branch_out, task_weight, preferred_element_type=jnp.float32
        ).astype(jnp.bfloat16),
        "ch",
    ).astype(jnp.float32)
    columns = jnp.arange(outs_count)
    task_of = (columns >= CLS).astype(jnp.int32) + (columns >= CLS + 1).astype(jnp.int32)
    select = (task_of[:, None] == jnp.arange(3)[None, :]).astype(jnp.float32)
    target = cotangent.reshape(pixels, outs_count) * valid
    task_float = task_weight.astype(jnp.float32)
    task_grads = jnp.einsum("po,ot,jco->tjpc", target, select, task_float, precision=highest)
    gram = lax.psum(
        jnp.einsum("tjpc,sjpc->ts", task_grads, task_grads, precision=highest), ("pix", "ch")
    )
    scales = task_scales(gram)
    branch_grad = jnp.einsum("t,tjpc->jpc", scales, task_grads, precision=highest)
    task_weight_grad = lax.psum(
        jnp.einsum("jpc,po->jco", branch_out.astype(jnp.float32), target, precision=highest), "pix"
    )
    grad_pre_branch = branch_grad * valid_branch * silu_slope(pre_branch)
    grad_branch, aspp_gain_grad, aspp_bias_grad = norm_grad(
        grad_pre_branch, norm_branch, scale_branch, branch_gain, count, valid_branch, (1,)
    )
    grad_full = gather_channels(grad_branch.astype(jnp.bfloat16).reshape(3 * pixels, -1)).reshape(
        3, rows_here, width, -1
    )
    grad_trunk = jnp.zeros((pixels, local_in), jnp.float32)
    aspp_list = []
    for j in range(3):
        rate = aspp_rates[j]
        grad_flat = grad_full[j].reshape(pixels, -1)
        per_row = []
        for a in range(3):
            back_rows = shift_rows(grad_full[j], -(a - 1) * rate)
            per_col = []
            for b in range(3):
                shifted = shift_cols(back_rows, -(b - 1) * rate)
                grad_trunk = grad_trunk + jnp.einsum(
                    "pa,ca->pc",
                    shifted.reshape(pixels, -1),
                    aspp_weight[j, a, b],
                    preferred_element_type=jnp.float32,
                )
                forward_tap = shift_cols(kept_rows[j][a], (b - 1) * rate).reshape(pixels, local_in)
                per_col.append(
                    jnp.einsum(
                        "pc,pa->ca", forward_tap, grad_flat, preferred_element_type=jnp.float32
                    )
                )
            per_row.append(jnp.stack(per_col))
        aspp_list.append(jnp.stack(per_row))
    aspp_weight_local = jnp.stack(aspp_list)
    grad_pre_three = grad_trunk * valid * silu_slope(pre_three)
    grad_three, expand_gain_grad, expand_bias_grad = norm_grad(
        grad_pre_three, norm_three, scale_three, expand_gain, count, valid, (0,)
    )
    grad_three_full = gather_channels(grad_three.astype(jnp.bfloat16))
    grad_act_two = jnp.einsum(
        "pc,dc->pd", grad_three_full, expand_weight, preferred_element_type=jnp.float32
    )
    expand_weight_local = jnp.einsum(
        "pd,pc->dc", act_two, grad_three_full, preferred_element_type=jnp.float32
    )
    grad_pre_two = grad_act_two * valid * silu_slope(pre_two)
    grad_two, dilated_gain_grad, dilated_bias_grad = norm_grad(
        grad_pre_two, norm_two, scale_two, dilated_gain, count, valid, (0,)
    )
    grad_two_full = gather_channels(grad_two.astype(jnp.bfloat16))
    padded_grad = halo_rows(grad_two_full.reshape(rows_here, width, full_mid))
    grad_act_one = jnp.zeros((pixels, local_mid), jnp.float32)
    dilated_rows = []
    for a in range(3):
        dilated_cols = []
        for b in range(3):
            shifted = shift_cols(
                padded_grad[4 - 2 * a : 4 - 2 * a + rows_here], -(b - 1) * inner_rate
            )
            grad_act_one = grad_act_one + jnp.einsum(
                "pe,de->pd",
                shifted.reshape(pixels, full_mid),
                dilated_weight[a, b],
                preferred_element_type=jnp.float32,
            )
            forward_tap = shift_cols(
                padded_one[2 * a : 2 * a + rows_here], (b - 1) * inner_rate
            ).reshape(pixels, local_mid)
            dilated_cols.append(
                jnp.einsum(
                    "pd,pe->de", forward_tap, grad_two_full, preferred_element_type=jnp.float32
                )
            )
        dilated_rows.append(jnp.stack(dilated_cols))
    dilated_weight_local = jnp.stack(dilated_rows)
    grad_pre_one = grad_act_one * valid * silu_slope(pre_one)
    grad_one, reduce_gain_grad, reduce_bias_grad = norm_grad(
        grad_pre_one, norm_one, scale_one, reduce_gain, count, valid, (0,)
    )
    grad_one_low = grad_one.astype(jnp.bfloat16)
    input_sum = sum_channels(
        jnp.einsum("pd,cd->pc", grad_one_low, reduce_weight, preferred_element_type=jnp.float32)
    )
    features_grad = (
        ((input_sum + grad_pre_three) * valid)
        .astype(jnp.bfloat16)
        .reshape(rows_here, width, local_in)
    )
    reduce_weight_local = jnp.einsum(
        "pc,pd->cd", inputs_full, grad_one_low, preferred_element_type=jnp.float32
    )
    reduce_weight_grad, dilated_weight_grad, expand_weight_grad, aspp_weight_grad = (
        lax.psum_scatter(reduce_weight_local, "pix", scatter_dimension=0, tiled=True),
        lax.psum_scatter(dilated_weight_local, "pix", scatter_dimension=3, tiled=True),
        lax.psum_scatter(expand_weight_local, "pix", scatter_dimension=1, tiled=True),
        lax.psum_scatter(aspp_weight_local, "pix", scatter_dimension=4, tiled=True),
    )
    return (
        predictions.reshape(rows_here, width, outs_count),
        features_grad,
        reduce_weight_grad,
        reduce_gain_grad.reshape(-1),
        reduce_bias_grad.reshape(-1),
        dilated_weight_grad,
        dilated_gain_grad.reshape(-1),
        dilated_bias_grad.reshape(-1),
        expand_weight_grad,
        expand_gain_grad.reshape(-1),
        expand_bias_grad.reshape(-1),
        aspp_weight_grad,
        aspp_gain_grad.reshape(3, -1),
        aspp_bias_grad.reshape(3, -1),
        task_weight_grad,
    )


MESH = pl.DeviceIdType.MESH
ROW_CLASSES, COL_CLASSES = 2, 4
PHASES = ROW_CLASSES * COL_CLASSES
SPLIT = 4
FAR_FIRST = (1, 2, 3, 4, 5, 6, 7)
f32, bf16 = jnp.float32, jnp.bfloat16
VMEM_BYTES = 60 << 20


def shape(dims, dtype):
    return jax.ShapeDtypeStruct(dims, dtype)


def call(name, cid, kernel, arrays, outs, scratch, hbm_ins=(), hbm_outs=()):
    vmem, hbm = pl.BlockSpec(memory_space=pltpu.VMEM), pl.BlockSpec(memory_space=pl.ANY)
    return pl.pallas_call(
        kernel,
        out_shape=outs,
        in_specs=[hbm if i in hbm_ins else vmem for i in range(len(arrays))],
        out_specs=[hbm if i in hbm_outs else vmem for i in range(len(outs))],
        scratch_shapes=scratch,
        compiler_params=pltpu.CompilerParams(
            collective_id=cid, has_side_effects=True, vmem_limit_bytes=VMEM_BYTES
        ),
        name=name,
    )(*arrays)


def dma(*dims):
    return pltpu.SemaphoreType.DMA(dims)


def greet(ch, pix):
    p, c = lax.axis_index("pix"), lax.axis_index("ch")
    barrier = pltpu.get_barrier_semaphore()
    for k in ch:
        pl.semaphore_signal(barrier, inc=1, device_id=(p, c ^ k), device_id_type=MESH)
    for k in pix:
        pl.semaphore_signal(barrier, inc=1, device_id=(p ^ k, c), device_id_type=MESH)
    return barrier, len(ch) + len(pix)


def push(src, dst, send, recv, device):
    copy = pltpu.make_async_remote_copy(
        src_ref=src,
        dst_ref=dst,
        send_sem=send,
        recv_sem=recv,
        device_id=device,
        device_id_type=MESH,
    )
    copy.start()
    return copy


def keep(src, dst, sem):
    copy = pltpu.make_async_copy(src, dst, sem)
    copy.start()
    return copy


def rows(start, size):
    return pl.ds(pl.multiple_of(start, size), size)


def fold(x):
    return jnp.sum(x.reshape(x.shape[0] // 8, 8, x.shape[1]), axis=0)


def total(x):
    return jnp.sum(x, axis=0, keepdims=True)


def loop(steps, body, init):
    return lax.fori_loop(0, steps, body, init)


def sum_over_ch(part, tile, tiles, own, out, near, cross, near_sems, far_sems):
    p, c = lax.axis_index("pix"), lax.axis_index("ch")
    k, x = lax.rem(c, 2), c // 2
    n = own.shape[2]
    copies = []
    for t in range(tiles):
        at = pl.ds(t * tile, tile)
        value = part(t)
        for d in range(SPLIT):
            block = value[:, d * n : (d + 1) * n]
            own[d, at] = block
            out[d, at] = block.astype(bf16)
        copies.append(
            [
                push(
                    out.at[2 * h + 1 - k, at],
                    near.at[h, at],
                    near_sems.at[0, t, h],
                    near_sems.at[1, t, h],
                    (p, c ^ 1),
                )
                for h in range(2)
            ]
        )
    crossing = []
    for t in range(tiles):
        at = pl.ds(t * tile, tile)
        for copy in copies[t]:
            copy.wait()
        cross[0, at] = (own[2 * (1 - x) + k, at] + near[1 - x, at].astype(f32)).astype(bf16)
        crossing.append(
            push(cross.at[0, at], cross.at[1, at], far_sems.at[0, t], far_sems.at[1, t], (p, c ^ 2))
        )

    def result(t):
        at = pl.ds(t * tile, tile)
        crossing[t].wait()
        return own[2 * x + k, at] + near[x, at].astype(f32) + cross[1, at].astype(f32)

    return result


def sum_scratch(pixels, n, tiles):
    return [
        pltpu.VMEM((SPLIT, pixels, n), f32),
        pltpu.VMEM((SPLIT, pixels, n), bf16),
        pltpu.VMEM((2, pixels, n), bf16),
        pltpu.VMEM((2, pixels, n), bf16),
        dma(2, tiles, 2),
        dma(2, tiles),
    ]


def pix_exchange(send, recv, sems):
    p, c = lax.axis_index("pix"), lax.axis_index("ch")
    copies = [
        push(send, recv.at[p], sems.at[0, k], sems.at[1, k], (p ^ k, c)) for k in FAR_FIRST
    ]
    recv[p] = send[...]
    for copy in copies:
        copy.wait()


def norm_stats(hidden, valid, pixels, send, recv, sems, counted=None):
    n = hidden.shape[1]
    tile = 128
    repeat = n // 128

    def mask(at):
        v = valid[at]
        return v if repeat == 1 else jnp.concatenate([v] * repeat, axis=1)

    def first(i, carry):
        at = rows(i * tile, tile)
        v = mask(at)
        return carry[0] + fold(hidden[at] * v), carry[1] + fold(v)

    zero = jnp.zeros((8, n), f32)
    sums, count = loop(pixels // tile, first, (zero, zero))
    sums, count = total(sums), total(count)
    center = sums / jnp.maximum(count, 1.0)

    def second(i, carry):
        at = rows(i * tile, tile)
        apart = hidden[at] - center
        return carry + fold(mask(at) * apart * apart)

    spread = total(loop(pixels // tile, second, zero))
    if counted is not None:
        groups = n // 128
        for i in range(groups):
            send[i : i + 1] = sums[:, i * 128 : (i + 1) * 128]
            send[groups + i : groups + i + 1] = spread[:, i * 128 : (i + 1) * 128]
        pix_exchange(send, recv, sems)
        sums = [
            jnp.concatenate([recv[d, i : i + 1] for i in range(groups)], axis=1) for d in range(PHASES)
        ]
        spreads = [
            jnp.concatenate([recv[d, groups + i : groups + i + 1] for i in range(groups)], axis=1)
            for d in range(PHASES)
        ]
        counts = [spread_lanes(counted[d, 2:3], n) for d in range(PHASES)]
        return join_parts(sums, spreads, counts)
    send[0:1] = sums
    send[1:2] = spread
    send[2:3] = count
    pix_exchange(send, recv, sems)
    return join(recv, PHASES)


def spread_lanes(v, n):
    return v if n == 128 else jnp.concatenate([v] * (n // 128), axis=1)


def join_parts(sums, spreads, counts):
    whole, count = sums[0], counts[0]
    for i in range(1, len(sums)):
        whole, count = whole + sums[i], count + counts[i]
    center = whole / count
    spread = jnp.zeros_like(whole)
    for i in range(len(sums)):
        apart = sums[i] / jnp.maximum(counts[i], 1.0) - center
        spread = spread + spreads[i] + counts[i] * apart * apart
    return center, lax.rsqrt(spread / count + epsilon), count


def join(recv, parts):
    return join_parts(*[[recv[i, row : row + 1] for i in range(parts)] for row in range(3)])


def stat_scratch(n):
    return [pltpu.VMEM((8, n), f32), pltpu.VMEM((PHASES, 8, n), f32), dma(2, PHASES)]


def silu(x):
    return x / (1.0 + jnp.exp(-x))


def gather_over_ch(full, n, tile, tiles, near_sems, far_sems, hop_sems, ready, between=None):
    p, c = lax.axis_index("pix"), lax.axis_index("ch")

    def part(owner, t):
        return full.at[pl.ds(t * tile, tile), rows(owner * n, n)]

    near, far, hops = [], [], []
    for t in range(tiles):
        ready(t)
        src = part(c, t)
        far.append(push(src, src, far_sems.at[0, t], far_sems.at[1, t], (p, c ^ 2)))
        near.append(push(src, src, near_sems.at[0, t], near_sems.at[1, t], (p, c ^ 1)))
    if between is not None:
        between()
    for t in range(tiles):
        far[t].wait_recv()
        src = part(c ^ 2, t)
        hops.append(push(src, src, hop_sems.at[0, t], hop_sems.at[1, t], (p, c ^ 1)))
    for t in range(tiles):
        far[t].wait_send()
        near[t].wait()
        hops[t].wait()


def gather_scratch(tiles):
    return [dma(2, tiles), dma(2, tiles), dma(2, tiles)]


def to_classes(x):
    rows, cols, n = x.shape
    x = x.reshape(rows // ROW_CLASSES, ROW_CLASSES, cols // COL_CLASSES, COL_CLASSES, n)
    return x.transpose(1, 3, 0, 2, 4).reshape(PHASES, -1, n)


def from_classes(x, rows, cols):
    n = x.shape[-1]
    x = x.reshape(ROW_CLASSES, COL_CLASSES, rows // ROW_CLASSES, cols // COL_CLASSES, n)
    return x.transpose(2, 0, 3, 1, 4).reshape(rows, cols, n)


RATE_ROWS = tuple(rate // ROW_CLASSES for rate in aspp_rates)
RATE_COLS = tuple(rate // COL_CLASSES for rate in aspp_rates)


def load_pyramid(weight, wide, sems):
    m = weight.shape[4]
    return [
        [keep(weight.at[j, a, b], wide.at[3 * j + a, :, b * m : (b + 1) * m], sems.at[3 * j + a, b]) for b in range(3)]
        for j in range(3)
        for a in range(3)
    ]


def move_cols(x, by):
    place = lax.broadcasted_iota(jnp.int32, x.shape, 0) % 32
    rolled = pltpu.roll(x, by % x.shape[0], 0)
    return jnp.where(place < by, 0.0, rolled) if by > 0 else jnp.where(place >= 32 + by, 0.0, rolled)


def ch_exchange(send, recv, sems):
    p, c = lax.axis_index("pix"), lax.axis_index("ch")
    copies = [push(send, recv.at[c], sems.at[0, k], sems.at[1, k], (p, c ^ k)) for k in (2, 3, 1)]
    recv[c] = send[...]
    for copy in copies:
        copy.wait()


def add_up(recv, parts):
    value = recv[0]
    for i in range(1, parts):
        value = value + recv[i]
    return value


def task_vector(square, weights):
    product = square * weights
    row = lax.broadcasted_iota(jnp.int32, (32, 32), 0)
    col = lax.broadcasted_iota(jnp.int32, (32, 32), 1)

    def task(i):
        return (i >= CLS).astype(jnp.int32) + (i >= CLS + 1).astype(jnp.int32)

    def entry(t, s):
        return jnp.sum(
            jnp.sum(jnp.where((task(row) == t) & (task(col) == s), product, 0.0), axis=1, keepdims=True),
            axis=0,
            keepdims=True,
        )

    gram = [[entry(t, s) for s in range(3)] for t in range(3)]
    norms = [jnp.sqrt(gram[k][k] + 1e-06) for k in range(3)]
    proj = [[gram[i][k] / norms[k] for k in range(3)] for i in range(3)]
    vector = [proj[0][0] - proj[0][b] for b in (1, 2)]
    matrix = [[proj[0][0] - proj[0][b] - proj[a][0] + proj[a][b] for b in (1, 2)] for a in (1, 2)]
    determinant = matrix[0][0] * matrix[1][1] - matrix[0][1] * matrix[1][0]
    second = (vector[0] * matrix[1][1] - vector[1] * matrix[1][0]) / determinant
    third = (vector[1] * matrix[0][0] - vector[0] * matrix[0][1]) / determinant
    which = task(lax.broadcasted_iota(jnp.int32, (32, 1), 0))
    return jnp.where(which == 0, 1.0 - second - third, jnp.where(which == 1, second, third))


def slope(x):
    s = 1.0 / (1.0 + jnp.exp(-x))
    return s * (1.0 + x * (1.0 - s))


def pyramid(trunk, loads, wide, moving, pass_inputs, head_copies, heads, heads_all, targets, square, *refs):
    (full, predictions, head_grad, sums, others, picks) = refs[:6]
    (sides, own, out, near, cross, hidden, grad, branch) = refs[6:14]
    (s_send, s_ch, s_mid, s_pix, b_send, b_ch, b_mid, b_pix) = refs[14:22]
    (h_send, h_ch, h_mid, h_pix, h_sum, p_send, p_ch) = refs[22:29]
    (near_sems, far_sems, ch_sems, pix_sems, g_near, g_far, g_hop, y_sems, picked, pick_sems) = refs[29:]
    p, c = lax.axis_index("pix"), lax.axis_index("ch")
    k, x = lax.rem(c, 2), c // 2
    m = wide.shape[2] // 3
    pixels, half = trunk.shape[1], trunk.shape[2]
    quarter = pixels // SPLIT
    contract0 = (((0,), (0,)), ((), ()))
    contract1 = (((1,), (1,)), ((), ()))
    mine = rows(c * quarter, quarter)
    part = pixels // SPLIT
    sharing = []

    def share(slot, quarters, own, k, first):
        for i, q in enumerate(quarters):
            at = pl.ds(q * part, part)
            src = trunk.at[:, at] if own else others.at[2 - k, :, at]
            sharing.append(
                push(src, others.at[slot, :, at], y_sems.at[0, first + i], y_sems.at[1, first + i], (p ^ k, c))
            )
        return sharing[-len(quarters) :]

    def convolve(j, h):
        s = RATE_ROWS[j] * 32
        for a in (1, 0, 2):
            if h == 0:
                for load in loads[3 * j + a]:
                    load.wait()
            w = wide[3 * j + a, h * half : (h + 1) * half]
            if a == 1:
                value = jnp.dot(trunk[h], w, preferred_element_type=f32)
                if h == 0:
                    sides[j] = value
                else:
                    sides[j] += value
            elif a == 0:
                sides[j, s:] += jnp.dot(trunk[h, : pixels - s], w, preferred_element_type=f32)
            else:
                sides[j, : pixels - s] += jnp.dot(trunk[h, s:], w, preferred_element_type=f32)

    for copy in moving[0]:
        copy.wait()
    for j in range(3):
        convolve(j, 0)
    inputs_done = pass_inputs()
    for copy in moving[1]:
        copy.wait()
    from_y = share(0, (0, 1), True, 1, 0)
    from_z = share(1, (2, 3), True, 2, 2)

    def pass_on(i):
        from_y[i].wait_recv()
        share(2, (i,), False, 2, 4 + i)
        from_z[i].wait_recv()
        share(2, (i + 2,), False, 1, 6 + i)

    copies = []
    for j in range(3):
        q = RATE_COLS[j]
        convolve(j, 1)
        if j == 2:
            pass_on(0)
        for d in range(SPLIT):
            at = slice(d * quarter, (d + 1) * quarter)
            value = (
                sides[j, at, m : 2 * m]
                + move_cols(sides[j, at, :m], q)
                + move_cols(sides[j, at, 2 * m :], -q)
            )
            own[d, j] = value
            out[d, j] = value.astype(bf16)
        copies.append(
            [
                push(out.at[2 * h + 1 - k, j], near.at[h, j], near_sems.at[0, j, h], near_sems.at[1, j, h], (p, c ^ 1))
                for h in range(2)
            ]
        )
        if j > 0:
            copies[j - 1] = cross_chips(copies[j - 1], j - 1, own, near, cross, far_sems)
    copies[2] = cross_chips(copies[2], 2, own, near, cross, far_sems)
    for copy in head_copies:
        copy.wait()
    each = m // SPLIT
    for j in range(3):
        for d in range(SPLIT):
            heads[:, (j * SPLIT + d) * each : (j * SPLIT + d + 1) * each] = heads_all[d, :, j * each : (j + 1) * each]
    gain, bias = heads[32:33], heads[33:34]
    head = heads[:32]
    scaled = head * task_vector(
        add_up(square, PHASES)[:, :32], lax.dot_general(head, head, contract1, precision=highest)
    )
    target = jnp.concatenate([targets[2 * c], targets[2 * c + 1]], axis=1)
    mask = lax.dot_general(
        target[24:].astype(bf16), jnp.ones((8, m), bf16), contract0, preferred_element_type=f32
    )
    grad[...] = lax.dot_general(target, scaled, contract0, precision=highest) * jnp.concatenate([mask] * 3, axis=1)
    pass_on(1)
    count = total(mask)
    for j in range(3):
        copies[j].wait()
        value = own[2 * x + k, j] + near[x, j].astype(f32) + cross[1, j].astype(f32)
        at = slice(j * m, (j + 1) * m)
        hidden[:, at] = value
        first = total(value * mask)
        apart = value - first / jnp.maximum(count, 1.0)
        s_send[j : j + 1] = first
        s_send[3 + j : 4 + j] = total(apart * apart * mask)
    s_send[6:7] = count
    s_send[7:8] = jnp.zeros((1, m), f32)

    def merge(recv, parts):
        number = recv[0, 6:7]
        for i in range(1, parts):
            number = number + recv[i, 6:7]
        whole, spread = recv[0, 0:3], recv[0, 3:6]
        for i in range(1, parts):
            whole, spread = whole + recv[i, 0:3], spread + recv[i, 3:6]
        center = whole / jnp.maximum(number, 1.0)
        for i in range(parts):
            n = recv[i, 6:7]
            apart = recv[i, 0:3] / jnp.maximum(n, 1.0) - center
            spread = spread + n * apart * apart
        return whole, spread, number

    ch_exchange(s_send, s_ch, ch_sems.at[0])
    whole, spread, number = merge(s_ch, SPLIT)
    s_mid[0:3] = whole
    s_mid[3:6] = spread
    s_mid[6:7] = number
    s_mid[7:8] = jnp.zeros((1, m), f32)
    pix_exchange(s_mid, s_pix, pix_sems.at[0])
    share(0, (2,), True, 1, 8)
    share(1, (0,), True, 2, 9)
    whole, spread, number = merge(s_pix, PHASES)
    center, scale = whole / number, lax.rsqrt(spread / number + epsilon)
    for j in range(3):
        at = slice(j * m, (j + 1) * m)
        norm = (hidden[:, at] - center[j : j + 1]) * scale[j : j + 1]
        hidden[:, at] = norm
        value = norm * gain[:, at] + bias[:, at]
        branch[:, at] = (silu(value) * mask).astype(bf16)
        back = grad[:, at] * slope(value)
        grad[:, at] = back
        b_send[j : j + 1] = total(back)
        b_send[3 + j : 4 + j] = total(back * norm)
    b_send[6:8] = jnp.zeros((2, m), f32)
    to_ch = [push(b_send, b_ch.at[c], ch_sems.at[3, 0, i], ch_sems.at[3, 1, i], (p, c ^ i)) for i in (2, 3, 1)]
    b_ch[c] = b_send[...]
    high = target.astype(bf16)
    rest = target - high.astype(f32)
    middle = rest.astype(bf16)
    low = (rest - middle.astype(f32)).astype(bf16)
    p_send[...] = lax.dot_general(
        head.astype(bf16), branch[...], contract1, preferred_element_type=f32
    )
    value = jnp.dot(jnp.concatenate([high, middle, low]), branch[...], preferred_element_type=f32)
    h_send[...] = value[:32] + (value[32:64] + value[64:])
    background = [push(p_send, p_ch.at[c], ch_sems.at[1, 0, i], ch_sems.at[1, 1, i], (p, c ^ i)) for i in (2, 3, 1)] + [
        push(h_send.at[rows((c ^ i) * 8, 8)], h_ch.at[c], ch_sems.at[2, 0, i], ch_sems.at[2, 1, i], (p, c ^ i))
        for i in (2, 3, 1)
    ]
    p_ch[c] = p_send[...]
    h_ch[c] = h_send[rows(c * 8, 8)]
    for copy in to_ch:
        copy.wait()
    b_mid[...] = add_up(b_ch, SPLIT)
    sending = [
        push(b_mid, b_pix.at[p], pix_sems.at[1, 0, i], pix_sems.at[1, 1, i], (p ^ i, c)) for i in FAR_FIRST
    ]
    b_pix[p] = b_mid[...]
    for copy in background:
        copy.wait()
    h_mid[...] = add_up(h_ch, SPLIT)

    def block(to):
        return p_ch.at[to // 2, :, rows(lax.rem(to, 2) * 128, 128)]

    background = [
        push(block(p ^ i), predictions.at[p], pix_sems.at[2, 0, i], pix_sems.at[2, 1, i], (p ^ i, c)) for i in FAR_FIRST
    ] + [push(h_mid, h_pix.at[p], pix_sems.at[3, 0, i], pix_sems.at[3, 1, i], (p ^ i, c)) for i in FAR_FIRST]
    predictions[p] = block(p)[...]
    h_pix[p] = h_mid[...]
    for copy in sending:
        copy.wait()
    summed = add_up(b_pix, PHASES)
    sums[...] = summed
    for j in range(3):
        at = slice(j * m, (j + 1) * m)
        value = grad[:, at] - mask * (summed[j : j + 1] + hidden[:, at] * summed[3 + j : 4 + j]) / number
        full[mine, at] = (gain[:, at] * scale[j : j + 1] * value).astype(bf16)
    far = push(full.at[mine], full.at[mine], g_far.at[0], g_far.at[1], (p, c ^ 2))
    by = push(full.at[mine], full.at[mine], g_near.at[0], g_near.at[1], (p, c ^ 1))
    group = lax.rem(p, 4)
    pick = pick_rows(m, m, 0)
    for j in range(3):
        value = lax.dot_general(
            pick, full[mine, j * m : (j + 1) * m], contract1, preferred_element_type=f32
        ).astype(bf16)
        for g in range(4):
            picked[g, j * 64 : (j + 1) * 64] = value[g * 64 : (g + 1) * 64]
    sent_picks = [
        push(picked.at[group ^ i], picks.at[i - 1], pick_sems.at[0, i], pick_sems.at[1, i], (p ^ i, c)) for i in (3, 1, 2)
    ]
    for copy in background:
        copy.wait()
    own_rows = add_up(h_pix, PHASES)
    h_sum[...] = own_rows
    head_grad[rows(c * 8, 8)] = own_rows
    last = [
        push(h_sum, head_grad.at[rows(c * 8, 8)], ch_sems.at[4, 0, i], ch_sems.at[4, 1, i], (p, c ^ i))
        for i in (2, 3, 1)
    ]
    far.wait_recv()
    theirs = rows((c ^ 2) * quarter, quarter)
    hop = push(full.at[theirs], full.at[theirs], g_hop.at[0], g_hop.at[1], (p, c ^ 1))
    far.wait_send()
    by.wait()
    hop.wait()
    for copy in last:
        copy.wait()
    for copy in from_y + from_z:
        copy.wait_send()
    for copy in sharing[4:] + sent_picks:
        copy.wait()
    inputs_done()


def pick_rows(m, count, first):
    row = lax.broadcasted_iota(jnp.int32, (count, m), 0)
    col = lax.broadcasted_iota(jnp.int32, (count, m), 1)
    source = (4 * (row % 64 // 32) + row // 64 + first) * 32 + row % 32
    return jnp.where(col == source, 1.0, 0.0).astype(bf16)


def cross_chips(near_copies, j, own, near, cross, sems):
    p, c = lax.axis_index("pix"), lax.axis_index("ch")
    k, x = lax.rem(c, 2), c // 2
    for copy in near_copies:
        copy.wait()
    cross[0, j] = (own[2 * (1 - x) + k, j] + near[1 - x, j].astype(f32)).astype(bf16)
    return push(cross.at[0, j], cross.at[1, j], sems.at[0, j], sems.at[1, j], (p, c ^ 2))


def pyramid_scratch(pixels, n, m):
    quarter = pixels // SPLIT
    small = [
        pltpu.VMEM((8, m), f32),
        pltpu.VMEM((SPLIT, 8, m), f32),
        pltpu.VMEM((8, m), f32),
        pltpu.VMEM((PHASES, 8, m), f32),
    ]
    return [
        pltpu.VMEM((3, pixels, 3 * m), f32),
        pltpu.VMEM((SPLIT, 3, quarter, m), f32),
        pltpu.VMEM((SPLIT, 3, quarter, m), bf16),
        pltpu.VMEM((2, 3, quarter, m), bf16),
        pltpu.VMEM((2, 3, quarter, m), bf16),
        pltpu.VMEM((quarter, 3 * m), f32),
        pltpu.VMEM((quarter, 3 * m), f32),
        pltpu.VMEM((quarter, 3 * m), bf16),
        *small,
        *small,
        pltpu.VMEM((32, 3 * m), f32),
        pltpu.VMEM((SPLIT, 8, 3 * m), f32),
        pltpu.VMEM((8, 3 * m), f32),
        pltpu.VMEM((PHASES, 8, 3 * m), f32),
        pltpu.VMEM((8, 3 * m), f32),
        pltpu.VMEM((32, quarter), f32),
        pltpu.VMEM((SPLIT, 32, quarter), f32),
        dma(2, 3, 2),
        dma(2, 3),
        dma(5, 2, SPLIT),
        dma(4, 2, PHASES),
        dma(2),
        dma(2),
        dma(2),
        dma(2, 10),
        pltpu.VMEM((4, 192, quarter), bf16),
        dma(2, 4),
    ]


TILES = 4


def one_hot(rows_count, cols_count, source):
    row = lax.broadcasted_iota(jnp.int32, (rows_count, cols_count), 0)
    col = lax.broadcasted_iota(jnp.int32, (rows_count, cols_count), 1)
    return col == source(row)


def stage_one(feat, mask, weight, expand, gain, bias, *refs):
    (masked, reduce_rows, expand_cols, norm, padded, stat, valid) = refs[:7]
    (wide, hidden, own, out, near, cross, near_sems, far_sems, send, recv, stat_sems) = refs[7:18]
    (weight_sems, local_sems, halo_sems) = refs[18:]
    p, c = lax.axis_index("pix"), lax.axis_index("ch")
    pixels, local_in = feat.shape
    local_mid = weight.shape[1]
    tile = pixels // TILES

    def piece(i, to):
        return (
            (weight.at[rows(to * local_in, local_in), :], reduce_rows.at[:, rows(c * local_mid, local_mid)]),
            (expand.at[:, rows(to * local_in, local_in)], expand_cols.at[rows(c * local_mid, local_mid), :]),
        )[i]

    def to_ch(i):
        return [
            push(*piece(i, c ^ k), weight_sems.at[0, k, i], weight_sems.at[1, k, i], (p, c ^ k)) for k in (2, 3, 1)
        ] + [keep(*piece(i, c), local_sems.at[i])]

    reduce_copies = to_ch(0)

    present = mask[...].astype(f32)
    order = one_hot(128, 128, lambda i: 4 * (i % 32) + i // 32)
    ones = jnp.ones((128, 128), bf16)
    for r in range(8):
        column = jnp.dot(
            jnp.where(order, present[r : r + 1], 0.0).astype(bf16), ones, preferred_element_type=f32
        )
        for b in range(COL_CLASSES):
            block = ((r % ROW_CLASSES) * COL_CLASSES + b) * 128 + (r // ROW_CLASSES) * 32
            valid[block : block + 32] = column[b * 32 : (b + 1) * 32]
    for r in range(8):
        for g in range(local_in // 128):
            lanes = slice(g * 128, (g + 1) * 128)
            wide[g] = feat[r * 128 : (r + 1) * 128, lanes].astype(f32)
            for b in range(COL_CLASSES):
                block = ((r % ROW_CLASSES) * COL_CLASSES + b) * 128 + (r // ROW_CLASSES) * 32
                value = wide[g, pl.ds(b, 32, stride=COL_CLASSES), :] * valid[block : block + 32]
                masked[block : block + 32, lanes] = value.astype(bf16)

    for copy in reduce_copies:
        copy.wait()

    def part(t):
        return jnp.dot(masked[t * tile : (t + 1) * tile], reduce_rows[...], preferred_element_type=f32)

    result = sum_over_ch(part, tile, TILES, own, out, near, cross, near_sems, far_sems)
    for t in range(TILES):
        hidden[t * tile : (t + 1) * tile] = result(t)
    later = to_ch(1)
    center, scale, count = norm_stats(hidden, valid, pixels, send, recv, stat_sems)
    stat[0:1] = center
    stat[1:2] = scale
    stat[2:3] = count
    for i in range(PHASES):
        at = pl.ds(i * 128, 128)
        value = (hidden[at] - center) * scale
        norm[at] = value
        act = silu(value * gain[...] + bias[...]) * valid[at]
        padded[i, 1:5] = act.astype(bf16).reshape(4, 32, local_mid)
    up = lambda: pltpu.make_async_remote_copy(
        src_ref=padded.at[:, 4],
        dst_ref=padded.at[:, 0],
        send_sem=halo_sems.at[0, 0],
        recv_sem=halo_sems.at[1, 0],
        device_id=(p + 1, c),
        device_id_type=MESH,
    )
    down = lambda: pltpu.make_async_remote_copy(
        src_ref=padded.at[:, 1],
        dst_ref=padded.at[:, 5],
        send_sem=halo_sems.at[0, 1],
        recv_sem=halo_sems.at[1, 1],
        device_id=(p - 1, c),
        device_id_type=MESH,
    )
    first, last = p == 0, p == PHASES - 1

    @pl.when(jnp.logical_not(last))
    def _():
        up().start()

    @pl.when(jnp.logical_not(first))
    def _():
        down().start()

    @pl.when(last)
    def _():
        padded[:, 5] = jnp.zeros((PHASES, 32, local_mid), bf16)

    @pl.when(first)
    def _():
        padded[:, 0] = jnp.zeros((PHASES, 32, local_mid), bf16)

    @pl.when(jnp.logical_not(last))
    def _():
        up().wait_send()
        down().wait_recv()

    @pl.when(jnp.logical_not(first))
    def _():
        down().wait_send()
        up().wait_recv()

    return later


def prepare_heads(mask, head_weight, head_gain, head_bias, cotangent, *refs):
    (heads_all, targets_all, square_all, heads, targets, square, image, head_sems, pix_sems, local_sems) = refs
    p, c = lax.axis_index("pix"), lax.axis_index("ch")
    contract1 = (((1,), (1,)), ((), ()))
    present = mask[...].astype(f32)
    columns, m = head_weight.shape[1], head_weight.shape[2]
    heads[...] = jnp.zeros(heads.shape, f32)
    for j in range(3):
        heads[:columns, j * m : (j + 1) * m] = head_weight[j].astype(f32)
        heads[32:33, j * m : (j + 1) * m] = head_gain[j : j + 1]
        heads[33:34, j * m : (j + 1) * m] = head_bias[j : j + 1]

    image[...] = jnp.zeros(image.shape, f32)
    for r in range(8):
        at = slice(r * 128, (r + 1) * 128)
        image[:columns, at] = cotangent[:, at] * present[r : r + 1]
        image[31:32, at] = present[r : r + 1]
    square[...] = jnp.zeros(square.shape, f32)
    square[:, :32] = lax.dot_general(
        image[...], image[...], contract1, precision=highest, preferred_element_type=f32
    )
    place = jnp.where(
        one_hot(512, 512, lambda i: i % 4 * 128 + i // 128 * 32 + i % 128 // 4), 1.0, 0.0
    )
    for a in range(ROW_CLASSES):
        some = jnp.concatenate([image[:, (2 * r + a) * 128 : (2 * r + a + 1) * 128] for r in range(4)], axis=1)
        value = jnp.dot(some, place, precision=highest, preferred_element_type=f32)
        for b in range(COL_CLASSES):
            targets[a * COL_CLASSES + b] = value[:, b * 128 : (b + 1) * 128]
    copies = [push(heads, heads_all.at[c], head_sems.at[0, k], head_sems.at[1, k], (p, c ^ k)) for k in (2, 3, 1)]
    copies += [
        push(targets.at[p ^ k], targets_all.at[p], pix_sems.at[0, k, 0], pix_sems.at[1, k, 0], (p ^ k, c))
        for k in FAR_FIRST
    ] + [push(square, square_all.at[p], pix_sems.at[0, k, 1], pix_sems.at[1, k, 1], (p ^ k, c)) for k in FAR_FIRST]
    copies.append(keep(heads, heads_all.at[c], local_sems.at[0]))
    copies.append(keep(targets.at[p], targets_all.at[p], local_sems.at[1]))
    copies.append(keep(square, square_all.at[p], local_sems.at[2]))
    return copies


def stage_two(padded, valid, weight, gain, bias, *refs):
    (norm, full, taps, stat) = refs[:4]
    (hidden, own, out, near, cross, near_sems, far_sems, send, recv, stat_sems) = refs[4:14]
    (g_near, g_far, g_hop) = refs[14:]
    p, c = lax.axis_index("pix"), lax.axis_index("ch")
    pixels = valid.shape[0]
    local_mid = padded.shape[3]
    tile = pixels // TILES
    place = lax.broadcasted_iota(jnp.int32, (192, local_mid), 0) % 32
    for i in range(PHASES):
        beta = i % COL_CLASSES
        plain = padded[i].reshape(192, local_mid)
        wide = plain.astype(f32)
        if beta >= 2:
            moved_by = jnp.where(place == 0, 0.0, pltpu.roll(wide, 1, 0)).astype(bf16)
        else:
            moved_by = jnp.where(place == 31, 0.0, pltpu.roll(wide, 191, 0)).astype(bf16)
        for a in range(3):
            at = slice(a * 32, a * 32 + 128)
            for b, other, value in (
                (1, beta, plain),
                (0, (beta + 2) % 4, moved_by if beta >= 2 else plain),
                (2, (beta + 2) % 4, plain if beta >= 2 else moved_by),
            ):
                to = (i - beta + other) * 128
                col = (a * 3 + b) * local_mid
                taps[to : to + 128, col : col + local_mid] = value[at]

    def part(t):
        return jnp.dot(taps[t * tile : (t + 1) * tile], weight[...], preferred_element_type=f32)

    result = sum_over_ch(part, tile, TILES, own, out, near, cross, near_sems, far_sems)
    for t in range(TILES):
        hidden[t * tile : (t + 1) * tile] = result(t)
    center, scale, count = norm_stats(hidden, valid, pixels, send, recv, stat_sems)
    stat[0:1] = center
    stat[1:2] = scale
    stat[2:3] = count

    def ready(t):
        for i in range(tile // 128):
            at = pl.ds(t * tile + i * 128, 128)
            value = (hidden[at] - center) * scale
            norm[at] = value
            act = silu(value * gain[...] + bias[...]) * valid[at]
            full[at, rows(c * local_mid, local_mid)] = act.astype(bf16)

    gather_over_ch(full, local_mid, tile, TILES, g_near, g_far, g_hop, ready)


def stage_three(full, weight, masked, valid, gain, bias, counted, *refs):
    (norm, classes, stat, inputs) = refs[:4]
    (hidden, trunk, send, recv, stat_sems, class_sems, own_sem, in_sems) = refs[4:]
    p, c = lax.axis_index("pix"), lax.axis_index("ch")
    pixels, n = masked.shape
    tile = pixels // TILES
    for t in range(TILES):
        at = pl.ds(t * tile, tile)
        hidden[at] = jnp.dot(full[at], weight[...], preferred_element_type=f32)
    far = push(masked, inputs.at[c], in_sems.at[0, 0], in_sems.at[1, 0], (p, c ^ 2))
    near = push(masked, inputs.at[c], in_sems.at[0, 1], in_sems.at[1, 1], (p, c ^ 1))
    mine = keep(masked, inputs.at[c], own_sem.at[2])
    center, scale, count = norm_stats(hidden, valid, pixels, send, recv, stat_sems, counted)
    stat[0:1] = center
    stat[1:2] = scale
    stat[2:3] = count

    half = n // 2

    def finish(to, h):
        lanes = slice(h * half, (h + 1) * half)

        def step(i, carry):
            at = rows(to * 128 + i * 64, 64)
            value = (hidden[at, lanes] - center[:, lanes]) * scale[:, lanes]
            norm[at, lanes] = value
            pre = value * gain[:, lanes] + bias[:, lanes] + masked[at, lanes].astype(f32)
            v = valid[at]
            trunk[h, at] = (silu(pre) * jnp.concatenate([v] * (half // 128), axis=1)).astype(bf16)
            return carry

        loop(2, step, 0)

    copies = []
    for h in range(2):
        some = []
        for k in FAR_FIRST:
            to = p ^ k
            finish(to, h)
            some.append(
                push(
                    trunk.at[h, rows(to * 128, 128)],
                    classes.at[h, rows(p * 128, 128)],
                    class_sems.at[0, h, k],
                    class_sems.at[1, h, k],
                    (to, c),
                )
            )
        finish(p, h)
        some.append(keep(trunk.at[h, rows(p * 128, 128)], classes.at[h, rows(p * 128, 128)], own_sem.at[h]))
        copies.append(some)

    def pass_inputs():
        far.wait_recv()
        hop = push(inputs.at[c ^ 2], inputs.at[c ^ 2], in_sems.at[0, 2], in_sems.at[1, 2], (p, c ^ 1))

        def done():
            far.wait_send()
            near.wait()
            mine.wait()
            hop.wait()

        return done

    return copies, pass_inputs


def forward(
    feat, mask, weight, expand, gain1, bias1, head_weight, head_gain, head_bias, cotangent, dilated, gain2, bias2,
    gain3, bias3, pyramid_weight, *refs
):
    saved, stats, (inputs, grads, predictions, head_grad, branch_sums, others, picks) = refs[:10], refs[10:13], refs[13:20]
    padded, wide, w_sems, heads_full, save_sems = refs[20:25]
    masked, reduce_rows, expand_cols, norm1, valid, norm2, full2, taps, norm3, classes = refs[25:35]
    stat1, stat2, stat3 = stats
    own = refs[35:]
    saving = []

    def save(*which):
        for i in which:
            saving.append(keep(refs[25 + i], saved[i], save_sems.at[i]))

    one, two, three, heads = 14, 13, 8, 10
    barrier, expected = greet((1, 2, 3), FAR_FIRST)
    loads = load_pyramid(pyramid_weight, wide, w_sems)
    pl.semaphore_wait(barrier, expected)
    expand_copies = stage_one(
        feat, mask, weight, expand, gain1, bias1, masked, reduce_rows, expand_cols, norm1, padded, stat1, valid, *own[:one]
    )
    counted = own[9]
    own = own[one:]
    save(0, 1, 3, 4)
    stage_two(padded, valid, dilated, gain2, bias2, norm2, full2, taps, stat2, *own[:two])
    own = own[two:]
    for copy in expand_copies:
        copy.wait()
    save(2, 5, 6, 7)
    moving, pass_inputs = stage_three(
        full2, expand_cols, masked, valid, gain3, bias3, counted, norm3, classes, stat3, inputs, *own[:three]
    )
    own = own[three:]
    save(8)
    head_copies = prepare_heads(mask, head_weight, head_gain, head_bias, cotangent, *own[:heads])
    pyramid(
        classes, loads, wide, moving, pass_inputs, head_copies, heads_full, *own[:3],
        grads, predictions, head_grad, branch_sums, others, picks, *own[heads:],
    )
    save(9)
    for copy in saving:
        copy.wait()


def run_forward(
    cid, feat, mask, weight, expand, gain1, bias1, head_weight, head_gain, head_bias, cotangent, dilated, gain2, bias2,
    gain3, bias3, pyramid_weight
):
    pixels, n = feat.shape
    mid = weight.shape[1]
    all_mid = SPLIT * mid
    m = pyramid_weight.shape[4]
    quarter = pixels // SPLIT
    saved = [
        ((pixels, n), bf16),
        ((n, all_mid), bf16),
        ((all_mid, n), bf16),
        ((pixels, mid), f32),
        ((pixels, 128), f32),
        ((pixels, mid), f32),
        ((pixels, all_mid), bf16),
        ((pixels, 9 * mid), bf16),
        ((pixels, n), f32),
        ((2, pixels, n // 2), bf16),
    ]
    outs = [shape(*each) for each in saved] + [
        shape((8, mid), f32),
        shape((8, mid), f32),
        shape((8, n), f32),
        shape((SPLIT, pixels, n), bf16),
        shape((pixels, 3 * m), bf16),
        shape((PHASES, 32, 128), f32),
        shape((32, 3 * m), f32),
        shape((8, m), f32),
        shape((3, 2, pixels, n // 2), bf16),
        shape((3, 192, quarter), bf16),
    ]
    scratch = [
        pltpu.VMEM((PHASES, 6, 32, mid), bf16),
        pltpu.VMEM((9, n, 3 * m), bf16),
        dma(9, 3),
        pltpu.VMEM((40, 3 * m), f32),
        dma(10),
        *[pltpu.VMEM(*each) for each in saved],
        pltpu.VMEM((n // 128, 128, 128), f32),
        pltpu.VMEM((pixels, mid), f32),
        *sum_scratch(pixels, mid, TILES),
        *stat_scratch(mid),
        dma(2, SPLIT, 2),
        dma(2),
        dma(2, 2),
        pltpu.VMEM((pixels, mid), f32),
        *sum_scratch(pixels, mid, TILES),
        *stat_scratch(mid),
        *gather_scratch(TILES),
        pltpu.VMEM((pixels, n), f32),
        pltpu.VMEM((2, pixels, n // 2), bf16),
        *stat_scratch(128),
        dma(2, 2, PHASES),
        dma(4),
        dma(2, 3),
        pltpu.VMEM((SPLIT, 40, 256), f32),
        pltpu.VMEM((PHASES, 32, 128), f32),
        pltpu.VMEM((PHASES, 32, 128), f32),
        pltpu.VMEM((40, 256), f32),
        pltpu.VMEM((PHASES, 32, 128), f32),
        pltpu.VMEM((32, 128), f32),
        pltpu.VMEM((32, pixels), f32),
        dma(2, SPLIT),
        dma(2, PHASES, 2),
        dma(3),
        *pyramid_scratch(pixels, n, m),
    ]
    arrays = [
        feat, mask, weight, expand, gain1, bias1, head_weight, head_gain, head_bias, cotangent, dilated, gain2, bias2,
        gain3, bias3, pyramid_weight,
    ]
    return call("forward", cid, forward, arrays, outs, scratch, hbm_ins=(15,), hbm_outs=(*range(10), 13, 18))


PACE = (1, 10, 20, 23)


def packed_sums(values, send):
    i = 0
    for value in values:
        for g in range(value.shape[1] // 128):
            send[i : i + 1] = value[:, g * 128 : (g + 1) * 128]
            i += 1


def unpacked_sums(recv, rows_each, count):
    out, i = [], 0
    for _ in range(count):
        parts = []
        for _ in range(rows_each):
            value = recv[0, i : i + 1]
            for d in range(1, PHASES):
                value = value + recv[d, i : i + 1]
            parts.append(value)
            i += 1
        out.append(parts[0] if rows_each == 1 else jnp.concatenate(parts, axis=1))
    return out


def backward(
    grads, trunk, others, weight, norm3, masked, valid, expand, gain3, bias3, norm2, gain2, bias2, full2, taps, dilated,
    norm1, gain1, bias1, reduce_rows, stats1, stats2, stats3, picks, inputs, *refs
):
    stored = (valid, norm3, masked, expand, norm2, full2, norm1, dilated, reduce_rows)
    valid, norm3, masked, expand, norm2, full2, norm1, dilated, reduce_rows, store_sems = refs[-10:]
    refs = refs[:-10]
    outs, scratch = refs[:6], refs[6:]
    (features_grad, aspp_parts, dilated_grad, expand_grad, reduce_grad, sums_out) = outs
    (wide, moved, acc, dsend, drecv, tpad, r_in, picked_in, turned, zsend, r_y) = scratch[:11]
    (gp3, g3, own, out, near, cross, hidden, gp2, g2, prod, edges, g1) = scratch[11:23]
    gp1, lanes = gp2, own
    (st3, st3r, st2, st2r, st1, st1r, e_part, e_mid, e_in, e_y, e_sum, d_part, d_in, d_y, d_sum, r_mid, r_sum) = scratch[23:40]
    (w_sems, d_sems, y_sems, z_sems, near_sems, far_sems, st_sems, gn, gf, gh, gn1, gf1, gh1, edge_sems, ch_sems, pix_sems, pair_sems, own_sems, tap_sems, in_sems, fill_sems, last_sems, slope1, d_near, d_far, mid_sems) = scratch[40:]
    p, c = lax.axis_index("pix"), lax.axis_index("ch")
    y, z = lax.rem(p, 2), p // 2
    lower = lax.rem(z, 2)
    pixels, n = norm3.shape
    m = weight.shape[4]
    mid = norm2.shape[1]
    tile = pixels // TILES
    contract0 = (((0,), (0,)), ((), ()))
    contract1 = (((1,), (1,)), ((), ()))
    count = stats1[2:3, :1]
    barrier, expected = greet((1, 2, 3), FAR_FIRST)
    loads = load_pyramid(weight, wide, w_sems)
    arrived = dict(
        zip(
            ("valid", "norm3", "masked", "expand", "norm2", "full2", "norm1", "dilated", "reduce"),
            [keep(a, b, store_sems.at[i]) for i, (a, b) in enumerate(
                zip(stored, (valid, norm3, masked, expand, norm2, full2, norm1, dilated, reduce_rows))
            )],
        )
    )

    group, upper = lax.rem(p, 4), p // 4
    quarter = picks.shape[2]
    pl.semaphore_wait(barrier, expected)
    mine = rows(c * quarter, quarter)
    sent_picks = [
        push(picks, picked_in.at[:, :, mine], y_sems.at[0, k], y_sems.at[1, k], (p, c ^ k)) for k in (2, 3, 1)
    ] + [keep(picks, picked_in.at[:, :, mine], y_sems.at[0, 0])]
    part = pixels // SPLIT
    filled = []
    for k in range(4):
        for h in range(2):
            cols = slice(h * m, (h + 1) * m)
            source = (others.at[k - 1] if k else trunk).at[h]
            here = {0: ((0, 4),), 1: ((0, 3),), 2: ((0, 1), (2, 4)), 3: ((0, 4),)}[k]
            for i, (first, end) in enumerate(here):
                at = pl.ds(first * part, (end - first) * part)
                filled.append(
                    keep(source.at[at], tpad.at[k, pl.ds(64 + first * part, (end - first) * part), cols], fill_sems.at[k, h, i])
                )
            if k in (1, 2):
                q = 3 if k == 1 else 1
                filled.append(
                    push(
                        trunk.at[h, pl.ds(q * part, part)],
                        tpad.at[k, pl.ds(64 + q * part, part), cols],
                        last_sems.at[0, k - 1, h],
                        last_sems.at[1, k - 1, h],
                        (p ^ k, c),
                    )
                )
    for i in range(4):
        tpad[i, :64] = jnp.zeros((64, n), bf16)
        tpad[i, 64 + pixels :] = jnp.zeros((64, n), bf16)

    for j in range(3):
        q = RATE_COLS[j]
        plain = grads[:, j * m : (j + 1) * m]
        value = plain.astype(f32)
        moved[j, :, :m] = move_cols(value, -q).astype(bf16)
        moved[j, :, m : 2 * m] = plain
        moved[j, :, 2 * m :] = move_cols(value, q).astype(bf16)
    back = []
    for h in range(2):
        half = slice(h * m, (h + 1) * m)
        for j in range(3):
            s = RATE_ROWS[j] * 32
            for a in (1, 0, 2):
                if h == 0:
                    for load in loads[3 * j + a]:
                        load.wait()
                w = wide[3 * j + a, half]
                if a == 1:
                    value = lax.dot_general(moved[j], w, contract1, preferred_element_type=f32)
                    if j == 0:
                        acc[...] = value
                    else:
                        acc[...] += value
                elif a == 0:
                    acc[: pixels - s] += lax.dot_general(moved[j, s:], w, contract1, preferred_element_type=f32)
                else:
                    acc[s:] += lax.dot_general(moved[j, : pixels - s], w, contract1, preferred_element_type=f32)
        dsend[h] = acc[...].astype(bf16)
        for k in FAR_FIRST:
            back.append(
                push(
                    dsend.at[h, rows((p ^ k) * 128, 128)],
                    drecv.at[h, rows(p * 128, 128)],
                    d_sems.at[0, h, k],
                    d_sems.at[1, h, k],
                    (p ^ k, c),
                )
            )
        back.append(keep(dsend.at[h, rows(p * 128, 128)], drecv.at[h, rows(p * 128, 128)], own_sems.at[h]))

    all_inputs = [
        keep(inputs.at[i // 2, pl.ds(i % 2 * n, n)], wide.at[i, :, :n], in_sems.at[i]) for i in range(8)
    ]
    cut = moved.shape[2]
    own_taps = [
        keep(taps.at[:, :cut], moved.at[0], tap_sems.at[0]),
        keep(taps.at[:, cut:], moved.at[1, :, : taps.shape[1] - cut], tap_sems.at[1]),
    ]

    place = lax.broadcasted_iota(jnp.int32, (64, pixels), 1) % 32

    def turn(i, part):
        at = slice(i * pixels, (i + 1) * pixels)
        for j in range(3):
            q = RATE_COLS[j]
            plain = part(j)
            value = plain.astype(f32)
            turned[j, :64, at] = jnp.where(place >= 32 - q, 0.0, pltpu.roll(value, pixels - q, 1)).astype(bf16)
            turned[j, 64:128, at] = plain
            turned[j, 128:, at] = jnp.where(place < q, 0.0, pltpu.roll(value, q, 1)).astype(bf16)

    pick = pick_rows(m, 64, group)
    turn(
        0,
        lambda j: lax.dot_general(
            pick, grads[:, j * m : (j + 1) * m], contract1, preferred_element_type=f32
        ).astype(bf16),
    )
    for copy in sent_picks:
        copy.wait()
    for k in (1, 2, 3):
        turn(k, lambda j: picked_in[k - 1, j * 64 : (j + 1) * 64])
    for copy in filled:
        copy.wait()
    for j in range(3):
        s = RATE_ROWS[j] * 32
        for a in range(3):
            if a == 1:
                low, high, start = 0, pixels, 64
            elif a == 0:
                low, high = s // 128 * 128, pixels
                start = 64 + low - s
            else:
                low, high, start = 0, -(-(pixels - s) // 128) * 128, 64 + s
            value = None
            for i in range(4):
                term = jnp.dot(
                    turned[j, :, i * pixels + low : i * pixels + high],
                    tpad[i, start : start + high - low],
                    preferred_element_type=f32,
                )
                value = term if value is None else value + term
            value = value.astype(bf16)
            for b in range(3):
                for to in range(2):
                    at = b * 64 + to * 32
                    zsend[to, (3 * j + a) * 3 + b] = value[at : at + 32]
    for name in ("valid", "norm3", "masked", "norm2", "norm1"):
        arrived[name].wait()

    def slopes(i, carry):
        at = rows(i * 32, 32)
        pre = norm3[at] * gain3[...] + bias3[...] + masked[at].astype(f32)
        gp3[at] = spread_lanes(valid[at], n) * slope(pre)
        gp2[at] = valid[at] * slope(norm2[at] * gain2[...] + bias2[...])
        slope1[at] = valid[at] * slope(norm1[at] * gain1[...] + bias1[...])
        return carry

    loop(pixels // 32, slopes, 0)
    zcopies = [keep(zsend.at[upper], aspp_parts.at[0], own_sems.at[2])]

    def send_parts(first, end):
        for i in range(first, end):
            zcopies.append(
                push(zsend.at[1 - upper, i], aspp_parts.at[1, i], z_sems.at[0, i], z_sems.at[1, i], (p ^ 4, c))
            )


    def over_z(blocks, sums, sems, own_sem):
        return [
            push(blocks.at[z ^ k], sums.at[z], sems.at[0, k], sems.at[1, k], (p ^ (2 * k), c)) for k in (3, 2, 1)
        ] + [keep(blocks.at[z], sums.at[z], own_sem)]

    def norm_back(grad, norm, sums, scale, gain, v):
        return gain * scale * (grad - v * (sums[0] + norm * sums[1]) / count)

    totals = []
    for h in range(2):
        for copy in back[h * PHASES : (h + 1) * PHASES]:
            copy.wait()
        if h == 1:
            send_parts(0, PACE[0])
        cols = slice(h * m, (h + 1) * m)

        def three(i, carry):
            at = rows(i * 64, 64)
            grad = drecv[h, at].astype(f32) * gp3[at, cols]
            gp3[at, cols] = grad
            return carry[0] + fold(grad), carry[1] + fold(grad * norm3[at, cols])

        zero = jnp.zeros((8, m), f32)
        bias, gain = loop(pixels // 64, three, (zero, zero))
        totals.append((total(bias), total(gain)))
    bias, gain = (jnp.concatenate([totals[0][i], totals[1][i]], axis=1) for i in range(2))
    packed_sums((bias, gain), st3)
    pix_exchange(st3, st3r, st_sems.at[0])
    send_parts(PACE[0], PACE[1])
    sums = unpacked_sums(st3r, n // 128, 2)
    sums_out[0:1] = sums[0]
    sums_out[1:2] = sums[1]

    arrived["expand"].wait()

    def part3(t):
        def step(i, carry):
            at = rows(t * tile + i * 32, 32)
            v = spread_lanes(valid[at], n)
            g3[at] = norm_back(gp3[at], norm3[at], sums, stats3[1:2], gain3[...], v).astype(bf16)
            return carry

        loop(tile // 32, step, 0)
        return lax.dot_general(g3[t * tile : (t + 1) * tile], expand[...], contract1, preferred_element_type=f32)

    result = sum_over_ch(part3, tile, TILES, own, out, near, cross, near_sems.at[0], far_sems.at[0])
    arrived["full2"].wait()
    value = lax.dot_general(full2[...], g3[...], contract0, preferred_element_type=f32).astype(bf16)
    for d in range(SPLIT):
        e_part[d] = value[d * mid : (d + 1) * mid]
    e_copies = [
        push(e_part.at[c ^ k], e_mid.at[c], ch_sems.at[0, 0, k], ch_sems.at[0, 1, k], (p, c ^ k)) for k in (2, 3, 1)
    ]
    e_copies.append(keep(e_part.at[c], e_mid.at[c], own_sems.at[3]))

    bias, gain = jnp.zeros((8, mid), f32), jnp.zeros((8, mid), f32)
    for t in range(TILES):
        hidden[t * tile : (t + 1) * tile] = result(t)

    def two(i, carry):
        at = rows(i * 128, 128)
        grad = hidden[at] * gp2[at]
        gp2[at] = grad
        return carry[0] + fold(grad), carry[1] + fold(grad * norm2[at])

    bias, gain = loop(pixels // 128, two, (bias, gain))
    packed_sums((total(bias), total(gain)), st2)
    pix_exchange(st2, st2r, st_sems.at[1])
    send_parts(PACE[1], PACE[2])
    for copy in e_copies:
        copy.wait()
    e_to_y = push(
        e_mid.at[:, :, rows((1 - y) * 256, 256)], e_in, pair_sems.at[0, 0], pair_sems.at[1, 0], (p ^ 1, c)
    )
    sums2 = unpacked_sums(st2r, 1, 2)
    sums_out[2:3, :mid] = sums2[0]
    sums_out[3:4, :mid] = sums2[1]

    def ready2(t):
        def step(i, carry):
            at = rows(t * tile + i * 128, 128)
            value = norm_back(gp2[at], norm2[at], sums2, stats2[1:2], gain2[...], valid[at])
            g2[at, rows(c * mid, mid)] = value.astype(bf16)
            return carry

        loop(tile // 128, step, 0)

    gather_over_ch(g2, mid, tile, TILES, gn, gf, gh, ready2)

    e_to_y.wait()
    for d in range(4):
        e_y[d] = (e_mid[d, :, rows(y * 256, 256)].astype(f32) + e_in[d].astype(f32)).astype(bf16)
    pix_copies = over_z(e_y, e_sum, pix_sems.at[0], own_sems.at[5])

    place = lax.broadcasted_iota(jnp.int32, (128, mid), 0) % 32

    def across(i, a):
        beta = i % COL_CLASSES
        two_on = (beta + 2) % 4 * 128
        here = slice(beta * 128, (beta + 1) * 128)
        there = slice(two_on, two_on + 128)
        lane = lambda b: slice((3 * a + b) * mid, (3 * a + b + 1) * mid)
        left, right = prod[there, lane(0)], prod[there, lane(2)]
        if beta >= 2:
            left = jnp.where(place == 31, 0.0, pltpu.roll(left, 127, 0))
        else:
            right = jnp.where(place == 0, 0.0, pltpu.roll(right, 1, 0))
        return prod[here, lane(1)] + left + right

    arrived["dilated"].wait()
    for i in range(PHASES):
        at = slice(i * 128, (i + 1) * 128)
        if i % COL_CLASSES == 0:
            prod[...] = lax.dot_general(
                g2[i * 128 : (i + COL_CLASSES) * 128], dilated[...], contract1, preferred_element_type=f32
            )
        up, same, down = across(i, 0), across(i, 1), across(i, 2)
        zero = jnp.zeros((32, mid), f32)
        hidden[at] = same + jnp.concatenate([up[32:], zero]) + jnp.concatenate([zero, down[:96]])
        edges[0, i] = up[:32].astype(bf16)
        edges[1, i] = down[96:].astype(bf16)
    first, last = p == 0, p == PHASES - 1
    to_next = lambda: pltpu.make_async_remote_copy(
        src_ref=edges.at[1], dst_ref=edges.at[2], send_sem=edge_sems.at[0, 0], recv_sem=edge_sems.at[1, 0],
        device_id=(p + 1, c), device_id_type=MESH,
    )
    to_last = lambda: pltpu.make_async_remote_copy(
        src_ref=edges.at[0], dst_ref=edges.at[3], send_sem=edge_sems.at[0, 1], recv_sem=edge_sems.at[1, 1],
        device_id=(p - 1, c), device_id_type=MESH,
    )

    @pl.when(jnp.logical_not(last))
    def _():
        to_next().start()

    @pl.when(jnp.logical_not(first))
    def _():
        to_last().start()

    @pl.when(first)
    def _():
        edges[2] = jnp.zeros((PHASES, 32, mid), bf16)

    @pl.when(last)
    def _():
        edges[3] = jnp.zeros((PHASES, 32, mid), bf16)

    for copy in own_taps:
        copy.wait()
    value = jnp.concatenate(
        [
            lax.dot_general(g2[...], moved[0], contract0, preferred_element_type=f32).astype(bf16),
            lax.dot_general(
                g2[...], moved[1, :, : taps.shape[1] - cut], contract0, preferred_element_type=f32
            ).astype(bf16),
        ],
        axis=1,
    )
    out_rows = SPLIT * mid // PHASES
    for d in range(PHASES):
        d_part[d % 2, d // 2] = value[d * out_rows : (d + 1) * out_rows]
    halves = [pl.ds(h * out_rows // 2, out_rows // 2) for h in range(2)]
    d_to_y = [
        push(d_part.at[1 - y, :, at], d_in.at[:, at], mid_sems.at[0, 4 + h], mid_sems.at[1, 4 + h], (p ^ 1, c))
        for h, at in enumerate(halves)
    ]
    d_to_z, d_across = [], []

    def add_y(h):
        at = halves[h]
        d_to_y[h].wait()
        for d in range(4):
            d_y[d // 2, d % 2, at] = (d_part[y, d, at].astype(f32) + d_in[d, at].astype(f32)).astype(bf16)
        d_to_z.append(
            push(d_y.at[:, 1 - lower, at], d_near.at[:, at], mid_sems.at[0, h], mid_sems.at[1, h], (p ^ 2, c))
        )

    def add_z(h):
        at = halves[h]
        d_to_z[h].wait()
        for d in range(2):
            d_sum[d, at] = (d_y[d, lower, at].astype(f32) + d_near[d, at].astype(f32)).astype(bf16)
        d_across.append(
            push(d_sum.at[1 - upper, at], d_far.at[at], mid_sems.at[0, 2 + h], mid_sems.at[1, 2 + h], (p ^ 4, c))
        )

    @pl.when(jnp.logical_not(last))
    def _():
        to_next().wait_send()
        to_last().wait_recv()

    @pl.when(jnp.logical_not(first))
    def _():
        to_last().wait_send()
        to_next().wait_recv()

    send_parts(PACE[2], PACE[3])

    bias, gain = jnp.zeros((8, mid), f32), jnp.zeros((8, mid), f32)
    for i in range(PHASES):
        at = slice(i * 128, (i + 1) * 128)
        zero = jnp.zeros((64, mid), f32)
        edge = jnp.concatenate([edges[2, i].astype(f32), zero, edges[3, i].astype(f32)])
        grad = (hidden[at] + edge) * slope1[at]
        gp1[at] = grad
        bias, gain = bias + fold(grad), gain + fold(grad * norm1[at])
    packed_sums((total(bias), total(gain)), st1)
    pix_exchange(st1, st1r, st_sems.at[2])
    add_y(0)
    send_parts(PACE[3], 27)
    sums1 = unpacked_sums(st1r, 1, 2)
    sums_out[4:5, :mid] = sums1[0]
    sums_out[5:6, :mid] = sums1[1]

    def ready1(t):
        def step(i, carry):
            at = rows(t * tile + i * 128, 128)
            value = norm_back(gp1[at], norm1[at], sums1, stats1[1:2], gain1[...], valid[at])
            g1[at, rows(c * mid, mid)] = value.astype(bf16)
            return carry

        loop(tile // 128, step, 0)

    late = []

    def between():
        for copy in all_inputs:
            copy.wait()
        own_g1 = g1[:, rows(c * mid, mid)]
        for i in range(SPLIT):
            value = lax.dot_general(wide[2 * i, :, :n], own_g1[:n], contract0, preferred_element_type=f32)
            value = value + lax.dot_general(wide[2 * i + 1, :, :n], own_g1[n:], contract0, preferred_element_type=f32)
            r_mid[i] = value.astype(bf16).reshape(2, 256, mid)
        late.append(push(r_mid.at[:, 1 - y], r_in, pair_sems.at[0, 2], pair_sems.at[1, 2], (p ^ 1, c)))
        add_y(1)
        add_z(0)

    gather_over_ch(g1, mid, tile, TILES, gn1, gf1, gh1, ready1, between)
    late[0].wait()
    for d in range(4):
        r_y[d] = (r_mid[d, y].astype(f32) + r_in[d].astype(f32)).astype(bf16)
    pix_copies += over_z(r_y, r_sum, pix_sems.at[2], own_sems.at[7])
    add_z(1)

    arrived["reduce"].wait()
    for i in range(PHASES):
        at = slice(i * 128, (i + 1) * 128)
        value = lax.dot_general(g1[at], reduce_rows[...], contract1, preferred_element_type=f32) + gp3[at]
        value = value * spread_lanes(valid[at], n)
        for g in range(n // 128):
            for r in range(4):
                start = (2 * r + i // COL_CLASSES) * 128 + i % COL_CLASSES
                lanes[g, pl.ds(start, 32, stride=COL_CLASSES), :] = value[r * 32 : (r + 1) * 32, g * 128 : (g + 1) * 128]
    for g in range(n // 128):
        features_grad[:, g * 128 : (g + 1) * 128] = lanes[g].astype(bf16)
    for copy in pix_copies:
        copy.wait()

    def gathered(parts):
        value = parts[0].astype(f32)
        for d in range(1, parts.shape[0]):
            value = value + parts[d].astype(f32)
        return value

    expand_grad[...] = gathered(e_sum)
    reduce_grad[...] = gathered(r_sum)
    for copy in d_across:
        copy.wait()
    value = d_sum[upper].astype(f32) + d_far[...].astype(f32)
    for i in range(9):
        dilated_grad[i] = value[:, i * mid : (i + 1) * mid]
    for copy in zcopies:
        copy.wait()


def run_backward(cid, arrays):
    (grads, trunk, others, weight, norm3, masked, valid, expand, gain3, bias3, norm2, gain2, bias2, full2, taps, dilated,
     norm1, gain1, bias1, reduce_rows, stats1, stats2, stats3, picks, inputs) = arrays
    pixels, n = norm3.shape
    m = weight.shape[4]
    mid = norm2.shape[1]
    all_mid = SPLIT * mid
    outs = [
        shape((pixels, n), bf16),
        shape((2, 27, 32, n), bf16),
        shape((9, all_mid // PHASES, mid), f32),
        shape((mid, 256), f32),
        shape((256, mid), f32),
        shape((8, n), f32),
    ]
    sums = sum_scratch(pixels, mid, TILES)
    scratch = [
        pltpu.VMEM((9, n, 3 * m), bf16),
        pltpu.VMEM((3, pixels, 3 * m), bf16),
        pltpu.VMEM((pixels, m), f32),
        pltpu.VMEM((2, pixels, m), bf16),
        pltpu.VMEM((2, pixels, m), bf16),
        pltpu.VMEM((4, pixels + 128, n), bf16),
        pltpu.VMEM((4, 256, mid), bf16),
        pltpu.VMEM((3, 192, pixels), bf16),
        pltpu.VMEM((3, 192, 4 * pixels), bf16),
        pltpu.VMEM((2, 27, 32, n), bf16),
        pltpu.VMEM((4, 256, mid), bf16),
        pltpu.VMEM((pixels, n), f32),
        pltpu.VMEM((pixels, n), bf16),
        *sums[:4],
        pltpu.VMEM((pixels, mid), f32),
        pltpu.VMEM((pixels, mid), f32),
        pltpu.VMEM((pixels, all_mid), bf16),
        pltpu.VMEM((pixels // ROW_CLASSES, 9 * mid), f32),
        pltpu.VMEM((4, PHASES, 32, mid), bf16),
        pltpu.VMEM((pixels, all_mid), bf16),
        pltpu.VMEM((8, 128), f32),
        pltpu.VMEM((PHASES, 8, 128), f32),
        pltpu.VMEM((8, 128), f32),
        pltpu.VMEM((PHASES, 8, 128), f32),
        pltpu.VMEM((8, 128), f32),
        pltpu.VMEM((PHASES, 8, 128), f32),
        pltpu.VMEM((SPLIT, mid, n), bf16),
        pltpu.VMEM((SPLIT, mid, n), bf16),
        pltpu.VMEM((4, mid, 256), bf16),
        pltpu.VMEM((4, mid, 256), bf16),
        pltpu.VMEM((4, mid, 256), bf16),
        pltpu.VMEM((2, 4, all_mid // PHASES, 9 * mid), bf16),
        pltpu.VMEM((4, all_mid // PHASES, 9 * mid), bf16),
        pltpu.VMEM((2, 2, all_mid // PHASES, 9 * mid), bf16),
        pltpu.VMEM((2, all_mid // PHASES, 9 * mid), bf16),
        pltpu.VMEM((4, 2, 256, mid), bf16),
        pltpu.VMEM((4, 256, mid), bf16),
        dma(9, 3),
        dma(2, 2, PHASES),
        dma(3, 4),
        dma(2, 27),
        dma(1, 2, TILES, 2),
        dma(1, 2, TILES),
        dma(3, 2, PHASES),
        *gather_scratch(TILES),
        *gather_scratch(TILES),
        dma(2, 2),
        dma(2, 2, SPLIT),
        dma(3, 2, PHASES),
        dma(2, 3),
        dma(8),
        dma(2),
        dma(8),
        dma(4, 2, 2),
        dma(2, 2, 2),
        pltpu.VMEM((pixels, mid), f32),
        pltpu.VMEM((2, all_mid // PHASES, 9 * mid), bf16),
        pltpu.VMEM((all_mid // PHASES, 9 * mid), bf16),
        dma(2, 6),
        pltpu.VMEM((pixels, 128), f32),
        pltpu.VMEM((pixels, n), f32),
        pltpu.VMEM((pixels, n), bf16),
        pltpu.VMEM((all_mid, n), bf16),
        pltpu.VMEM((pixels, mid), f32),
        pltpu.VMEM((pixels, all_mid), bf16),
        pltpu.VMEM((pixels, mid), f32),
        pltpu.VMEM((9 * mid, all_mid), bf16),
        pltpu.VMEM((n, all_mid), bf16),
        dma(9),
    ]
    vmem = pl.BlockSpec(memory_space=pltpu.VMEM)
    specs = [vmem] * len(arrays)
    for i in (1, 2, 3, 4, 5, 6, 7, 10, 13, 14, 15, 16, 19, 24):
        specs[i] = pl.BlockSpec(memory_space=pl.ANY)
    return pl.pallas_call(
        backward,
        out_shape=outs,
        in_specs=specs,
        out_specs=[vmem, pl.BlockSpec(memory_space=pl.ANY)] + [vmem] * (len(outs) - 2),
        scratch_shapes=scratch,
        compiler_params=pltpu.CompilerParams(
            collective_id=cid, has_side_effects=True, vmem_limit_bytes=VMEM_BYTES
        ),
        name="backward",
    )(*arrays)


def publish(features, parts, dilated, expand, reduce, norm_sums, predictions, head_grad, branch_sums, *outs):
    (o_predictions, o_features, o_reduce, o_gain1, o_bias1, o_dilated, o_gain2, o_bias2, o_expand, o_gain3, o_bias3,
     o_parts, o_branch_gain, o_branch_bias, o_heads) = outs
    c = lax.axis_index("ch")
    columns, mid = o_predictions.shape[0], o_gain1.shape[1]
    m = o_heads.shape[2]
    o_features[...] = features[...]
    o_reduce[...] = reduce[...]
    o_expand[...] = expand[...]
    o_dilated[...] = dilated[...]
    for i in range(parts.shape[1]):
        o_parts[i] = parts[0, i].astype(f32) + parts[1, i].astype(f32)
    o_bias3[...] = norm_sums[0:1]
    o_gain3[...] = norm_sums[1:2]
    o_bias2[...] = norm_sums[2:3, :mid]
    o_gain2[...] = norm_sums[3:4, :mid]
    o_bias1[...] = norm_sums[4:5, :mid]
    o_gain1[...] = norm_sums[5:6, :mid]

    def own(value):
        return jnp.where(lax.rem(c, 2) == 1, value[:, m:], value[:, :m])

    lanes = rows(c // 2 * 2 * m, 2 * m)
    value = own(branch_sums[:, lanes])
    o_branch_bias[...] = value[0:3]
    o_branch_gain[...] = value[3:6]
    for j in range(3):
        value = own(head_grad[:, rows(j * SPLIT * m + c // 2 * 2 * m, 2 * m)])
        o_heads[j] = value[:columns]
    place = jnp.where(
        one_hot(512, 512, lambda i: i % 128 // 32 * 128 + 4 * (i % 32) + i // 128), 1.0, 0.0
    ).astype(bf16)
    for a in range(ROW_CLASSES):
        value = jnp.concatenate([predictions[a * COL_CLASSES + b] for b in range(COL_CLASSES)], axis=1)
        high = value.astype(bf16)
        rest = value - high.astype(f32)
        middle = rest.astype(bf16)
        low = (rest - middle.astype(f32)).astype(bf16)
        value = jnp.dot(jnp.concatenate([high, middle, low]), place, preferred_element_type=f32)
        value = value[:32] + (value[32:64] + value[64:])
        for r in range(4):
            o_predictions[:, 2 * r + a, :] = value[:columns, r * 128 : (r + 1) * 128]


def run_publish(columns, m, arrays):
    features, parts, dilated, expand, reduce = arrays[:5]
    n, mid = features.shape[1], reduce.shape[1]
    outs = [
        shape((columns, 8, 128), f32),
        shape(features.shape, bf16),
        shape(reduce.shape, f32),
        shape((1, mid), f32),
        shape((1, mid), f32),
        shape(dilated.shape, f32),
        shape((1, mid), f32),
        shape((1, mid), f32),
        shape(expand.shape, f32),
        shape((1, n), f32),
        shape((1, n), f32),
        shape(parts.shape[1:], f32),
        shape((3, m), f32),
        shape((3, m), f32),
        shape((3, columns, m), f32),
    ]
    vmem = pl.BlockSpec(memory_space=pltpu.VMEM)
    return pl.pallas_call(
        publish,
        out_shape=outs,
        in_specs=[vmem] * len(arrays),
        out_specs=[vmem] * len(outs),
        compiler_params=pltpu.CompilerParams(vmem_limit_bytes=VMEM_BYTES),
        name="publish",
    )(*arrays)


def fast_device(
    features,
    pixel_mask,
    reduce_weight,
    reduce_gain,
    reduce_bias,
    dilated_weight,
    dilated_gain,
    dilated_bias,
    expand_weight,
    expand_gain,
    expand_bias,
    aspp_weight,
    aspp_gain,
    aspp_bias,
    task_weight,
    cotangent,
):
    rows_here, width, local_in = features.shape
    pixels = rows_here * width
    local_mid = reduce_weight.shape[1]
    full_mid = dilated_weight.shape[3]
    branch_width = aspp_weight.shape[4]
    own_branch = task_weight.shape[1]
    outs_count = task_weight.shape[2]
    line = lambda v: v.reshape(1, -1)
    dilated_rows = dilated_weight.reshape(9 * local_mid, full_mid)
    (
        masked, reduce_rows, expand_cols, norm_one, valid, norm_two, act_two_full, taps_one, norm_three, trunk_class,
        stat_one, stat_two, stat_three, inputs_all, grad_full, predictions, head_grad, branch_sums, trunk_others, picks,
    ) = run_forward(
        1,
        features.reshape(pixels, local_in),
        pixel_mask,
        reduce_weight,
        expand_weight,
        line(reduce_gain),
        line(reduce_bias),
        task_weight.transpose(0, 2, 1),
        aspp_gain,
        aspp_bias,
        cotangent.transpose(2, 0, 1).reshape(outs_count, pixels),
        dilated_rows,
        line(dilated_gain),
        line(dilated_bias),
        line(expand_gain),
        line(expand_bias),
        aspp_weight,
    )
    features_grad, aspp_parts, dilated_sum, expand_weight_grad, reduce_weight_grad, norm_sums = run_backward(
        2,
        [
            grad_full, trunk_class, trunk_others, aspp_weight, norm_three, masked, valid, expand_cols,
            line(expand_gain), line(expand_bias), norm_two, line(dilated_gain), line(dilated_bias), act_two_full,
            taps_one, dilated_rows, norm_one, line(reduce_gain), line(reduce_bias), reduce_rows, stat_one, stat_two,
            stat_three, picks, inputs_all,
        ],
    )
    (
        predictions, features_grad, reduce_weight_grad, reduce_gain_grad, reduce_bias_grad, dilated_weight_grad,
        dilated_gain_grad, dilated_bias_grad, expand_weight_grad, expand_gain_grad, expand_bias_grad, aspp_weight_grad,
        aspp_gain_grad, aspp_bias_grad, task_weight_grad,
    ) = run_publish(
        outs_count,
        own_branch,
        [
            features_grad, aspp_parts, dilated_sum, expand_weight_grad, reduce_weight_grad, norm_sums, predictions,
            head_grad, branch_sums,
        ],
    )
    return (
        predictions.transpose(1, 2, 0),
        features_grad.reshape(rows_here, width, local_in),
        reduce_weight_grad,
        reduce_gain_grad.reshape(-1),
        reduce_bias_grad.reshape(-1),
        dilated_weight_grad.reshape(3, 3, -1, local_mid).transpose(0, 1, 3, 2),
        dilated_gain_grad.reshape(-1),
        dilated_bias_grad.reshape(-1),
        expand_weight_grad,
        expand_gain_grad.reshape(-1),
        expand_bias_grad.reshape(-1),
        aspp_weight_grad.reshape(3, 3, 3, -1, local_in).transpose(0, 1, 2, 4, 3),
        aspp_gain_grad,
        aspp_bias_grad,
        task_weight_grad.transpose(0, 2, 1),
    )


def solution(mesh):
    placed = (
        P("pix", None, "ch"),
        P("pix", None),
        P(None, "ch"),
        P("ch"),
        P("ch"),
        P(None, None, "ch", None),
        P("ch"),
        P("ch"),
        P("ch", None),
        P("ch"),
        P("ch"),
        P(None, None, None, "ch", None),
        P(None, "ch"),
        P(None, "ch"),
        P(None, "ch", None),
        P("pix", None, None),
    )
    return jax.shard_map(
        fast_device if (mesh.shape["pix"], mesh.shape["ch"]) == (PHASES, 4) else on_device,
        mesh=mesh,
        in_specs=placed,
        out_specs=(
            P("pix", None, None),
            P("pix", None, "ch"),
            P("pix", "ch"),
            P("ch"),
            P("ch"),
            P(None, None, "ch", "pix"),
            P("ch"),
            P("ch"),
            P("ch", "pix"),
            P("ch"),
            P("ch"),
            P(None, None, None, "ch", "pix"),
            P(None, "ch"),
            P(None, "ch"),
            P(None, "ch", None),
        ),
        check_vma=False,
    )
```

```python
import jax
import jax.numpy as jnp
from jax import lax
from jax.experimental import pallas as pl
from jax.experimental.pallas import tpu as pltpu
from jax.sharding import PartitionSpec as P

CLS = 19


epsilon = 1e-05
highest = lax.Precision.HIGHEST
aspp_rates = (12, 24, 36)
inner_rate = 2


def from_behind(value, axis, steps):
    count = lax.axis_size(axis)
    first, last = (max(0, -steps), min(count, count - steps))
    return lax.ppermute(value, axis, [(source, source + steps) for source in range(first, last)])


def with_halo(shard, sides, width):
    for axis, dim in sides:
        devices, length = (lax.axis_size(axis), shard.shape[dim])
        up = [(i, (i + 1) % devices) for i in range(devices - 1)]
        down = [(j, i) for i, j in up]
        last = lax.slice_in_dim(shard, length - width, length, axis=dim)
        first = lax.slice_in_dim(shard, 0, width, axis=dim)
        before = lax.ppermute(last, axis, up)
        after = lax.ppermute(first, axis, down)
        shard = jnp.concatenate([before, shard, after], axis=dim)
    return shard


def silu_slope(value):
    sigma = jax.nn.sigmoid(value)
    return sigma * (1.0 + value * (1.0 - sigma))


def shift_cols(value, offset):
    if offset == 0:
        return value
    margin = abs(offset)
    widths = [(0, 0)] * value.ndim
    widths[1] = (margin, margin)
    padded = jnp.pad(value, widths)
    return lax.slice_in_dim(padded, margin + offset, margin + offset + value.shape[1], axis=1)


def moved(piece, distance):
    return from_behind(piece, "pix", -distance)


def shift_rows(value, offset):
    if offset == 0:
        return value
    steps_over, inner = divmod(offset, value.shape[0])
    first = moved(value, steps_over)[inner:]
    if inner == 0:
        return first
    second = moved(value, steps_over + 1)[:inner]
    return jnp.concatenate([first, second], axis=0)


def halo_rows(value):
    return with_halo(value, (("pix", 0),), inner_rate)


def gather_channels(value):
    return lax.all_gather(value, "ch", axis=1, tiled=True)


def sum_channels(value):
    return lax.psum_scatter(
        value.astype(jnp.bfloat16), "ch", scatter_dimension=1, tiled=True
    ).astype(jnp.float32)


def normalized(hidden, valid, axes):
    total, count = lax.psum(
        (jnp.sum(hidden * valid, axis=axes, keepdims=True), jnp.sum(valid)), "pix"
    )
    center = total / count
    spread_sum = lax.psum(jnp.sum(valid * (hidden - center) ** 2, axis=axes, keepdims=True), "pix")
    variance = spread_sum / count
    scale = lax.rsqrt(variance + epsilon)
    return ((hidden - center) * scale, scale, count)


def norm_grad(grad_out, centered, scale, gain, count, valid, axes):
    sum_out, sum_cross = lax.psum(
        (
            jnp.sum(grad_out, axis=axes, keepdims=True),
            jnp.sum(grad_out * centered, axis=axes, keepdims=True),
        ),
        "pix",
    )
    grad_in = gain * scale * (grad_out - valid * (sum_out + centered * sum_cross) / count)
    return (grad_in, sum_cross, sum_out)


def task_scales(gram):
    norms = jnp.sqrt(jnp.diagonal(gram) + 1e-06)
    proj = gram / norms[None, :]
    vector = proj[0, 0] - proj[0, 1:]
    matrix = proj[0, 0] - proj[0, 1:][None, :] - proj[1:, 0][:, None] + proj[1:, 1:]
    determinant = matrix[0, 0] * matrix[1, 1] - matrix[0, 1] * matrix[1, 0]
    second = (vector[0] * matrix[1, 1] - vector[1] * matrix[1, 0]) / determinant
    third = (vector[1] * matrix[0, 0] - vector[0] * matrix[0, 1]) / determinant
    return jnp.stack([1.0 - second - third, second, third])


def on_device(
    features,
    pixel_mask,
    reduce_weight,
    reduce_gain,
    reduce_bias,
    dilated_weight,
    dilated_gain,
    dilated_bias,
    expand_weight,
    expand_gain,
    expand_bias,
    aspp_weight,
    aspp_gain,
    aspp_bias,
    task_weight,
    cotangent,
):
    rows_here, width, local_in = features.shape
    pixels = rows_here * width
    local_mid = reduce_weight.shape[1]
    full_mid = dilated_weight.shape[3]
    branch_width = aspp_weight.shape[4]
    outs_count = task_weight.shape[2]
    valid = pixel_mask.astype(jnp.float32).reshape(pixels, 1)
    valid_branch = valid[None]
    masked = features.reshape(pixels, local_in) * valid.astype(jnp.bfloat16)
    inputs_full = gather_channels(masked)
    hidden_one = jnp.dot(inputs_full, reduce_weight, preferred_element_type=jnp.float32)
    norm_one, scale_one, count = normalized(hidden_one, valid, (0,))
    pre_one = norm_one * reduce_gain + reduce_bias
    act_one = (jax.nn.silu(pre_one) * valid).astype(jnp.bfloat16)
    padded_one = halo_rows(act_one.reshape(rows_here, width, local_mid))
    partial_value = jnp.zeros((pixels, full_mid), jnp.float32)
    for a in range(3):
        for b in range(3):
            shifted = shift_cols(padded_one[2 * a : 2 * a + rows_here], (b - 1) * inner_rate)
            partial_value = partial_value + jnp.dot(
                shifted.reshape(pixels, local_mid),
                dilated_weight[a, b],
                preferred_element_type=jnp.float32,
            )
    hidden_two = sum_channels(partial_value)
    norm_two, scale_two, _ = normalized(hidden_two, valid, (0,))
    pre_two = norm_two * dilated_gain + dilated_bias
    act_two = (jax.nn.silu(pre_two) * valid).astype(jnp.bfloat16)
    hidden_three = sum_channels(jnp.dot(act_two, expand_weight, preferred_element_type=jnp.float32))
    norm_three, scale_three, _ = normalized(hidden_three, valid, (0,))
    pre_three = norm_three * expand_gain + expand_bias + masked.astype(jnp.float32)
    trunk_out = (
        (jax.nn.silu(pre_three) * valid).astype(jnp.bfloat16).reshape(rows_here, width, local_in)
    )
    kept_rows = []
    partials = []
    for j in range(3):
        rate = aspp_rates[j]
        running = jnp.zeros((pixels, branch_width), jnp.float32)
        shifted_rows = []
        for a in range(3):
            row_shift = shift_rows(trunk_out, (a - 1) * rate)
            shifted_rows.append(row_shift)
            for b in range(3):
                shifted = shift_cols(row_shift, (b - 1) * rate)
                running = running + jnp.dot(
                    shifted.reshape(pixels, local_in),
                    aspp_weight[j, a, b],
                    preferred_element_type=jnp.float32,
                )
        kept_rows.append(shifted_rows)
        partials.append(running)
    branch_sum = sum_channels(jnp.stack(partials).reshape(3 * pixels, branch_width)).reshape(
        3, pixels, -1
    )
    branch_gain = aspp_gain[:, None, :]
    norm_branch, scale_branch, _ = normalized(branch_sum, valid_branch, (1,))
    pre_branch = norm_branch * branch_gain + aspp_bias[:, None, :]
    branch_out = (jax.nn.silu(pre_branch) * valid_branch).astype(jnp.bfloat16)
    predictions = lax.psum(
        jnp.einsum(
            "jpc,jco->po", branch_out, task_weight, preferred_element_type=jnp.float32
        ).astype(jnp.bfloat16),
        "ch",
    ).astype(jnp.float32)
    columns = jnp.arange(outs_count)
    task_of = (columns >= CLS).astype(jnp.int32) + (columns >= CLS + 1).astype(jnp.int32)
    select = (task_of[:, None] == jnp.arange(3)[None, :]).astype(jnp.float32)
    target = cotangent.reshape(pixels, outs_count) * valid
    task_float = task_weight.astype(jnp.float32)
    task_grads = jnp.einsum("po,ot,jco->tjpc", target, select, task_float, precision=highest)
    gram = lax.psum(
        jnp.einsum("tjpc,sjpc->ts", task_grads, task_grads, precision=highest), ("pix", "ch")
    )
    scales = task_scales(gram)
    branch_grad = jnp.einsum("t,tjpc->jpc", scales, task_grads, precision=highest)
    task_weight_grad = lax.psum(
        jnp.einsum("jpc,po->jco", branch_out.astype(jnp.float32), target, precision=highest), "pix"
    )
    grad_pre_branch = branch_grad * valid_branch * silu_slope(pre_branch)
    grad_branch, aspp_gain_grad, aspp_bias_grad = norm_grad(
        grad_pre_branch, norm_branch, scale_branch, branch_gain, count, valid_branch, (1,)
    )
    grad_full = gather_channels(grad_branch.astype(jnp.bfloat16).reshape(3 * pixels, -1)).reshape(
        3, rows_here, width, -1
    )
    grad_trunk = jnp.zeros((pixels, local_in), jnp.float32)
    aspp_list = []
    for j in range(3):
        rate = aspp_rates[j]
        grad_flat = grad_full[j].reshape(pixels, -1)
        per_row = []
        for a in range(3):
            back_rows = shift_rows(grad_full[j], -(a - 1) * rate)
            per_col = []
            for b in range(3):
                shifted = shift_cols(back_rows, -(b - 1) * rate)
                grad_trunk = grad_trunk + jnp.einsum(
                    "pa,ca->pc",
                    shifted.reshape(pixels, -1),
                    aspp_weight[j, a, b],
                    preferred_element_type=jnp.float32,
                )
                forward_tap = shift_cols(kept_rows[j][a], (b - 1) * rate).reshape(pixels, local_in)
                per_col.append(
                    jnp.einsum(
                        "pc,pa->ca", forward_tap, grad_flat, preferred_element_type=jnp.float32
                    )
                )
            per_row.append(jnp.stack(per_col))
        aspp_list.append(jnp.stack(per_row))
    aspp_weight_local = jnp.stack(aspp_list)
    grad_pre_three = grad_trunk * valid * silu_slope(pre_three)
    grad_three, expand_gain_grad, expand_bias_grad = norm_grad(
        grad_pre_three, norm_three, scale_three, expand_gain, count, valid, (0,)
    )
    grad_three_full = gather_channels(grad_three.astype(jnp.bfloat16))
    grad_act_two = jnp.einsum(
        "pc,dc->pd", grad_three_full, expand_weight, preferred_element_type=jnp.float32
    )
    expand_weight_local = jnp.einsum(
        "pd,pc->dc", act_two, grad_three_full, preferred_element_type=jnp.float32
    )
    grad_pre_two = grad_act_two * valid * silu_slope(pre_two)
    grad_two, dilated_gain_grad, dilated_bias_grad = norm_grad(
        grad_pre_two, norm_two, scale_two, dilated_gain, count, valid, (0,)
    )
    grad_two_full = gather_channels(grad_two.astype(jnp.bfloat16))
    padded_grad = halo_rows(grad_two_full.reshape(rows_here, width, full_mid))
    grad_act_one = jnp.zeros((pixels, local_mid), jnp.float32)
    dilated_rows = []
    for a in range(3):
        dilated_cols = []
        for b in range(3):
            shifted = shift_cols(
                padded_grad[4 - 2 * a : 4 - 2 * a + rows_here], -(b - 1) * inner_rate
            )
            grad_act_one = grad_act_one + jnp.einsum(
                "pe,de->pd",
                shifted.reshape(pixels, full_mid),
                dilated_weight[a, b],
                preferred_element_type=jnp.float32,
            )
            forward_tap = shift_cols(
                padded_one[2 * a : 2 * a + rows_here], (b - 1) * inner_rate
            ).reshape(pixels, local_mid)
            dilated_cols.append(
                jnp.einsum(
                    "pd,pe->de", forward_tap, grad_two_full, preferred_element_type=jnp.float32
                )
            )
        dilated_rows.append(jnp.stack(dilated_cols))
    dilated_weight_local = jnp.stack(dilated_rows)
    grad_pre_one = grad_act_one * valid * silu_slope(pre_one)
    grad_one, reduce_gain_grad, reduce_bias_grad = norm_grad(
        grad_pre_one, norm_one, scale_one, reduce_gain, count, valid, (0,)
    )
    grad_one_low = grad_one.astype(jnp.bfloat16)
    input_sum = sum_channels(
        jnp.einsum("pd,cd->pc", grad_one_low, reduce_weight, preferred_element_type=jnp.float32)
    )
    features_grad = (
        ((input_sum + grad_pre_three) * valid)
        .astype(jnp.bfloat16)
        .reshape(rows_here, width, local_in)
    )
    reduce_weight_local = jnp.einsum(
        "pc,pd->cd", inputs_full, grad_one_low, preferred_element_type=jnp.float32
    )
    reduce_weight_grad, dilated_weight_grad, expand_weight_grad, aspp_weight_grad = (
        lax.psum_scatter(reduce_weight_local, "pix", scatter_dimension=0, tiled=True),
        lax.psum_scatter(dilated_weight_local, "pix", scatter_dimension=3, tiled=True),
        lax.psum_scatter(expand_weight_local, "pix", scatter_dimension=1, tiled=True),
        lax.psum_scatter(aspp_weight_local, "pix", scatter_dimension=4, tiled=True),
    )
    return (
        predictions.reshape(rows_here, width, outs_count),
        features_grad,
        reduce_weight_grad,
        reduce_gain_grad.reshape(-1),
        reduce_bias_grad.reshape(-1),
        dilated_weight_grad,
        dilated_gain_grad.reshape(-1),
        dilated_bias_grad.reshape(-1),
        expand_weight_grad,
        expand_gain_grad.reshape(-1),
        expand_bias_grad.reshape(-1),
        aspp_weight_grad,
        aspp_gain_grad.reshape(3, -1),
        aspp_bias_grad.reshape(3, -1),
        task_weight_grad,
    )


MESH = pl.DeviceIdType.MESH
ROW_CLASSES, COL_CLASSES = 2, 4
PHASES = ROW_CLASSES * COL_CLASSES
SPLIT = 4
FAR_FIRST = (1, 2, 3, 4, 5, 6, 7)
f32, bf16 = jnp.float32, jnp.bfloat16
VMEM_BYTES = 60 << 20


def shape(dims, dtype):
    return jax.ShapeDtypeStruct(dims, dtype)


def call(name, cid, kernel, arrays, outs, scratch, hbm_ins=(), hbm_outs=()):
    vmem, hbm = pl.BlockSpec(memory_space=pltpu.VMEM), pl.BlockSpec(memory_space=pl.ANY)
    return pl.pallas_call(
        kernel,
        out_shape=outs,
        in_specs=[hbm if i in hbm_ins else vmem for i in range(len(arrays))],
        out_specs=[hbm if i in hbm_outs else vmem for i in range(len(outs))],
        scratch_shapes=scratch,
        compiler_params=pltpu.CompilerParams(
            collective_id=cid, has_side_effects=True, vmem_limit_bytes=VMEM_BYTES
        ),
        name=name,
    )(*arrays)


def dma(*dims):
    return pltpu.SemaphoreType.DMA(dims)


def greet(ch, pix):
    p, c = lax.axis_index("pix"), lax.axis_index("ch")
    barrier = pltpu.get_barrier_semaphore()
    for k in ch:
        pl.semaphore_signal(barrier, inc=1, device_id=(p, c ^ k), device_id_type=MESH)
    for k in pix:
        pl.semaphore_signal(barrier, inc=1, device_id=(p ^ k, c), device_id_type=MESH)
    return barrier, len(ch) + len(pix)


def push(src, dst, send, recv, device):
    copy = pltpu.make_async_remote_copy(
        src_ref=src,
        dst_ref=dst,
        send_sem=send,
        recv_sem=recv,
        device_id=device,
        device_id_type=MESH,
    )
    copy.start()
    return copy


def keep(src, dst, sem):
    copy = pltpu.make_async_copy(src, dst, sem)
    copy.start()
    return copy


def rows(start, size):
    return pl.ds(pl.multiple_of(start, size), size)


def fold(x):
    return jnp.sum(x.reshape(x.shape[0] // 8, 8, x.shape[1]), axis=0)


def total(x):
    return jnp.sum(x, axis=0, keepdims=True)


def loop(steps, body, init):
    return lax.fori_loop(0, steps, body, init)


def sum_over_ch(part, tile, tiles, own, out, near, cross, near_sems, far_sems):
    p, c = lax.axis_index("pix"), lax.axis_index("ch")
    k, x = lax.rem(c, 2), c // 2
    n = own.shape[2]
    copies = []
    for t in range(tiles):
        at = pl.ds(t * tile, tile)
        value = part(t)
        for d in range(SPLIT):
            block = value[:, d * n : (d + 1) * n]
            own[d, at] = block
            out[d, at] = block.astype(bf16)
        copies.append(
            [
                push(
                    out.at[2 * h + 1 - k, at],
                    near.at[h, at],
                    near_sems.at[0, t, h],
                    near_sems.at[1, t, h],
                    (p, c ^ 1),
                )
                for h in range(2)
            ]
        )
    crossing = []
    for t in range(tiles):
        at = pl.ds(t * tile, tile)
        for copy in copies[t]:
            copy.wait()
        cross[0, at] = (own[2 * (1 - x) + k, at] + near[1 - x, at].astype(f32)).astype(bf16)
        crossing.append(
            push(cross.at[0, at], cross.at[1, at], far_sems.at[0, t], far_sems.at[1, t], (p, c ^ 2))
        )

    def result(t):
        at = pl.ds(t * tile, tile)
        crossing[t].wait()
        return own[2 * x + k, at] + near[x, at].astype(f32) + cross[1, at].astype(f32)

    return result


def sum_scratch(pixels, n, tiles):
    return [
        pltpu.VMEM((SPLIT, pixels, n), f32),
        pltpu.VMEM((SPLIT, pixels, n), bf16),
        pltpu.VMEM((2, pixels, n), bf16),
        pltpu.VMEM((2, pixels, n), bf16),
        dma(2, tiles, 2),
        dma(2, tiles),
    ]


def pix_exchange(send, recv, sems):
    p, c = lax.axis_index("pix"), lax.axis_index("ch")
    copies = [
        push(send, recv.at[p], sems.at[0, k], sems.at[1, k], (p ^ k, c)) for k in FAR_FIRST
    ]
    recv[p] = send[...]
    for copy in copies:
        copy.wait()


def norm_stats(hidden, valid, pixels, send, recv, sems, counted=None):
    n = hidden.shape[1]
    tile = 128
    repeat = n // 128

    def mask(at):
        v = valid[at]
        return v if repeat == 1 else jnp.concatenate([v] * repeat, axis=1)

    def first(i, carry):
        at = rows(i * tile, tile)
        v = mask(at)
        return carry[0] + fold(hidden[at] * v), carry[1] + fold(v)

    zero = jnp.zeros((8, n), f32)
    sums, count = loop(pixels // tile, first, (zero, zero))
    sums, count = total(sums), total(count)
    center = sums / jnp.maximum(count, 1.0)

    def second(i, carry):
        at = rows(i * tile, tile)
        apart = hidden[at] - center
        return carry + fold(mask(at) * apart * apart)

    spread = total(loop(pixels // tile, second, zero))
    if counted is not None:
        groups = n // 128
        for i in range(groups):
            send[i : i + 1] = sums[:, i * 128 : (i + 1) * 128]
            send[groups + i : groups + i + 1] = spread[:, i * 128 : (i + 1) * 128]
        pix_exchange(send, recv, sems)
        sums = [
            jnp.concatenate([recv[d, i : i + 1] for i in range(groups)], axis=1) for d in range(PHASES)
        ]
        spreads = [
            jnp.concatenate([recv[d, groups + i : groups + i + 1] for i in range(groups)], axis=1)
            for d in range(PHASES)
        ]
        counts = [spread_lanes(counted[d, 2:3], n) for d in range(PHASES)]
        return join_parts(sums, spreads, counts)
    send[0:1] = sums
    send[1:2] = spread
    send[2:3] = count
    pix_exchange(send, recv, sems)
    return join(recv, PHASES)


def spread_lanes(v, n):
    return v if n == 128 else jnp.concatenate([v] * (n // 128), axis=1)


def join_parts(sums, spreads, counts):
    whole, count = sums[0], counts[0]
    for i in range(1, len(sums)):
        whole, count = whole + sums[i], count + counts[i]
    center = whole / count
    spread = jnp.zeros_like(whole)
    for i in range(len(sums)):
        apart = sums[i] / jnp.maximum(counts[i], 1.0) - center
        spread = spread + spreads[i] + counts[i] * apart * apart
    return center, lax.rsqrt(spread / count + epsilon), count


def join(recv, parts):
    return join_parts(*[[recv[i, row : row + 1] for i in range(parts)] for row in range(3)])


def stat_scratch(n):
    return [pltpu.VMEM((8, n), f32), pltpu.VMEM((PHASES, 8, n), f32), dma(2, PHASES)]


def silu(x):
    return x / (1.0 + jnp.exp(-x))


def gather_over_ch(full, n, tile, tiles, near_sems, far_sems, hop_sems, ready, between=None):
    p, c = lax.axis_index("pix"), lax.axis_index("ch")

    def part(owner, t):
        return full.at[pl.ds(t * tile, tile), rows(owner * n, n)]

    near, far, hops = [], [], []
    for t in range(tiles):
        ready(t)
        src = part(c, t)
        far.append(push(src, src, far_sems.at[0, t], far_sems.at[1, t], (p, c ^ 2)))
        near.append(push(src, src, near_sems.at[0, t], near_sems.at[1, t], (p, c ^ 1)))
    if between is not None:
        between()
    for t in range(tiles):
        far[t].wait_recv()
        src = part(c ^ 2, t)
        hops.append(push(src, src, hop_sems.at[0, t], hop_sems.at[1, t], (p, c ^ 1)))
    for t in range(tiles):
        far[t].wait_send()
        near[t].wait()
        hops[t].wait()


def gather_scratch(tiles):
    return [dma(2, tiles), dma(2, tiles), dma(2, tiles)]


def to_classes(x):
    rows, cols, n = x.shape
    x = x.reshape(rows // ROW_CLASSES, ROW_CLASSES, cols // COL_CLASSES, COL_CLASSES, n)
    return x.transpose(1, 3, 0, 2, 4).reshape(PHASES, -1, n)


def from_classes(x, rows, cols):
    n = x.shape[-1]
    x = x.reshape(ROW_CLASSES, COL_CLASSES, rows // ROW_CLASSES, cols // COL_CLASSES, n)
    return x.transpose(2, 0, 3, 1, 4).reshape(rows, cols, n)


RATE_ROWS = tuple(rate // ROW_CLASSES for rate in aspp_rates)
RATE_COLS = tuple(rate // COL_CLASSES for rate in aspp_rates)


def load_pyramid(weight, wide, sems):
    m = weight.shape[4]
    return [
        [keep(weight.at[j, a, b], wide.at[3 * j + a, :, b * m : (b + 1) * m], sems.at[3 * j + a, b]) for b in range(3)]
        for j in range(3)
        for a in range(3)
    ]


def move_cols(x, by):
    place = lax.broadcasted_iota(jnp.int32, x.shape, 0) % 32
    rolled = pltpu.roll(x, by % x.shape[0], 0)
    return jnp.where(place < by, 0.0, rolled) if by > 0 else jnp.where(place >= 32 + by, 0.0, rolled)


def ch_exchange(send, recv, sems):
    p, c = lax.axis_index("pix"), lax.axis_index("ch")
    copies = [push(send, recv.at[c], sems.at[0, k], sems.at[1, k], (p, c ^ k)) for k in (2, 3, 1)]
    recv[c] = send[...]
    for copy in copies:
        copy.wait()


def add_up(recv, parts):
    value = recv[0]
    for i in range(1, parts):
        value = value + recv[i]
    return value


def task_vector(square, weights):
    product = square * weights
    row = lax.broadcasted_iota(jnp.int32, (32, 32), 0)
    col = lax.broadcasted_iota(jnp.int32, (32, 32), 1)

    def task(i):
        return (i >= CLS).astype(jnp.int32) + (i >= CLS + 1).astype(jnp.int32)

    def entry(t, s):
        return jnp.sum(
            jnp.sum(jnp.where((task(row) == t) & (task(col) == s), product, 0.0), axis=1, keepdims=True),
            axis=0,
            keepdims=True,
        )

    gram = [[entry(t, s) for s in range(3)] for t in range(3)]
    norms = [jnp.sqrt(gram[k][k] + 1e-06) for k in range(3)]
    proj = [[gram[i][k] / norms[k] for k in range(3)] for i in range(3)]
    vector = [proj[0][0] - proj[0][b] for b in (1, 2)]
    matrix = [[proj[0][0] - proj[0][b] - proj[a][0] + proj[a][b] for b in (1, 2)] for a in (1, 2)]
    determinant = matrix[0][0] * matrix[1][1] - matrix[0][1] * matrix[1][0]
    second = (vector[0] * matrix[1][1] - vector[1] * matrix[1][0]) / determinant
    third = (vector[1] * matrix[0][0] - vector[0] * matrix[0][1]) / determinant
    which = task(lax.broadcasted_iota(jnp.int32, (32, 1), 0))
    return jnp.where(which == 0, 1.0 - second - third, jnp.where(which == 1, second, third))


def slope(x):
    s = 1.0 / (1.0 + jnp.exp(-x))
    return s * (1.0 + x * (1.0 - s))


def pyramid(trunk, loads, wide, moving, pass_inputs, head_copies, heads, heads_all, targets, square, *refs):
    (full, predictions, head_grad, sums, others, picks) = refs[:6]
    (sides, own, out, near, cross, hidden, grad, branch) = refs[6:14]
    (s_send, s_ch, s_mid, s_pix, b_send, b_ch, b_mid, b_pix) = refs[14:22]
    (h_send, h_ch, h_mid, h_pix, h_sum, p_send, p_ch) = refs[22:29]
    (near_sems, far_sems, ch_sems, pix_sems, g_near, g_far, g_hop, y_sems, picked, pick_sems) = refs[29:]
    p, c = lax.axis_index("pix"), lax.axis_index("ch")
    k, x = lax.rem(c, 2), c // 2
    m = wide.shape[2] // 3
    pixels, half = trunk.shape[1], trunk.shape[2]
    quarter = pixels // SPLIT
    contract0 = (((0,), (0,)), ((), ()))
    contract1 = (((1,), (1,)), ((), ()))
    mine = rows(c * quarter, quarter)
    part = pixels // SPLIT
    sharing = []

    def share(slot, quarters, own, k, first):
        for i, q in enumerate(quarters):
            at = pl.ds(q * part, part)
            src = trunk.at[:, at] if own else others.at[2 - k, :, at]
            sharing.append(
                push(src, others.at[slot, :, at], y_sems.at[0, first + i], y_sems.at[1, first + i], (p ^ k, c))
            )
        return sharing[-len(quarters) :]

    def convolve(j, h):
        s = RATE_ROWS[j] * 32
        for a in (1, 0, 2):
            if h == 0:
                for load in loads[3 * j + a]:
                    load.wait()
            w = wide[3 * j + a, h * half : (h + 1) * half]
            if a == 1:
                value = jnp.dot(trunk[h], w, preferred_element_type=f32)
                if h == 0:
                    sides[j] = value
                else:
                    sides[j] += value
            elif a == 0:
                sides[j, s:] += jnp.dot(trunk[h, : pixels - s], w, preferred_element_type=f32)
            else:
                sides[j, : pixels - s] += jnp.dot(trunk[h, s:], w, preferred_element_type=f32)

    for copy in moving[0]:
        copy.wait()
    for j in range(3):
        convolve(j, 0)
    inputs_done = pass_inputs()
    for copy in moving[1]:
        copy.wait()
    from_y = share(0, (0, 1), True, 1, 0)
    from_z = share(1, (2, 3), True, 2, 2)

    def pass_on(i):
        from_y[i].wait_recv()
        share(2, (i,), False, 2, 4 + i)
        from_z[i].wait_recv()
        share(2, (i + 2,), False, 1, 6 + i)

    copies = []
    for j in range(3):
        q = RATE_COLS[j]
        convolve(j, 1)
        if j == 2:
            pass_on(0)
        for d in range(SPLIT):
            at = slice(d * quarter, (d + 1) * quarter)
            value = (
                sides[j, at, m : 2 * m]
                + move_cols(sides[j, at, :m], q)
                + move_cols(sides[j, at, 2 * m :], -q)
            )
            own[d, j] = value
            out[d, j] = value.astype(bf16)
        copies.append(
            [
                push(out.at[2 * h + 1 - k, j], near.at[h, j], near_sems.at[0, j, h], near_sems.at[1, j, h], (p, c ^ 1))
                for h in range(2)
            ]
        )
        if j > 0:
            copies[j - 1] = cross_chips(copies[j - 1], j - 1, own, near, cross, far_sems)
    copies[2] = cross_chips(copies[2], 2, own, near, cross, far_sems)
    for copy in head_copies:
        copy.wait()
    each = m // SPLIT
    for j in range(3):
        for d in range(SPLIT):
            heads[:, (j * SPLIT + d) * each : (j * SPLIT + d + 1) * each] = heads_all[d, :, j * each : (j + 1) * each]
    gain, bias = heads[32:33], heads[33:34]
    head = heads[:32]
    scaled = head * task_vector(
        add_up(square, PHASES)[:, :32], lax.dot_general(head, head, contract1, precision=highest)
    )
    target = jnp.concatenate([targets[2 * c], targets[2 * c + 1]], axis=1)
    mask = lax.dot_general(
        target[24:].astype(bf16), jnp.ones((8, m), bf16), contract0, preferred_element_type=f32
    )
    grad[...] = lax.dot_general(target, scaled, contract0, precision=highest) * jnp.concatenate([mask] * 3, axis=1)
    pass_on(1)
    count = total(mask)
    for j in range(3):
        copies[j].wait()
        value = own[2 * x + k, j] + near[x, j].astype(f32) + cross[1, j].astype(f32)
        at = slice(j * m, (j + 1) * m)
        hidden[:, at] = value
        first = total(value * mask)
        apart = value - first / jnp.maximum(count, 1.0)
        s_send[j : j + 1] = first
        s_send[3 + j : 4 + j] = total(apart * apart * mask)
    s_send[6:7] = count
    s_send[7:8] = jnp.zeros((1, m), f32)

    def merge(recv, parts):
        number = recv[0, 6:7]
        for i in range(1, parts):
            number = number + recv[i, 6:7]
        whole, spread = recv[0, 0:3], recv[0, 3:6]
        for i in range(1, parts):
            whole, spread = whole + recv[i, 0:3], spread + recv[i, 3:6]
        center = whole / jnp.maximum(number, 1.0)
        for i in range(parts):
            n = recv[i, 6:7]
            apart = recv[i, 0:3] / jnp.maximum(n, 1.0) - center
            spread = spread + n * apart * apart
        return whole, spread, number

    ch_exchange(s_send, s_ch, ch_sems.at[0])
    whole, spread, number = merge(s_ch, SPLIT)
    s_mid[0:3] = whole
    s_mid[3:6] = spread
    s_mid[6:7] = number
    s_mid[7:8] = jnp.zeros((1, m), f32)
    pix_exchange(s_mid, s_pix, pix_sems.at[0])
    share(0, (2,), True, 1, 8)
    share(1, (0,), True, 2, 9)
    whole, spread, number = merge(s_pix, PHASES)
    center, scale = whole / number, lax.rsqrt(spread / number + epsilon)
    for j in range(3):
        at = slice(j * m, (j + 1) * m)
        norm = (hidden[:, at] - center[j : j + 1]) * scale[j : j + 1]
        hidden[:, at] = norm
        value = norm * gain[:, at] + bias[:, at]
        branch[:, at] = (silu(value) * mask).astype(bf16)
        back = grad[:, at] * slope(value)
        grad[:, at] = back
        b_send[j : j + 1] = total(back)
        b_send[3 + j : 4 + j] = total(back * norm)
    b_send[6:8] = jnp.zeros((2, m), f32)
    to_ch = [push(b_send, b_ch.at[c], ch_sems.at[3, 0, i], ch_sems.at[3, 1, i], (p, c ^ i)) for i in (2, 3, 1)]
    b_ch[c] = b_send[...]
    high = target.astype(bf16)
    rest = target - high.astype(f32)
    middle = rest.astype(bf16)
    low = (rest - middle.astype(f32)).astype(bf16)
    p_send[...] = lax.dot_general(
        head.astype(bf16), branch[...], contract1, preferred_element_type=f32
    )
    value = jnp.dot(jnp.concatenate([high, middle, low]), branch[...], preferred_element_type=f32)
    h_send[...] = value[:32] + (value[32:64] + value[64:])
    background = [push(p_send, p_ch.at[c], ch_sems.at[1, 0, i], ch_sems.at[1, 1, i], (p, c ^ i)) for i in (2, 3, 1)] + [
        push(h_send.at[rows((c ^ i) * 8, 8)], h_ch.at[c], ch_sems.at[2, 0, i], ch_sems.at[2, 1, i], (p, c ^ i))
        for i in (2, 3, 1)
    ]
    p_ch[c] = p_send[...]
    h_ch[c] = h_send[rows(c * 8, 8)]
    for copy in to_ch:
        copy.wait()
    b_mid[...] = add_up(b_ch, SPLIT)
    sending = [
        push(b_mid, b_pix.at[p], pix_sems.at[1, 0, i], pix_sems.at[1, 1, i], (p ^ i, c)) for i in FAR_FIRST
    ]
    b_pix[p] = b_mid[...]
    for copy in background:
        copy.wait()
    h_mid[...] = add_up(h_ch, SPLIT)

    def block(to):
        return p_ch.at[to // 2, :, rows(lax.rem(to, 2) * 128, 128)]

    background = [
        push(block(p ^ i), predictions.at[p], pix_sems.at[2, 0, i], pix_sems.at[2, 1, i], (p ^ i, c)) for i in FAR_FIRST
    ] + [push(h_mid, h_pix.at[p], pix_sems.at[3, 0, i], pix_sems.at[3, 1, i], (p ^ i, c)) for i in FAR_FIRST]
    predictions[p] = block(p)[...]
    h_pix[p] = h_mid[...]
    for copy in sending:
        copy.wait()
    summed = add_up(b_pix, PHASES)
    sums[...] = summed
    for j in range(3):
        at = slice(j * m, (j + 1) * m)
        value = grad[:, at] - mask * (summed[j : j + 1] + hidden[:, at] * summed[3 + j : 4 + j]) / number
        full[mine, at] = (gain[:, at] * scale[j : j + 1] * value).astype(bf16)
    far = push(full.at[mine], full.at[mine], g_far.at[0], g_far.at[1], (p, c ^ 2))
    by = push(full.at[mine], full.at[mine], g_near.at[0], g_near.at[1], (p, c ^ 1))
    group = lax.rem(p, 4)
    pick = pick_rows(m, m, 0)
    for j in range(3):
        value = lax.dot_general(
            pick, full[mine, j * m : (j + 1) * m], contract1, preferred_element_type=f32
        ).astype(bf16)
        for g in range(4):
            picked[g, j * 64 : (j + 1) * 64] = value[g * 64 : (g + 1) * 64]
    sent_picks = [
        push(picked.at[group ^ i], picks.at[i - 1], pick_sems.at[0, i], pick_sems.at[1, i], (p ^ i, c)) for i in (3, 1, 2)
    ]
    for copy in background:
        copy.wait()
    own_rows = add_up(h_pix, PHASES)
    h_sum[...] = own_rows
    head_grad[rows(c * 8, 8)] = own_rows
    last = [
        push(h_sum, head_grad.at[rows(c * 8, 8)], ch_sems.at[4, 0, i], ch_sems.at[4, 1, i], (p, c ^ i))
        for i in (2, 3, 1)
    ]
    far.wait_recv()
    theirs = rows((c ^ 2) * quarter, quarter)
    hop = push(full.at[theirs], full.at[theirs], g_hop.at[0], g_hop.at[1], (p, c ^ 1))
    far.wait_send()
    by.wait()
    hop.wait()
    for copy in last:
        copy.wait()
    for copy in from_y + from_z:
        copy.wait_send()
    for copy in sharing[4:] + sent_picks:
        copy.wait()
    inputs_done()


def pick_rows(m, count, first):
    row = lax.broadcasted_iota(jnp.int32, (count, m), 0)
    col = lax.broadcasted_iota(jnp.int32, (count, m), 1)
    source = (4 * (row % 64 // 32) + row // 64 + first) * 32 + row % 32
    return jnp.where(col == source, 1.0, 0.0).astype(bf16)


def cross_chips(near_copies, j, own, near, cross, sems):
    p, c = lax.axis_index("pix"), lax.axis_index("ch")
    k, x = lax.rem(c, 2), c // 2
    for copy in near_copies:
        copy.wait()
    cross[0, j] = (own[2 * (1 - x) + k, j] + near[1 - x, j].astype(f32)).astype(bf16)
    return push(cross.at[0, j], cross.at[1, j], sems.at[0, j], sems.at[1, j], (p, c ^ 2))


def pyramid_scratch(pixels, n, m):
    quarter = pixels // SPLIT
    small = [
        pltpu.VMEM((8, m), f32),
        pltpu.VMEM((SPLIT, 8, m), f32),
        pltpu.VMEM((8, m), f32),
        pltpu.VMEM((PHASES, 8, m), f32),
    ]
    return [
        pltpu.VMEM((3, pixels, 3 * m), f32),
        pltpu.VMEM((SPLIT, 3, quarter, m), f32),
        pltpu.VMEM((SPLIT, 3, quarter, m), bf16),
        pltpu.VMEM((2, 3, quarter, m), bf16),
        pltpu.VMEM((2, 3, quarter, m), bf16),
        pltpu.VMEM((quarter, 3 * m), f32),
        pltpu.VMEM((quarter, 3 * m), f32),
        pltpu.VMEM((quarter, 3 * m), bf16),
        *small,
        *small,
        pltpu.VMEM((32, 3 * m), f32),
        pltpu.VMEM((SPLIT, 8, 3 * m), f32),
        pltpu.VMEM((8, 3 * m), f32),
        pltpu.VMEM((PHASES, 8, 3 * m), f32),
        pltpu.VMEM((8, 3 * m), f32),
        pltpu.VMEM((32, quarter), f32),
        pltpu.VMEM((SPLIT, 32, quarter), f32),
        dma(2, 3, 2),
        dma(2, 3),
        dma(5, 2, SPLIT),
        dma(4, 2, PHASES),
        dma(2),
        dma(2),
        dma(2),
        dma(2, 10),
        pltpu.VMEM((4, 192, quarter), bf16),
        dma(2, 4),
    ]


TILES = 4


def one_hot(rows_count, cols_count, source):
    row = lax.broadcasted_iota(jnp.int32, (rows_count, cols_count), 0)
    col = lax.broadcasted_iota(jnp.int32, (rows_count, cols_count), 1)
    return col == source(row)


def stage_one(feat, mask, weight, expand, gain, bias, *refs):
    (masked, reduce_rows, expand_cols, norm, padded, stat, valid) = refs[:7]
    (wide, hidden, own, out, near, cross, near_sems, far_sems, send, recv, stat_sems) = refs[7:18]
    (weight_sems, local_sems, halo_sems) = refs[18:]
    p, c = lax.axis_index("pix"), lax.axis_index("ch")
    pixels, local_in = feat.shape
    local_mid = weight.shape[1]
    tile = pixels // TILES

    def piece(i, to):
        return (
            (weight.at[rows(to * local_in, local_in), :], reduce_rows.at[:, rows(c * local_mid, local_mid)]),
            (expand.at[:, rows(to * local_in, local_in)], expand_cols.at[rows(c * local_mid, local_mid), :]),
        )[i]

    def to_ch(i):
        return [
            push(*piece(i, c ^ k), weight_sems.at[0, k, i], weight_sems.at[1, k, i], (p, c ^ k)) for k in (2, 3, 1)
        ] + [keep(*piece(i, c), local_sems.at[i])]

    reduce_copies = to_ch(0)

    present = mask[...].astype(f32)
    order = one_hot(128, 128, lambda i: 4 * (i % 32) + i // 32)
    ones = jnp.ones((128, 128), bf16)
    for r in range(8):
        column = jnp.dot(
            jnp.where(order, present[r : r + 1], 0.0).astype(bf16), ones, preferred_element_type=f32
        )
        for b in range(COL_CLASSES):
            block = ((r % ROW_CLASSES) * COL_CLASSES + b) * 128 + (r // ROW_CLASSES) * 32
            valid[block : block + 32] = column[b * 32 : (b + 1) * 32]
    for r in range(8):
        for g in range(local_in // 128):
            lanes = slice(g * 128, (g + 1) * 128)
            wide[g] = feat[r * 128 : (r + 1) * 128, lanes].astype(f32)
            for b in range(COL_CLASSES):
                block = ((r % ROW_CLASSES) * COL_CLASSES + b) * 128 + (r // ROW_CLASSES) * 32
                value = wide[g, pl.ds(b, 32, stride=COL_CLASSES), :] * valid[block : block + 32]
                masked[block : block + 32, lanes] = value.astype(bf16)

    for copy in reduce_copies:
        copy.wait()

    def part(t):
        return jnp.dot(masked[t * tile : (t + 1) * tile], reduce_rows[...], preferred_element_type=f32)

    result = sum_over_ch(part, tile, TILES, own, out, near, cross, near_sems, far_sems)
    for t in range(TILES):
        hidden[t * tile : (t + 1) * tile] = result(t)
    later = to_ch(1)
    center, scale, count = norm_stats(hidden, valid, pixels, send, recv, stat_sems)
    stat[0:1] = center
    stat[1:2] = scale
    stat[2:3] = count
    for i in range(PHASES):
        at = pl.ds(i * 128, 128)
        value = (hidden[at] - center) * scale
        norm[at] = value
        act = silu(value * gain[...] + bias[...]) * valid[at]
        padded[i, 1:5] = act.astype(bf16).reshape(4, 32, local_mid)
    up = lambda: pltpu.make_async_remote_copy(
        src_ref=padded.at[:, 4],
        dst_ref=padded.at[:, 0],
        send_sem=halo_sems.at[0, 0],
        recv_sem=halo_sems.at[1, 0],
        device_id=(p + 1, c),
        device_id_type=MESH,
    )
    down = lambda: pltpu.make_async_remote_copy(
        src_ref=padded.at[:, 1],
        dst_ref=padded.at[:, 5],
        send_sem=halo_sems.at[0, 1],
        recv_sem=halo_sems.at[1, 1],
        device_id=(p - 1, c),
        device_id_type=MESH,
    )
    first, last = p == 0, p == PHASES - 1

    @pl.when(jnp.logical_not(last))
    def _():
        up().start()

    @pl.when(jnp.logical_not(first))
    def _():
        down().start()

    @pl.when(last)
    def _():
        padded[:, 5] = jnp.zeros((PHASES, 32, local_mid), bf16)

    @pl.when(first)
    def _():
        padded[:, 0] = jnp.zeros((PHASES, 32, local_mid), bf16)

    @pl.when(jnp.logical_not(last))
    def _():
        up().wait_send()
        down().wait_recv()

    @pl.when(jnp.logical_not(first))
    def _():
        down().wait_send()
        up().wait_recv()

    return later


def prepare_heads(mask, head_weight, head_gain, head_bias, cotangent, *refs):
    (heads_all, targets_all, square_all, heads, targets, square, image, head_sems, pix_sems, local_sems) = refs
    p, c = lax.axis_index("pix"), lax.axis_index("ch")
    contract1 = (((1,), (1,)), ((), ()))
    present = mask[...].astype(f32)
    columns, m = head_weight.shape[1], head_weight.shape[2]
    heads[...] = jnp.zeros(heads.shape, f32)
    for j in range(3):
        heads[:columns, j * m : (j + 1) * m] = head_weight[j].astype(f32)
        heads[32:33, j * m : (j + 1) * m] = head_gain[j : j + 1]
        heads[33:34, j * m : (j + 1) * m] = head_bias[j : j + 1]

    image[...] = jnp.zeros(image.shape, f32)
    for r in range(8):
        at = slice(r * 128, (r + 1) * 128)
        image[:columns, at] = cotangent[:, r, :] * present[r : r + 1]
        image[31:32, at] = present[r : r + 1]
    square[...] = jnp.zeros(square.shape, f32)
    square[:, :32] = lax.dot_general(
        image[...], image[...], contract1, precision=highest, preferred_element_type=f32
    )
    place = jnp.where(
        one_hot(512, 512, lambda i: i % 4 * 128 + i // 128 * 32 + i % 128 // 4), 1.0, 0.0
    )
    for a in range(ROW_CLASSES):
        some = jnp.concatenate([image[:, (2 * r + a) * 128 : (2 * r + a + 1) * 128] for r in range(4)], axis=1)
        value = jnp.dot(some, place, precision=highest, preferred_element_type=f32)
        for b in range(COL_CLASSES):
            targets[a * COL_CLASSES + b] = value[:, b * 128 : (b + 1) * 128]
    copies = [push(heads, heads_all.at[c], head_sems.at[0, k], head_sems.at[1, k], (p, c ^ k)) for k in (2, 3, 1)]
    copies += [
        push(targets.at[p ^ k], targets_all.at[p], pix_sems.at[0, k, 0], pix_sems.at[1, k, 0], (p ^ k, c))
        for k in FAR_FIRST
    ] + [push(square, square_all.at[p], pix_sems.at[0, k, 1], pix_sems.at[1, k, 1], (p ^ k, c)) for k in FAR_FIRST]
    copies.append(keep(heads, heads_all.at[c], local_sems.at[0]))
    copies.append(keep(targets.at[p], targets_all.at[p], local_sems.at[1]))
    copies.append(keep(square, square_all.at[p], local_sems.at[2]))
    return copies


def stage_two(padded, valid, weight, gain, bias, *refs):
    (norm, full, taps, stat) = refs[:4]
    (hidden, own, out, near, cross, near_sems, far_sems, send, recv, stat_sems) = refs[4:14]
    (g_near, g_far, g_hop) = refs[14:]
    p, c = lax.axis_index("pix"), lax.axis_index("ch")
    pixels = valid.shape[0]
    local_mid = padded.shape[3]
    tile = pixels // TILES
    place = lax.broadcasted_iota(jnp.int32, (192, local_mid), 0) % 32
    for i in range(PHASES):
        beta = i % COL_CLASSES
        plain = padded[i].reshape(192, local_mid)
        wide = plain.astype(f32)
        if beta >= 2:
            moved_by = jnp.where(place == 0, 0.0, pltpu.roll(wide, 1, 0)).astype(bf16)
        else:
            moved_by = jnp.where(place == 31, 0.0, pltpu.roll(wide, 191, 0)).astype(bf16)
        for a in range(3):
            at = slice(a * 32, a * 32 + 128)
            for b, other, value in (
                (1, beta, plain),
                (0, (beta + 2) % 4, moved_by if beta >= 2 else plain),
                (2, (beta + 2) % 4, plain if beta >= 2 else moved_by),
            ):
                to = (i - beta + other) * 128
                col = (a * 3 + b) * local_mid
                taps[to : to + 128, col : col + local_mid] = value[at]

    def part(t):
        return jnp.dot(taps[t * tile : (t + 1) * tile], weight[...], preferred_element_type=f32)

    result = sum_over_ch(part, tile, TILES, own, out, near, cross, near_sems, far_sems)
    for t in range(TILES):
        hidden[t * tile : (t + 1) * tile] = result(t)
    center, scale, count = norm_stats(hidden, valid, pixels, send, recv, stat_sems)
    stat[0:1] = center
    stat[1:2] = scale
    stat[2:3] = count

    def ready(t):
        for i in range(tile // 128):
            at = pl.ds(t * tile + i * 128, 128)
            value = (hidden[at] - center) * scale
            norm[at] = value
            act = silu(value * gain[...] + bias[...]) * valid[at]
            full[at, rows(c * local_mid, local_mid)] = act.astype(bf16)

    gather_over_ch(full, local_mid, tile, TILES, g_near, g_far, g_hop, ready)


def stage_three(full, weight, masked, valid, gain, bias, counted, *refs):
    (norm, classes, stat, inputs) = refs[:4]
    (hidden, trunk, send, recv, stat_sems, class_sems, own_sem, in_sems) = refs[4:]
    p, c = lax.axis_index("pix"), lax.axis_index("ch")
    pixels, n = masked.shape
    tile = pixels // TILES
    for t in range(TILES):
        at = pl.ds(t * tile, tile)
        hidden[at] = jnp.dot(full[at], weight[...], preferred_element_type=f32)
    far = push(masked, inputs.at[c], in_sems.at[0, 0], in_sems.at[1, 0], (p, c ^ 2))
    near = push(masked, inputs.at[c], in_sems.at[0, 1], in_sems.at[1, 1], (p, c ^ 1))
    mine = keep(masked, inputs.at[c], own_sem.at[2])
    center, scale, count = norm_stats(hidden, valid, pixels, send, recv, stat_sems, counted)
    stat[0:1] = center
    stat[1:2] = scale
    stat[2:3] = count

    half = n // 2

    def finish(to, h):
        lanes = slice(h * half, (h + 1) * half)

        def step(i, carry):
            at = rows(to * 128 + i * 64, 64)
            value = (hidden[at, lanes] - center[:, lanes]) * scale[:, lanes]
            norm[at, lanes] = value
            pre = value * gain[:, lanes] + bias[:, lanes] + masked[at, lanes].astype(f32)
            v = valid[at]
            trunk[h, at] = (silu(pre) * jnp.concatenate([v] * (half // 128), axis=1)).astype(bf16)
            return carry

        loop(2, step, 0)

    copies = []
    for h in range(2):
        some = []
        for k in FAR_FIRST:
            to = p ^ k
            finish(to, h)
            some.append(
                push(
                    trunk.at[h, rows(to * 128, 128)],
                    classes.at[h, rows(p * 128, 128)],
                    class_sems.at[0, h, k],
                    class_sems.at[1, h, k],
                    (to, c),
                )
            )
        finish(p, h)
        some.append(keep(trunk.at[h, rows(p * 128, 128)], classes.at[h, rows(p * 128, 128)], own_sem.at[h]))
        copies.append(some)

    def pass_inputs():
        far.wait_recv()
        hop = push(inputs.at[c ^ 2], inputs.at[c ^ 2], in_sems.at[0, 2], in_sems.at[1, 2], (p, c ^ 1))

        def done():
            far.wait_send()
            near.wait()
            mine.wait()
            hop.wait()

        return done

    return copies, pass_inputs


def forward(
    feat, mask, weight, expand, gain1, bias1, head_weight, head_gain, head_bias, cotangent, dilated, gain2, bias2,
    gain3, bias3, pyramid_weight, *refs
):
    saved, stats, (inputs, grads, predictions, head_grad, branch_sums, others, picks) = refs[:10], refs[10:13], refs[13:20]
    padded, wide, w_sems, heads_full, save_sems = refs[20:25]
    masked, reduce_rows, expand_cols, norm1, valid, norm2, full2, taps, norm3, classes = refs[25:35]
    stat1, stat2, stat3 = stats
    own = refs[35:]
    saving = []

    def save(*which):
        for i in which:
            saving.append(keep(refs[25 + i], saved[i], save_sems.at[i]))

    one, two, three, heads = 14, 13, 8, 10
    barrier, expected = greet((1, 2, 3), FAR_FIRST)
    loads = load_pyramid(pyramid_weight, wide, w_sems)
    pl.semaphore_wait(barrier, expected)
    expand_copies = stage_one(
        feat, mask, weight, expand, gain1, bias1, masked, reduce_rows, expand_cols, norm1, padded, stat1, valid, *own[:one]
    )
    counted = own[9]
    own = own[one:]
    save(0, 1, 3, 4)
    stage_two(padded, valid, dilated, gain2, bias2, norm2, full2, taps, stat2, *own[:two])
    own = own[two:]
    for copy in expand_copies:
        copy.wait()
    save(2, 5, 6, 7)
    moving, pass_inputs = stage_three(
        full2, expand_cols, masked, valid, gain3, bias3, counted, norm3, classes, stat3, inputs, *own[:three]
    )
    own = own[three:]
    save(8)
    head_copies = prepare_heads(mask, head_weight, head_gain, head_bias, cotangent, *own[:heads])
    pyramid(
        classes, loads, wide, moving, pass_inputs, head_copies, heads_full, *own[:3],
        grads, predictions, head_grad, branch_sums, others, picks, *own[heads:],
    )
    save(9)
    for copy in saving:
        copy.wait()


def run_forward(
    cid, feat, mask, weight, expand, gain1, bias1, head_weight, head_gain, head_bias, cotangent, dilated, gain2, bias2,
    gain3, bias3, pyramid_weight
):
    pixels, n = feat.shape
    mid = weight.shape[1]
    all_mid = SPLIT * mid
    m = pyramid_weight.shape[4]
    quarter = pixels // SPLIT
    saved = [
        ((pixels, n), bf16),
        ((n, all_mid), bf16),
        ((all_mid, n), bf16),
        ((pixels, mid), f32),
        ((pixels, 128), f32),
        ((pixels, mid), f32),
        ((pixels, all_mid), bf16),
        ((pixels, 9 * mid), bf16),
        ((pixels, n), f32),
        ((2, pixels, n // 2), bf16),
    ]
    outs = [shape(*each) for each in saved] + [
        shape((8, mid), f32),
        shape((8, mid), f32),
        shape((8, n), f32),
        shape((SPLIT, pixels, n), bf16),
        shape((pixels, 3 * m), bf16),
        shape((PHASES, 32, 128), f32),
        shape((32, 3 * m), f32),
        shape((8, m), f32),
        shape((3, 2, pixels, n // 2), bf16),
        shape((3, 192, quarter), bf16),
    ]
    scratch = [
        pltpu.VMEM((PHASES, 6, 32, mid), bf16),
        pltpu.VMEM((9, n, 3 * m), bf16),
        dma(9, 3),
        pltpu.VMEM((40, 3 * m), f32),
        dma(10),
        *[pltpu.VMEM(*each) for each in saved],
        pltpu.VMEM((n // 128, 128, 128), f32),
        pltpu.VMEM((pixels, mid), f32),
        *sum_scratch(pixels, mid, TILES),
        *stat_scratch(mid),
        dma(2, SPLIT, 2),
        dma(2),
        dma(2, 2),
        pltpu.VMEM((pixels, mid), f32),
        *sum_scratch(pixels, mid, TILES),
        *stat_scratch(mid),
        *gather_scratch(TILES),
        pltpu.VMEM((pixels, n), f32),
        pltpu.VMEM((2, pixels, n // 2), bf16),
        *stat_scratch(128),
        dma(2, 2, PHASES),
        dma(4),
        dma(2, 3),
        pltpu.VMEM((SPLIT, 40, 256), f32),
        pltpu.VMEM((PHASES, 32, 128), f32),
        pltpu.VMEM((PHASES, 32, 128), f32),
        pltpu.VMEM((40, 256), f32),
        pltpu.VMEM((PHASES, 32, 128), f32),
        pltpu.VMEM((32, 128), f32),
        pltpu.VMEM((32, pixels), f32),
        dma(2, SPLIT),
        dma(2, PHASES, 2),
        dma(3),
        *pyramid_scratch(pixels, n, m),
    ]
    arrays = [
        feat, mask, weight, expand, gain1, bias1, head_weight, head_gain, head_bias, cotangent, dilated, gain2, bias2,
        gain3, bias3, pyramid_weight,
    ]
    return call("forward", cid, forward, arrays, outs, scratch, hbm_ins=(15,), hbm_outs=(*range(10), 13, 18))


PACE = (1, 10, 20, 23)


def packed_sums(values, send):
    i = 0
    for value in values:
        for g in range(value.shape[1] // 128):
            send[i : i + 1] = value[:, g * 128 : (g + 1) * 128]
            i += 1


def unpacked_sums(recv, rows_each, count):
    out, i = [], 0
    for _ in range(count):
        parts = []
        for _ in range(rows_each):
            value = recv[0, i : i + 1]
            for d in range(1, PHASES):
                value = value + recv[d, i : i + 1]
            parts.append(value)
            i += 1
        out.append(parts[0] if rows_each == 1 else jnp.concatenate(parts, axis=1))
    return out


def backward(
    grads, trunk, others, weight, norm3, masked, valid, expand, gain3, bias3, norm2, gain2, bias2, full2, taps, dilated,
    norm1, gain1, bias1, reduce_rows, stats1, stats2, stats3, picks, inputs, *refs
):
    stored = (valid, norm3, masked, expand, norm2, full2, norm1, dilated, reduce_rows)
    valid, norm3, masked, expand, norm2, full2, norm1, dilated, reduce_rows, store_sems = refs[-10:]
    refs = refs[:-10]
    outs, scratch = refs[:6], refs[6:]
    (features_grad, aspp_parts, dilated_grad, expand_grad, reduce_grad, sums_out) = outs
    (wide, moved, acc, dsend, drecv, tpad, r_in, picked_in, turned, zsend, r_y) = scratch[:11]
    (gp3, g3, own, out, near, cross, hidden, gp2, g2, prod, edges, g1) = scratch[11:23]
    gp1, lanes = gp2, own
    (st3, st3r, st2, st2r, st1, st1r, e_part, e_mid, e_in, e_y, e_sum, d_part, d_in, d_y, d_sum, r_mid, r_sum) = scratch[23:40]
    (w_sems, d_sems, y_sems, z_sems, near_sems, far_sems, st_sems, gn, gf, gh, gn1, gf1, gh1, edge_sems, ch_sems, pix_sems, pair_sems, own_sems, tap_sems, in_sems, fill_sems, last_sems, slope1, d_near, d_far, mid_sems) = scratch[40:]
    p, c = lax.axis_index("pix"), lax.axis_index("ch")
    y, z = lax.rem(p, 2), p // 2
    lower = lax.rem(z, 2)
    pixels, n = norm3.shape
    m = weight.shape[4]
    mid = norm2.shape[1]
    tile = pixels // TILES
    contract0 = (((0,), (0,)), ((), ()))
    contract1 = (((1,), (1,)), ((), ()))
    count = stats1[2:3, :1]
    barrier, expected = greet((1, 2, 3), FAR_FIRST)
    loads = load_pyramid(weight, wide, w_sems)
    arrived = dict(
        zip(
            ("valid", "norm3", "masked", "expand", "norm2", "full2", "norm1", "dilated", "reduce"),
            [keep(a, b, store_sems.at[i]) for i, (a, b) in enumerate(
                zip(stored, (valid, norm3, masked, expand, norm2, full2, norm1, dilated, reduce_rows))
            )],
        )
    )

    group, upper = lax.rem(p, 4), p // 4
    quarter = picks.shape[2]
    pl.semaphore_wait(barrier, expected)
    mine = rows(c * quarter, quarter)
    sent_picks = [
        push(picks, picked_in.at[:, :, mine], y_sems.at[0, k], y_sems.at[1, k], (p, c ^ k)) for k in (2, 3, 1)
    ] + [keep(picks, picked_in.at[:, :, mine], y_sems.at[0, 0])]
    part = pixels // SPLIT
    filled = []
    for k in range(4):
        for h in range(2):
            cols = slice(h * m, (h + 1) * m)
            source = (others.at[k - 1] if k else trunk).at[h]
            here = {0: ((0, 4),), 1: ((0, 3),), 2: ((0, 1), (2, 4)), 3: ((0, 4),)}[k]
            for i, (first, end) in enumerate(here):
                at = pl.ds(first * part, (end - first) * part)
                filled.append(
                    keep(source.at[at], tpad.at[k, pl.ds(64 + first * part, (end - first) * part), cols], fill_sems.at[k, h, i])
                )
            if k in (1, 2):
                q = 3 if k == 1 else 1
                filled.append(
                    push(
                        trunk.at[h, pl.ds(q * part, part)],
                        tpad.at[k, pl.ds(64 + q * part, part), cols],
                        last_sems.at[0, k - 1, h],
                        last_sems.at[1, k - 1, h],
                        (p ^ k, c),
                    )
                )
    for i in range(4):
        tpad[i, :64] = jnp.zeros((64, n), bf16)
        tpad[i, 64 + pixels :] = jnp.zeros((64, n), bf16)

    for j in range(3):
        q = RATE_COLS[j]
        plain = grads[:, j * m : (j + 1) * m]
        value = plain.astype(f32)
        moved[j, :, :m] = move_cols(value, -q).astype(bf16)
        moved[j, :, m : 2 * m] = plain
        moved[j, :, 2 * m :] = move_cols(value, q).astype(bf16)
    back = []
    for h in range(2):
        half = slice(h * m, (h + 1) * m)
        for j in range(3):
            s = RATE_ROWS[j] * 32
            for a in (1, 0, 2):
                if h == 0:
                    for load in loads[3 * j + a]:
                        load.wait()
                w = wide[3 * j + a, half]
                if a == 1:
                    value = lax.dot_general(moved[j], w, contract1, preferred_element_type=f32)
                    if j == 0:
                        acc[...] = value
                    else:
                        acc[...] += value
                elif a == 0:
                    acc[: pixels - s] += lax.dot_general(moved[j, s:], w, contract1, preferred_element_type=f32)
                else:
                    acc[s:] += lax.dot_general(moved[j, : pixels - s], w, contract1, preferred_element_type=f32)
        dsend[h] = acc[...].astype(bf16)
        for k in FAR_FIRST:
            back.append(
                push(
                    dsend.at[h, rows((p ^ k) * 128, 128)],
                    drecv.at[h, rows(p * 128, 128)],
                    d_sems.at[0, h, k],
                    d_sems.at[1, h, k],
                    (p ^ k, c),
                )
            )
        back.append(keep(dsend.at[h, rows(p * 128, 128)], drecv.at[h, rows(p * 128, 128)], own_sems.at[h]))

    all_inputs = [
        keep(inputs.at[i // 2, pl.ds(i % 2 * n, n)], wide.at[i, :, :n], in_sems.at[i]) for i in range(8)
    ]
    cut = moved.shape[2]
    own_taps = [
        keep(taps.at[:, :cut], moved.at[0], tap_sems.at[0]),
        keep(taps.at[:, cut:], moved.at[1, :, : taps.shape[1] - cut], tap_sems.at[1]),
    ]

    place = lax.broadcasted_iota(jnp.int32, (64, pixels), 1) % 32

    def turn(i, part):
        at = slice(i * pixels, (i + 1) * pixels)
        for j in range(3):
            q = RATE_COLS[j]
            plain = part(j)
            value = plain.astype(f32)
            turned[j, :64, at] = jnp.where(place >= 32 - q, 0.0, pltpu.roll(value, pixels - q, 1)).astype(bf16)
            turned[j, 64:128, at] = plain
            turned[j, 128:, at] = jnp.where(place < q, 0.0, pltpu.roll(value, q, 1)).astype(bf16)

    pick = pick_rows(m, 64, group)
    turn(
        0,
        lambda j: lax.dot_general(
            pick, grads[:, j * m : (j + 1) * m], contract1, preferred_element_type=f32
        ).astype(bf16),
    )
    for copy in sent_picks:
        copy.wait()
    for k in (1, 2, 3):
        turn(k, lambda j: picked_in[k - 1, j * 64 : (j + 1) * 64])
    for copy in filled:
        copy.wait()
    for j in range(3):
        s = RATE_ROWS[j] * 32
        for a in range(3):
            if a == 1:
                low, high, start = 0, pixels, 64
            elif a == 0:
                low, high = s // 128 * 128, pixels
                start = 64 + low - s
            else:
                low, high, start = 0, -(-(pixels - s) // 128) * 128, 64 + s
            value = None
            for i in range(4):
                term = jnp.dot(
                    turned[j, :, i * pixels + low : i * pixels + high],
                    tpad[i, start : start + high - low],
                    preferred_element_type=f32,
                )
                value = term if value is None else value + term
            value = value.astype(bf16)
            for b in range(3):
                for to in range(2):
                    at = b * 64 + to * 32
                    zsend[to, (3 * j + a) * 3 + b] = value[at : at + 32]
    for name in ("valid", "norm3", "masked", "norm2", "norm1"):
        arrived[name].wait()

    def slopes(i, carry):
        at = rows(i * 32, 32)
        pre = norm3[at] * gain3[...] + bias3[...] + masked[at].astype(f32)
        gp3[at] = spread_lanes(valid[at], n) * slope(pre)
        gp2[at] = valid[at] * slope(norm2[at] * gain2[...] + bias2[...])
        slope1[at] = valid[at] * slope(norm1[at] * gain1[...] + bias1[...])
        return carry

    loop(pixels // 32, slopes, 0)
    zcopies = [keep(zsend.at[upper], aspp_parts.at[0], own_sems.at[2])]

    def send_parts(first, end):
        for i in range(first, end):
            zcopies.append(
                push(zsend.at[1 - upper, i], aspp_parts.at[1, i], z_sems.at[0, i], z_sems.at[1, i], (p ^ 4, c))
            )


    def over_z(blocks, sums, sems, own_sem):
        return [
            push(blocks.at[z ^ k], sums.at[z], sems.at[0, k], sems.at[1, k], (p ^ (2 * k), c)) for k in (3, 2, 1)
        ] + [keep(blocks.at[z], sums.at[z], own_sem)]

    def norm_back(grad, norm, sums, scale, gain, v):
        return gain * scale * (grad - v * (sums[0] + norm * sums[1]) / count)

    totals = []
    for h in range(2):
        for copy in back[h * PHASES : (h + 1) * PHASES]:
            copy.wait()
        if h == 1:
            send_parts(0, PACE[0])
        cols = slice(h * m, (h + 1) * m)

        def three(i, carry):
            at = rows(i * 64, 64)
            grad = drecv[h, at].astype(f32) * gp3[at, cols]
            gp3[at, cols] = grad
            return carry[0] + fold(grad), carry[1] + fold(grad * norm3[at, cols])

        zero = jnp.zeros((8, m), f32)
        bias, gain = loop(pixels // 64, three, (zero, zero))
        totals.append((total(bias), total(gain)))
    bias, gain = (jnp.concatenate([totals[0][i], totals[1][i]], axis=1) for i in range(2))
    packed_sums((bias, gain), st3)
    pix_exchange(st3, st3r, st_sems.at[0])
    send_parts(PACE[0], PACE[1])
    sums = unpacked_sums(st3r, n // 128, 2)
    sums_out[0:1] = sums[0]
    sums_out[1:2] = sums[1]

    arrived["expand"].wait()

    def part3(t):
        def step(i, carry):
            at = rows(t * tile + i * 32, 32)
            v = spread_lanes(valid[at], n)
            g3[at] = norm_back(gp3[at], norm3[at], sums, stats3[1:2], gain3[...], v).astype(bf16)
            return carry

        loop(tile // 32, step, 0)
        return lax.dot_general(g3[t * tile : (t + 1) * tile], expand[...], contract1, preferred_element_type=f32)

    result = sum_over_ch(part3, tile, TILES, own, out, near, cross, near_sems.at[0], far_sems.at[0])
    arrived["full2"].wait()
    value = lax.dot_general(full2[...], g3[...], contract0, preferred_element_type=f32).astype(bf16)
    for d in range(SPLIT):
        e_part[d] = value[d * mid : (d + 1) * mid]
    e_copies = [
        push(e_part.at[c ^ k], e_mid.at[c], ch_sems.at[0, 0, k], ch_sems.at[0, 1, k], (p, c ^ k)) for k in (2, 3, 1)
    ]
    e_copies.append(keep(e_part.at[c], e_mid.at[c], own_sems.at[3]))

    bias, gain = jnp.zeros((8, mid), f32), jnp.zeros((8, mid), f32)
    for t in range(TILES):
        hidden[t * tile : (t + 1) * tile] = result(t)

    def two(i, carry):
        at = rows(i * 128, 128)
        grad = hidden[at] * gp2[at]
        gp2[at] = grad
        return carry[0] + fold(grad), carry[1] + fold(grad * norm2[at])

    bias, gain = loop(pixels // 128, two, (bias, gain))
    packed_sums((total(bias), total(gain)), st2)
    pix_exchange(st2, st2r, st_sems.at[1])
    send_parts(PACE[1], PACE[2])
    for copy in e_copies:
        copy.wait()
    e_to_y = push(
        e_mid.at[:, :, rows((1 - y) * 256, 256)], e_in, pair_sems.at[0, 0], pair_sems.at[1, 0], (p ^ 1, c)
    )
    sums2 = unpacked_sums(st2r, 1, 2)
    sums_out[2:3, :mid] = sums2[0]
    sums_out[3:4, :mid] = sums2[1]

    def ready2(t):
        def step(i, carry):
            at = rows(t * tile + i * 128, 128)
            value = norm_back(gp2[at], norm2[at], sums2, stats2[1:2], gain2[...], valid[at])
            g2[at, rows(c * mid, mid)] = value.astype(bf16)
            return carry

        loop(tile // 128, step, 0)

    gather_over_ch(g2, mid, tile, TILES, gn, gf, gh, ready2)

    e_to_y.wait()
    for d in range(4):
        e_y[d] = (e_mid[d, :, rows(y * 256, 256)].astype(f32) + e_in[d].astype(f32)).astype(bf16)
    pix_copies = over_z(e_y, e_sum, pix_sems.at[0], own_sems.at[5])

    place = lax.broadcasted_iota(jnp.int32, (128, mid), 0) % 32

    def across(i, a):
        beta = i % COL_CLASSES
        two_on = (beta + 2) % 4 * 128
        here = slice(beta * 128, (beta + 1) * 128)
        there = slice(two_on, two_on + 128)
        lane = lambda b: slice((3 * a + b) * mid, (3 * a + b + 1) * mid)
        left, right = prod[there, lane(0)], prod[there, lane(2)]
        if beta >= 2:
            left = jnp.where(place == 31, 0.0, pltpu.roll(left, 127, 0))
        else:
            right = jnp.where(place == 0, 0.0, pltpu.roll(right, 1, 0))
        return prod[here, lane(1)] + left + right

    arrived["dilated"].wait()
    for i in range(PHASES):
        at = slice(i * 128, (i + 1) * 128)
        if i % COL_CLASSES == 0:
            prod[...] = lax.dot_general(
                g2[i * 128 : (i + COL_CLASSES) * 128], dilated[...], contract1, preferred_element_type=f32
            )
        up, same, down = across(i, 0), across(i, 1), across(i, 2)
        zero = jnp.zeros((32, mid), f32)
        hidden[at] = same + jnp.concatenate([up[32:], zero]) + jnp.concatenate([zero, down[:96]])
        edges[0, i] = up[:32].astype(bf16)
        edges[1, i] = down[96:].astype(bf16)
    first, last = p == 0, p == PHASES - 1
    to_next = lambda: pltpu.make_async_remote_copy(
        src_ref=edges.at[1], dst_ref=edges.at[2], send_sem=edge_sems.at[0, 0], recv_sem=edge_sems.at[1, 0],
        device_id=(p + 1, c), device_id_type=MESH,
    )
    to_last = lambda: pltpu.make_async_remote_copy(
        src_ref=edges.at[0], dst_ref=edges.at[3], send_sem=edge_sems.at[0, 1], recv_sem=edge_sems.at[1, 1],
        device_id=(p - 1, c), device_id_type=MESH,
    )

    @pl.when(jnp.logical_not(last))
    def _():
        to_next().start()

    @pl.when(jnp.logical_not(first))
    def _():
        to_last().start()

    @pl.when(first)
    def _():
        edges[2] = jnp.zeros((PHASES, 32, mid), bf16)

    @pl.when(last)
    def _():
        edges[3] = jnp.zeros((PHASES, 32, mid), bf16)

    for copy in own_taps:
        copy.wait()
    value = jnp.concatenate(
        [
            lax.dot_general(g2[...], moved[0], contract0, preferred_element_type=f32).astype(bf16),
            lax.dot_general(
                g2[...], moved[1, :, : taps.shape[1] - cut], contract0, preferred_element_type=f32
            ).astype(bf16),
        ],
        axis=1,
    )
    out_rows = SPLIT * mid // PHASES
    for d in range(PHASES):
        d_part[d % 2, d // 2] = value[d * out_rows : (d + 1) * out_rows]
    halves = [pl.ds(h * out_rows // 2, out_rows // 2) for h in range(2)]
    d_to_y = [
        push(d_part.at[1 - y, :, at], d_in.at[:, at], mid_sems.at[0, 4 + h], mid_sems.at[1, 4 + h], (p ^ 1, c))
        for h, at in enumerate(halves)
    ]
    d_to_z, d_across = [], []

    def add_y(h):
        at = halves[h]
        d_to_y[h].wait()
        for d in range(4):
            d_y[d // 2, d % 2, at] = (d_part[y, d, at].astype(f32) + d_in[d, at].astype(f32)).astype(bf16)
        d_to_z.append(
            push(d_y.at[:, 1 - lower, at], d_near.at[:, at], mid_sems.at[0, h], mid_sems.at[1, h], (p ^ 2, c))
        )

    def add_z(h):
        at = halves[h]
        d_to_z[h].wait()
        for d in range(2):
            d_sum[d, at] = (d_y[d, lower, at].astype(f32) + d_near[d, at].astype(f32)).astype(bf16)
        d_across.append(
            push(d_sum.at[1 - upper, at], d_far.at[at], mid_sems.at[0, 2 + h], mid_sems.at[1, 2 + h], (p ^ 4, c))
        )

    @pl.when(jnp.logical_not(last))
    def _():
        to_next().wait_send()
        to_last().wait_recv()

    @pl.when(jnp.logical_not(first))
    def _():
        to_last().wait_send()
        to_next().wait_recv()

    send_parts(PACE[2], PACE[3])

    bias, gain = jnp.zeros((8, mid), f32), jnp.zeros((8, mid), f32)
    for i in range(PHASES):
        at = slice(i * 128, (i + 1) * 128)
        zero = jnp.zeros((64, mid), f32)
        edge = jnp.concatenate([edges[2, i].astype(f32), zero, edges[3, i].astype(f32)])
        grad = (hidden[at] + edge) * slope1[at]
        gp1[at] = grad
        bias, gain = bias + fold(grad), gain + fold(grad * norm1[at])
    packed_sums((total(bias), total(gain)), st1)
    pix_exchange(st1, st1r, st_sems.at[2])
    add_y(0)
    send_parts(PACE[3], 27)
    sums1 = unpacked_sums(st1r, 1, 2)
    sums_out[4:5, :mid] = sums1[0]
    sums_out[5:6, :mid] = sums1[1]

    def ready1(t):
        def step(i, carry):
            at = rows(t * tile + i * 128, 128)
            value = norm_back(gp1[at], norm1[at], sums1, stats1[1:2], gain1[...], valid[at])
            g1[at, rows(c * mid, mid)] = value.astype(bf16)
            return carry

        loop(tile // 128, step, 0)

    late = []

    def between():
        for copy in all_inputs:
            copy.wait()
        own_g1 = g1[:, rows(c * mid, mid)]
        for i in range(SPLIT):
            value = lax.dot_general(wide[2 * i, :, :n], own_g1[:n], contract0, preferred_element_type=f32)
            value = value + lax.dot_general(wide[2 * i + 1, :, :n], own_g1[n:], contract0, preferred_element_type=f32)
            r_mid[i] = value.astype(bf16).reshape(2, 256, mid)
        late.append(push(r_mid.at[:, 1 - y], r_in, pair_sems.at[0, 2], pair_sems.at[1, 2], (p ^ 1, c)))
        add_y(1)
        add_z(0)

    gather_over_ch(g1, mid, tile, TILES, gn1, gf1, gh1, ready1, between)
    late[0].wait()
    for d in range(4):
        r_y[d] = (r_mid[d, y].astype(f32) + r_in[d].astype(f32)).astype(bf16)
    pix_copies += over_z(r_y, r_sum, pix_sems.at[2], own_sems.at[7])
    add_z(1)

    arrived["reduce"].wait()
    for i in range(PHASES):
        at = slice(i * 128, (i + 1) * 128)
        value = lax.dot_general(g1[at], reduce_rows[...], contract1, preferred_element_type=f32) + gp3[at]
        value = value * spread_lanes(valid[at], n)
        for g in range(n // 128):
            for r in range(4):
                start = (2 * r + i // COL_CLASSES) * 128 + i % COL_CLASSES
                lanes[g, pl.ds(start, 32, stride=COL_CLASSES), :] = value[r * 32 : (r + 1) * 32, g * 128 : (g + 1) * 128]
    for g in range(n // 128):
        features_grad[:, g * 128 : (g + 1) * 128] = lanes[g].astype(bf16)
    for copy in pix_copies:
        copy.wait()

    def gathered(parts):
        value = parts[0].astype(f32)
        for d in range(1, parts.shape[0]):
            value = value + parts[d].astype(f32)
        return value

    expand_grad[...] = gathered(e_sum)
    reduce_grad[...] = gathered(r_sum)
    for copy in d_across:
        copy.wait()
    value = d_sum[upper].astype(f32) + d_far[...].astype(f32)
    for i in range(9):
        dilated_grad[i] = value[:, i * mid : (i + 1) * mid]
    for copy in zcopies:
        copy.wait()


def run_backward(cid, arrays):
    (grads, trunk, others, weight, norm3, masked, valid, expand, gain3, bias3, norm2, gain2, bias2, full2, taps, dilated,
     norm1, gain1, bias1, reduce_rows, stats1, stats2, stats3, picks, inputs) = arrays
    pixels, n = norm3.shape
    m = weight.shape[4]
    mid = norm2.shape[1]
    all_mid = SPLIT * mid
    outs = [
        shape((pixels, n), bf16),
        shape((2, 27, 32, n), bf16),
        shape((9, all_mid // PHASES, mid), f32),
        shape((mid, 256), f32),
        shape((256, mid), f32),
        shape((8, n), f32),
    ]
    sums = sum_scratch(pixels, mid, TILES)
    scratch = [
        pltpu.VMEM((9, n, 3 * m), bf16),
        pltpu.VMEM((3, pixels, 3 * m), bf16),
        pltpu.VMEM((pixels, m), f32),
        pltpu.VMEM((2, pixels, m), bf16),
        pltpu.VMEM((2, pixels, m), bf16),
        pltpu.VMEM((4, pixels + 128, n), bf16),
        pltpu.VMEM((4, 256, mid), bf16),
        pltpu.VMEM((3, 192, pixels), bf16),
        pltpu.VMEM((3, 192, 4 * pixels), bf16),
        pltpu.VMEM((2, 27, 32, n), bf16),
        pltpu.VMEM((4, 256, mid), bf16),
        pltpu.VMEM((pixels, n), f32),
        pltpu.VMEM((pixels, n), bf16),
        *sums[:4],
        pltpu.VMEM((pixels, mid), f32),
        pltpu.VMEM((pixels, mid), f32),
        pltpu.VMEM((pixels, all_mid), bf16),
        pltpu.VMEM((pixels // ROW_CLASSES, 9 * mid), f32),
        pltpu.VMEM((4, PHASES, 32, mid), bf16),
        pltpu.VMEM((pixels, all_mid), bf16),
        pltpu.VMEM((8, 128), f32),
        pltpu.VMEM((PHASES, 8, 128), f32),
        pltpu.VMEM((8, 128), f32),
        pltpu.VMEM((PHASES, 8, 128), f32),
        pltpu.VMEM((8, 128), f32),
        pltpu.VMEM((PHASES, 8, 128), f32),
        pltpu.VMEM((SPLIT, mid, n), bf16),
        pltpu.VMEM((SPLIT, mid, n), bf16),
        pltpu.VMEM((4, mid, 256), bf16),
        pltpu.VMEM((4, mid, 256), bf16),
        pltpu.VMEM((4, mid, 256), bf16),
        pltpu.VMEM((2, 4, all_mid // PHASES, 9 * mid), bf16),
        pltpu.VMEM((4, all_mid // PHASES, 9 * mid), bf16),
        pltpu.VMEM((2, 2, all_mid // PHASES, 9 * mid), bf16),
        pltpu.VMEM((2, all_mid // PHASES, 9 * mid), bf16),
        pltpu.VMEM((4, 2, 256, mid), bf16),
        pltpu.VMEM((4, 256, mid), bf16),
        dma(9, 3),
        dma(2, 2, PHASES),
        dma(3, 4),
        dma(2, 27),
        dma(1, 2, TILES, 2),
        dma(1, 2, TILES),
        dma(3, 2, PHASES),
        *gather_scratch(TILES),
        *gather_scratch(TILES),
        dma(2, 2),
        dma(2, 2, SPLIT),
        dma(3, 2, PHASES),
        dma(2, 3),
        dma(8),
        dma(2),
        dma(8),
        dma(4, 2, 2),
        dma(2, 2, 2),
        pltpu.VMEM((pixels, mid), f32),
        pltpu.VMEM((2, all_mid // PHASES, 9 * mid), bf16),
        pltpu.VMEM((all_mid // PHASES, 9 * mid), bf16),
        dma(2, 6),
        pltpu.VMEM((pixels, 128), f32),
        pltpu.VMEM((pixels, n), f32),
        pltpu.VMEM((pixels, n), bf16),
        pltpu.VMEM((all_mid, n), bf16),
        pltpu.VMEM((pixels, mid), f32),
        pltpu.VMEM((pixels, all_mid), bf16),
        pltpu.VMEM((pixels, mid), f32),
        pltpu.VMEM((9 * mid, all_mid), bf16),
        pltpu.VMEM((n, all_mid), bf16),
        dma(9),
    ]
    vmem = pl.BlockSpec(memory_space=pltpu.VMEM)
    specs = [vmem] * len(arrays)
    for i in (1, 2, 3, 4, 5, 6, 7, 10, 13, 14, 15, 16, 19, 24):
        specs[i] = pl.BlockSpec(memory_space=pl.ANY)
    return pl.pallas_call(
        backward,
        out_shape=outs,
        in_specs=specs,
        out_specs=[vmem, pl.BlockSpec(memory_space=pl.ANY)] + [vmem] * (len(outs) - 2),
        scratch_shapes=scratch,
        compiler_params=pltpu.CompilerParams(
            collective_id=cid, has_side_effects=True, vmem_limit_bytes=VMEM_BYTES
        ),
        name="backward",
    )(*arrays)


def publish(features, parts, dilated, expand, reduce, norm_sums, predictions, head_grad, branch_sums, *outs):
    (o_predictions, o_features, o_reduce, o_gain1, o_bias1, o_dilated, o_gain2, o_bias2, o_expand, o_gain3, o_bias3,
     o_parts, o_branch_gain, o_branch_bias, o_heads) = outs
    c = lax.axis_index("ch")
    columns, mid = o_predictions.shape[0], o_gain1.shape[1]
    m = o_heads.shape[2]
    o_features[...] = features[...]
    o_reduce[...] = reduce[...]
    o_expand[...] = expand[...]
    o_dilated[...] = dilated[...]
    for i in range(parts.shape[1]):
        o_parts[i] = parts[0, i].astype(f32) + parts[1, i].astype(f32)
    o_bias3[...] = norm_sums[0:1]
    o_gain3[...] = norm_sums[1:2]
    o_bias2[...] = norm_sums[2:3, :mid]
    o_gain2[...] = norm_sums[3:4, :mid]
    o_bias1[...] = norm_sums[4:5, :mid]
    o_gain1[...] = norm_sums[5:6, :mid]

    def own(value):
        return jnp.where(lax.rem(c, 2) == 1, value[:, m:], value[:, :m])

    lanes = rows(c // 2 * 2 * m, 2 * m)
    value = own(branch_sums[:, lanes])
    o_branch_bias[...] = value[0:3]
    o_branch_gain[...] = value[3:6]
    for j in range(3):
        value = own(head_grad[:, rows(j * SPLIT * m + c // 2 * 2 * m, 2 * m)])
        o_heads[j] = value[:columns]
    place = jnp.where(
        one_hot(512, 512, lambda i: i % 128 // 32 * 128 + 4 * (i % 32) + i // 128), 1.0, 0.0
    ).astype(bf16)
    for a in range(ROW_CLASSES):
        value = jnp.concatenate([predictions[a * COL_CLASSES + b] for b in range(COL_CLASSES)], axis=1)
        high = value.astype(bf16)
        rest = value - high.astype(f32)
        middle = rest.astype(bf16)
        low = (rest - middle.astype(f32)).astype(bf16)
        value = jnp.dot(jnp.concatenate([high, middle, low]), place, preferred_element_type=f32)
        value = value[:32] + (value[32:64] + value[64:])
        for r in range(4):
            o_predictions[:, 2 * r + a, :] = value[:columns, r * 128 : (r + 1) * 128]


def run_publish(columns, m, arrays):
    features, parts, dilated, expand, reduce = arrays[:5]
    n, mid = features.shape[1], reduce.shape[1]
    outs = [
        shape((columns, 8, 128), f32),
        shape(features.shape, bf16),
        shape(reduce.shape, f32),
        shape((1, mid), f32),
        shape((1, mid), f32),
        shape(dilated.shape, f32),
        shape((1, mid), f32),
        shape((1, mid), f32),
        shape(expand.shape, f32),
        shape((1, n), f32),
        shape((1, n), f32),
        shape(parts.shape[1:], f32),
        shape((3, m), f32),
        shape((3, m), f32),
        shape((3, columns, m), f32),
    ]
    vmem = pl.BlockSpec(memory_space=pltpu.VMEM)
    return pl.pallas_call(
        publish,
        out_shape=outs,
        in_specs=[vmem] * len(arrays),
        out_specs=[vmem] * len(outs),
        compiler_params=pltpu.CompilerParams(vmem_limit_bytes=VMEM_BYTES),
        name="publish",
    )(*arrays)


def fast_device(
    features,
    pixel_mask,
    reduce_weight,
    reduce_gain,
    reduce_bias,
    dilated_weight,
    dilated_gain,
    dilated_bias,
    expand_weight,
    expand_gain,
    expand_bias,
    aspp_weight,
    aspp_gain,
    aspp_bias,
    task_weight,
    cotangent,
):
    rows_here, width, local_in = features.shape
    pixels = rows_here * width
    local_mid = reduce_weight.shape[1]
    full_mid = dilated_weight.shape[3]
    branch_width = aspp_weight.shape[4]
    own_branch = task_weight.shape[1]
    outs_count = task_weight.shape[2]
    line = lambda v: v.reshape(1, -1)
    dilated_rows = dilated_weight.reshape(9 * local_mid, full_mid)
    (
        masked, reduce_rows, expand_cols, norm_one, valid, norm_two, act_two_full, taps_one, norm_three, trunk_class,
        stat_one, stat_two, stat_three, inputs_all, grad_full, predictions, head_grad, branch_sums, trunk_others, picks,
    ) = run_forward(
        1,
        features.reshape(pixels, local_in),
        pixel_mask,
        reduce_weight,
        expand_weight,
        line(reduce_gain),
        line(reduce_bias),
        task_weight.transpose(0, 2, 1),
        aspp_gain,
        aspp_bias,
        cotangent.transpose(2, 0, 1),
        dilated_rows,
        line(dilated_gain),
        line(dilated_bias),
        line(expand_gain),
        line(expand_bias),
        aspp_weight,
    )
    features_grad, aspp_parts, dilated_sum, expand_weight_grad, reduce_weight_grad, norm_sums = run_backward(
        2,
        [
            grad_full, trunk_class, trunk_others, aspp_weight, norm_three, masked, valid, expand_cols,
            line(expand_gain), line(expand_bias), norm_two, line(dilated_gain), line(dilated_bias), act_two_full,
            taps_one, dilated_rows, norm_one, line(reduce_gain), line(reduce_bias), reduce_rows, stat_one, stat_two,
            stat_three, picks, inputs_all,
        ],
    )
    (
        predictions, features_grad, reduce_weight_grad, reduce_gain_grad, reduce_bias_grad, dilated_weight_grad,
        dilated_gain_grad, dilated_bias_grad, expand_weight_grad, expand_gain_grad, expand_bias_grad, aspp_weight_grad,
        aspp_gain_grad, aspp_bias_grad, task_weight_grad,
    ) = run_publish(
        outs_count,
        own_branch,
        [
            features_grad, aspp_parts, dilated_sum, expand_weight_grad, reduce_weight_grad, norm_sums, predictions,
            head_grad, branch_sums,
        ],
    )
    return (
        predictions.transpose(1, 2, 0),
        features_grad.reshape(rows_here, width, local_in),
        reduce_weight_grad,
        reduce_gain_grad.reshape(-1),
        reduce_bias_grad.reshape(-1),
        dilated_weight_grad.reshape(3, 3, -1, local_mid).transpose(0, 1, 3, 2),
        dilated_gain_grad.reshape(-1),
        dilated_bias_grad.reshape(-1),
        expand_weight_grad,
        expand_gain_grad.reshape(-1),
        expand_bias_grad.reshape(-1),
        aspp_weight_grad.reshape(3, 3, 3, -1, local_in).transpose(0, 1, 2, 4, 3),
        aspp_gain_grad,
        aspp_bias_grad,
        task_weight_grad.transpose(0, 2, 1),
    )


def solution(mesh):
    placed = (
        P("pix", None, "ch"),
        P("pix", None),
        P(None, "ch"),
        P("ch"),
        P("ch"),
        P(None, None, "ch", None),
        P("ch"),
        P("ch"),
        P("ch", None),
        P("ch"),
        P("ch"),
        P(None, None, None, "ch", None),
        P(None, "ch"),
        P(None, "ch"),
        P(None, "ch", None),
        P("pix", None, None),
    )
    return jax.shard_map(
        fast_device if (mesh.shape["pix"], mesh.shape["ch"]) == (PHASES, 4) else on_device,
        mesh=mesh,
        in_specs=placed,
        out_specs=(
            P("pix", None, None),
            P("pix", None, "ch"),
            P("pix", "ch"),
            P("ch"),
            P("ch"),
            P(None, None, "ch", "pix"),
            P("ch"),
            P("ch"),
            P("ch", "pix"),
            P("ch"),
            P("ch"),
            P(None, None, None, "ch", "pix"),
            P(None, "ch"),
            P(None, "ch"),
            P(None, "ch", None),
        ),
        check_vma=False,
    )
```
